32 devices in a mesh: ep: 16 (over z, x, core), hs: 2 (over y).
Axes of the slice: x: 2, y: 2, z: 4, core: 2. Of those that a mesh axis runs over, the one named last changes fastest.
Arguments:
- tokens: bfloat16 [8192, 1024], P(('ep', 'hs')), may hold values from -6 to 6
- segment_ids: int32 [32, 256], P(('ep', 'hs')), may hold values from 0 to 3, never falling along the last dimension, each value on 1 to 128 neighbouring positions
- live_mask: int32 [32, 256], P(('ep', 'hs')), may hold values 0 or 1
- routes: int32 [8192, 8], P(('ep', 'hs')), may hold values from 0 to 15, all different within a row; in each aligned block of 256 rows (0 to 255, 256 to 511, ...) at most 256 rows name the same one
- attn_gain: float32 [1024], replicated, may hold values from 0.25 to 1.75
- w_query: bfloat16 [1024, 1024], replicated, may hold values from -0.1875 to 0.1875
- key_weight: bfloat16 [1024, 512], replicated, may hold values from -0.1875 to 0.1875
- value_weight: bfloat16 [1024, 512], replicated, may hold values from -0.1875 to 0.1875
- w_out: bfloat16 [1024, 1024], replicated, may hold values from -1 to 1
- moe_gain: float32 [1024], replicated, may hold values from 0.25 to 1.75
- router: bfloat16 [1024, 16], replicated, may hold values from -0.09375 to 0.09375
- w_gate: bfloat16 [16, 1024, 512], P('ep', None, 'hs'), may hold values from -0.1875 to 0.1875
- w_up: bfloat16 [16, 1024, 512], P('ep', None, 'hs'), may hold values from -0.1875 to 0.1875
- w_down: bfloat16 [16, 512, 1024], P('ep', 'hs'), may hold values from -0.75 to 0.75
- cotangent: bfloat16 [8192, 1024], P(('ep', 'hs')), may hold values from -6 to 6
Outputs:
- output: bfloat16 [8192, 1024], P(('ep', 'hs'))
- input_grad: float32 [8192, 1024], P(('ep', 'hs'))
- attn_gain_grad: float32 [1024], replicated
- query_grad: float32 [1024, 1024], replicated
- key_grad: float32 [1024, 512], replicated
- value_grad: float32 [1024, 512], replicated
- out_grad: float32 [1024, 1024], replicated
- moe_gain_grad: float32 [1024], replicated
- router_grad: float32 [1024, 16], replicated
- gate_grad: float32 [16, 1024, 512], P('ep', None, 'hs')
- up_grad: float32 [16, 1024, 512], P('ep', None, 'hs')
- down_grad: float32 [16, 512, 1024], P('ep', 'hs')
- expert_counts: int32 [16], replicated
The draws below stay inside these ranges and needn't reach their ends.
Inputs may be any that keep to these rules, and one draw needn't show every extreme that they name: `segment_ids`: document numbers never fall along a row; a document has at most 128 tokens, and one has exactly that many. `routes`: each token names 8 different experts. The 256 tokens of one row name one expert at most 256 times, a bound that some block reaches.
All inputs are finite; a program needn't handle non-finite values. No bound on the sum of `live_mask` on one device may be relied on, other than what follows from the above.
Results may differ from the reference program's by a relative error of at most 0.013.
The reference program's roundings to bfloat16 on the way count: a program that leaves them out, or rounds other values in their place, can miss the bound.
Values may be sent and summed in bfloat16 or wider, within the bound.
A program may use at most 384 MiB of HBM per device.

```python
import math
import jax
import jax.numpy as jnp
import numpy as np
from jax import lax

MODEL_WIDTH = 1024
QUERY_HEADS = 16
KEY_VALUE_HEADS = 8
HEAD_SIZE = 64
FF = 512
TOP = 8
TOK_DEV = 256
SEGS = 4
SEG_MOST = 128
EXPERTS = 16
ROWS = 32
TOKENS = 8192
CAP = 256
HGROUPS = 2


def place_ends(array, rng, least, largest):
    longest = array.shape.index(max(array.shape))
    spots = []
    for shift in (0, 1):
        where = [jax.random.randint(jax.random.fold_in(rng, axis), (), 0, length) for axis, length in enumerate(array.shape)]
        where[longest] = (where[longest] + shift) % array.shape[longest]
        spots.append(tuple(where))
    return array.at[spots[0]].set(least).at[spots[1]].set(largest)


def block_scale(stream_key, dims, cuts, low, largest):
    def one(position, blocks):
        draws = jax.random.uniform(jax.random.fold_in(jax.random.fold_in(stream_key, 6), position), (blocks,), jnp.float32, low / len(cuts), largest / len(cuts))
        return jnp.repeat(jnp.exp(draws), dims[position] // blocks).reshape((-1,) + (1,) * (len(dims) - position - 1))

    gain = one(*cuts[0])
    for cut in cuts[1:]:
        gain = gain * one(*cut)
    return gain


def length_profile(count, total, reach, lean):
    portions = [(1 << 20) // math.isqrt(standing ** lean) + 1 for standing in range(2, count + 1)]
    rest, holding = total - reach - (count - 1), [1] * (count - 1)
    while rest > 0:
        movable = [i for i in range(count - 1) if holding[i] < reach]
        whole, budget = sum([portions[i] for i in movable]), rest
        for i in movable:
            addition = min(reach - holding[i], max(1, budget * portions[i] // whole), rest)
            holding[i] = holding[i] + addition
            rest = rest - addition
    return np.array([reach] + holding)


def uneven_parts(own_key, number_of, total, limit, lean):
    if number_of == 2:
        one = jax.random.randint(own_key, (), max(1, total - limit), min(limit, total - 1) + 1)
        return jnp.stack([one, total - one])
    tallies = jnp.asarray(length_profile(number_of, total, limit, lean), jnp.int32)
    couples = (number_of - 1) // 2
    source_of, sink = tallies[1:1 + 2 * couples:2], tallies[2:2 + 2 * couples:2]
    room = jnp.minimum(source_of - 1, limit - sink)
    moved = jax.random.randint(jax.random.fold_in(own_key, 1), (couples,), 0, 1 << 20) % (room + 1)
    tallies = tallies.at[1:1 + 2 * couples:2].set(source_of - moved).at[2:2 + 2 * couples:2].set(sink + moved)
    return tallies[jax.random.permutation(jax.random.fold_in(own_key, 2), number_of)]


def deal_out(stream_key, own, number, rows, number_of, top, most, lean):
    sequence = jax.random.permutation(stream_key, number_of)
    crowded, ordinary = shares(number_of, rows * top, most, lean, True), shares(number_of, rows * top, most, lean, False)
    places = jnp.arange(number_of)

    def named(tallies, offset_by):
        used = int((tallies > 0).sum())
        fixed = max(1, used // 4)
        shifted = fixed + (places - fixed + offset_by * (used - fixed)) % max(1, number_of - fixed)
        return jnp.zeros((number_of,), jnp.int32).at[sequence[jnp.where(places < fixed, places, shifted)]].set(jnp.asarray(tallies, jnp.int32))

    tallies = jnp.where(number % 4 == 0, named(crowded, number // 4), named(ordinary, number - number // 4 - 1))
    mixed = jax.random.permutation(jax.random.fold_in(own, 3), number_of)
    source_of, sink = mixed[0:number_of // 2 * 2:2], mixed[1:number_of // 2 * 2:2]
    margin = jnp.minimum(tallies[source_of] - 1, most - tallies[sink]) // 2
    margin = jnp.where((source_of == sequence[0]) | (sink == sequence[0]) | (tallies[sink] == 0), 0, jnp.maximum(margin, 0))
    shifted = jax.random.randint(jax.random.fold_in(own, 4), (number_of // 2,), 0, 1 << 20) % (margin + 1)
    tallies = tallies.at[source_of].add(-shifted).at[sink].add(shifted)
    items = jnp.searchsorted(jnp.cumsum(tallies), jnp.arange(rows * top), side="right").astype(jnp.int32)
    listing = items.reshape(top, rows).T
    listing = listing[jax.random.permutation(jax.random.fold_in(own, 1), rows)]
    offset_by = jax.random.randint(jax.random.fold_in(own, 2), (rows, 1), 0, top)
    return jnp.take_along_axis(listing, (jnp.arange(top)[None, :] + offset_by) % top, axis=1)


def shares(amount, total, limit, slope, full):
    weights = [(1 << 20) // math.isqrt(standing ** slope) + 1 for standing in range(1, amount + 1)]
    largest = limit if full else min(limit, max(-(-total // amount), total * weights[0] // sum(weights)))
    least = 1 if total - largest >= amount - 1 else 0
    holding, rest = [largest] + [least] * (amount - 1), total - largest - least * (amount - 1)
    while rest > 0:
        free = [i for i in range(1, amount) if holding[i] < largest] or [i for i in range(1, amount) if holding[i] < limit]
        pool, remaining = sum([weights[i] for i in free]), rest
        for i in free:
            more = min(limit - holding[i], max(1, remaining * weights[i] // pool), rest)
            holding[i] = holding[i] + more
            rest = rest - more
    return np.array(holding)


def noise(stream_key, extent, spread, bound, shards=(), kind=jnp.bfloat16):
    drawn = spread * jax.random.normal(stream_key, extent, jnp.float32)
    if shards:
        drawn = drawn * block_scale(stream_key, extent, shards, -0.22, 0.18)
    return jnp.clip(drawn, -bound, bound).astype(kind)


def setup_inputs(seed: int = 0) -> dict:
    streams_of = jax.random.split(jax.random.key(seed), 16)
    tokens = noise(streams_of[0], (TOKENS, MODEL_WIDTH), 1.0, 6.0, ((0, 32),))
    segment_ids = jax.vmap(lambda own: jnp.searchsorted(jnp.cumsum(uneven_parts(own, SEGS, TOK_DEV, SEG_MOST, 2)), jnp.arange(TOK_DEV), side="right"))(jax.random.split(streams_of[1], ROWS)).reshape((ROWS, TOK_DEV)).astype(jnp.int32)
    live_mask = place_ends((jax.random.randint(streams_of[2], (ROWS, TOK_DEV), 0, 16) < 15).astype(jnp.int32), jax.random.fold_in(streams_of[2], 1), 0, 1)
    routes_keys = jax.random.split(jax.random.fold_in(streams_of[3], 1), TOKENS // TOK_DEV)
    routes_turns = jax.random.permutation(jax.random.fold_in(streams_of[3], 3), TOKENS // TOK_DEV)
    routes = jax.vmap(lambda own, number: deal_out(jax.random.fold_in(streams_of[3], 2), own, number, TOK_DEV, EXPERTS, TOP, CAP, 1))(routes_keys, routes_turns).reshape((TOKENS, TOP))
    attn_gain = jnp.clip(1.0 + 0.15 * jax.random.normal(streams_of[4], (MODEL_WIDTH,), jnp.float32), 0.25, 1.75)
    w_query = noise(streams_of[5], (MODEL_WIDTH, QUERY_HEADS * HEAD_SIZE), MODEL_WIDTH ** -0.5, 0.1875)
    key_weight = noise(streams_of[6], (MODEL_WIDTH, KEY_VALUE_HEADS * HEAD_SIZE), MODEL_WIDTH ** -0.5, 0.1875)
    value_weight = noise(streams_of[7], (MODEL_WIDTH, KEY_VALUE_HEADS * HEAD_SIZE), MODEL_WIDTH ** -0.5, 0.1875)
    w_out = noise(streams_of[8], (QUERY_HEADS * HEAD_SIZE, MODEL_WIDTH), (QUERY_HEADS * HEAD_SIZE // 32) ** -0.5, 1.0)
    moe_gain = jnp.clip(1.0 + 0.15 * jax.random.normal(streams_of[9], (MODEL_WIDTH,), jnp.float32), 0.25, 1.75)
    router = noise(streams_of[10], (MODEL_WIDTH, EXPERTS), (4 * MODEL_WIDTH) ** -0.5, 0.09375)
    w_gate = noise(streams_of[11], (EXPERTS, MODEL_WIDTH, FF), MODEL_WIDTH ** -0.5, 0.1875, ((0, 16), (2, 2)))
    w_up = noise(streams_of[12], (EXPERTS, MODEL_WIDTH, FF), MODEL_WIDTH ** -0.5, 0.1875, ((0, 16), (2, 2)))
    w_down = noise(streams_of[13], (EXPERTS, FF, MODEL_WIDTH), (FF // 8) ** -0.5, 0.75, ((0, 16), (1, 2)))
    cotangent = noise(streams_of[14], (TOKENS, MODEL_WIDTH), 1.0, 6.0, ((0, 32),))
    return dict(tokens=tokens, segment_ids=segment_ids, live_mask=live_mask, routes=routes, attn_gain=attn_gain, w_query=w_query, key_weight=key_weight, value_weight=value_weight, w_out=w_out, moe_gain=moe_gain, router=router, w_gate=w_gate, w_up=w_up, w_down=w_down, cotangent=cotangent)


@jax.custom_vjp
def lower_precision(v):
    return lax.optimization_barrier(v.astype(jnp.bfloat16)).astype(jnp.float32)

@jax.custom_vjp
def lower_precision_back(v):
    return v

def low_keep(v):
    return (lower_precision(v), None)

def low_pass(kept, grad):
    return (grad,)

def back_keep(v):
    return (v, None)

def back_low(kept, grad):
    return (lower_precision(grad),)
lower_precision.defvjp(low_keep, low_pass)
lower_precision_back.defvjp(back_keep, back_low)

def matrix_product(left, right):
    return jnp.dot(left, right, precision=lax.Precision.HIGHEST, preferred_element_type=jnp.float32)

def rms_scale(value_rows, norm_gain):
    inverse = lax.rsqrt(lax.optimization_barrier(jnp.mean(value_rows * value_rows, axis=-1, keepdims=True)) + 1e-05)
    return value_rows * inverse * norm_gain

def positions_of(segment):
    sequence_length = segment.shape[-1]
    indices = jnp.arange(sequence_length, dtype=jnp.int32)
    starts = jnp.concatenate([jnp.ones((1,), dtype=bool), segment[1:] != segment[:-1]])
    first_index = lax.cummax(jnp.where(starts, indices, 0), axis=0)
    return indices - first_index

def rotary_tables(positions, head_dim):
    half_dim = head_dim // 2
    frequency = 10000.0 ** (-(jnp.arange(half_dim, dtype=jnp.float32) * 2.0) / head_dim)
    angles = positions.astype(jnp.float32)[:, None] * frequency[None, :]
    return (jnp.cos(angles)[:, None, :], jnp.sin(angles)[:, None, :])

def rotary(heads, positions):
    half_dim = heads.shape[-1] // 2
    cosine_table, sine_table = rotary_tables(positions, heads.shape[-1])
    first_half = heads[..., :half_dim]
    second_half = heads[..., half_dim:]
    return jnp.concatenate([first_half * cosine_table - second_half * sine_table, second_half * cosine_table + first_half * sine_table], axis=-1)

def attend_one(packed):
    query_rows, key_rows, value_rows, segment, live_row = packed
    sequence_length = query_rows.shape[0]
    grouped_rows = query_rows.reshape(sequence_length, KEY_VALUE_HEADS, QUERY_HEADS // KEY_VALUE_HEADS, HEAD_SIZE)
    scores = jnp.einsum('qgrd,kgd->grqk', grouped_rows, key_rows, precision=lax.Precision.HIGHEST) * HEAD_SIZE ** (-0.5)
    scores = lower_precision_back(scores)
    indices = jnp.arange(sequence_length)
    allowed = (segment[:, None] == segment[None, :]) & (indices[None, :] <= indices[:, None]) & ((live_row[None, :] > 0) | (indices[None, :] == indices[:, None]))
    scores = jnp.where(allowed, scores, -1e+30)
    highest = lax.optimization_barrier(jnp.max(scores, axis=-1, keepdims=True))
    weights_exp = jnp.exp(scores - highest)
    probabilities = weights_exp / lax.optimization_barrier(jnp.sum(weights_exp, axis=-1, keepdims=True))
    mixed = jnp.einsum('grqk,kgd->qgrd', lower_precision(probabilities), value_rows, precision=lax.Precision.HIGHEST)
    return mixed.reshape(sequence_length, QUERY_HEADS * HEAD_SIZE)

def expert_apply(moe_in, gate_w, up_w, down_w):
    dispatched = lower_precision_back(moe_in)
    group_width = FF // HGROUPS
    total = jnp.zeros(moe_in.shape, jnp.float32)
    for group_index in range(HGROUPS):
        lower = group_index * group_width
        upper = lower + group_width
        copy_rows = lower_precision_back(dispatched)
        gate_part = lower_precision_back(matrix_product(copy_rows, gate_w[:, lower:upper]))
        up_part = lower_precision_back(matrix_product(copy_rows, up_w[:, lower:upper]))
        hidden = lower_precision(jax.nn.silu(gate_part) * up_part)
        total = total + lower_precision(matrix_product(hidden, down_w[lower:upper, :]))
    return lower_precision_back(lower_precision(total))

def block_forward(inputs, segments, lives, route_rows, weights):
    attn_gain, w_query, key_weight, value_weight, w_out, moe_gain, router, w_gate, w_up, w_down = weights
    sequence_count = inputs.shape[0]
    sequence_length = inputs.shape[1]
    flat_inputs = inputs.reshape(sequence_count * sequence_length, MODEL_WIDTH)
    normed_rows = lower_precision(rms_scale(flat_inputs, attn_gain))
    positions = jax.vmap(positions_of)(segments)
    query_rows = lower_precision_back(matrix_product(normed_rows, w_query)).reshape(sequence_count, sequence_length, QUERY_HEADS, HEAD_SIZE)
    key_rows = lower_precision_back(matrix_product(normed_rows, key_weight)).reshape(sequence_count, sequence_length, KEY_VALUE_HEADS, HEAD_SIZE)
    value_rows = lower_precision(lower_precision_back(matrix_product(normed_rows, value_weight))).reshape(sequence_count, sequence_length, KEY_VALUE_HEADS, HEAD_SIZE)
    query_rot = lower_precision(jax.vmap(rotary)(query_rows, positions))
    key_rot = lower_precision(jax.vmap(rotary)(key_rows, positions))
    mixed = lax.map(jax.checkpoint(attend_one), (query_rot, key_rot, value_rows, segments, lives))
    mixed = lower_precision(lower_precision_back(mixed.reshape(sequence_count * sequence_length, QUERY_HEADS * HEAD_SIZE)))
    middle = flat_inputs + lower_precision_back(matrix_product(mixed, w_out))
    moe_in = lower_precision(rms_scale(middle, moe_gain))
    logits = lower_precision_back(matrix_product(moe_in, router))
    route_hot = (route_rows[:, :, None] == jnp.arange(EXPERTS)[None, None, :]).astype(jnp.float32)
    chosen = lax.optimization_barrier(jnp.sum(route_hot * logits[:, None, :], axis=-1))
    live_flat = lives.reshape(-1).astype(jnp.float32)
    route_gates = jax.nn.softmax(chosen, axis=-1) * live_flat[:, None]
    dense_gates = lax.optimization_barrier(jnp.sum(route_gates[:, :, None] * route_hot, axis=1))

    def expert_step(running, packed):
        gate_w, up_w, down_w, column = packed
        return (running + column[:, None] * expert_apply(moe_in, gate_w, up_w, down_w), None)
    combined, unused = lax.scan(jax.checkpoint(expert_step), jnp.zeros(middle.shape, jnp.float32), (w_gate, w_up, w_down, dense_gates.T))
    return (middle + combined).reshape(sequence_count, sequence_length, MODEL_WIDTH)

def reference(tokens, segment_ids, live_mask, routes, attn_gain, w_query, key_weight, value_weight, w_out, moe_gain, router, w_gate, w_up, w_down, cotangent):
    weights = tuple((item.astype(jnp.float32) for item in (attn_gain, w_query, key_weight, value_weight, w_out, moe_gain, router, w_gate, w_up, w_down)))
    per_group = math.gcd(ROWS, max(1, 4096 // TOK_DEV))
    group_count = ROWS // per_group
    tokens_grouped = tokens.astype(jnp.float32).reshape(group_count, per_group, TOK_DEV, MODEL_WIDTH)
    cot_grouped = cotangent.astype(jnp.float32).reshape(group_count, per_group, TOK_DEV, MODEL_WIDTH)
    seg_grouped = segment_ids.reshape(group_count, per_group, TOK_DEV)
    live_grouped = live_mask.reshape(group_count, per_group, TOK_DEV)
    route_grouped = routes.reshape(group_count, per_group * TOK_DEV, TOP)

    def group_step(running_sum, packed):
        inputs, cot_part, segments, lives, route_rows = packed

        def forward(inputs, *weight_list):
            return block_forward(inputs, segments, lives, route_rows, weight_list)
        output, pullback = jax.vjp(forward, inputs, *weights)
        gradients = pullback(cot_part)
        running_sum = tuple((before + extra for before, extra in zip(running_sum, gradients[1:])))
        return (running_sum, (output, gradients[0]))
    zero_grads = tuple((jnp.zeros_like(item) for item in weights))
    totals, stacked = lax.scan(group_step, zero_grads, (tokens_grouped, cot_grouped, seg_grouped, live_grouped, route_grouped))
    outputs, input_grads = stacked
    route_hot = (routes[:, :, None] == jnp.arange(EXPERTS)[None, None, :]).astype(jnp.int32)
    expert_counts = lax.optimization_barrier(jnp.sum(route_hot * live_mask.reshape(-1)[:, None, None], axis=(0, 1))).astype(jnp.int32)
    return (outputs.reshape(TOKENS, MODEL_WIDTH).astype(jnp.bfloat16), input_grads.reshape(TOKENS, MODEL_WIDTH), totals[0], totals[1], totals[2], totals[3], totals[4], totals[5], totals[6], totals[7], totals[8], totals[9], expert_counts)
```

```python
import jax
import jax.numpy as jnp
from jax import lax
from jax.sharding import PartitionSpec as P

QUERY_HEADS = 16
KEY_VALUE_HEADS = 8
HEAD_SIZE = 64
TOP = 8


EPSILON = 1e-05


def rms_forward(value_rows, norm_gain):
    inverse = lax.rsqrt(jnp.mean(value_rows * value_rows, axis=-1, keepdims=True) + EPSILON)
    return (value_rows * inverse * norm_gain, inverse)


def rms_backward(value_rows, inverse, norm_gain, upstream):
    scaled = upstream * norm_gain
    gain_grad = jnp.sum(upstream * value_rows * inverse, axis=0)
    input_grad = inverse * (
        scaled
        - value_rows * inverse * inverse * jnp.mean(scaled * value_rows, axis=-1, keepdims=True)
    )
    return (input_grad, gain_grad)


def positions_of(segment):
    before = (segment[None, :] < segment[:, None]).astype(jnp.int32)
    return jnp.arange(segment.shape[-1], dtype=jnp.int32) - jnp.sum(before, axis=1)


def rotary_tables(positions, head_dim):
    half_dim = head_dim // 2
    frequency = 10000.0 ** (-(jnp.arange(half_dim, dtype=jnp.float32) * 2.0) / head_dim)
    angles = positions.astype(jnp.float32)[:, None] * frequency[None, :]
    return (jnp.cos(angles)[:, None, :], jnp.sin(angles)[:, None, :])


def rotary(heads, cosine_table, sine_table):
    half_dim = heads.shape[-1] // 2
    first_half = heads[..., :half_dim]
    second_half = heads[..., half_dim:]
    return jnp.concatenate(
        [
            first_half * cosine_table - second_half * sine_table,
            second_half * cosine_table + first_half * sine_table,
        ],
        axis=-1,
    )


def rotary_backward(grads, cosine_table, sine_table):
    half_dim = grads.shape[-1] // 2
    first_half = grads[..., :half_dim]
    second_half = grads[..., half_dim:]
    return jnp.concatenate(
        [
            first_half * cosine_table + second_half * sine_table,
            second_half * cosine_table - first_half * sine_table,
        ],
        axis=-1,
    )


def to_bf16(value):
    return lax.reduce_precision(value, 8, 7)


def expert_pass(rows, upstream, gates, gate_w, up_w, down_w):
    groups, model_dim, width = gate_w.shape
    gate_all = jnp.concatenate([gate_w[j] for j in range(groups)], axis=1)
    up_all = jnp.concatenate([up_w[j] for j in range(groups)], axis=1)
    down_all = down_w.reshape(groups * width, model_dim)
    gate_pre = jnp.dot(rows, gate_all, preferred_element_type=jnp.float32)
    up_pre = jnp.dot(rows, up_all, preferred_element_type=jnp.float32)
    sigmoid_part = jax.nn.sigmoid(gate_pre)
    activated = gate_pre * sigmoid_part
    hidden = (activated * up_pre).astype(jnp.bfloat16)
    total = jnp.zeros(rows.shape, jnp.float32)
    for j in range(groups):
        total = total + to_bf16(
            jnp.dot(hidden[:, j * width : (j + 1) * width], down_w[j], preferred_element_type=jnp.float32)
        )
    total = to_bf16(total)
    upstream_f = upstream.astype(jnp.float32)
    gate_upstream = jnp.sum(upstream_f * total, axis=-1)
    weighted = (gates[:, None] * total).astype(jnp.bfloat16)
    upstream_e = (gates[:, None] * upstream_f).astype(jnp.bfloat16)
    hidden_grad = jnp.einsum("td,fd->tf", upstream_e, down_all, preferred_element_type=jnp.float32)
    up_pre_grad = (hidden_grad * activated).astype(jnp.bfloat16)
    gate_pre_grad = (
        hidden_grad * up_pre * sigmoid_part * (1.0 + gate_pre * (1.0 - sigmoid_part))
    ).astype(jnp.bfloat16)
    down_grad = jnp.einsum("tf,td->fd", hidden, upstream_e, preferred_element_type=jnp.float32)
    gate_grad = jnp.einsum("td,tf->df", rows, gate_pre_grad, preferred_element_type=jnp.float32)
    up_grad = jnp.einsum("td,tf->df", rows, up_pre_grad, preferred_element_type=jnp.float32)
    back = jnp.zeros(rows.shape, jnp.float32)
    for j in range(groups):
        cut = slice(j * width, (j + 1) * width)
        back = back + to_bf16(
            jnp.einsum("tf,df->td", gate_pre_grad[:, cut], gate_w[j], preferred_element_type=jnp.float32)
            + jnp.einsum("tf,df->td", up_pre_grad[:, cut], up_w[j], preferred_element_type=jnp.float32)
        )
    return (weighted, back.astype(jnp.bfloat16), gate_upstream, gate_grad, up_grad, down_grad)


def local(
    tokens,
    segment_ids,
    live_mask,
    routes,
    attn_gain,
    w_query,
    key_weight,
    value_weight,
    w_out,
    moe_gain,
    router,
    w_gate,
    w_up,
    w_down,
    cotangent,
):
    sequence_length = tokens.shape[0]
    model_dim = tokens.shape[1]
    experts_all = router.shape[1]
    query_per_key_head = QUERY_HEADS // KEY_VALUE_HEADS
    score_scale = HEAD_SIZE ** (-0.5)
    upstream_all = lax.all_gather(cotangent, "ep", axis=0, tiled=True)
    gate_all = lax.all_gather(w_gate, "hs", axis=0, tiled=True)
    up_all = lax.all_gather(w_up, "hs", axis=0, tiled=True)
    down_all = lax.all_gather(w_down, "hs", axis=0, tiled=True)
    segment = segment_ids[0]
    live_row = live_mask[0]
    inputs = tokens.astype(jnp.float32)
    normed_rows, inverse_one = rms_forward(inputs, attn_gain)
    normed_rows_back = normed_rows.astype(jnp.bfloat16)
    query_pre = jnp.dot(normed_rows_back, w_query, preferred_element_type=jnp.float32).reshape(
        sequence_length, QUERY_HEADS, HEAD_SIZE
    )
    key_before_rotary = jnp.dot(
        normed_rows_back, key_weight, preferred_element_type=jnp.float32
    ).reshape(sequence_length, KEY_VALUE_HEADS, HEAD_SIZE)
    value_b = (
        jnp.dot(normed_rows_back, value_weight, preferred_element_type=jnp.float32)
        .astype(jnp.bfloat16)
        .reshape(sequence_length, KEY_VALUE_HEADS, HEAD_SIZE)
    )
    positions = positions_of(segment)
    cosine_table, sine_table = rotary_tables(positions, HEAD_SIZE)
    query_back_rows = rotary(query_pre, cosine_table, sine_table).astype(jnp.bfloat16)
    key_b = rotary(key_before_rotary, cosine_table, sine_table).astype(jnp.bfloat16)
    indices = jnp.arange(sequence_length)
    allowed = (
        (segment[:, None] == segment[None, :])
        & (indices[None, :] <= indices[:, None])
        & ((live_row[None, :] > 0) | (indices[None, :] == indices[:, None]))
    )
    grouped_rows = query_back_rows.reshape(
        sequence_length, KEY_VALUE_HEADS, query_per_key_head, HEAD_SIZE
    )
    scores = (
        jnp.einsum("qgrd,kgd->grqk", grouped_rows, key_b, preferred_element_type=jnp.float32)
        * score_scale
    )
    scores = jnp.where(allowed, scores, -1e30)
    highest = jnp.max(scores, axis=-1, keepdims=True)
    weights_exp = jnp.exp(scores - highest)
    denominator = jnp.sum(weights_exp, axis=-1, keepdims=True)
    log_total = highest + jnp.log(denominator)
    probabilities = weights_exp / denominator
    mixed = jnp.einsum(
        "grqk,kgd->qgrd",
        probabilities.astype(jnp.bfloat16),
        value_b,
        preferred_element_type=jnp.float32,
    )
    mixed_b = mixed.reshape(sequence_length, QUERY_HEADS * HEAD_SIZE).astype(jnp.bfloat16)
    middle = inputs + jnp.dot(mixed_b, w_out, preferred_element_type=jnp.float32)
    moe_normed, inverse_two = rms_forward(middle, moe_gain)
    moe_in = moe_normed.astype(jnp.bfloat16)
    logits = jnp.dot(moe_in, router, preferred_element_type=jnp.float32)
    route_hot = (routes[:, :, None] == jnp.arange(experts_all)[None, None, :]).astype(jnp.float32)
    chosen = jnp.sum(route_hot * logits[:, None, :], axis=-1)
    route_soft = jax.nn.softmax(chosen, axis=-1)
    live_column = live_row.astype(jnp.float32)[:, None]
    route_gates = route_soft * live_column
    counts_local = jnp.sum(route_hot * live_column[:, :, None], axis=(0, 1))
    dense_gates = jnp.sum(route_hot * route_gates[:, :, None], axis=1)
    rows_all = lax.all_gather(moe_in, "ep", axis=0, tiled=True)
    gates_all = lax.all_to_all(
        dense_gates.T.reshape(experts_all, 1, sequence_length), "ep", split_axis=0, concat_axis=1, tiled=True
    ).reshape(-1)
    weighted, back, gate_upstream_all, gate_w_grad, up_w_grad, down_w_grad = expert_pass(
        rows_all, upstream_all, gates_all, gate_all, up_all, down_all
    )
    combined = lax.psum_scatter(weighted, "ep", scatter_dimension=0, tiled=True).astype(jnp.float32)
    expert_input_grad = lax.psum_scatter(back, "ep", scatter_dimension=0, tiled=True).astype(jnp.float32)
    output = (middle + combined).astype(jnp.bfloat16)
    upstream = cotangent.astype(jnp.float32)
    gate_upstream_dense = lax.all_to_all(
        gate_upstream_all.reshape(experts_all, 1, sequence_length), "ep", split_axis=0, concat_axis=1, tiled=True
    ).reshape(experts_all, sequence_length).T
    gate_upstream = jnp.sum(route_hot * gate_upstream_dense[:, None, :], axis=-1)
    gate_w_grad = lax.psum_scatter(gate_w_grad, "hs", scatter_dimension=1, tiled=True)[None]
    up_w_grad = lax.psum_scatter(up_w_grad, "hs", scatter_dimension=1, tiled=True)[None]
    down_w_grad = lax.psum_scatter(down_w_grad, "hs", scatter_dimension=0, tiled=True)[None]
    soft_upstream = gate_upstream * live_column
    chosen_grad = route_soft * (
        soft_upstream - jnp.sum(route_soft * soft_upstream, axis=-1, keepdims=True)
    )
    logit_grad = jnp.sum(route_hot * chosen_grad[:, :, None], axis=1).astype(jnp.bfloat16)
    router_w_grad = jnp.einsum("td,te->de", moe_in, logit_grad, preferred_element_type=jnp.float32)
    moe_in_grad = expert_input_grad + jnp.einsum(
        "te,de->td", logit_grad, router, preferred_element_type=jnp.float32
    )
    middle_norm_grad, moe_gain_grad = rms_backward(middle, inverse_two, moe_gain, moe_in_grad)
    middle_grad = upstream + middle_norm_grad
    attn_grad_b = middle_grad.astype(jnp.bfloat16)
    out_w_grad = jnp.einsum("tm,td->md", mixed_b, attn_grad_b, preferred_element_type=jnp.float32)
    attention_mixed_grad = jnp.einsum(
        "td,md->tm", attn_grad_b, w_out, preferred_element_type=jnp.float32
    ).astype(jnp.bfloat16)
    attention_mixed_grad = attention_mixed_grad.reshape(
        sequence_length, KEY_VALUE_HEADS, query_per_key_head, HEAD_SIZE
    )
    scores_again = (
        jnp.einsum("qgrd,kgd->grqk", grouped_rows, key_b, preferred_element_type=jnp.float32)
        * score_scale
    )
    scores_again = jnp.where(allowed, scores_again, -1e30)
    probs_again = jnp.exp(scores_again - log_total)
    prob_grad = jnp.einsum(
        "qgrd,kgd->grqk", attention_mixed_grad, value_b, preferred_element_type=jnp.float32
    )
    value_per_head_grad = jnp.einsum(
        "grqk,qgrd->kgd",
        probs_again.astype(jnp.bfloat16),
        attention_mixed_grad,
        preferred_element_type=jnp.float32,
    )
    value_per_head_grad = value_per_head_grad.astype(jnp.bfloat16).reshape(
        sequence_length, KEY_VALUE_HEADS * HEAD_SIZE
    )
    row_delta = jnp.sum(probs_again * prob_grad, axis=-1, keepdims=True)
    score_grad = (probs_again * (prob_grad - row_delta)).astype(jnp.bfloat16)
    query_rot_grad = (
        jnp.einsum("grqk,kgd->qgrd", score_grad, key_b, preferred_element_type=jnp.float32)
        * score_scale
    )
    rotated_key_grad = (
        jnp.einsum("grqk,qgrd->kgd", score_grad, grouped_rows, preferred_element_type=jnp.float32)
        * score_scale
    )
    query_head_grad = (
        rotary_backward(
            query_rot_grad.reshape(sequence_length, QUERY_HEADS, HEAD_SIZE),
            cosine_table,
            sine_table,
        )
        .astype(jnp.bfloat16)
        .reshape(sequence_length, QUERY_HEADS * HEAD_SIZE)
    )
    key_head_grad = (
        rotary_backward(rotated_key_grad, cosine_table, sine_table)
        .astype(jnp.bfloat16)
        .reshape(sequence_length, KEY_VALUE_HEADS * HEAD_SIZE)
    )
    query_w_grad = jnp.einsum(
        "td,te->de", normed_rows_back, query_head_grad, preferred_element_type=jnp.float32
    )
    key_w_grad = jnp.einsum(
        "td,te->de", normed_rows_back, key_head_grad, preferred_element_type=jnp.float32
    )
    value_w_grad = jnp.einsum(
        "td,te->de", normed_rows_back, value_per_head_grad, preferred_element_type=jnp.float32
    )
    normed_grad = jnp.einsum(
        "te,de->td", query_head_grad, w_query, preferred_element_type=jnp.float32
    )
    normed_grad = normed_grad + jnp.einsum(
        "te,de->td", key_head_grad, key_weight, preferred_element_type=jnp.float32
    )
    normed_grad = normed_grad + jnp.einsum(
        "te,de->td", value_per_head_grad, value_weight, preferred_element_type=jnp.float32
    )
    input_norm_grad, attn_gain_grad = rms_backward(inputs, inverse_one, attn_gain, normed_grad)
    input_grad = middle_grad + input_norm_grad
    shared = lax.psum(
        (
            attn_gain_grad,
            query_w_grad,
            key_w_grad,
            value_w_grad,
            out_w_grad,
            moe_gain_grad,
            router_w_grad,
            counts_local,
        ),
        ("ep", "hs"),
    )
    return (
        output,
        input_grad,
        shared[0],
        shared[1],
        shared[2],
        shared[3],
        shared[4],
        shared[5],
        shared[6],
        gate_w_grad,
        up_w_grad,
        down_w_grad,
        shared[7].astype(jnp.int32),
    )


def solution(mesh):
    in_specs = (
        P(("ep", "hs"), None),
        P(("ep", "hs"), None),
        P(("ep", "hs"), None),
        P(("ep", "hs"), None),
        P(),
        P(),
        P(),
        P(),
        P(),
        P(),
        P(),
        P("ep", None, "hs"),
        P("ep", None, "hs"),
        P("ep", "hs", None),
        P(("ep", "hs"), None),
    )
    out_specs = (
        P(("ep", "hs"), None),
        P(("ep", "hs"), None),
        P(),
        P(),
        P(),
        P(),
        P(),
        P(),
        P(),
        P("ep", None, "hs"),
        P("ep", None, "hs"),
        P("ep", "hs", None),
        P(),
    )
    return jax.shard_map(local, mesh=mesh, in_specs=in_specs, out_specs=out_specs, check_vma=False)
```

```python
import functools

import jax
import jax.numpy as jnp
from jax import lax
from jax.experimental import pallas as pl
from jax.experimental.pallas import tpu as pltpu
from jax.sharding import PartitionSpec as P

QUERY_HEADS = 16
KEY_VALUE_HEADS = 8
HEAD_SIZE = 64
TOP = 8


EPSILON = 1e-05


def rms_forward(value_rows, norm_gain):
    inverse = lax.rsqrt(jnp.mean(value_rows * value_rows, axis=-1, keepdims=True) + EPSILON)
    return (value_rows * inverse * norm_gain, inverse)


def rms_backward(value_rows, inverse, norm_gain, upstream):
    scaled = upstream * norm_gain
    gain_grad = jnp.sum(upstream * value_rows * inverse, axis=0)
    input_grad = inverse * (
        scaled
        - value_rows * inverse * inverse * jnp.mean(scaled * value_rows, axis=-1, keepdims=True)
    )
    return (input_grad, gain_grad)


def positions_of(segment):
    before = (segment[None, :] < segment[:, None]).astype(jnp.int32)
    return jnp.arange(segment.shape[-1], dtype=jnp.int32) - jnp.sum(before, axis=1)


def rotary_tables(positions, head_dim):
    half_dim = head_dim // 2
    frequency = 10000.0 ** (-(jnp.arange(half_dim, dtype=jnp.float32) * 2.0) / head_dim)
    angles = positions.astype(jnp.float32)[:, None] * frequency[None, :]
    return (jnp.cos(angles)[:, None, :], jnp.sin(angles)[:, None, :])


def rotary(heads, cosine_table, sine_table):
    half_dim = heads.shape[-1] // 2
    first_half = heads[..., :half_dim]
    second_half = heads[..., half_dim:]
    return jnp.concatenate(
        [
            first_half * cosine_table - second_half * sine_table,
            second_half * cosine_table + first_half * sine_table,
        ],
        axis=-1,
    )


def rotary_backward(grads, cosine_table, sine_table):
    half_dim = grads.shape[-1] // 2
    first_half = grads[..., :half_dim]
    second_half = grads[..., half_dim:]
    return jnp.concatenate(
        [
            first_half * cosine_table + second_half * sine_table,
            second_half * cosine_table - first_half * sine_table,
        ],
        axis=-1,
    )


def to_bf16(value):
    return lax.reduce_precision(value, 8, 7)


def expert_pass(rows, upstream, gates, gate_w, up_w, down_w):
    groups, model_dim, width = gate_w.shape
    gate_all = jnp.concatenate([gate_w[j] for j in range(groups)], axis=1)
    up_all = jnp.concatenate([up_w[j] for j in range(groups)], axis=1)
    down_all = down_w.reshape(groups * width, model_dim)
    gate_pre = jnp.dot(rows, gate_all, preferred_element_type=jnp.float32)
    up_pre = jnp.dot(rows, up_all, preferred_element_type=jnp.float32)
    sigmoid_part = jax.nn.sigmoid(gate_pre)
    activated = gate_pre * sigmoid_part
    hidden = (activated * up_pre).astype(jnp.bfloat16)
    total = jnp.zeros(rows.shape, jnp.float32)
    for j in range(groups):
        total = total + to_bf16(
            jnp.dot(hidden[:, j * width : (j + 1) * width], down_w[j], preferred_element_type=jnp.float32)
        )
    total = to_bf16(total)
    upstream_f = upstream.astype(jnp.float32)
    gate_upstream = jnp.sum(upstream_f * total, axis=-1)
    weighted = (gates[:, None] * total).astype(jnp.bfloat16)
    upstream_e = (gates[:, None] * upstream_f).astype(jnp.bfloat16)
    hidden_grad = jnp.einsum("td,fd->tf", upstream_e, down_all, preferred_element_type=jnp.float32)
    up_pre_grad = (hidden_grad * activated).astype(jnp.bfloat16)
    gate_pre_grad = (
        hidden_grad * up_pre * sigmoid_part * (1.0 + gate_pre * (1.0 - sigmoid_part))
    ).astype(jnp.bfloat16)
    down_grad = jnp.einsum("tf,td->fd", hidden, upstream_e, preferred_element_type=jnp.float32)
    gate_grad = jnp.einsum("td,tf->df", rows, gate_pre_grad, preferred_element_type=jnp.float32)
    up_grad = jnp.einsum("td,tf->df", rows, up_pre_grad, preferred_element_type=jnp.float32)
    back = jnp.zeros(rows.shape, jnp.float32)
    for j in range(groups):
        cut = slice(j * width, (j + 1) * width)
        back = back + to_bf16(
            jnp.einsum("tf,df->td", gate_pre_grad[:, cut], gate_w[j], preferred_element_type=jnp.float32)
            + jnp.einsum("tf,df->td", up_pre_grad[:, cut], up_w[j], preferred_element_type=jnp.float32)
        )
    return (weighted, back.astype(jnp.bfloat16), gate_upstream, gate_grad, up_grad, down_grad)


def sum_halves(grad, dim):
    return lax.psum_scatter(
        grad.astype(jnp.bfloat16), "hs", scatter_dimension=dim, tiled=True
    ).astype(jnp.float32)


MESH = pl.DeviceIdType.MESH
UNIT = 16


def place():
    ep, hs = lax.axis_index("ep"), lax.axis_index("hs")
    return (ep // 4, (ep // 2) % 2, ep % 2, hs)


def device(z, x, c, y):
    return (z * 4 + x * 2 + c, y)


def greet(peers):
    barrier = pltpu.get_barrier_semaphore()
    for peer in peers:
        pl.semaphore_signal(barrier, inc=1, device_id=peer, device_id_type=MESH)
    pl.semaphore_wait(barrier, len(peers))


def sum_kernel(count, *refs):
    grads, small = refs[:count], refs[count]
    outs, small_out = refs[count + 1 : 2 * count + 1], refs[2 * count + 1]
    rest = refs[2 * count + 2 :]
    halves, totals, fulls = rest[:count], rest[count : 2 * count], rest[2 * count : 3 * count]
    firsts, seconds, lines = rest[3 * count : 4 * count], rest[4 * count : 5 * count], rest[5 * count : 6 * count]
    small_sum, small_in, send, recv, small_send, small_recv, local_sem = rest[6 * count :]
    z, x, c, y = place()
    sibling, beside, across = device(z, x, 1 - c, y), device(z, 1 - x, c, y), device(z, x, c, 1 - y)
    along = [device((z + k) % 4, x, c, y) for k in (1, 2, 3)]
    greet([sibling, beside, across] + along)
    bits = ((x, y), (y, x))
    partners = ((beside, across), (across, beside))

    def push(i, slot, source, target, peer):
        copy = pltpu.make_async_remote_copy(
            src_ref=source,
            dst_ref=target,
            send_sem=send.at[i, slot],
            recv_sem=recv.at[i, slot],
            device_id=peer,
            device_id_type=MESH,
        )
        copy.start()
        return copy

    def combine(i, target, start, length, terms):
        def body(u, carry):
            value = totals[i][start + u].astype(jnp.float32)
            for ref, base in terms:
                value = value + ref[base + u].astype(jnp.float32)
            target[0][target[1] + u] = value.astype(jnp.bfloat16)
            return carry

        lax.fori_loop(0, length, body, 0)

    copies = {}

    def stage(i, step):
        if step == 0:
            copies[i, 0] = [
                push(i, 0, grads[i].at[pl.ds((1 - c) * 32, 32)], halves[i], sibling)
            ]
        if step == 1:
            copies[i, 0][0].wait_recv()

            def body(u, carry):
                value = grads[i][c * 32 + u].astype(jnp.float32) + halves[i][u].astype(jnp.float32)
                totals[i][u] = value.astype(jnp.bfloat16)
                return carry

            lax.fori_loop(0, 32, body, 0)
            copies[i, 1] = [
                push(
                    i,
                    1 + part,
                    totals[i].at[pl.ds(part * 16 + (1 - bits[part][0]) * 8, 8)],
                    firsts[i].at[part],
                    partners[part][0],
                )
                for part in (0, 1)
            ]
        if step == 2:
            copies[i, 2] = []
            for part in (0, 1):
                copies[i, 1][part].wait_recv()
                base = part * 16 + bits[part][0] * 8
                combine(i, (totals[i], base), base, 8, [(firsts[i].at[part], 0)])
                copies[i, 2].append(
                    push(
                        i,
                        3 + part,
                        totals[i].at[pl.ds(base + (1 - bits[part][1]) * 4, 4)],
                        seconds[i].at[part],
                        partners[part][1],
                    )
                )
        if step == 3:
            copies[i, 3] = []
            for part in (0, 1):
                copies[i, 2][part].wait_recv()
                base = part * 16 + bits[part][0] * 8 + bits[part][1] * 4
                combine(i, (totals[i], base), base, 4, [(seconds[i].at[part], 0)])
                for k in (1, 2, 3):
                    copies[i, 3].append(
                        push(
                            i,
                            5 + part * 3 + k - 1,
                            totals[i].at[base + (z + k) % 4],
                            lines[i].at[part, k - 1],
                            along[k - 1],
                        )
                    )
        if step == 4:
            copies[i, 4] = []
            for part in (0, 1):
                for k in (1, 2, 3):
                    copies[i, 3][part * 3 + k - 1].wait_recv()
                base = part * 16 + bits[part][0] * 8 + bits[part][1] * 4
                combine(
                    i, (fulls[i], c * 32 + base + z), base + z, 1, [(lines[i].at[part], k) for k in (0, 1, 2)]
                )
                for k in (1, 2, 3):
                    piece = fulls[i].at[c * 32 + base + z]
                    copies[i, 4].append(push(i, 11 + part * 3 + k - 1, piece, piece, along[k - 1]))
        if step == 5:
            copies[i, 5] = []
            for part in (0, 1):
                for k in (1, 2, 3):
                    copies[i, 4][part * 3 + k - 1].wait_recv()
                piece = fulls[i].at[pl.ds(c * 32 + part * 16 + bits[part][0] * 8 + bits[part][1] * 4, 4)]
                copies[i, 5].append(push(i, 17 + part, piece, piece, partners[part][1]))
        if step == 6:
            copies[i, 6] = []
            for part in (0, 1):
                copies[i, 5][part].wait_recv()
                piece = fulls[i].at[pl.ds(c * 32 + part * 16 + bits[part][0] * 8, 8)]
                copies[i, 6].append(push(i, 19 + part, piece, piece, partners[part][0]))
        if step == 7:
            for part in (0, 1):
                copies[i, 6][part].wait_recv()
            piece = fulls[i].at[pl.ds(c * 32, 32)]
            copies[i, 7] = [push(i, 21, piece, piece, sibling)]
        if step == 8:
            copies[i, 7][0].wait_recv()
            done = pltpu.make_async_copy(fulls[i], outs[i], local_sem.at[i])
            done.start()
            copies[i, 8] = [done]

    def small_push(slot, peer, target):
        copy = pltpu.make_async_remote_copy(
            src_ref=small_sum.at[slot],
            dst_ref=small_in.at[target],
            send_sem=small_send.at[target],
            recv_sem=small_recv.at[target],
            device_id=peer,
            device_id_type=MESH,
        )
        copy.start()
        return copy

    def small_stage(step):
        if step == 0:
            small_sum[0] = small[...]
            copies["s", 0] = [small_push(0, sibling, 0)]
        if step in (1, 2):
            copies["s", step - 1][0].wait_recv()
            small_sum[step] = small_sum[step - 1] + small_in[step - 1]
            copies["s", step] = [small_push(step, (beside, across)[step - 1], step)]
        if step == 3:
            copies["s", 2][0].wait_recv()
            small_sum[3] = small_sum[2] + small_in[2]
            copies["s", 3] = []
            for k in (1, 2, 3):
                copy = pltpu.make_async_remote_copy(
                    src_ref=small_sum.at[3],
                    dst_ref=small_in.at[3 + z],
                    send_sem=small_send.at[2 + k],
                    recv_sem=small_recv.at[2 + k],
                    device_id=along[k - 1],
                    device_id_type=MESH,
                )
                copy.start()
                copies["s", 3].append(copy)
            small_in[3 + z] = small_sum[3]
        if step == 4:
            for copy in copies["s", 3]:
                copy.wait_recv()
            small_out[...] = (small_in[3] + small_in[4]) + (small_in[5] + small_in[6])

    for tick in range(count + 8):
        for i in range(count):
            if 0 <= tick - i <= 8:
                stage(i, tick - i)
        if tick <= 4:
            small_stage(tick)
    for key, group in copies.items():
        for copy in group:
            if key[0] != "s" and key[1] == 8:
                copy.wait()
            else:
                copy.wait_send()


def sum_everywhere(arrays, small):
    count = len(arrays)
    units = [a.reshape(a.shape[0] // UNIT, UNIT, a.shape[1]) for a in arrays]
    vmem = pl.BlockSpec(memory_space=pltpu.VMEM)

    def scratch(lead):
        return [pltpu.VMEM((*lead, UNIT, a.shape[1]), jnp.bfloat16) for a in arrays]

    out = pl.pallas_call(
        functools.partial(sum_kernel, count),
        out_shape=[jax.ShapeDtypeStruct(u.shape, u.dtype) for u in units]
        + [jax.ShapeDtypeStruct(small.shape, small.dtype)],
        in_specs=[vmem] * (count + 1),
        out_specs=[pl.BlockSpec(memory_space=pl.ANY)] * count + [vmem],
        scratch_shapes=[
            *scratch((32,)),
            *scratch((32,)),
            *scratch((64,)),
            *scratch((2, 8)),
            *scratch((2, 4)),
            *scratch((2, 3)),
            pltpu.VMEM((4, *small.shape), jnp.float32),
            pltpu.VMEM((7, *small.shape), jnp.float32),
            pltpu.SemaphoreType.DMA((count, 22)),
            pltpu.SemaphoreType.DMA((count, 22)),
            pltpu.SemaphoreType.DMA((6,)),
            pltpu.SemaphoreType.DMA((6,)),
            pltpu.SemaphoreType.DMA((count,)),
        ],
        compiler_params=pltpu.CompilerParams(
            collective_id=0, has_side_effects=True, vmem_limit_bytes=56 << 20
        ),
        name="sum_everywhere",
    )(*units, small)
    return [o.reshape(a.shape).astype(jnp.float32) for o, a in zip(out, arrays)] + [out[-1]]


def local(
    tokens,
    segment_ids,
    live_mask,
    routes,
    attn_gain,
    w_query,
    key_weight,
    value_weight,
    w_out,
    moe_gain,
    router,
    w_gate,
    w_up,
    w_down,
    cotangent,
):
    sequence_length = tokens.shape[0]
    model_dim = tokens.shape[1]
    experts_all = router.shape[1]
    query_per_key_head = QUERY_HEADS // KEY_VALUE_HEADS
    score_scale = HEAD_SIZE ** (-0.5)
    upstream_all = lax.all_gather(cotangent, "ep", axis=0, tiled=True)
    gate_all = lax.all_gather(w_gate, "hs", axis=0, tiled=True)
    up_all = lax.all_gather(w_up, "hs", axis=0, tiled=True)
    down_all = lax.all_gather(w_down, "hs", axis=0, tiled=True)
    segment = segment_ids[0]
    live_row = live_mask[0]
    inputs = tokens.astype(jnp.float32)
    normed_rows, inverse_one = rms_forward(inputs, attn_gain)
    normed_rows_back = normed_rows.astype(jnp.bfloat16)
    query_pre = jnp.dot(normed_rows_back, w_query, preferred_element_type=jnp.float32).reshape(
        sequence_length, QUERY_HEADS, HEAD_SIZE
    )
    key_before_rotary = jnp.dot(
        normed_rows_back, key_weight, preferred_element_type=jnp.float32
    ).reshape(sequence_length, KEY_VALUE_HEADS, HEAD_SIZE)
    value_b = (
        jnp.dot(normed_rows_back, value_weight, preferred_element_type=jnp.float32)
        .astype(jnp.bfloat16)
        .reshape(sequence_length, KEY_VALUE_HEADS, HEAD_SIZE)
    )
    positions = positions_of(segment)
    cosine_table, sine_table = rotary_tables(positions, HEAD_SIZE)
    query_back_rows = rotary(query_pre, cosine_table, sine_table).astype(jnp.bfloat16)
    key_b = rotary(key_before_rotary, cosine_table, sine_table).astype(jnp.bfloat16)
    indices = jnp.arange(sequence_length)
    allowed = (
        (segment[:, None] == segment[None, :])
        & (indices[None, :] <= indices[:, None])
        & ((live_row[None, :] > 0) | (indices[None, :] == indices[:, None]))
    )
    grouped_rows = query_back_rows.reshape(
        sequence_length, KEY_VALUE_HEADS, query_per_key_head, HEAD_SIZE
    )
    scores = (
        jnp.einsum("qgrd,kgd->grqk", grouped_rows, key_b, preferred_element_type=jnp.float32)
        * score_scale
    )
    scores = jnp.where(allowed, scores, -1e30)
    highest = jnp.max(scores, axis=-1, keepdims=True)
    weights_exp = jnp.exp(scores - highest)
    denominator = jnp.sum(weights_exp, axis=-1, keepdims=True)
    log_total = highest + jnp.log(denominator)
    probabilities = weights_exp / denominator
    mixed = jnp.einsum(
        "grqk,kgd->qgrd",
        probabilities.astype(jnp.bfloat16),
        value_b,
        preferred_element_type=jnp.float32,
    )
    mixed_b = mixed.reshape(sequence_length, QUERY_HEADS * HEAD_SIZE).astype(jnp.bfloat16)
    middle = inputs + jnp.dot(mixed_b, w_out, preferred_element_type=jnp.float32)
    moe_normed, inverse_two = rms_forward(middle, moe_gain)
    moe_in = moe_normed.astype(jnp.bfloat16)
    logits = jnp.dot(moe_in, router, preferred_element_type=jnp.float32)
    route_hot = (routes[:, :, None] == jnp.arange(experts_all)[None, None, :]).astype(jnp.float32)
    chosen = jnp.sum(route_hot * logits[:, None, :], axis=-1)
    route_soft = jax.nn.softmax(chosen, axis=-1)
    live_column = live_row.astype(jnp.float32)[:, None]
    route_gates = route_soft * live_column
    counts_local = jnp.sum(route_hot * live_column[:, :, None], axis=(0, 1))
    dense_gates = jnp.sum(route_hot * route_gates[:, :, None], axis=1)
    rows_all = lax.all_gather(moe_in, "ep", axis=0, tiled=True)
    gates_all = lax.all_to_all(
        dense_gates.T.reshape(experts_all, 1, sequence_length), "ep", split_axis=0, concat_axis=1, tiled=True
    ).reshape(-1)
    weighted, back, gate_upstream_all, gate_w_grad, up_w_grad, down_w_grad = expert_pass(
        rows_all, upstream_all, gates_all, gate_all, up_all, down_all
    )
    combined = lax.psum_scatter(weighted, "ep", scatter_dimension=0, tiled=True).astype(jnp.float32)
    expert_input_grad = lax.psum_scatter(back, "ep", scatter_dimension=0, tiled=True).astype(jnp.float32)
    output = (middle + combined).astype(jnp.bfloat16)
    upstream = cotangent.astype(jnp.float32)
    gate_upstream_dense = lax.all_to_all(
        gate_upstream_all.reshape(experts_all, 1, sequence_length), "ep", split_axis=0, concat_axis=1, tiled=True
    ).reshape(experts_all, sequence_length).T
    gate_upstream = jnp.sum(route_hot * gate_upstream_dense[:, None, :], axis=-1)
    gate_w_grad = sum_halves(gate_w_grad, 1)[None]
    up_w_grad = sum_halves(up_w_grad, 1)[None]
    down_w_grad = sum_halves(down_w_grad, 0)[None]
    soft_upstream = gate_upstream * live_column
    chosen_grad = route_soft * (
        soft_upstream - jnp.sum(route_soft * soft_upstream, axis=-1, keepdims=True)
    )
    logit_grad = jnp.sum(route_hot * chosen_grad[:, :, None], axis=1).astype(jnp.bfloat16)
    router_w_grad = jnp.einsum("td,te->de", moe_in, logit_grad, preferred_element_type=jnp.float32)
    moe_in_grad = expert_input_grad + jnp.einsum(
        "te,de->td", logit_grad, router, preferred_element_type=jnp.float32
    )
    middle_norm_grad, moe_gain_grad = rms_backward(middle, inverse_two, moe_gain, moe_in_grad)
    middle_grad = upstream + middle_norm_grad
    attn_grad_b = middle_grad.astype(jnp.bfloat16)
    out_w_grad = jnp.einsum("tm,td->md", mixed_b, attn_grad_b, preferred_element_type=jnp.float32)
    attention_mixed_grad = jnp.einsum(
        "td,md->tm", attn_grad_b, w_out, preferred_element_type=jnp.float32
    ).astype(jnp.bfloat16)
    attention_mixed_grad = attention_mixed_grad.reshape(
        sequence_length, KEY_VALUE_HEADS, query_per_key_head, HEAD_SIZE
    )
    scores_again = (
        jnp.einsum("qgrd,kgd->grqk", grouped_rows, key_b, preferred_element_type=jnp.float32)
        * score_scale
    )
    scores_again = jnp.where(allowed, scores_again, -1e30)
    probs_again = jnp.exp(scores_again - log_total)
    prob_grad = jnp.einsum(
        "qgrd,kgd->grqk", attention_mixed_grad, value_b, preferred_element_type=jnp.float32
    )
    value_per_head_grad = jnp.einsum(
        "grqk,qgrd->kgd",
        probs_again.astype(jnp.bfloat16),
        attention_mixed_grad,
        preferred_element_type=jnp.float32,
    )
    value_per_head_grad = value_per_head_grad.astype(jnp.bfloat16).reshape(
        sequence_length, KEY_VALUE_HEADS * HEAD_SIZE
    )
    row_delta = jnp.sum(probs_again * prob_grad, axis=-1, keepdims=True)
    score_grad = (probs_again * (prob_grad - row_delta)).astype(jnp.bfloat16)
    query_rot_grad = (
        jnp.einsum("grqk,kgd->qgrd", score_grad, key_b, preferred_element_type=jnp.float32)
        * score_scale
    )
    rotated_key_grad = (
        jnp.einsum("grqk,qgrd->kgd", score_grad, grouped_rows, preferred_element_type=jnp.float32)
        * score_scale
    )
    query_head_grad = (
        rotary_backward(
            query_rot_grad.reshape(sequence_length, QUERY_HEADS, HEAD_SIZE),
            cosine_table,
            sine_table,
        )
        .astype(jnp.bfloat16)
        .reshape(sequence_length, QUERY_HEADS * HEAD_SIZE)
    )
    key_head_grad = (
        rotary_backward(rotated_key_grad, cosine_table, sine_table)
        .astype(jnp.bfloat16)
        .reshape(sequence_length, KEY_VALUE_HEADS * HEAD_SIZE)
    )
    query_w_grad = jnp.einsum(
        "td,te->de", normed_rows_back, query_head_grad, preferred_element_type=jnp.float32
    )
    key_w_grad = jnp.einsum(
        "td,te->de", normed_rows_back, key_head_grad, preferred_element_type=jnp.float32
    )
    value_w_grad = jnp.einsum(
        "td,te->de", normed_rows_back, value_per_head_grad, preferred_element_type=jnp.float32
    )
    normed_grad = jnp.einsum(
        "te,de->td", query_head_grad, w_query, preferred_element_type=jnp.float32
    )
    normed_grad = normed_grad + jnp.einsum(
        "te,de->td", key_head_grad, key_weight, preferred_element_type=jnp.float32
    )
    normed_grad = normed_grad + jnp.einsum(
        "te,de->td", value_per_head_grad, value_weight, preferred_element_type=jnp.float32
    )
    input_norm_grad, attn_gain_grad = rms_backward(inputs, inverse_one, attn_gain, normed_grad)
    input_grad = middle_grad + input_norm_grad
    if lax.axis_size("ep") == 16 and lax.axis_size("hs") == 2:
        small = jnp.zeros((24, model_dim), jnp.float32)
        small = small.at[:experts_all].set(router_w_grad.T)
        small = small.at[16].set(attn_gain_grad).at[17].set(moe_gain_grad)
        small = small.at[18, :experts_all].set(counts_local)
        wide = [g.astype(jnp.bfloat16) for g in (out_w_grad, query_w_grad, key_w_grad, value_w_grad)]
        out_w_grad, query_w_grad, key_w_grad, value_w_grad, small = sum_everywhere(wide, small)
        router_w_grad = small[:experts_all].T
        attn_gain_grad, moe_gain_grad, counts = small[16], small[17], small[18, :experts_all]
    else:
        (
            attn_gain_grad,
            query_w_grad,
            key_w_grad,
            value_w_grad,
            out_w_grad,
            moe_gain_grad,
            router_w_grad,
            counts,
        ) = lax.psum(
            (
                attn_gain_grad,
                query_w_grad,
                key_w_grad,
                value_w_grad,
                out_w_grad,
                moe_gain_grad,
                router_w_grad,
                counts_local,
            ),
            ("ep", "hs"),
        )
    return (
        output,
        input_grad,
        attn_gain_grad,
        query_w_grad,
        key_w_grad,
        value_w_grad,
        out_w_grad,
        moe_gain_grad,
        router_w_grad,
        gate_w_grad,
        up_w_grad,
        down_w_grad,
        counts.astype(jnp.int32),
    )


def solution(mesh):
    in_specs = (
        P(("ep", "hs"), None),
        P(("ep", "hs"), None),
        P(("ep", "hs"), None),
        P(("ep", "hs"), None),
        P(),
        P(),
        P(),
        P(),
        P(),
        P(),
        P(),
        P("ep", None, "hs"),
        P("ep", None, "hs"),
        P("ep", "hs", None),
        P(("ep", "hs"), None),
    )
    out_specs = (
        P(("ep", "hs"), None),
        P(("ep", "hs"), None),
        P(),
        P(),
        P(),
        P(),
        P(),
        P(),
        P(),
        P("ep", None, "hs"),
        P("ep", None, "hs"),
        P("ep", "hs", None),
        P(),
    )
    return jax.shard_map(local, mesh=mesh, in_specs=in_specs, out_specs=out_specs, check_vma=False)
```

```python
import functools

import jax
import jax.numpy as jnp
from jax import lax
from jax.experimental import pallas as pl
from jax.experimental.pallas import tpu as pltpu
from jax.sharding import PartitionSpec as P

QUERY_HEADS = 16
KEY_VALUE_HEADS = 8
HEAD_SIZE = 64
TOP = 8


EPSILON = 1e-05


def rms_forward(value_rows, norm_gain):
    inverse = lax.rsqrt(jnp.mean(value_rows * value_rows, axis=-1, keepdims=True) + EPSILON)
    return (value_rows * inverse * norm_gain, inverse)


def rms_backward(value_rows, inverse, norm_gain, upstream):
    scaled = upstream * norm_gain
    gain_grad = jnp.sum(upstream * value_rows * inverse, axis=0)
    input_grad = inverse * (
        scaled
        - value_rows * inverse * inverse * jnp.mean(scaled * value_rows, axis=-1, keepdims=True)
    )
    return (input_grad, gain_grad)


def positions_of(segment):
    before = (segment[None, :] < segment[:, None]).astype(jnp.int32)
    return jnp.arange(segment.shape[-1], dtype=jnp.int32) - jnp.sum(before, axis=1)


def rotary_tables(positions, head_dim):
    half_dim = head_dim // 2
    frequency = 10000.0 ** (-(jnp.arange(half_dim, dtype=jnp.float32) * 2.0) / head_dim)
    angles = positions.astype(jnp.float32)[:, None] * frequency[None, :]
    return (jnp.cos(angles)[:, None, :], jnp.sin(angles)[:, None, :])


def rotary(heads, cosine_table, sine_table):
    half_dim = heads.shape[-1] // 2
    first_half = heads[..., :half_dim]
    second_half = heads[..., half_dim:]
    return jnp.concatenate(
        [
            first_half * cosine_table - second_half * sine_table,
            second_half * cosine_table + first_half * sine_table,
        ],
        axis=-1,
    )


def rotary_backward(grads, cosine_table, sine_table):
    half_dim = grads.shape[-1] // 2
    first_half = grads[..., :half_dim]
    second_half = grads[..., half_dim:]
    return jnp.concatenate(
        [
            first_half * cosine_table + second_half * sine_table,
            second_half * cosine_table - first_half * sine_table,
        ],
        axis=-1,
    )


def to_bf16(value):
    return lax.reduce_precision(value, 8, 7)


def expert_pass(rows, upstream, gates, gate_w, up_w, down_w):
    groups, model_dim, width = gate_w.shape
    gate_all = jnp.concatenate([gate_w[j] for j in range(groups)], axis=1)
    up_all = jnp.concatenate([up_w[j] for j in range(groups)], axis=1)
    down_all = down_w.reshape(groups * width, model_dim)
    gate_pre = jnp.dot(rows, gate_all, preferred_element_type=jnp.float32)
    up_pre = jnp.dot(rows, up_all, preferred_element_type=jnp.float32)
    sigmoid_part = jax.nn.sigmoid(gate_pre)
    activated = gate_pre * sigmoid_part
    hidden = (activated * up_pre).astype(jnp.bfloat16)
    total = jnp.zeros(rows.shape, jnp.float32)
    for j in range(groups):
        total = total + to_bf16(
            jnp.dot(hidden[:, j * width : (j + 1) * width], down_w[j], preferred_element_type=jnp.float32)
        )
    total = to_bf16(total)
    upstream_f = upstream.astype(jnp.float32)
    gate_upstream = jnp.sum(upstream_f * total, axis=-1)
    weighted = (gates[:, None] * total).astype(jnp.bfloat16)
    upstream_e = (gates[:, None] * upstream_f).astype(jnp.bfloat16)
    hidden_grad = jnp.einsum("td,fd->tf", upstream_e, down_all, preferred_element_type=jnp.float32)
    up_pre_grad = (hidden_grad * activated).astype(jnp.bfloat16)
    gate_pre_grad = (
        hidden_grad * up_pre * sigmoid_part * (1.0 + gate_pre * (1.0 - sigmoid_part))
    ).astype(jnp.bfloat16)
    down_grad = jnp.einsum("tf,td->fd", hidden, upstream_e, preferred_element_type=jnp.float32)
    gate_grad = jnp.einsum("td,tf->df", rows, gate_pre_grad, preferred_element_type=jnp.float32)
    up_grad = jnp.einsum("td,tf->df", rows, up_pre_grad, preferred_element_type=jnp.float32)
    back = jnp.zeros(rows.shape, jnp.float32)
    for j in range(groups):
        cut = slice(j * width, (j + 1) * width)
        back = back + to_bf16(
            jnp.einsum("tf,df->td", gate_pre_grad[:, cut], gate_w[j], preferred_element_type=jnp.float32)
            + jnp.einsum("tf,df->td", up_pre_grad[:, cut], up_w[j], preferred_element_type=jnp.float32)
        )
    return (weighted, back.astype(jnp.bfloat16), gate_upstream, gate_grad, up_grad, down_grad)


def sum_halves(grad, dim):
    return lax.psum_scatter(
        grad.astype(jnp.bfloat16), "hs", scatter_dimension=dim, tiled=True
    ).astype(jnp.float32)


MESH = pl.DeviceIdType.MESH
UNIT = 16


def place():
    ep, hs = lax.axis_index("ep"), lax.axis_index("hs")
    return (ep // 4, (ep // 2) % 2, ep % 2, hs)


def device(z, x, c, y):
    return (z * 4 + x * 2 + c, y)


def greet(peers):
    barrier = pltpu.get_barrier_semaphore()
    for peer in peers:
        pl.semaphore_signal(barrier, inc=1, device_id=peer, device_id_type=MESH)
    pl.semaphore_wait(barrier, len(peers))


def sum_kernel(count, *refs):
    grads, small = refs[:count], refs[count]
    outs, small_out = refs[count + 1 : 2 * count + 1], refs[2 * count + 1]
    rest = refs[2 * count + 2 :]
    halves, totals, fulls = rest[:count], rest[count : 2 * count], rest[2 * count : 3 * count]
    firsts, seconds, lines = rest[3 * count : 4 * count], rest[4 * count : 5 * count], rest[5 * count : 6 * count]
    small_sum, small_in, send, recv, small_send, small_recv, local_sem = rest[6 * count :]
    z, x, c, y = place()
    sibling, beside, across = device(z, x, 1 - c, y), device(z, 1 - x, c, y), device(z, x, c, 1 - y)
    along = [device((z + k) % 4, x, c, y) for k in (1, 2, 3)]
    greet([sibling, beside, across] + along)
    bits = ((x, y), (y, x))
    partners = ((beside, across), (across, beside))

    def push(i, slot, source, target, peer):
        copy = pltpu.make_async_remote_copy(
            src_ref=source,
            dst_ref=target,
            send_sem=send.at[i, slot],
            recv_sem=recv.at[i, slot],
            device_id=peer,
            device_id_type=MESH,
        )
        copy.start()
        return copy

    def combine(i, target, start, length, terms):
        def body(u, carry):
            value = totals[i][start + u].astype(jnp.float32)
            for ref, base in terms:
                value = value + ref[base + u].astype(jnp.float32)
            target[0][target[1] + u] = value.astype(jnp.bfloat16)
            return carry

        lax.fori_loop(0, length, body, 0)

    copies = {}

    def stage(i, step):
        if step == 0:
            copies[i, 0] = [
                push(i, 0, grads[i].at[pl.ds((1 - c) * 32, 32)], halves[i], sibling)
            ]
        if step == 1:
            copies[i, 0][0].wait_recv()

            def body(u, carry):
                value = grads[i][c * 32 + u].astype(jnp.float32) + halves[i][u].astype(jnp.float32)
                totals[i][u] = value.astype(jnp.bfloat16)
                return carry

            lax.fori_loop(0, 32, body, 0)
            copies[i, 1] = [
                push(
                    i,
                    1 + part,
                    totals[i].at[pl.ds(part * 16 + (1 - bits[part][0]) * 8, 8)],
                    firsts[i].at[part],
                    partners[part][0],
                )
                for part in (0, 1)
            ]
        if step == 2:
            copies[i, 2] = []
            for part in (0, 1):
                copies[i, 1][part].wait_recv()
                base = part * 16 + bits[part][0] * 8
                combine(i, (totals[i], base), base, 8, [(firsts[i].at[part], 0)])
                copies[i, 2].append(
                    push(
                        i,
                        3 + part,
                        totals[i].at[pl.ds(base + (1 - bits[part][1]) * 4, 4)],
                        seconds[i].at[part],
                        partners[part][1],
                    )
                )
        if step == 3:
            copies[i, 3] = []
            for part in (0, 1):
                copies[i, 2][part].wait_recv()
                base = part * 16 + bits[part][0] * 8 + bits[part][1] * 4
                combine(i, (totals[i], base), base, 4, [(seconds[i].at[part], 0)])
                for k in (1, 2, 3):
                    copies[i, 3].append(
                        push(
                            i,
                            5 + part * 3 + k - 1,
                            totals[i].at[base + (z + k) % 4],
                            lines[i].at[part, k - 1],
                            along[k - 1],
                        )
                    )
        if step == 4:
            copies[i, 4] = []
            for part in (0, 1):
                for k in (1, 2, 3):
                    copies[i, 3][part * 3 + k - 1].wait_recv()
                base = part * 16 + bits[part][0] * 8 + bits[part][1] * 4
                combine(
                    i, (fulls[i], c * 32 + base + z), base + z, 1, [(lines[i].at[part], k) for k in (0, 1, 2)]
                )
                for k in (1, 2, 3):
                    piece = fulls[i].at[c * 32 + base + z]
                    copies[i, 4].append(push(i, 11 + part * 3 + k - 1, piece, piece, along[k - 1]))
        if step == 5:
            copies[i, 5] = []
            for part in (0, 1):
                for k in (1, 2, 3):
                    copies[i, 4][part * 3 + k - 1].wait_recv()
                piece = fulls[i].at[pl.ds(c * 32 + part * 16 + bits[part][0] * 8 + bits[part][1] * 4, 4)]
                copies[i, 5].append(push(i, 17 + part, piece, piece, partners[part][1]))
        if step == 6:
            copies[i, 6] = []
            for part in (0, 1):
                copies[i, 5][part].wait_recv()
                piece = fulls[i].at[pl.ds(c * 32 + part * 16 + bits[part][0] * 8, 8)]
                copies[i, 6].append(push(i, 19 + part, piece, piece, partners[part][0]))
        if step == 7:
            for part in (0, 1):
                copies[i, 6][part].wait_recv()
            piece = fulls[i].at[pl.ds(c * 32, 32)]
            copies[i, 7] = [push(i, 21, piece, piece, sibling)]
        if step == 8:
            copies[i, 7][0].wait_recv()
            done = pltpu.make_async_copy(fulls[i], outs[i], local_sem.at[i])
            done.start()
            copies[i, 8] = [done]

    def small_push(slot, peer, target):
        copy = pltpu.make_async_remote_copy(
            src_ref=small_sum.at[slot],
            dst_ref=small_in.at[target],
            send_sem=small_send.at[target],
            recv_sem=small_recv.at[target],
            device_id=peer,
            device_id_type=MESH,
        )
        copy.start()
        return copy

    def small_stage(step):
        if step == 0:
            small_sum[0] = small[...]
            copies["s", 0] = [small_push(0, sibling, 0)]
        if step in (1, 2):
            copies["s", step - 1][0].wait_recv()
            small_sum[step] = small_sum[step - 1] + small_in[step - 1]
            copies["s", step] = [small_push(step, (beside, across)[step - 1], step)]
        if step == 3:
            copies["s", 2][0].wait_recv()
            small_sum[3] = small_sum[2] + small_in[2]
            copies["s", 3] = []
            for k in (1, 2, 3):
                copy = pltpu.make_async_remote_copy(
                    src_ref=small_sum.at[3],
                    dst_ref=small_in.at[3 + z],
                    send_sem=small_send.at[2 + k],
                    recv_sem=small_recv.at[2 + k],
                    device_id=along[k - 1],
                    device_id_type=MESH,
                )
                copy.start()
                copies["s", 3].append(copy)
            small_in[3 + z] = small_sum[3]
        if step == 4:
            for copy in copies["s", 3]:
                copy.wait_recv()
            small_out[...] = (small_in[3] + small_in[4]) + (small_in[5] + small_in[6])

    for tick in range(count + 8):
        for i in range(count):
            if 0 <= tick - i <= 8:
                stage(i, tick - i)
        if tick <= 4:
            small_stage(tick)
    for key, group in copies.items():
        for copy in group:
            if key[0] != "s" and key[1] == 8:
                copy.wait()
            else:
                copy.wait_send()


def sum_everywhere(arrays, small):
    count = len(arrays)
    units = [a.reshape(a.shape[0] // UNIT, UNIT, a.shape[1]) for a in arrays]
    vmem = pl.BlockSpec(memory_space=pltpu.VMEM)

    def scratch(lead):
        return [pltpu.VMEM((*lead, UNIT, a.shape[1]), jnp.bfloat16) for a in arrays]

    out = pl.pallas_call(
        functools.partial(sum_kernel, count),
        out_shape=[jax.ShapeDtypeStruct(u.shape, u.dtype) for u in units]
        + [jax.ShapeDtypeStruct(small.shape, small.dtype)],
        in_specs=[vmem] * (count + 1),
        out_specs=[pl.BlockSpec(memory_space=pl.ANY)] * count + [vmem],
        scratch_shapes=[
            *scratch((32,)),
            *scratch((32,)),
            *scratch((64,)),
            *scratch((2, 8)),
            *scratch((2, 4)),
            *scratch((2, 3)),
            pltpu.VMEM((4, *small.shape), jnp.float32),
            pltpu.VMEM((7, *small.shape), jnp.float32),
            pltpu.SemaphoreType.DMA((count, 22)),
            pltpu.SemaphoreType.DMA((count, 22)),
            pltpu.SemaphoreType.DMA((6,)),
            pltpu.SemaphoreType.DMA((6,)),
            pltpu.SemaphoreType.DMA((count,)),
        ],
        compiler_params=pltpu.CompilerParams(
            collective_id=0, has_side_effects=True, vmem_limit_bytes=56 << 20
        ),
        name="sum_everywhere",
    )(*units, small)
    return [o.reshape(a.shape).astype(jnp.float32) for o, a in zip(out, arrays)] + [out[-1]]


def contract(left, right, left_dim, right_dim):
    return lax.dot_general(
        left, right, (((left_dim,), (right_dim,)), ((), ())), preferred_element_type=jnp.float32
    )


def expert_kernel(
    rows_in,
    upstream_in,
    gates_in,
    gate_w,
    up_w,
    down_w,
    weighted_out,
    back_out,
    slope_out,
    gate_out,
    up_out,
    down_out,
    streams,
    gates,
    slopes,
    slopes_in,
    w_gate,
    w_up,
    w_down,
    sums,
    partial,
    from_sibling,
    from_line,
    staged,
    returned,
    load_sem,
    gather_send,
    gather_recv,
    gate_send,
    gate_recv,
    slope_send,
    slope_recv,
    weight_send,
    weight_recv,
    pair_send,
    pair_recv,
    line_send,
    line_recv,
    grad_send,
    grad_recv,
):
    z, x, c, y = place()
    near, far, last = 1 + z % 2, (2 + 3 * z) % 5, 3 - 3 * (z // 2)
    middle = (z == 1) | (z == 2)
    edge = (z == 0) | (z == 3)
    sibling, beside, across = device(z, x, 1 - c, y), device(z, 1 - x, c, y), device(z, x, c, 1 - y)
    corner = device(z, 1 - x, c, 1 - y)
    line = [((z + k) % 4, (c + d) % 2) for k in range(4) for d in range(2) if k or d]
    greet([device(a, x, b, y) for a, b in line] + [beside, across, corner])

    def chip(k):
        half = z // 2
        inner = z + half * (3 - 2 * z)
        spot = k + inner * (1 - 3 * (k // 2) + 2 * (k // 3))
        return spot + half * (3 - 2 * spot)

    def remote(source, target, send, recv, peer):
        return pltpu.make_async_remote_copy(
            src_ref=source, dst_ref=target, send_sem=send, recv_sem=recv, device_id=peer, device_id_type=MESH
        )

    own = [
        pltpu.make_async_copy(ref, streams.at[s, z, c], load_sem.at[s])
        for s, ref in enumerate((rows_in, upstream_in))
    ]
    gates_own = pltpu.make_async_copy(gates_in.at[z, c], gates.at[z, c], load_sem.at[2])
    weights_own = [
        pltpu.make_async_copy(ref, held.at[x, y], load_sem.at[3 + a])
        for a, (ref, held) in enumerate(((gate_w, w_gate), (up_w, w_up), (down_w, w_down)))
    ]
    for copy in (*own, gates_own, *weights_own):
        copy.start()

    def gather(s, block, slot, peer):
        piece = streams.at[s, block, c]
        return remote(piece, piece, gather_send.at[s, slot], gather_recv.at[s, block, c], peer)

    def arrive(s, block, core):
        piece = streams.at[s, block, core]
        pltpu.make_async_copy(piece, piece, gather_recv.at[s, block, core]).wait()

    for s in (0, 1):
        own[s].wait()
        gather(s, z, 0, device(near, x, c, y)).start()
        gather(s, z, 1, device(far, x, c, y)).start()
        gather(s, z, 2, sibling).start()
    gate_copies = [
        remote(
            gates_in.at[a, b], gates.at[z, c], gate_send.at[n], gate_recv.at[z, c], device(a, x, b, y)
        )
        for n, (a, b) in enumerate(line)
    ]
    for copy in gate_copies:
        copy.start()
    weight_copies = []
    for a, held in enumerate((w_gate, w_up, w_down)):
        weights_own[a].wait()
        for n, peer in enumerate((across, beside, corner)):
            piece = held.at[x, y]
            weight_copies.append(
                remote(piece, piece, weight_send.at[n, a], weight_recv.at[x, y, a], peer)
            )
    for n in range(3):
        for a in range(3):
            weight_copies[a * 3 + n].start()

    def weights_here(expert, group):
        for a, held in enumerate((w_gate, w_up, w_down)):
            piece = held.at[expert, group]
            pltpu.make_async_copy(piece, piece, weight_recv.at[expert, group, a]).wait()

    def zero(u, carry):
        for e in (0, 1):
            for a in range(3):
                sums[e, a, u // 16, pl.ds(pl.multiple_of((u % 16) * 16, 16), 16), :] = jnp.zeros(
                    (16, 1024), jnp.float32
                )
        return carry

    lax.fori_loop(0, 32, zero, 0)

    def handle(k):
        block = chip(k)
        for s in (0, 1):
            arrive(s, block, c)
            gather(s, block, 4 + k, sibling).start()
            if k != 2:

                @pl.when(middle)
                def _():
                    gather(s, block, 2 + (k + 1) // 2, device(far, x, c, y)).start()

    handle(1)
    gates_own.wait()
    for a, b in line:
        pltpu.make_async_copy(gates.at[a, b], gates.at[a, b], gate_recv.at[a, b]).wait()
    weights_here(x, 1 - y)
    row_id = lax.broadcasted_iota(jnp.int32, (256, 256), 0)
    lane_id = lax.broadcasted_iota(jnp.int32, (256, 256), 1)

    def compute(expert, block, core, first):
        diagonal = row_id == lane_id
        gate_row = gates[block, core, pl.ds(expert, 1), :]
        gate = jnp.sum(jnp.where(diagonal, gate_row, 0.0), axis=1, keepdims=True)
        rows = streams[0, block, core]
        total = jnp.zeros((256, 1024), jnp.float32)
        kept = []
        for j in (0, 1):
            gate_pre = contract(rows, w_gate[expert, j], 1, 0)
            up_pre = contract(rows, w_up[expert, j], 1, 0)
            sigmoid_part = jax.nn.sigmoid(gate_pre)
            activated = gate_pre * sigmoid_part
            hidden = (activated * up_pre).astype(jnp.bfloat16)
            part = contract(hidden, w_down[expert, j], 1, 0)
            total = total + part.astype(jnp.bfloat16).astype(jnp.float32)
            inner = up_pre * sigmoid_part * (1.0 + gate_pre * (1.0 - sigmoid_part))
            kept.append((activated, inner, hidden))
        total = total.astype(jnp.bfloat16).astype(jnp.float32)
        upstream = streams[1, block, core].astype(jnp.float32)
        slope = jnp.sum(upstream * total, axis=1, keepdims=True)
        slopes[block, core, pl.ds(expert, 1), :] = jnp.sum(
            jnp.where(diagonal, slope, 0.0), axis=0, keepdims=True
        )
        weighted = gate * total
        if not first:
            weighted = weighted + partial[1, block, core].astype(jnp.float32)
        partial[1, block, core] = weighted.astype(jnp.bfloat16)
        upstream = (gate * upstream).astype(jnp.bfloat16)
        back = jnp.zeros((256, 1024), jnp.float32)
        for j in (0, 1):
            activated, inner, hidden = kept[j]
            hidden_grad = contract(upstream, w_down[expert, j], 1, 1)
            up_grad = (hidden_grad * activated).astype(jnp.bfloat16)
            gate_grad = (hidden_grad * inner).astype(jnp.bfloat16)
            sums[expert, 0, j] += contract(gate_grad, rows, 0, 0)
            sums[expert, 1, j] += contract(up_grad, rows, 0, 0)
            sums[expert, 2, j] += contract(hidden, upstream, 0, 0)
            step = contract(gate_grad, w_gate[expert, j], 1, 1) + contract(up_grad, w_up[expert, j], 1, 1)
            back = back + step.astype(jnp.bfloat16).astype(jnp.float32)
        if not first:
            back = back + partial[0, block, core].astype(jnp.float32)
        partial[0, block, core] = back.astype(jnp.bfloat16)

    def first_pass(i, carry):
        k = i // 2
        block, core = chip(k), (c + i) % 2

        @pl.when(i == 1)
        def _():
            for s in (0, 1):
                arrive(s, z, 1 - c)

        @pl.when((i == 2) & middle | (i == 4) & edge)
        def _():
            handle(2)

        @pl.when((i == 4) & middle | (i == 6) & edge)
        def _():
            handle(3)

        @pl.when((i % 2 == 1) & (i > 1))
        def _():
            for s in (0, 1):
                arrive(s, block, 1 - c)

        compute(x, block, core, True)
        return carry

    lax.fori_loop(0, 8, first_pass, 0)

    def stage_grads(place_at, expert, group):
        def body(u, carry):
            at = pl.ds(pl.multiple_of(u * 32, 32), 32)
            for a in range(3):
                staged[place_at, a, at, :] = sums[expert, a, group, at, :].astype(jnp.bfloat16)
            return carry

        lax.fori_loop(0, 8, body, 0)

    def grad_copy(n, a, peer):
        return remote(staged.at[n, a], returned.at[n, a], grad_send.at[n, a], grad_recv.at[n, a], peer)

    stage_grads(0, x, 1 - y)
    for a in range(3):
        grad_copy(0, a, across).start()
    weights_here(1 - x, y)
    weights_here(1 - x, 1 - y)

    def pair_copy(s, block):
        return remote(
            partial.at[s, block, 1 - c],
            from_sibling.at[s, block],
            pair_send.at[s, block],
            pair_recv.at[s, block],
            sibling,
        )

    def line_copy(s, block):
        return remote(
            partial.at[s, block, c],
            from_line.at[s, z],
            line_send.at[s, block],
            line_recv.at[s, z],
            device(block, x, c, y),
        )

    def second_pass(i, carry):
        block, core = chip(3 - i // 2), (c + 1 + i) % 2
        compute(1 - x, block, core, False)

        @pl.when(i % 2 == 0)
        def _():
            for s in (0, 1):
                pair_copy(s, block).start()

        @pl.when((i % 2 == 1) & (i < 6))
        def _():
            for s in (0, 1):
                pair_copy(s, block).wait_recv()

                def body(u, inner_carry):
                    at = pl.ds(pl.multiple_of(u * 32, 32), 32)
                    value = partial[s, block, c, at, :].astype(jnp.float32)
                    value = value + from_sibling[s, block, at, :].astype(jnp.float32)
                    partial[s, block, c, at, :] = value.astype(jnp.bfloat16)
                    return inner_carry

                lax.fori_loop(0, 8, body, 0)
                line_copy(s, block).start()

        return carry

    lax.fori_loop(0, 8, second_pass, 0)
    stage_grads(1, 1 - x, y)
    for a in range(3):
        grad_copy(1, a, beside).start()
    stage_grads(2, 1 - x, 1 - y)
    for a in range(3):
        grad_copy(2, a, corner).start()
    slope_copies = [
        remote(
            slopes.at[a, b], slopes_in.at[z, c], slope_send.at[n], slope_recv.at[z, c], device(a, x, b, y)
        )
        for n, (a, b) in enumerate(line)
    ]
    for copy in slope_copies:
        copy.start()
    slopes_in[z, c] = slopes[z, c]
    for s in (0, 1):
        pair_copy(s, z).wait_recv()
        for k in (1, 2, 3):
            source = chip(k)
            pltpu.make_async_copy(from_line.at[s, source], from_line.at[s, source], line_recv.at[s, source]).wait()

        def body(u, carry):
            at = pl.ds(pl.multiple_of(u * 32, 32), 32)
            value = partial[s, z, c, at, :].astype(jnp.float32)
            value = value + from_sibling[s, z, at, :].astype(jnp.float32)
            for k in (1, 2, 3):
                value = value + from_line[s, chip(k), at, :].astype(jnp.float32)
            (back_out, weighted_out)[s][at, :] = value
            return carry

        lax.fori_loop(0, 8, body, 0)
    for a, b in line:
        pltpu.make_async_copy(slopes_in.at[a, b], slopes_in.at[a, b], slope_recv.at[a, b]).wait()
    slope_out[...] = slopes_in[...]
    stores = []
    for a, out in enumerate((gate_out, up_out, down_out)):
        for n, peer in enumerate((across, beside, corner)):
            grad_copy(n, a, peer).wait_recv()

        def body(u, carry):
            at = pl.ds(pl.multiple_of(u * 32, 32), 32)
            value = sums[x, a, y, at, :]
            for n in range(3):
                value = value + returned[n, a, at, :].astype(jnp.float32)
            sums[x, a, y, at, :] = value
            return carry

        lax.fori_loop(0, 8, body, 0)
        stores.append(pltpu.make_async_copy(sums.at[x, a, y], out, load_sem.at[a]))
        stores[a].start()
    for s in (0, 1):
        gather(s, z, 0, device(near, x, c, y)).wait_send()
        gather(s, z, 1, device(far, x, c, y)).wait_send()
        gather(s, z, 2, sibling).wait_send()
        for k in (1, 2, 3):
            gather(s, chip(k), 4 + k, sibling).wait_send()
            line_copy(s, chip(k)).wait_send()

        @pl.when(middle)
        def _():
            for k in (1, 3):
                gather(s, chip(k), 2 + (k + 1) // 2, device(far, x, c, y)).wait_send()

        for k in range(4):
            pair_copy(s, chip(k)).wait_send()
    for copy in (*gate_copies, *weight_copies, *slope_copies):
        copy.wait_send()
    for n, peer in enumerate((across, beside, corner)):
        for a in range(3):
            grad_copy(n, a, peer).wait_send()
    for copy in stores:
        copy.wait()


def expert_part(rows, upstream, gates, gate_w, up_w, down_w):
    tokens, model_dim = rows.shape
    width = gate_w.shape[1]
    vmem, anywhere = pl.BlockSpec(memory_space=pltpu.VMEM), pl.BlockSpec(memory_space=pl.ANY)
    f32, bf16, dma = jnp.float32, jnp.bfloat16, pltpu.SemaphoreType.DMA
    grad = jax.ShapeDtypeStruct((width, model_dim), f32)
    by_owner = gates.T.reshape(4, 2, 2, tokens).swapaxes(1, 2)
    by_owner = jnp.pad(by_owner, ((0, 0), (0, 0), (0, 6), (0, 0)))
    weighted, back, slopes, gate_grad, up_grad, down_grad = pl.pallas_call(
        expert_kernel,
        out_shape=[
            jax.ShapeDtypeStruct((tokens, model_dim), f32),
            jax.ShapeDtypeStruct((tokens, model_dim), f32),
            jax.ShapeDtypeStruct((4, 2, 8, tokens), f32),
            grad,
            grad,
            grad,
        ],
        in_specs=[anywhere, anywhere, vmem, anywhere, anywhere, anywhere],
        out_specs=[vmem, vmem, vmem, anywhere, anywhere, anywhere],
        scratch_shapes=[
            pltpu.VMEM((2, 4, 2, tokens, model_dim), bf16),
            pltpu.VMEM((4, 2, 8, tokens), f32),
            pltpu.VMEM((4, 2, 8, tokens), f32),
            pltpu.VMEM((4, 2, 8, tokens), f32),
            pltpu.VMEM((2, 2, model_dim, width), bf16),
            pltpu.VMEM((2, 2, model_dim, width), bf16),
            pltpu.VMEM((2, 2, width, model_dim), bf16),
            pltpu.VMEM((2, 3, 2, width, model_dim), f32),
            pltpu.VMEM((2, 4, 2, tokens, model_dim), bf16),
            pltpu.VMEM((2, 4, tokens, model_dim), bf16),
            pltpu.VMEM((2, 4, tokens, model_dim), bf16),
            pltpu.VMEM((3, 3, width, model_dim), bf16),
            pltpu.VMEM((3, 3, width, model_dim), bf16),
            dma((6,)),
            dma((2, 8)),
            dma((2, 4, 2)),
            dma((7,)),
            dma((4, 2)),
            dma((7,)),
            dma((4, 2)),
            dma((3, 3)),
            dma((2, 2, 3)),
            dma((2, 4)),
            dma((2, 4)),
            dma((2, 4)),
            dma((2, 4)),
            dma((3, 3)),
            dma((3, 3)),
        ],
        compiler_params=pltpu.CompilerParams(
            collective_id=1, has_side_effects=True, vmem_limit_bytes=62 << 20
        ),
        name="expert_part",
    )(rows, upstream, by_owner, gate_w, up_w, down_w)
    slopes = slopes[:, :, :2].swapaxes(1, 2).reshape(gates.shape[1], tokens).T
    return (weighted, back, slopes, gate_grad.T, up_grad.T, down_grad)


def local(
    tokens,
    segment_ids,
    live_mask,
    routes,
    attn_gain,
    w_query,
    key_weight,
    value_weight,
    w_out,
    moe_gain,
    router,
    w_gate,
    w_up,
    w_down,
    cotangent,
):
    sequence_length = tokens.shape[0]
    model_dim = tokens.shape[1]
    experts_all = router.shape[1]
    query_per_key_head = QUERY_HEADS // KEY_VALUE_HEADS
    score_scale = HEAD_SIZE ** (-0.5)
    special = lax.axis_size("ep") == 16 and lax.axis_size("hs") == 2
    segment = segment_ids[0]
    live_row = live_mask[0]
    inputs = tokens.astype(jnp.float32)
    normed_rows, inverse_one = rms_forward(inputs, attn_gain)
    normed_rows_back = normed_rows.astype(jnp.bfloat16)
    query_pre = jnp.dot(normed_rows_back, w_query, preferred_element_type=jnp.float32).reshape(
        sequence_length, QUERY_HEADS, HEAD_SIZE
    )
    key_before_rotary = jnp.dot(
        normed_rows_back, key_weight, preferred_element_type=jnp.float32
    ).reshape(sequence_length, KEY_VALUE_HEADS, HEAD_SIZE)
    value_b = (
        jnp.dot(normed_rows_back, value_weight, preferred_element_type=jnp.float32)
        .astype(jnp.bfloat16)
        .reshape(sequence_length, KEY_VALUE_HEADS, HEAD_SIZE)
    )
    positions = positions_of(segment)
    cosine_table, sine_table = rotary_tables(positions, HEAD_SIZE)
    query_back_rows = rotary(query_pre, cosine_table, sine_table).astype(jnp.bfloat16)
    key_b = rotary(key_before_rotary, cosine_table, sine_table).astype(jnp.bfloat16)
    indices = jnp.arange(sequence_length)
    allowed = (
        (segment[:, None] == segment[None, :])
        & (indices[None, :] <= indices[:, None])
        & ((live_row[None, :] > 0) | (indices[None, :] == indices[:, None]))
    )
    grouped_rows = query_back_rows.reshape(
        sequence_length, KEY_VALUE_HEADS, query_per_key_head, HEAD_SIZE
    )
    scores = (
        jnp.einsum("qgrd,kgd->grqk", grouped_rows, key_b, preferred_element_type=jnp.float32)
        * score_scale
    )
    scores = jnp.where(allowed, scores, -1e30)
    highest = jnp.max(scores, axis=-1, keepdims=True)
    weights_exp = jnp.exp(scores - highest)
    denominator = jnp.sum(weights_exp, axis=-1, keepdims=True)
    log_total = highest + jnp.log(denominator)
    probabilities = weights_exp / denominator
    mixed = jnp.einsum(
        "grqk,kgd->qgrd",
        probabilities.astype(jnp.bfloat16),
        value_b,
        preferred_element_type=jnp.float32,
    )
    mixed_b = mixed.reshape(sequence_length, QUERY_HEADS * HEAD_SIZE).astype(jnp.bfloat16)
    middle = inputs + jnp.dot(mixed_b, w_out, preferred_element_type=jnp.float32)
    moe_normed, inverse_two = rms_forward(middle, moe_gain)
    moe_in = moe_normed.astype(jnp.bfloat16)
    logits = jnp.dot(moe_in, router, preferred_element_type=jnp.float32)
    route_hot = (routes[:, :, None] == jnp.arange(experts_all)[None, None, :]).astype(jnp.float32)
    chosen = jnp.sum(route_hot * logits[:, None, :], axis=-1)
    route_soft = jax.nn.softmax(chosen, axis=-1)
    live_column = live_row.astype(jnp.float32)[:, None]
    route_gates = route_soft * live_column
    counts_local = jnp.sum(route_hot * live_column[:, :, None], axis=(0, 1))
    dense_gates = jnp.sum(route_hot * route_gates[:, :, None], axis=1)
    if special:
        combined, expert_input_grad, gate_upstream_dense, gate_w_grad, up_w_grad, down_w_grad = expert_part(
            moe_in, cotangent, dense_gates, w_gate[0], w_up[0], w_down[0]
        )
        gate_w_grad, up_w_grad, down_w_grad = gate_w_grad[None], up_w_grad[None], down_w_grad[None]
    else:
        upstream_all = lax.all_gather(cotangent, "ep", axis=0, tiled=True)
        gate_all = lax.all_gather(w_gate, "hs", axis=0, tiled=True)
        up_all = lax.all_gather(w_up, "hs", axis=0, tiled=True)
        down_all = lax.all_gather(w_down, "hs", axis=0, tiled=True)
        rows_all = lax.all_gather(moe_in, "ep", axis=0, tiled=True)
        gates_all = lax.all_to_all(
            dense_gates.T.reshape(experts_all, 1, sequence_length), "ep", split_axis=0, concat_axis=1, tiled=True
        ).reshape(-1)
        weighted, back, gate_upstream_all, gate_w_grad, up_w_grad, down_w_grad = expert_pass(
            rows_all, upstream_all, gates_all, gate_all, up_all, down_all
        )
        combined = lax.psum_scatter(weighted, "ep", scatter_dimension=0, tiled=True).astype(jnp.float32)
        expert_input_grad = lax.psum_scatter(back, "ep", scatter_dimension=0, tiled=True).astype(jnp.float32)
        gate_upstream_dense = lax.all_to_all(
            gate_upstream_all.reshape(experts_all, 1, sequence_length), "ep", split_axis=0, concat_axis=1, tiled=True
        ).reshape(experts_all, sequence_length).T
        gate_w_grad = sum_halves(gate_w_grad, 1)[None]
        up_w_grad = sum_halves(up_w_grad, 1)[None]
        down_w_grad = sum_halves(down_w_grad, 0)[None]
    output = (middle + combined).astype(jnp.bfloat16)
    upstream = cotangent.astype(jnp.float32)
    gate_upstream = jnp.sum(route_hot * gate_upstream_dense[:, None, :], axis=-1)
    soft_upstream = gate_upstream * live_column
    chosen_grad = route_soft * (
        soft_upstream - jnp.sum(route_soft * soft_upstream, axis=-1, keepdims=True)
    )
    logit_grad = jnp.sum(route_hot * chosen_grad[:, :, None], axis=1).astype(jnp.bfloat16)
    router_w_grad = jnp.einsum("td,te->de", moe_in, logit_grad, preferred_element_type=jnp.float32)
    moe_in_grad = expert_input_grad + jnp.einsum(
        "te,de->td", logit_grad, router, preferred_element_type=jnp.float32
    )
    middle_norm_grad, moe_gain_grad = rms_backward(middle, inverse_two, moe_gain, moe_in_grad)
    middle_grad = upstream + middle_norm_grad
    attn_grad_b = middle_grad.astype(jnp.bfloat16)
    out_w_grad = jnp.einsum("tm,td->md", mixed_b, attn_grad_b, preferred_element_type=jnp.float32)
    attention_mixed_grad = jnp.einsum(
        "td,md->tm", attn_grad_b, w_out, preferred_element_type=jnp.float32
    ).astype(jnp.bfloat16)
    attention_mixed_grad = attention_mixed_grad.reshape(
        sequence_length, KEY_VALUE_HEADS, query_per_key_head, HEAD_SIZE
    )
    scores_again = (
        jnp.einsum("qgrd,kgd->grqk", grouped_rows, key_b, preferred_element_type=jnp.float32)
        * score_scale
    )
    scores_again = jnp.where(allowed, scores_again, -1e30)
    probs_again = jnp.exp(scores_again - log_total)
    prob_grad = jnp.einsum(
        "qgrd,kgd->grqk", attention_mixed_grad, value_b, preferred_element_type=jnp.float32
    )
    value_per_head_grad = jnp.einsum(
        "grqk,qgrd->kgd",
        probs_again.astype(jnp.bfloat16),
        attention_mixed_grad,
        preferred_element_type=jnp.float32,
    )
    value_per_head_grad = value_per_head_grad.astype(jnp.bfloat16).reshape(
        sequence_length, KEY_VALUE_HEADS * HEAD_SIZE
    )
    row_delta = jnp.sum(probs_again * prob_grad, axis=-1, keepdims=True)
    score_grad = (probs_again * (prob_grad - row_delta)).astype(jnp.bfloat16)
    query_rot_grad = (
        jnp.einsum("grqk,kgd->qgrd", score_grad, key_b, preferred_element_type=jnp.float32)
        * score_scale
    )
    rotated_key_grad = (
        jnp.einsum("grqk,qgrd->kgd", score_grad, grouped_rows, preferred_element_type=jnp.float32)
        * score_scale
    )
    query_head_grad = (
        rotary_backward(
            query_rot_grad.reshape(sequence_length, QUERY_HEADS, HEAD_SIZE),
            cosine_table,
            sine_table,
        )
        .astype(jnp.bfloat16)
        .reshape(sequence_length, QUERY_HEADS * HEAD_SIZE)
    )
    key_head_grad = (
        rotary_backward(rotated_key_grad, cosine_table, sine_table)
        .astype(jnp.bfloat16)
        .reshape(sequence_length, KEY_VALUE_HEADS * HEAD_SIZE)
    )
    query_w_grad = jnp.einsum(
        "td,te->de", normed_rows_back, query_head_grad, preferred_element_type=jnp.float32
    )
    key_w_grad = jnp.einsum(
        "td,te->de", normed_rows_back, key_head_grad, preferred_element_type=jnp.float32
    )
    value_w_grad = jnp.einsum(
        "td,te->de", normed_rows_back, value_per_head_grad, preferred_element_type=jnp.float32
    )
    normed_grad = jnp.einsum(
        "te,de->td", query_head_grad, w_query, preferred_element_type=jnp.float32
    )
    normed_grad = normed_grad + jnp.einsum(
        "te,de->td", key_head_grad, key_weight, preferred_element_type=jnp.float32
    )
    normed_grad = normed_grad + jnp.einsum(
        "te,de->td", value_per_head_grad, value_weight, preferred_element_type=jnp.float32
    )
    input_norm_grad, attn_gain_grad = rms_backward(inputs, inverse_one, attn_gain, normed_grad)
    input_grad = middle_grad + input_norm_grad
    if special:
        small = jnp.zeros((24, model_dim), jnp.float32)
        small = small.at[:experts_all].set(router_w_grad.T)
        small = small.at[16].set(attn_gain_grad).at[17].set(moe_gain_grad)
        small = small.at[18, :experts_all].set(counts_local)
        wide = [g.astype(jnp.bfloat16) for g in (out_w_grad, query_w_grad, key_w_grad, value_w_grad)]
        out_w_grad, query_w_grad, key_w_grad, value_w_grad, small = sum_everywhere(wide, small)
        router_w_grad = small[:experts_all].T
        attn_gain_grad, moe_gain_grad, counts = small[16], small[17], small[18, :experts_all]
    else:
        (
            attn_gain_grad,
            query_w_grad,
            key_w_grad,
            value_w_grad,
            out_w_grad,
            moe_gain_grad,
            router_w_grad,
            counts,
        ) = lax.psum(
            (
                attn_gain_grad,
                query_w_grad,
                key_w_grad,
                value_w_grad,
                out_w_grad,
                moe_gain_grad,
                router_w_grad,
                counts_local,
            ),
            ("ep", "hs"),
        )
    return (
        output,
        input_grad,
        attn_gain_grad,
        query_w_grad,
        key_w_grad,
        value_w_grad,
        out_w_grad,
        moe_gain_grad,
        router_w_grad,
        gate_w_grad,
        up_w_grad,
        down_w_grad,
        counts.astype(jnp.int32),
    )


def solution(mesh):
    in_specs = (
        P(("ep", "hs"), None),
        P(("ep", "hs"), None),
        P(("ep", "hs"), None),
        P(("ep", "hs"), None),
        P(),
        P(),
        P(),
        P(),
        P(),
        P(),
        P(),
        P("ep", None, "hs"),
        P("ep", None, "hs"),
        P("ep", "hs", None),
        P(("ep", "hs"), None),
    )
    out_specs = (
        P(("ep", "hs"), None),
        P(("ep", "hs"), None),
        P(),
        P(),
        P(),
        P(),
        P(),
        P(),
        P(),
        P("ep", None, "hs"),
        P("ep", None, "hs"),
        P("ep", "hs", None),
        P(),
    )
    return jax.shard_map(local, mesh=mesh, in_specs=in_specs, out_specs=out_specs, check_vma=False)
```

```python
import functools

import jax
import jax.numpy as jnp
from jax import lax
from jax.experimental import pallas as pl
from jax.experimental.pallas import tpu as pltpu
from jax.sharding import PartitionSpec as P

QUERY_HEADS = 16
KEY_VALUE_HEADS = 8
HEAD_SIZE = 64
TOP = 8


EPSILON = 1e-05


def rms_forward(value_rows, norm_gain):
    inverse = lax.rsqrt(jnp.mean(value_rows * value_rows, axis=-1, keepdims=True) + EPSILON)
    return (value_rows * inverse * norm_gain, inverse)


def rms_backward(value_rows, inverse, norm_gain, upstream):
    scaled = upstream * norm_gain
    gain_grad = jnp.sum(upstream * value_rows * inverse, axis=0)
    input_grad = inverse * (
        scaled
        - value_rows * inverse * inverse * jnp.mean(scaled * value_rows, axis=-1, keepdims=True)
    )
    return (input_grad, gain_grad)


def positions_of(segment):
    before = (segment[None, :] < segment[:, None]).astype(jnp.int32)
    return jnp.arange(segment.shape[-1], dtype=jnp.int32) - jnp.sum(before, axis=1)


def rotary_tables(positions, head_dim):
    half_dim = head_dim // 2
    frequency = 10000.0 ** (-(jnp.arange(half_dim, dtype=jnp.float32) * 2.0) / head_dim)
    angles = positions.astype(jnp.float32)[:, None] * frequency[None, :]
    return (jnp.cos(angles)[:, None, :], jnp.sin(angles)[:, None, :])


def rotary(heads, cosine_table, sine_table):
    half_dim = heads.shape[-1] // 2
    first_half = heads[..., :half_dim]
    second_half = heads[..., half_dim:]
    return jnp.concatenate(
        [
            first_half * cosine_table - second_half * sine_table,
            second_half * cosine_table + first_half * sine_table,
        ],
        axis=-1,
    )


def rotary_backward(grads, cosine_table, sine_table):
    half_dim = grads.shape[-1] // 2
    first_half = grads[..., :half_dim]
    second_half = grads[..., half_dim:]
    return jnp.concatenate(
        [
            first_half * cosine_table + second_half * sine_table,
            second_half * cosine_table - first_half * sine_table,
        ],
        axis=-1,
    )


def to_bf16(value):
    return lax.reduce_precision(value, 8, 7)


def expert_pass(rows, upstream, gates, gate_w, up_w, down_w):
    groups, model_dim, width = gate_w.shape
    gate_all = jnp.concatenate([gate_w[j] for j in range(groups)], axis=1)
    up_all = jnp.concatenate([up_w[j] for j in range(groups)], axis=1)
    down_all = down_w.reshape(groups * width, model_dim)
    gate_pre = jnp.dot(rows, gate_all, preferred_element_type=jnp.float32)
    up_pre = jnp.dot(rows, up_all, preferred_element_type=jnp.float32)
    sigmoid_part = jax.nn.sigmoid(gate_pre)
    activated = gate_pre * sigmoid_part
    hidden = (activated * up_pre).astype(jnp.bfloat16)
    total = jnp.zeros(rows.shape, jnp.float32)
    for j in range(groups):
        total = total + to_bf16(
            jnp.dot(hidden[:, j * width : (j + 1) * width], down_w[j], preferred_element_type=jnp.float32)
        )
    total = to_bf16(total)
    upstream_f = upstream.astype(jnp.float32)
    gate_upstream = jnp.sum(upstream_f * total, axis=-1)
    weighted = (gates[:, None] * total).astype(jnp.bfloat16)
    upstream_e = (gates[:, None] * upstream_f).astype(jnp.bfloat16)
    hidden_grad = jnp.einsum("td,fd->tf", upstream_e, down_all, preferred_element_type=jnp.float32)
    up_pre_grad = (hidden_grad * activated).astype(jnp.bfloat16)
    gate_pre_grad = (
        hidden_grad * up_pre * sigmoid_part * (1.0 + gate_pre * (1.0 - sigmoid_part))
    ).astype(jnp.bfloat16)
    down_grad = jnp.einsum("tf,td->fd", hidden, upstream_e, preferred_element_type=jnp.float32)
    gate_grad = jnp.einsum("td,tf->df", rows, gate_pre_grad, preferred_element_type=jnp.float32)
    up_grad = jnp.einsum("td,tf->df", rows, up_pre_grad, preferred_element_type=jnp.float32)
    back = jnp.zeros(rows.shape, jnp.float32)
    for j in range(groups):
        cut = slice(j * width, (j + 1) * width)
        back = back + to_bf16(
            jnp.einsum("tf,df->td", gate_pre_grad[:, cut], gate_w[j], preferred_element_type=jnp.float32)
            + jnp.einsum("tf,df->td", up_pre_grad[:, cut], up_w[j], preferred_element_type=jnp.float32)
        )
    return (weighted, back.astype(jnp.bfloat16), gate_upstream, gate_grad, up_grad, down_grad)


def sum_halves(grad, dim):
    return lax.psum_scatter(
        grad.astype(jnp.bfloat16), "hs", scatter_dimension=dim, tiled=True
    ).astype(jnp.float32)


MESH = pl.DeviceIdType.MESH
UNIT = 16


def place():
    ep, hs = lax.axis_index("ep"), lax.axis_index("hs")
    return (ep // 4, (ep // 2) % 2, ep % 2, hs)


def device(z, x, c, y):
    return (z * 4 + x * 2 + c, y)


def greet(peers):
    barrier = pltpu.get_barrier_semaphore()
    for peer in peers:
        pl.semaphore_signal(barrier, inc=1, device_id=peer, device_id_type=MESH)
    pl.semaphore_wait(barrier, len(peers))


def sum_kernel(count, *refs):
    grads, small = refs[:count], refs[count]
    outs, small_out = refs[count + 1 : 2 * count + 1], refs[2 * count + 1]
    rest = refs[2 * count + 2 :]
    halves, totals, fulls = rest[:count], rest[count : 2 * count], rest[2 * count : 3 * count]
    firsts, seconds, lines = rest[3 * count : 4 * count], rest[4 * count : 5 * count], rest[5 * count : 6 * count]
    small_sum, small_in, send, recv, small_send, small_recv, local_sem = rest[6 * count :]
    z, x, c, y = place()
    sibling, beside, across = device(z, x, 1 - c, y), device(z, 1 - x, c, y), device(z, x, c, 1 - y)
    along = [device((z + k) % 4, x, c, y) for k in (1, 2, 3)]
    greet([sibling, beside, across] + along)
    bits = ((x, y), (y, x))
    partners = ((beside, across), (across, beside))

    def push(i, slot, source, target, peer):
        copy = pltpu.make_async_remote_copy(
            src_ref=source,
            dst_ref=target,
            send_sem=send.at[i, slot],
            recv_sem=recv.at[i, slot],
            device_id=peer,
            device_id_type=MESH,
        )
        copy.start()
        return copy

    def combine(i, target, start, length, terms):
        def body(u, carry):
            value = totals[i][start + u].astype(jnp.float32)
            for ref, base in terms:
                value = value + ref[base + u].astype(jnp.float32)
            target[0][target[1] + u] = value.astype(jnp.bfloat16)
            return carry

        lax.fori_loop(0, length, body, 0)

    copies = {}

    def stage(i, step):
        if step == 0:
            copies[i, 0] = [
                push(i, 0, grads[i].at[pl.ds((1 - c) * 32, 32)], halves[i], sibling)
            ]
        if step == 1:
            copies[i, 0][0].wait_recv()

            def body(u, carry):
                value = grads[i][c * 32 + u].astype(jnp.float32) + halves[i][u].astype(jnp.float32)
                totals[i][u] = value.astype(jnp.bfloat16)
                return carry

            lax.fori_loop(0, 32, body, 0)
            copies[i, 1] = [
                push(
                    i,
                    1 + part,
                    totals[i].at[pl.ds(part * 16 + (1 - bits[part][0]) * 8, 8)],
                    firsts[i].at[part],
                    partners[part][0],
                )
                for part in (0, 1)
            ]
        if step == 2:
            copies[i, 2] = []
            for part in (0, 1):
                copies[i, 1][part].wait_recv()
                base = part * 16 + bits[part][0] * 8
                combine(i, (totals[i], base), base, 8, [(firsts[i].at[part], 0)])
                copies[i, 2].append(
                    push(
                        i,
                        3 + part,
                        totals[i].at[pl.ds(base + (1 - bits[part][1]) * 4, 4)],
                        seconds[i].at[part],
                        partners[part][1],
                    )
                )
        if step == 3:
            copies[i, 3] = []
            for part in (0, 1):
                copies[i, 2][part].wait_recv()
                base = part * 16 + bits[part][0] * 8 + bits[part][1] * 4
                combine(i, (totals[i], base), base, 4, [(seconds[i].at[part], 0)])
                for k in (1, 2, 3):
                    copies[i, 3].append(
                        push(
                            i,
                            5 + part * 3 + k - 1,
                            totals[i].at[base + (z + k) % 4],
                            lines[i].at[part, k - 1],
                            along[k - 1],
                        )
                    )
        if step == 4:
            copies[i, 4] = []
            for part in (0, 1):
                for k in (1, 2, 3):
                    copies[i, 3][part * 3 + k - 1].wait_recv()
                base = part * 16 + bits[part][0] * 8 + bits[part][1] * 4
                combine(
                    i, (fulls[i], c * 32 + base + z), base + z, 1, [(lines[i].at[part], k) for k in (0, 1, 2)]
                )
                for k in (1, 2, 3):
                    piece = fulls[i].at[c * 32 + base + z]
                    copies[i, 4].append(push(i, 11 + part * 3 + k - 1, piece, piece, along[k - 1]))
        if step == 5:
            copies[i, 5] = []
            for part in (0, 1):
                for k in (1, 2, 3):
                    copies[i, 4][part * 3 + k - 1].wait_recv()
                piece = fulls[i].at[pl.ds(c * 32 + part * 16 + bits[part][0] * 8 + bits[part][1] * 4, 4)]
                copies[i, 5].append(push(i, 17 + part, piece, piece, partners[part][1]))
        if step == 6:
            copies[i, 6] = []
            for part in (0, 1):
                copies[i, 5][part].wait_recv()
                piece = fulls[i].at[pl.ds(c * 32 + part * 16 + bits[part][0] * 8, 8)]
                copies[i, 6].append(push(i, 19 + part, piece, piece, partners[part][0]))
        if step == 7:
            for part in (0, 1):
                copies[i, 6][part].wait_recv()
            piece = fulls[i].at[pl.ds(c * 32, 32)]
            copies[i, 7] = [push(i, 21, piece, piece, sibling)]
        if step == 8:
            copies[i, 7][0].wait_recv()
            done = pltpu.make_async_copy(fulls[i], outs[i], local_sem.at[i])
            done.start()
            copies[i, 8] = [done]

    def small_push(slot, peer, target):
        copy = pltpu.make_async_remote_copy(
            src_ref=small_sum.at[slot],
            dst_ref=small_in.at[target],
            send_sem=small_send.at[target],
            recv_sem=small_recv.at[target],
            device_id=peer,
            device_id_type=MESH,
        )
        copy.start()
        return copy

    def small_stage(step):
        if step == 0:
            small_sum[0] = small[...]
            copies["s", 0] = [small_push(0, sibling, 0)]
        if step in (1, 2):
            copies["s", step - 1][0].wait_recv()
            small_sum[step] = small_sum[step - 1] + small_in[step - 1]
            copies["s", step] = [small_push(step, (beside, across)[step - 1], step)]
        if step == 3:
            copies["s", 2][0].wait_recv()
            small_sum[3] = small_sum[2] + small_in[2]
            copies["s", 3] = []
            for k in (1, 2, 3):
                copy = pltpu.make_async_remote_copy(
                    src_ref=small_sum.at[3],
                    dst_ref=small_in.at[3 + z],
                    send_sem=small_send.at[2 + k],
                    recv_sem=small_recv.at[2 + k],
                    device_id=along[k - 1],
                    device_id_type=MESH,
                )
                copy.start()
                copies["s", 3].append(copy)
            small_in[3 + z] = small_sum[3]
        if step == 4:
            for copy in copies["s", 3]:
                copy.wait_recv()
            small_out[...] = (small_in[3] + small_in[4]) + (small_in[5] + small_in[6])

    for tick in range(count + 8):
        for i in range(count):
            if 0 <= tick - i <= 8:
                stage(i, tick - i)
        if tick <= 4:
            small_stage(tick)
    for key, group in copies.items():
        for copy in group:
            if key[0] != "s" and key[1] == 8:
                copy.wait()
            else:
                copy.wait_send()


def sum_everywhere(arrays, small):
    count = len(arrays)
    units = [a.reshape(a.shape[0] // UNIT, UNIT, a.shape[1]) for a in arrays]
    vmem = pl.BlockSpec(memory_space=pltpu.VMEM)

    def scratch(lead):
        return [pltpu.VMEM((*lead, UNIT, a.shape[1]), jnp.bfloat16) for a in arrays]

    out = pl.pallas_call(
        functools.partial(sum_kernel, count),
        out_shape=[jax.ShapeDtypeStruct(u.shape, u.dtype) for u in units]
        + [jax.ShapeDtypeStruct(small.shape, small.dtype)],
        in_specs=[vmem] * (count + 1),
        out_specs=[pl.BlockSpec(memory_space=pl.ANY)] * count + [vmem],
        scratch_shapes=[
            *scratch((32,)),
            *scratch((32,)),
            *scratch((64,)),
            *scratch((2, 8)),
            *scratch((2, 4)),
            *scratch((2, 3)),
            pltpu.VMEM((4, *small.shape), jnp.float32),
            pltpu.VMEM((7, *small.shape), jnp.float32),
            pltpu.SemaphoreType.DMA((count, 22)),
            pltpu.SemaphoreType.DMA((count, 22)),
            pltpu.SemaphoreType.DMA((6,)),
            pltpu.SemaphoreType.DMA((6,)),
            pltpu.SemaphoreType.DMA((count,)),
        ],
        compiler_params=pltpu.CompilerParams(
            collective_id=0, has_side_effects=True, vmem_limit_bytes=56 << 20
        ),
        name="sum_everywhere",
    )(*units, small)
    return [o.reshape(a.shape).astype(jnp.float32) for o, a in zip(out, arrays)] + [out[-1]]


EDGE_ORDER = (0, 1, 2, 6, 5, 4, 7, 3)
MIDDLE_ORDER = (0, 1, 2, 3, 7, 5, 6, 4)


def contract(left, right, left_dim, right_dim):
    return lax.dot_general(
        left, right, (((left_dim,), (right_dim,)), ((), ())), preferred_element_type=jnp.float32
    )


def expert_kernel(
    rows_in,
    upstream_in,
    gates_in,
    gate_w,
    up_w,
    down_w,
    weighted_out,
    back_out,
    slope_out,
    gate_out,
    up_out,
    down_out,
    streams,
    gates,
    slopes,
    slopes_in,
    w_gate,
    w_up,
    w_down,
    sums,
    partial,
    from_sibling,
    from_line,
    staged_x,
    staged_y,
    staged_again,
    returned_x,
    returned_y,
    returned_again,
    load_sem,
    gather_send,
    gather_recv,
    gate_send,
    gate_recv,
    slope_send,
    slope_recv,
    weight_send,
    weight_recv,
    pair_send,
    pair_recv,
    line_send,
    line_recv,
    grad_send,
    grad_recv,
):
    z, x, c, y = place()
    near, far, last = 1 + z % 2, (2 + 3 * z) % 5, 3 - 3 * (z // 2)
    middle = (z == 1) | (z == 2)
    edge = (z == 0) | (z == 3)
    sibling, beside, across = device(z, x, 1 - c, y), device(z, 1 - x, c, y), device(z, x, c, 1 - y)
    corner = device(z, 1 - x, c, 1 - y)
    line = [((z + k) % 4, (c + d) % 2) for k in range(4) for d in range(2) if k or d]
    greet([device(a, x, b, y) for a, b in line] + [beside, across, corner])

    def chip(k):
        half = z // 2
        inner = z + half * (3 - 2 * z)
        spot = k + inner * (1 - 3 * (k // 2) + 2 * (k // 3))
        return spot + half * (3 - 2 * spot)

    def remote(source, target, send, recv, peer):
        return pltpu.make_async_remote_copy(
            src_ref=source, dst_ref=target, send_sem=send, recv_sem=recv, device_id=peer, device_id_type=MESH
        )

    own = [
        pltpu.make_async_copy(ref, streams.at[s, z, c], load_sem.at[s])
        for s, ref in enumerate((rows_in, upstream_in))
    ]
    gates_own = pltpu.make_async_copy(gates_in.at[z, c], gates.at[z, c], load_sem.at[2])
    weights_own = [
        pltpu.make_async_copy(ref, held.at[x, y], load_sem.at[3 + a])
        for a, (ref, held) in enumerate(((gate_w, w_gate), (up_w, w_up), (down_w, w_down)))
    ]
    for copy in (*own, gates_own, *weights_own):
        copy.start()

    def gather(s, block, slot, peer):
        piece = streams.at[s, block, c]
        return remote(piece, piece, gather_send.at[s, slot], gather_recv.at[s, block, c], peer)

    def arrive(s, block, core):
        piece = streams.at[s, block, core]
        pltpu.make_async_copy(piece, piece, gather_recv.at[s, block, core]).wait()

    for s in (0, 1):
        own[s].wait()
        gather(s, z, 0, device(near, x, c, y)).start()
        gather(s, z, 2, sibling).start()

        @pl.when(middle)
        def _():
            gather(s, z, 1, device(far, x, c, y)).start()

    gate_copies = [
        remote(
            gates_in.at[a, b], gates.at[z, c], gate_send.at[n], gate_recv.at[z, c], device(a, x, b, y)
        )
        for n, (a, b) in enumerate(line)
    ]
    for copy in gate_copies:
        copy.start()
    weight_copies = []
    for a, held in enumerate((w_gate, w_up, w_down)):
        weights_own[a].wait()
        for n, peer in enumerate((across, beside, corner)):
            piece = held.at[x, y]
            weight_copies.append(
                remote(piece, piece, weight_send.at[n, a], weight_recv.at[x, y, a], peer)
            )
    for n in range(3):
        for a in range(3):
            weight_copies[a * 3 + n].start()

    def weights_here(expert, group):
        for a, held in enumerate((w_gate, w_up, w_down)):
            piece = held.at[expert, group]
            pltpu.make_async_copy(piece, piece, weight_recv.at[expert, group, a]).wait()

    def zero(u, carry):
        for e in (0, 1):
            for a in range(3):
                sums[e, a, u // 16, pl.ds(pl.multiple_of((u % 16) * 16, 16), 16), :] = jnp.zeros(
                    (16, 1024), jnp.float32
                )
            partial[e, u // 8, (u // 4) % 2, pl.ds(pl.multiple_of((u % 4) * 64, 64), 64), :] = jnp.zeros(
                (64, 1024), jnp.bfloat16
            )
        return carry

    lax.fori_loop(0, 32, zero, 0)

    @pl.when(edge)
    def _():
        for s in (0, 1):
            gather(s, z, 0, device(near, x, c, y)).wait_send()
            gather(s, z, 1, device(far, x, c, y)).start()

    def handle(k):
        block = chip(k)
        for s in (0, 1):
            arrive(s, block, c)
            gather(s, block, 4 + k, sibling).start()
            if k != 2:

                @pl.when(middle)
                def _():
                    gather(s, block, 2 + (k + 1) // 2, device(far, x, c, y)).start()

    handle(1)
    gates_own.wait()
    for a, b in line:
        pltpu.make_async_copy(gates.at[a, b], gates.at[a, b], gate_recv.at[a, b]).wait()
    weights_here(x, 1 - y)
    row_id = lax.broadcasted_iota(jnp.int32, (256, 256), 0)
    lane_id = lax.broadcasted_iota(jnp.int32, (256, 256), 1)

    def compute(expert, block, core):
        diagonal = row_id == lane_id
        gate_row = gates[block, core, pl.ds(expert, 1), :]
        gate = jnp.sum(jnp.where(diagonal, gate_row, 0.0), axis=1, keepdims=True)
        rows = streams[0, block, core]
        total = jnp.zeros((256, 1024), jnp.float32)
        kept = []
        for j in (0, 1):
            gate_pre = contract(rows, w_gate[expert, j], 1, 0)
            up_pre = contract(rows, w_up[expert, j], 1, 0)
            sigmoid_part = jax.nn.sigmoid(gate_pre)
            activated = gate_pre * sigmoid_part
            hidden = (activated * up_pre).astype(jnp.bfloat16)
            part = contract(hidden, w_down[expert, j], 1, 0)
            total = total + part.astype(jnp.bfloat16).astype(jnp.float32)
            inner = up_pre * sigmoid_part * (1.0 + gate_pre * (1.0 - sigmoid_part))
            kept.append((activated, inner, hidden))
        total = total.astype(jnp.bfloat16).astype(jnp.float32)
        upstream = streams[1, block, core].astype(jnp.float32)
        slope = jnp.sum(upstream * total, axis=1, keepdims=True)
        slopes[block, core, pl.ds(expert, 1), :] = jnp.sum(
            jnp.where(diagonal, slope, 0.0), axis=0, keepdims=True
        )
        weighted = gate * total + partial[1, block, core].astype(jnp.float32)
        partial[1, block, core] = weighted.astype(jnp.bfloat16)
        upstream = (gate * upstream).astype(jnp.bfloat16)
        back = jnp.zeros((256, 1024), jnp.float32)
        for j in (0, 1):
            activated, inner, hidden = kept[j]
            hidden_grad = contract(upstream, w_down[expert, j], 1, 1)
            up_grad = (hidden_grad * activated).astype(jnp.bfloat16)
            gate_grad = (hidden_grad * inner).astype(jnp.bfloat16)
            sums[expert, 0, j] += contract(gate_grad, rows, 0, 0)
            sums[expert, 1, j] += contract(up_grad, rows, 0, 0)
            sums[expert, 2, j] += contract(hidden, upstream, 0, 0)
            step = contract(gate_grad, w_gate[expert, j], 1, 1) + contract(up_grad, w_up[expert, j], 1, 1)
            back = back + step.astype(jnp.bfloat16).astype(jnp.float32)
        back = back + partial[0, block, core].astype(jnp.float32)
        partial[0, block, core] = back.astype(jnp.bfloat16)

    def grad_copy(n, source, target, peer):
        return remote(source, target, grad_send.at[n], grad_recv.at[n], peer)

    def pair_copy(s, block):
        return remote(
            partial.at[s, block, 1 - c],
            from_sibling.at[s, block],
            pair_send.at[s, block],
            pair_recv.at[s, block],
            sibling,
        )

    def line_copy(s, block, slot, peer):
        return remote(
            partial.at[s, block, c],
            from_line.at[s, slot],
            line_send.at[s, block],
            line_recv.at[s, slot],
            device(peer, x, c, y),
        )

    def line_wait(s, slot):
        piece = from_line.at[s, slot]
        pltpu.make_async_copy(piece, piece, line_recv.at[s, slot]).wait()

    def add_to(s, block, ref):
        def body(u, carry):
            at = pl.ds(pl.multiple_of(u * 32, 32), 32)
            value = partial[s, block, c, at, :].astype(jnp.float32) + ref[at, :].astype(jnp.float32)
            partial[s, block, c, at, :] = value.astype(jnp.bfloat16)
            return carry

        lax.fori_loop(0, 8, body, 0)

    at_edge = (z * z - 3 * z + 2) // 2
    orders = [sum(code << (3 * t) for t, code in enumerate(codes)) for codes in (EDGE_ORDER, MIDDLE_ORDER)]
    order = at_edge * orders[0] + (1 - at_edge) * orders[1]

    def step(i, carry):
        t = i // 2
        code = lax.shift_right_logical(order, 3 * t) % 8
        again = at_edge * ((t // 3) % 2 + t // 7) + (1 - at_edge) * (t // 4)
        k = code % 4
        expert = x + (code // 4) * (1 - 2 * x)
        block, core = chip(k), (c + i + again) % 2

        @pl.when((i == 2) & middle | (i == 4) & edge)
        def _():
            handle(2)

        @pl.when((i == 4) & middle | (i == 12) & edge)
        def _():
            handle(3)

        @pl.when((i == 8) & middle | (i == 6) & edge)
        def _():
            weights_here(1 - x, y)
            weights_here(1 - x, 1 - y)

        @pl.when((i % 2 == 1) & (again == 0))
        def _():
            for s in (0, 1):
                arrive(s, block, 1 - c)

        compute(expert, block, core)

        @pl.when((i % 2 == 0) & (again == 1))
        def _():
            for s in (0, 1):
                pair_copy(s, block).start()

        @pl.when((i % 2 == 1) & (again == 1) & (k > 0))
        def _():
            for s in (0, 1):
                pair_copy(s, block).wait_recv()
                add_to(s, block, from_sibling.at[s, block])

                @pl.when(edge & (k == 2))
                def _():
                    line_copy(s, block, 3, near).start()

                @pl.when(edge & (k == 1))
                def _():
                    line_copy(s, block, 1, near).start()

                @pl.when(edge & (k == 3))
                def _():
                    line_copy(s, block, 2, last).start()

                @pl.when(middle & (k == 3))
                def _():
                    line_copy(s, block, 1, last).start()

                @pl.when(middle & (k == 2))
                def _():
                    line_copy(s, block, 0, far).start()

        return carry

    lax.fori_loop(0, 16, step, 0)
    low, high = pl.ds(0, 512), pl.ds(512, 512)

    def each(body):
        def rows_of(u, carry):
            at = pl.ds(pl.multiple_of(u * 32, 32), 32)
            for a in range(3):
                body(a, at)
            return carry

        lax.fori_loop(0, 8, rows_of, 0)

    def stage_low(a, at):
        for j in (0, 1):
            staged_x[j, a, at, :] = sums[1 - x, a, j, at, low].astype(jnp.bfloat16)

    def stage_high(a, at):
        staged_y[0, a, at, :] = sums[1 - x, a, 1 - y, at, high].astype(jnp.bfloat16)
        staged_y[1, a, at, :] = sums[x, a, 1 - y, at, high].astype(jnp.bfloat16)

    each(stage_low)
    grad_copy(0, staged_x, returned_x, beside).start()
    each(stage_high)
    grad_copy(1, staged_y, returned_y, across).start()
    slope_copies = [
        remote(
            slopes.at[a, b], slopes_in.at[z, c], slope_send.at[n], slope_recv.at[z, c], device(a, x, b, y)
        )
        for n, (a, b) in enumerate(line)
    ]
    for copy in slope_copies:
        copy.start()
    slopes_in[z, c] = slopes[z, c]

    @pl.when(middle)
    def _():
        for s in (0, 1):
            line_wait(s, 3)
            add_to(s, near, from_line.at[s, 3])
            line_copy(s, near, 0, near).start()

    grad_copy(0, staged_x, returned_x, beside).wait_recv()

    def second_low(a, at):
        value = sums[x, a, 1 - y, at, low] + returned_x[1 - y, a, at, :].astype(jnp.float32)
        staged_again[0, a, at, :] = value.astype(jnp.bfloat16)

    each(second_low)
    grad_copy(2, staged_again.at[0], returned_again.at[0], across).start()
    grad_copy(1, staged_y, returned_y, across).wait_recv()

    def second_high(a, at):
        value = sums[1 - x, a, y, at, high] + returned_y[0, a, at, :].astype(jnp.float32)
        staged_again[1, a, at, :] = value.astype(jnp.bfloat16)

    each(second_high)
    grad_copy(3, staged_again.at[1], returned_again.at[1], beside).start()

    def finish(slots):
        for s in (0, 1):
            for slot in slots:
                line_wait(s, slot)

            def body(u, carry):
                at = pl.ds(pl.multiple_of(u * 32, 32), 32)
                value = partial[s, z, c, at, :].astype(jnp.float32)
                value = value + from_sibling[s, z, at, :].astype(jnp.float32)
                for slot in slots:
                    value = value + from_line[s, slot, at, :].astype(jnp.float32)
                (back_out, weighted_out)[s][at, :] = value
                return carry

            lax.fori_loop(0, 8, body, 0)

    for s in (0, 1):
        pair_copy(s, z).wait_recv()

    @pl.when(middle)
    def _():
        finish((0, 1))

    @pl.when(edge)
    def _():
        finish((0, 1, 2))

    for a, b in line:
        pltpu.make_async_copy(slopes_in.at[a, b], slopes_in.at[a, b], slope_recv.at[a, b]).wait()
    slope_out[...] = slopes_in[...]
    grad_copy(2, staged_again.at[0], returned_again.at[0], across).wait_recv()
    grad_copy(3, staged_again.at[1], returned_again.at[1], beside).wait_recv()

    def final_grad(a, at):
        value = sums[x, a, y, at, low] + returned_x[y, a, at, :].astype(jnp.float32)
        sums[x, a, y, at, low] = value + returned_again[0, a, at, :].astype(jnp.float32)
        value = sums[x, a, y, at, high] + returned_y[1, a, at, :].astype(jnp.float32)
        sums[x, a, y, at, high] = value + returned_again[1, a, at, :].astype(jnp.float32)

    each(final_grad)
    stores = [
        pltpu.make_async_copy(sums.at[x, a, y], out, load_sem.at[a])
        for a, out in enumerate((gate_out, up_out, down_out))
    ]
    for copy in stores:
        copy.start()
    for s in (0, 1):

        @pl.when(middle)
        def _():
            gather(s, z, 0, device(near, x, c, y)).wait_send()

        gather(s, z, 1, device(far, x, c, y)).wait_send()
        gather(s, z, 2, sibling).wait_send()
        for k in (1, 2, 3):
            gather(s, chip(k), 4 + k, sibling).wait_send()
            line_copy(s, chip(k), 0, near).wait_send()

        @pl.when(middle)
        def _():
            for k in (1, 3):
                gather(s, chip(k), 2 + (k + 1) // 2, device(far, x, c, y)).wait_send()

        for k in range(4):
            pair_copy(s, chip(k)).wait_send()
    for copy in (*gate_copies, *weight_copies, *slope_copies):
        copy.wait_send()
    grad_copy(0, staged_x, returned_x, beside).wait_send()
    grad_copy(1, staged_y, returned_y, across).wait_send()
    grad_copy(2, staged_again.at[0], returned_again.at[0], across).wait_send()
    grad_copy(3, staged_again.at[1], returned_again.at[1], beside).wait_send()
    for copy in stores:
        copy.wait()


def expert_part(rows, upstream, gates, gate_w, up_w, down_w):
    tokens, model_dim = rows.shape
    width = gate_w.shape[1]
    vmem, anywhere = pl.BlockSpec(memory_space=pltpu.VMEM), pl.BlockSpec(memory_space=pl.ANY)
    f32, bf16, dma = jnp.float32, jnp.bfloat16, pltpu.SemaphoreType.DMA
    grad = jax.ShapeDtypeStruct((width, model_dim), f32)
    by_owner = gates.T.reshape(4, 2, 2, tokens).swapaxes(1, 2)
    by_owner = jnp.pad(by_owner, ((0, 0), (0, 0), (0, 6), (0, 0)))
    weighted, back, slopes, gate_grad, up_grad, down_grad = pl.pallas_call(
        expert_kernel,
        out_shape=[
            jax.ShapeDtypeStruct((tokens, model_dim), f32),
            jax.ShapeDtypeStruct((tokens, model_dim), f32),
            jax.ShapeDtypeStruct((4, 2, 8, tokens), f32),
            grad,
            grad,
            grad,
        ],
        in_specs=[anywhere, anywhere, vmem, anywhere, anywhere, anywhere],
        out_specs=[vmem, vmem, vmem, anywhere, anywhere, anywhere],
        scratch_shapes=[
            pltpu.VMEM((2, 4, 2, tokens, model_dim), bf16),
            pltpu.VMEM((4, 2, 8, tokens), f32),
            pltpu.VMEM((4, 2, 8, tokens), f32),
            pltpu.VMEM((4, 2, 8, tokens), f32),
            pltpu.VMEM((2, 2, model_dim, width), bf16),
            pltpu.VMEM((2, 2, model_dim, width), bf16),
            pltpu.VMEM((2, 2, width, model_dim), bf16),
            pltpu.VMEM((2, 3, 2, width, model_dim), f32),
            pltpu.VMEM((2, 4, 2, tokens, model_dim), bf16),
            pltpu.VMEM((2, 4, tokens, model_dim), bf16),
            pltpu.VMEM((2, 4, tokens, model_dim), bf16),
            *[pltpu.VMEM((2, 3, width, model_dim // 2), bf16)] * 6,
            dma((6,)),
            dma((2, 8)),
            dma((2, 4, 2)),
            dma((7,)),
            dma((4, 2)),
            dma((7,)),
            dma((4, 2)),
            dma((3, 3)),
            dma((2, 2, 3)),
            dma((2, 4)),
            dma((2, 4)),
            dma((2, 4)),
            dma((2, 4)),
            dma((4,)),
            dma((4,)),
        ],
        compiler_params=pltpu.CompilerParams(
            collective_id=1, has_side_effects=True, vmem_limit_bytes=62 << 20
        ),
        name="expert_part",
    )(rows, upstream, by_owner, gate_w, up_w, down_w)
    slopes = slopes[:, :, :2].swapaxes(1, 2).reshape(gates.shape[1], tokens).T
    return (weighted, back, slopes, gate_grad.T, up_grad.T, down_grad)


def local(
    tokens,
    segment_ids,
    live_mask,
    routes,
    attn_gain,
    w_query,
    key_weight,
    value_weight,
    w_out,
    moe_gain,
    router,
    w_gate,
    w_up,
    w_down,
    cotangent,
):
    sequence_length = tokens.shape[0]
    model_dim = tokens.shape[1]
    experts_all = router.shape[1]
    query_per_key_head = QUERY_HEADS // KEY_VALUE_HEADS
    score_scale = HEAD_SIZE ** (-0.5)
    special = lax.axis_size("ep") == 16 and lax.axis_size("hs") == 2
    segment = segment_ids[0]
    live_row = live_mask[0]
    inputs = tokens.astype(jnp.float32)
    normed_rows, inverse_one = rms_forward(inputs, attn_gain)
    normed_rows_back = normed_rows.astype(jnp.bfloat16)
    query_pre = jnp.dot(normed_rows_back, w_query, preferred_element_type=jnp.float32).reshape(
        sequence_length, QUERY_HEADS, HEAD_SIZE
    )
    key_before_rotary = jnp.dot(
        normed_rows_back, key_weight, preferred_element_type=jnp.float32
    ).reshape(sequence_length, KEY_VALUE_HEADS, HEAD_SIZE)
    value_b = (
        jnp.dot(normed_rows_back, value_weight, preferred_element_type=jnp.float32)
        .astype(jnp.bfloat16)
        .reshape(sequence_length, KEY_VALUE_HEADS, HEAD_SIZE)
    )
    positions = positions_of(segment)
    cosine_table, sine_table = rotary_tables(positions, HEAD_SIZE)
    query_back_rows = rotary(query_pre, cosine_table, sine_table).astype(jnp.bfloat16)
    key_b = rotary(key_before_rotary, cosine_table, sine_table).astype(jnp.bfloat16)
    indices = jnp.arange(sequence_length)
    allowed = (
        (segment[:, None] == segment[None, :])
        & (indices[None, :] <= indices[:, None])
        & ((live_row[None, :] > 0) | (indices[None, :] == indices[:, None]))
    )
    grouped_rows = query_back_rows.reshape(
        sequence_length, KEY_VALUE_HEADS, query_per_key_head, HEAD_SIZE
    )
    scores = (
        jnp.einsum("qgrd,kgd->grqk", grouped_rows, key_b, preferred_element_type=jnp.float32)
        * score_scale
    )
    scores = jnp.where(allowed, scores, -1e30)
    highest = jnp.max(scores, axis=-1, keepdims=True)
    weights_exp = jnp.exp(scores - highest)
    denominator = jnp.sum(weights_exp, axis=-1, keepdims=True)
    log_total = highest + jnp.log(denominator)
    probabilities = weights_exp / denominator
    mixed = jnp.einsum(
        "grqk,kgd->qgrd",
        probabilities.astype(jnp.bfloat16),
        value_b,
        preferred_element_type=jnp.float32,
    )
    mixed_b = mixed.reshape(sequence_length, QUERY_HEADS * HEAD_SIZE).astype(jnp.bfloat16)
    middle = inputs + jnp.dot(mixed_b, w_out, preferred_element_type=jnp.float32)
    moe_normed, inverse_two = rms_forward(middle, moe_gain)
    moe_in = moe_normed.astype(jnp.bfloat16)
    logits = jnp.dot(moe_in, router, preferred_element_type=jnp.float32)
    route_hot = (routes[:, :, None] == jnp.arange(experts_all)[None, None, :]).astype(jnp.float32)
    chosen = jnp.sum(route_hot * logits[:, None, :], axis=-1)
    route_soft = jax.nn.softmax(chosen, axis=-1)
    live_column = live_row.astype(jnp.float32)[:, None]
    route_gates = route_soft * live_column
    counts_local = jnp.sum(route_hot * live_column[:, :, None], axis=(0, 1))
    dense_gates = jnp.sum(route_hot * route_gates[:, :, None], axis=1)
    if special:
        combined, expert_input_grad, gate_upstream_dense, gate_w_grad, up_w_grad, down_w_grad = expert_part(
            moe_in, cotangent, dense_gates, w_gate[0], w_up[0], w_down[0]
        )
        gate_w_grad, up_w_grad, down_w_grad = gate_w_grad[None], up_w_grad[None], down_w_grad[None]
    else:
        upstream_all = lax.all_gather(cotangent, "ep", axis=0, tiled=True)
        gate_all = lax.all_gather(w_gate, "hs", axis=0, tiled=True)
        up_all = lax.all_gather(w_up, "hs", axis=0, tiled=True)
        down_all = lax.all_gather(w_down, "hs", axis=0, tiled=True)
        rows_all = lax.all_gather(moe_in, "ep", axis=0, tiled=True)
        gates_all = lax.all_to_all(
            dense_gates.T.reshape(experts_all, 1, sequence_length), "ep", split_axis=0, concat_axis=1, tiled=True
        ).reshape(-1)
        weighted, back, gate_upstream_all, gate_w_grad, up_w_grad, down_w_grad = expert_pass(
            rows_all, upstream_all, gates_all, gate_all, up_all, down_all
        )
        combined = lax.psum_scatter(weighted, "ep", scatter_dimension=0, tiled=True).astype(jnp.float32)
        expert_input_grad = lax.psum_scatter(back, "ep", scatter_dimension=0, tiled=True).astype(jnp.float32)
        gate_upstream_dense = lax.all_to_all(
            gate_upstream_all.reshape(experts_all, 1, sequence_length), "ep", split_axis=0, concat_axis=1, tiled=True
        ).reshape(experts_all, sequence_length).T
        gate_w_grad = sum_halves(gate_w_grad, 1)[None]
        up_w_grad = sum_halves(up_w_grad, 1)[None]
        down_w_grad = sum_halves(down_w_grad, 0)[None]
    output = (middle + combined).astype(jnp.bfloat16)
    upstream = cotangent.astype(jnp.float32)
    gate_upstream = jnp.sum(route_hot * gate_upstream_dense[:, None, :], axis=-1)
    soft_upstream = gate_upstream * live_column
    chosen_grad = route_soft * (
        soft_upstream - jnp.sum(route_soft * soft_upstream, axis=-1, keepdims=True)
    )
    logit_grad = jnp.sum(route_hot * chosen_grad[:, :, None], axis=1).astype(jnp.bfloat16)
    router_w_grad = jnp.einsum("td,te->de", moe_in, logit_grad, preferred_element_type=jnp.float32)
    moe_in_grad = expert_input_grad + jnp.einsum(
        "te,de->td", logit_grad, router, preferred_element_type=jnp.float32
    )
    middle_norm_grad, moe_gain_grad = rms_backward(middle, inverse_two, moe_gain, moe_in_grad)
    middle_grad = upstream + middle_norm_grad
    attn_grad_b = middle_grad.astype(jnp.bfloat16)
    out_w_grad = jnp.einsum("tm,td->md", mixed_b, attn_grad_b, preferred_element_type=jnp.float32)
    attention_mixed_grad = jnp.einsum(
        "td,md->tm", attn_grad_b, w_out, preferred_element_type=jnp.float32
    ).astype(jnp.bfloat16)
    attention_mixed_grad = attention_mixed_grad.reshape(
        sequence_length, KEY_VALUE_HEADS, query_per_key_head, HEAD_SIZE
    )
    scores_again = (
        jnp.einsum("qgrd,kgd->grqk", grouped_rows, key_b, preferred_element_type=jnp.float32)
        * score_scale
    )
    scores_again = jnp.where(allowed, scores_again, -1e30)
    probs_again = jnp.exp(scores_again - log_total)
    prob_grad = jnp.einsum(
        "qgrd,kgd->grqk", attention_mixed_grad, value_b, preferred_element_type=jnp.float32
    )
    value_per_head_grad = jnp.einsum(
        "grqk,qgrd->kgd",
        probs_again.astype(jnp.bfloat16),
        attention_mixed_grad,
        preferred_element_type=jnp.float32,
    )
    value_per_head_grad = value_per_head_grad.astype(jnp.bfloat16).reshape(
        sequence_length, KEY_VALUE_HEADS * HEAD_SIZE
    )
    row_delta = jnp.sum(probs_again * prob_grad, axis=-1, keepdims=True)
    score_grad = (probs_again * (prob_grad - row_delta)).astype(jnp.bfloat16)
    query_rot_grad = (
        jnp.einsum("grqk,kgd->qgrd", score_grad, key_b, preferred_element_type=jnp.float32)
        * score_scale
    )
    rotated_key_grad = (
        jnp.einsum("grqk,qgrd->kgd", score_grad, grouped_rows, preferred_element_type=jnp.float32)
        * score_scale
    )
    query_head_grad = (
        rotary_backward(
            query_rot_grad.reshape(sequence_length, QUERY_HEADS, HEAD_SIZE),
            cosine_table,
            sine_table,
        )
        .astype(jnp.bfloat16)
        .reshape(sequence_length, QUERY_HEADS * HEAD_SIZE)
    )
    key_head_grad = (
        rotary_backward(rotated_key_grad, cosine_table, sine_table)
        .astype(jnp.bfloat16)
        .reshape(sequence_length, KEY_VALUE_HEADS * HEAD_SIZE)
    )
    query_w_grad = jnp.einsum(
        "td,te->de", normed_rows_back, query_head_grad, preferred_element_type=jnp.float32
    )
    key_w_grad = jnp.einsum(
        "td,te->de", normed_rows_back, key_head_grad, preferred_element_type=jnp.float32
    )
    value_w_grad = jnp.einsum(
        "td,te->de", normed_rows_back, value_per_head_grad, preferred_element_type=jnp.float32
    )
    normed_grad = jnp.einsum(
        "te,de->td", query_head_grad, w_query, preferred_element_type=jnp.float32
    )
    normed_grad = normed_grad + jnp.einsum(
        "te,de->td", key_head_grad, key_weight, preferred_element_type=jnp.float32
    )
    normed_grad = normed_grad + jnp.einsum(
        "te,de->td", value_per_head_grad, value_weight, preferred_element_type=jnp.float32
    )
    input_norm_grad, attn_gain_grad = rms_backward(inputs, inverse_one, attn_gain, normed_grad)
    input_grad = middle_grad + input_norm_grad
    if special:
        small = jnp.zeros((24, model_dim), jnp.float32)
        small = small.at[:experts_all].set(router_w_grad.T)
        small = small.at[16].set(attn_gain_grad).at[17].set(moe_gain_grad)
        small = small.at[18, :experts_all].set(counts_local)
        wide = [g.astype(jnp.bfloat16) for g in (out_w_grad, query_w_grad, key_w_grad, value_w_grad)]
        out_w_grad, query_w_grad, key_w_grad, value_w_grad, small = sum_everywhere(wide, small)
        router_w_grad = small[:experts_all].T
        attn_gain_grad, moe_gain_grad, counts = small[16], small[17], small[18, :experts_all]
    else:
        (
            attn_gain_grad,
            query_w_grad,
            key_w_grad,
            value_w_grad,
            out_w_grad,
            moe_gain_grad,
            router_w_grad,
            counts,
        ) = lax.psum(
            (
                attn_gain_grad,
                query_w_grad,
                key_w_grad,
                value_w_grad,
                out_w_grad,
                moe_gain_grad,
                router_w_grad,
                counts_local,
            ),
            ("ep", "hs"),
        )
    return (
        output,
        input_grad,
        attn_gain_grad,
        query_w_grad,
        key_w_grad,
        value_w_grad,
        out_w_grad,
        moe_gain_grad,
        router_w_grad,
        gate_w_grad,
        up_w_grad,
        down_w_grad,
        counts.astype(jnp.int32),
    )


def solution(mesh):
    in_specs = (
        P(("ep", "hs"), None),
        P(("ep", "hs"), None),
        P(("ep", "hs"), None),
        P(("ep", "hs"), None),
        P(),
        P(),
        P(),
        P(),
        P(),
        P(),
        P(),
        P("ep", None, "hs"),
        P("ep", None, "hs"),
        P("ep", "hs", None),
        P(("ep", "hs"), None),
    )
    out_specs = (
        P(("ep", "hs"), None),
        P(("ep", "hs"), None),
        P(),
        P(),
        P(),
        P(),
        P(),
        P(),
        P(),
        P("ep", None, "hs"),
        P("ep", None, "hs"),
        P("ep", "hs", None),
        P(),
    )
    return jax.shard_map(local, mesh=mesh, in_specs=in_specs, out_specs=out_specs, check_vma=False)
```

```python
import functools

import jax
import jax.numpy as jnp
from jax import lax
from jax.experimental import pallas as pl
from jax.experimental.pallas import tpu as pltpu
from jax.sharding import PartitionSpec as P

QUERY_HEADS = 16
KEY_VALUE_HEADS = 8
HEAD_SIZE = 64
TOP = 8


EPSILON = 1e-05


def rms_forward(value_rows, norm_gain):
    inverse = lax.rsqrt(jnp.mean(value_rows * value_rows, axis=-1, keepdims=True) + EPSILON)
    return (value_rows * inverse * norm_gain, inverse)


def rms_backward(value_rows, inverse, norm_gain, upstream):
    scaled = upstream * norm_gain
    gain_grad = jnp.sum(upstream * value_rows * inverse, axis=0)
    input_grad = inverse * (
        scaled
        - value_rows * inverse * inverse * jnp.mean(scaled * value_rows, axis=-1, keepdims=True)
    )
    return (input_grad, gain_grad)


def positions_of(segment):
    before = (segment[None, :] < segment[:, None]).astype(jnp.int32)
    return jnp.arange(segment.shape[-1], dtype=jnp.int32) - jnp.sum(before, axis=1)


def rotary_tables(positions, head_dim):
    half_dim = head_dim // 2
    frequency = 10000.0 ** (-(jnp.arange(half_dim, dtype=jnp.float32) * 2.0) / head_dim)
    angles = positions.astype(jnp.float32)[:, None] * frequency[None, :]
    return (jnp.cos(angles)[:, None, :], jnp.sin(angles)[:, None, :])


def rotary(heads, cosine_table, sine_table):
    half_dim = heads.shape[-1] // 2
    first_half = heads[..., :half_dim]
    second_half = heads[..., half_dim:]
    return jnp.concatenate(
        [
            first_half * cosine_table - second_half * sine_table,
            second_half * cosine_table + first_half * sine_table,
        ],
        axis=-1,
    )


def rotary_backward(grads, cosine_table, sine_table):
    half_dim = grads.shape[-1] // 2
    first_half = grads[..., :half_dim]
    second_half = grads[..., half_dim:]
    return jnp.concatenate(
        [
            first_half * cosine_table + second_half * sine_table,
            second_half * cosine_table - first_half * sine_table,
        ],
        axis=-1,
    )


def to_bf16(value):
    return lax.reduce_precision(value, 8, 7)


def expert_pass(rows, upstream, gates, gate_w, up_w, down_w):
    groups, model_dim, width = gate_w.shape
    gate_all = jnp.concatenate([gate_w[j] for j in range(groups)], axis=1)
    up_all = jnp.concatenate([up_w[j] for j in range(groups)], axis=1)
    down_all = down_w.reshape(groups * width, model_dim)
    gate_pre = jnp.dot(rows, gate_all, preferred_element_type=jnp.float32)
    up_pre = jnp.dot(rows, up_all, preferred_element_type=jnp.float32)
    sigmoid_part = jax.nn.sigmoid(gate_pre)
    activated = gate_pre * sigmoid_part
    hidden = (activated * up_pre).astype(jnp.bfloat16)
    total = jnp.zeros(rows.shape, jnp.float32)
    for j in range(groups):
        total = total + to_bf16(
            jnp.dot(hidden[:, j * width : (j + 1) * width], down_w[j], preferred_element_type=jnp.float32)
        )
    total = to_bf16(total)
    upstream_f = upstream.astype(jnp.float32)
    gate_upstream = jnp.sum(upstream_f * total, axis=-1)
    weighted = (gates[:, None] * total).astype(jnp.bfloat16)
    upstream_e = (gates[:, None] * upstream_f).astype(jnp.bfloat16)
    hidden_grad = jnp.einsum("td,fd->tf", upstream_e, down_all, preferred_element_type=jnp.float32)
    up_pre_grad = (hidden_grad * activated).astype(jnp.bfloat16)
    gate_pre_grad = (
        hidden_grad * up_pre * sigmoid_part * (1.0 + gate_pre * (1.0 - sigmoid_part))
    ).astype(jnp.bfloat16)
    down_grad = jnp.einsum("tf,td->fd", hidden, upstream_e, preferred_element_type=jnp.float32)
    gate_grad = jnp.einsum("td,tf->df", rows, gate_pre_grad, preferred_element_type=jnp.float32)
    up_grad = jnp.einsum("td,tf->df", rows, up_pre_grad, preferred_element_type=jnp.float32)
    back = jnp.zeros(rows.shape, jnp.float32)
    for j in range(groups):
        cut = slice(j * width, (j + 1) * width)
        back = back + to_bf16(
            jnp.einsum("tf,df->td", gate_pre_grad[:, cut], gate_w[j], preferred_element_type=jnp.float32)
            + jnp.einsum("tf,df->td", up_pre_grad[:, cut], up_w[j], preferred_element_type=jnp.float32)
        )
    return (weighted, back.astype(jnp.bfloat16), gate_upstream, gate_grad, up_grad, down_grad)


def sum_halves(grad, dim):
    return lax.psum_scatter(
        grad.astype(jnp.bfloat16), "hs", scatter_dimension=dim, tiled=True
    ).astype(jnp.float32)


MESH = pl.DeviceIdType.MESH
UNIT = 16


def place():
    ep, hs = lax.axis_index("ep"), lax.axis_index("hs")
    return (ep // 4, (ep // 2) % 2, ep % 2, hs)


def device(z, x, c, y):
    return (z * 4 + x * 2 + c, y)


def greet(peers):
    barrier = pltpu.get_barrier_semaphore()
    for peer in peers:
        pl.semaphore_signal(barrier, inc=1, device_id=peer, device_id_type=MESH)
    pl.semaphore_wait(barrier, len(peers))


EDGE_ORDER = (0, 1, 2, 6, 5, 4, 7, 3)
MIDDLE_ORDER = (0, 1, 2, 3, 7, 5, 6, 4)


def contract(left, right, left_dim, right_dim):
    return lax.dot_general(
        left, right, (((left_dim,), (right_dim,)), ((), ())), preferred_element_type=jnp.float32
    )


def expert_kernel(
    rows_in,
    upstream_in,
    gates_in,
    gate_w,
    up_w,
    down_w,
    weighted_out,
    back_out,
    slope_out,
    own_out,
    again_out,
    streams,
    gates,
    slopes,
    slopes_in,
    w_gate,
    w_up,
    w_down,
    sums,
    partial,
    from_sibling,
    from_line,
    staged_x,
    staged_y,
    staged_again,
    returned_x,
    returned_y,
    load_sem,
    gather_send,
    gather_recv,
    gate_send,
    gate_recv,
    slope_send,
    slope_recv,
    weight_send,
    weight_recv,
    pair_send,
    pair_recv,
    line_send,
    line_recv,
    grad_send,
    grad_recv,
):
    z, x, c, y = place()
    near, far, last = 1 + z % 2, (2 + 3 * z) % 5, 3 - 3 * (z // 2)
    middle = (z == 1) | (z == 2)
    edge = (z == 0) | (z == 3)
    sibling, beside, across = device(z, x, 1 - c, y), device(z, 1 - x, c, y), device(z, x, c, 1 - y)
    corner = device(z, 1 - x, c, 1 - y)
    line = [((z + k) % 4, (c + d) % 2) for k in range(4) for d in range(2) if k or d]
    greet([device(a, x, b, y) for a, b in line] + [beside, across, corner])

    def chip(k):
        half = z // 2
        inner = z + half * (3 - 2 * z)
        spot = k + inner * (1 - 3 * (k // 2) + 2 * (k // 3))
        return spot + half * (3 - 2 * spot)

    def remote(source, target, send, recv, peer):
        return pltpu.make_async_remote_copy(
            src_ref=source, dst_ref=target, send_sem=send, recv_sem=recv, device_id=peer, device_id_type=MESH
        )

    own = [
        pltpu.make_async_copy(ref, streams.at[s, z, c], load_sem.at[s])
        for s, ref in enumerate((rows_in, upstream_in))
    ]
    gates_own = pltpu.make_async_copy(gates_in.at[z, c], gates.at[z, c], load_sem.at[2])
    weights_own = [
        pltpu.make_async_copy(ref, held.at[x, y], load_sem.at[3 + a])
        for a, (ref, held) in enumerate(((gate_w, w_gate), (up_w, w_up), (down_w, w_down)))
    ]
    for copy in (*own, gates_own, *weights_own):
        copy.start()

    def gather(s, block, slot, peer):
        piece = streams.at[s, block, c]
        return remote(piece, piece, gather_send.at[s, slot], gather_recv.at[s, block, c], peer)

    def arrive(s, block, core):
        piece = streams.at[s, block, core]
        pltpu.make_async_copy(piece, piece, gather_recv.at[s, block, core]).wait()

    for s in (0, 1):
        own[s].wait()
        gather(s, z, 0, device(near, x, c, y)).start()
        gather(s, z, 2, sibling).start()

        @pl.when(middle)
        def _():
            gather(s, z, 1, device(far, x, c, y)).start()

    gate_copies = [
        remote(
            gates_in.at[a, b], gates.at[z, c], gate_send.at[n], gate_recv.at[z, c], device(a, x, b, y)
        )
        for n, (a, b) in enumerate(line)
    ]
    for copy in gate_copies:
        copy.start()
    weight_copies = []
    for a, held in enumerate((w_gate, w_up, w_down)):
        weights_own[a].wait()
        for n, peer in enumerate((across, beside, corner)):
            piece = held.at[x, y]
            weight_copies.append(
                remote(piece, piece, weight_send.at[n, a], weight_recv.at[x, y, a], peer)
            )
    for n in range(3):
        for a in range(3):
            weight_copies[a * 3 + n].start()

    def weights_here(expert, group):
        for a, held in enumerate((w_gate, w_up, w_down)):
            piece = held.at[expert, group]
            pltpu.make_async_copy(piece, piece, weight_recv.at[expert, group, a]).wait()

    def zero(u, carry):
        for e in (0, 1):
            for a in range(3):
                sums[e, a, u // 16, pl.ds(pl.multiple_of((u % 16) * 16, 16), 16), :] = jnp.zeros(
                    (16, 1024), jnp.float32
                )
            partial[e, u // 8, (u // 4) % 2, pl.ds(pl.multiple_of((u % 4) * 64, 64), 64), :] = jnp.zeros(
                (64, 1024), jnp.bfloat16
            )
        return carry

    lax.fori_loop(0, 32, zero, 0)

    @pl.when(edge)
    def _():
        for s in (0, 1):
            gather(s, z, 0, device(near, x, c, y)).wait_send()
            gather(s, z, 1, device(far, x, c, y)).start()

    def handle(k):
        block = chip(k)
        for s in (0, 1):
            arrive(s, block, c)
            gather(s, block, 4 + k, sibling).start()
            if k != 2:

                @pl.when(middle)
                def _():
                    gather(s, block, 2 + (k + 1) // 2, device(far, x, c, y)).start()

    handle(1)
    gates_own.wait()
    for a, b in line:
        pltpu.make_async_copy(gates.at[a, b], gates.at[a, b], gate_recv.at[a, b]).wait()
    weights_here(x, 1 - y)
    row_id = lax.broadcasted_iota(jnp.int32, (256, 256), 0)
    lane_id = lax.broadcasted_iota(jnp.int32, (256, 256), 1)

    def compute(expert, block, core):
        diagonal = row_id == lane_id
        gate_row = gates[block, core, pl.ds(expert, 1), :]
        gate = jnp.sum(jnp.where(diagonal, gate_row, 0.0), axis=1, keepdims=True)
        rows = streams[0, block, core]
        total = jnp.zeros((256, 1024), jnp.float32)
        kept = []
        for j in (0, 1):
            gate_pre = contract(rows, w_gate[expert, j], 1, 0)
            up_pre = contract(rows, w_up[expert, j], 1, 0)
            sigmoid_part = jax.nn.sigmoid(gate_pre)
            activated = gate_pre * sigmoid_part
            hidden = (activated * up_pre).astype(jnp.bfloat16)
            part = contract(hidden, w_down[expert, j], 1, 0)
            total = total + part.astype(jnp.bfloat16).astype(jnp.float32)
            inner = up_pre * sigmoid_part * (1.0 + gate_pre * (1.0 - sigmoid_part))
            kept.append((activated, inner, hidden))
        total = total.astype(jnp.bfloat16).astype(jnp.float32)
        upstream = streams[1, block, core].astype(jnp.float32)
        slope = jnp.sum(upstream * total, axis=1, keepdims=True)
        slopes[block, core, pl.ds(expert, 1), :] = jnp.sum(
            jnp.where(diagonal, slope, 0.0), axis=0, keepdims=True
        )
        weighted = gate * total + partial[1, block, core].astype(jnp.float32)
        partial[1, block, core] = weighted.astype(jnp.bfloat16)
        upstream = (gate * upstream).astype(jnp.bfloat16)
        back = jnp.zeros((256, 1024), jnp.float32)
        for j in (0, 1):
            activated, inner, hidden = kept[j]
            hidden_grad = contract(upstream, w_down[expert, j], 1, 1)
            up_grad = (hidden_grad * activated).astype(jnp.bfloat16)
            gate_grad = (hidden_grad * inner).astype(jnp.bfloat16)
            sums[expert, 0, j] += contract(gate_grad, rows, 0, 0)
            sums[expert, 1, j] += contract(up_grad, rows, 0, 0)
            sums[expert, 2, j] += contract(hidden, upstream, 0, 0)
            step = contract(gate_grad, w_gate[expert, j], 1, 1) + contract(up_grad, w_up[expert, j], 1, 1)
            back = back + step.astype(jnp.bfloat16).astype(jnp.float32)
        back = back + partial[0, block, core].astype(jnp.float32)
        partial[0, block, core] = back.astype(jnp.bfloat16)

    def grad_copy(n, source, target, peer):
        return remote(source, target, grad_send.at[n], grad_recv.at[n], peer)

    def pair_copy(s, block):
        return remote(
            partial.at[s, block, 1 - c],
            from_sibling.at[s, block],
            pair_send.at[s, block],
            pair_recv.at[s, block],
            sibling,
        )

    def line_copy(s, block, slot, peer):
        return remote(
            partial.at[s, block, c],
            from_line.at[s, slot],
            line_send.at[s, block],
            line_recv.at[s, slot],
            device(peer, x, c, y),
        )

    def line_wait(s, slot):
        piece = from_line.at[s, slot]
        pltpu.make_async_copy(piece, piece, line_recv.at[s, slot]).wait()

    def add_to(s, block, ref):
        def body(u, carry):
            at = pl.ds(pl.multiple_of(u * 32, 32), 32)
            value = partial[s, block, c, at, :].astype(jnp.float32) + ref[at, :].astype(jnp.float32)
            partial[s, block, c, at, :] = value.astype(jnp.bfloat16)
            return carry

        lax.fori_loop(0, 8, body, 0)

    at_edge = (z * z - 3 * z + 2) // 2
    orders = [sum(code << (3 * t) for t, code in enumerate(codes)) for codes in (EDGE_ORDER, MIDDLE_ORDER)]
    order = at_edge * orders[0] + (1 - at_edge) * orders[1]

    def step(i, carry):
        t = i // 2
        code = lax.shift_right_logical(order, 3 * t) % 8
        again = at_edge * ((t // 3) % 2 + t // 7) + (1 - at_edge) * (t // 4)
        k = code % 4
        expert = x + (code // 4) * (1 - 2 * x)
        block, core = chip(k), (c + i + again) % 2

        @pl.when((i == 2) & middle | (i == 4) & edge)
        def _():
            handle(2)

        @pl.when((i == 4) & middle | (i == 12) & edge)
        def _():
            handle(3)

        @pl.when((i == 8) & middle | (i == 6) & edge)
        def _():
            weights_here(1 - x, y)
            weights_here(1 - x, 1 - y)

        @pl.when((i % 2 == 1) & (again == 0))
        def _():
            for s in (0, 1):
                arrive(s, block, 1 - c)

        compute(expert, block, core)

        @pl.when((i % 2 == 0) & (again == 1))
        def _():
            for s in (0, 1):
                pair_copy(s, block).start()

        @pl.when((i % 2 == 1) & (again == 1) & (k > 0))
        def _():
            for s in (0, 1):
                pair_copy(s, block).wait_recv()
                add_to(s, block, from_sibling.at[s, block])

                @pl.when(edge & (k == 2))
                def _():
                    line_copy(s, block, 3, near).start()

                @pl.when(edge & (k == 1))
                def _():
                    line_copy(s, block, 1, near).start()

                @pl.when(edge & (k == 3))
                def _():
                    line_copy(s, block, 2, last).start()

                @pl.when(middle & (k == 3))
                def _():
                    line_copy(s, block, 1, last).start()

                @pl.when(middle & (k == 2))
                def _():
                    line_copy(s, block, 0, far).start()

        return carry

    lax.fori_loop(0, 16, step, 0)
    low, high = pl.ds(0, 512), pl.ds(512, 512)

    def each(body):
        def rows_of(u, carry):
            at = pl.ds(pl.multiple_of(u * 32, 32), 32)
            for a in range(3):
                body(a, at)
            return carry

        lax.fori_loop(0, 8, rows_of, 0)

    def stage_low(a, at):
        for j in (0, 1):
            staged_x[j, a, at, :] = sums[1 - x, a, j, at, low].astype(jnp.bfloat16)

    def stage_high(a, at):
        staged_y[0, a, at, :] = sums[1 - x, a, 1 - y, at, high].astype(jnp.bfloat16)
        staged_y[1, a, at, :] = sums[x, a, 1 - y, at, high].astype(jnp.bfloat16)

    each(stage_low)
    grad_copy(0, staged_x, returned_x, beside).start()
    each(stage_high)
    grad_copy(1, staged_y, returned_y, across).start()
    slope_copies = [
        remote(
            slopes.at[a, b], slopes_in.at[z, c], slope_send.at[n], slope_recv.at[z, c], device(a, x, b, y)
        )
        for n, (a, b) in enumerate(line)
    ]
    for copy in slope_copies:
        copy.start()
    slopes_in[z, c] = slopes[z, c]

    @pl.when(middle)
    def _():
        for s in (0, 1):
            line_wait(s, 3)
            add_to(s, near, from_line.at[s, 3])
            line_copy(s, near, 0, near).start()

    grad_copy(0, staged_x, returned_x, beside).wait_recv()

    def second_low(a, at):
        value = sums[x, a, 1 - y, at, low] + returned_x[1 - y, a, at, :].astype(jnp.float32)
        staged_again[0, a, at, :] = value.astype(jnp.bfloat16)

    each(second_low)
    again_stores = [pltpu.make_async_copy(staged_again.at[0], again_out.at[0], load_sem.at[3])]
    again_stores[0].start()
    grad_copy(1, staged_y, returned_y, across).wait_recv()

    def second_high(a, at):
        value = sums[1 - x, a, y, at, high] + returned_y[0, a, at, :].astype(jnp.float32)
        staged_again[1, a, at, :] = value.astype(jnp.bfloat16)

    each(second_high)
    again_stores.append(pltpu.make_async_copy(staged_again.at[1], again_out.at[1], load_sem.at[4]))
    again_stores[1].start()

    def own_grad(a, at):
        sums[x, a, y, at, low] += returned_x[y, a, at, :].astype(jnp.float32)
        sums[x, a, y, at, high] += returned_y[1, a, at, :].astype(jnp.float32)

    each(own_grad)
    stores = [pltpu.make_async_copy(sums.at[x, a, y], own_out.at[a], load_sem.at[a]) for a in range(3)]
    for copy in stores:
        copy.start()

    def finish(slots):
        for s in (0, 1):
            for slot in slots:
                line_wait(s, slot)

            def body(u, carry):
                at = pl.ds(pl.multiple_of(u * 32, 32), 32)
                value = partial[s, z, c, at, :].astype(jnp.float32)
                value = value + from_sibling[s, z, at, :].astype(jnp.float32)
                for slot in slots:
                    value = value + from_line[s, slot, at, :].astype(jnp.float32)
                (back_out, weighted_out)[s][at, :] = value
                return carry

            lax.fori_loop(0, 8, body, 0)

    for s in (0, 1):
        pair_copy(s, z).wait_recv()

    @pl.when(middle)
    def _():
        finish((0, 1))

    @pl.when(edge)
    def _():
        finish((0, 1, 2))

    for a, b in line:
        pltpu.make_async_copy(slopes_in.at[a, b], slopes_in.at[a, b], slope_recv.at[a, b]).wait()
    slope_out[...] = slopes_in[...]
    for s in (0, 1):

        @pl.when(middle)
        def _():
            gather(s, z, 0, device(near, x, c, y)).wait_send()

        gather(s, z, 1, device(far, x, c, y)).wait_send()
        gather(s, z, 2, sibling).wait_send()
        for k in (1, 2, 3):
            gather(s, chip(k), 4 + k, sibling).wait_send()
            line_copy(s, chip(k), 0, near).wait_send()

        @pl.when(middle)
        def _():
            for k in (1, 3):
                gather(s, chip(k), 2 + (k + 1) // 2, device(far, x, c, y)).wait_send()

        for k in range(4):
            pair_copy(s, chip(k)).wait_send()
    for copy in (*gate_copies, *weight_copies, *slope_copies):
        copy.wait_send()
    grad_copy(0, staged_x, returned_x, beside).wait_send()
    grad_copy(1, staged_y, returned_y, across).wait_send()
    for copy in (*stores, *again_stores):
        copy.wait()


def expert_part(rows, upstream, gates, gate_w, up_w, down_w):
    tokens, model_dim = rows.shape
    width = gate_w.shape[1]
    vmem, anywhere = pl.BlockSpec(memory_space=pltpu.VMEM), pl.BlockSpec(memory_space=pl.ANY)
    f32, bf16, dma = jnp.float32, jnp.bfloat16, pltpu.SemaphoreType.DMA
    by_owner = gates.T.reshape(4, 2, 2, tokens).swapaxes(1, 2)
    by_owner = jnp.pad(by_owner, ((0, 0), (0, 0), (0, 6), (0, 0)))
    return pl.pallas_call(
        expert_kernel,
        out_shape=[
            jax.ShapeDtypeStruct((tokens, model_dim), f32),
            jax.ShapeDtypeStruct((tokens, model_dim), f32),
            jax.ShapeDtypeStruct((4, 2, 8, tokens), f32),
            jax.ShapeDtypeStruct((3, width, model_dim), f32),
            jax.ShapeDtypeStruct((2, 3, width, model_dim // 2), bf16),
        ],
        in_specs=[anywhere, anywhere, vmem, anywhere, anywhere, anywhere],
        out_specs=[vmem, vmem, vmem, anywhere, anywhere],
        scratch_shapes=[
            pltpu.VMEM((2, 4, 2, tokens, model_dim), bf16),
            pltpu.VMEM((4, 2, 8, tokens), f32),
            pltpu.VMEM((4, 2, 8, tokens), f32),
            pltpu.VMEM((4, 2, 8, tokens), f32),
            pltpu.VMEM((2, 2, model_dim, width), bf16),
            pltpu.VMEM((2, 2, model_dim, width), bf16),
            pltpu.VMEM((2, 2, width, model_dim), bf16),
            pltpu.VMEM((2, 3, 2, width, model_dim), f32),
            pltpu.VMEM((2, 4, 2, tokens, model_dim), bf16),
            pltpu.VMEM((2, 4, tokens, model_dim), bf16),
            pltpu.VMEM((2, 4, tokens, model_dim), bf16),
            *[pltpu.VMEM((2, 3, width, model_dim // 2), bf16)] * 5,
            dma((6,)),
            dma((2, 8)),
            dma((2, 4, 2)),
            dma((7,)),
            dma((4, 2)),
            dma((7,)),
            dma((4, 2)),
            dma((3, 3)),
            dma((2, 2, 3)),
            dma((2, 4)),
            dma((2, 4)),
            dma((2, 4)),
            dma((2, 4)),
            dma((2,)),
            dma((2,)),
        ],
        compiler_params=pltpu.CompilerParams(
            collective_id=1, has_side_effects=True, vmem_limit_bytes=62 << 20
        ),
        name="expert_part",
    )(rows, upstream, by_owner, gate_w, up_w, down_w)
TAIL_ORDER = (
    (0, 4), (2, 1), (3, 1), (4, 1), (5, 1), (1, 4), (0, 5), (2, 2), (1, 5), (3, 2),
    (4, 2), (5, 2), (0, 6), (2, 3), (1, 6), (3, 3), (4, 3), (2, 4), (5, 3), (3, 4),
    (0, 7), (4, 4), (0, 8), (1, 7), (2, 5), (1, 8), (5, 4), (2, 6), (3, 5), (2, 7),
    (4, 5), (3, 6), (2, 8), (5, 5), (4, 6), (3, 7), (5, 6), (3, 8), (4, 7), (4, 8),
    (5, 7), (5, 8),
)


def turn(value, cosine, sine):
    lane = lax.broadcasted_iota(jnp.int32, value.shape, 1) % HEAD_SIZE
    swapped = jnp.where(
        lane < HEAD_SIZE // 2, pltpu.roll(value, 128 - HEAD_SIZE // 2, 1), pltpu.roll(value, HEAD_SIZE // 2, 1)
    )
    return value * cosine + swapped * sine


def tail_kernel(
    tokens,
    normed,
    query,
    key,
    value,
    mixed,
    middle,
    moe_in,
    upstream_in,
    combined,
    back,
    slopes,
    soft,
    live,
    counts,
    router,
    cosine,
    sine,
    bias,
    attn_gain,
    moe_gain,
    w_query_in,
    w_key_in,
    w_value_in,
    w_out_in,
    again_in,
    own_in,
    output,
    input_grad,
    out_sum,
    query_sum,
    key_sum,
    value_sum,
    small_out,
    tiny_out,
    gate_grad,
    up_grad,
    down_grad,
    w_query,
    w_key,
    w_value,
    w_out,
    keys,
    values,
    key_slopes,
    value_slopes,
    mixed_slope,
    query_slope,
    again,
    returned_again,
    own,
    *rest,
):
    count = 6
    grads, halves, totals, fulls, firsts, seconds, lines = [rest[n * count : (n + 1) * count] for n in range(7)]
    small_sum, small_in, tiny_sum, tiny_in, send, recv, small_send, small_recv, local_sem, load_sem, again_send, again_recv = rest[7 * count :]
    outs = [ref.at[:, :, pl.ds(n * 512, 512)] for ref in (out_sum, query_sum) for n in (0, 1)]
    outs += [key_sum, value_sum]
    z, x, c, y = place()
    sibling, beside, across = device(z, x, 1 - c, y), device(z, 1 - x, c, y), device(z, x, c, 1 - y)
    along = [device((z + k) % 4, x, c, y) for k in (1, 2, 3)]
    loads = [
        pltpu.make_async_copy(source, target, load_sem.at[n])
        for n, (source, target) in enumerate(
            (
                (again_in, again),
                (w_out_in, w_out),
                (w_query_in, w_query),
                (w_key_in, w_key),
                (w_value_in, w_value),
                (own_in, own),
            )
        )
    ]
    for copy in loads:
        copy.start()
    greet([sibling, beside, across] + along)
    loads[0].wait()
    again_copies = [
        pltpu.make_async_remote_copy(
            src_ref=again.at[n],
            dst_ref=returned_again.at[n],
            send_sem=again_send.at[n],
            recv_sem=again_recv.at[n],
            device_id=peer,
            device_id_type=MESH,
        )
        for n, peer in enumerate((across, beside))
    ]
    for copy in again_copies:
        copy.start()
    bits = ((x, y), (y, x))
    partners = ((beside, across), (across, beside))

    def push(i, slot, source, target, peer):
        copy = pltpu.make_async_remote_copy(
            src_ref=source,
            dst_ref=target,
            send_sem=send.at[i, slot],
            recv_sem=recv.at[i, slot],
            device_id=peer,
            device_id_type=MESH,
        )
        copy.start()
        return copy

    def combine(i, target, start, length, terms):
        def body(u, carry):
            value = totals[i][start + u].astype(jnp.float32)
            for ref, base in terms:
                value = value + ref[base + u].astype(jnp.float32)
            target[0][target[1] + u] = value.astype(jnp.bfloat16)
            return carry

        lax.fori_loop(0, length, body, 0)

    copies = {}

    def stage(i, step):
        if step == 0:
            copies[i, 0] = [
                push(i, 0, grads[i].at[pl.ds((1 - c) * 32, 32)], halves[i], sibling)
            ]
        if step == 1:
            copies[i, 0][0].wait_recv()

            def body(u, carry):
                value = grads[i][c * 32 + u].astype(jnp.float32) + halves[i][u].astype(jnp.float32)
                totals[i][u] = value.astype(jnp.bfloat16)
                return carry

            lax.fori_loop(0, 32, body, 0)
            copies[i, 1] = [
                push(
                    i,
                    1 + part,
                    totals[i].at[pl.ds(part * 16 + (1 - bits[part][0]) * 8, 8)],
                    firsts[i].at[part],
                    partners[part][0],
                )
                for part in (0, 1)
            ]
        if step == 2:
            copies[i, 2] = []
            for part in (0, 1):
                copies[i, 1][part].wait_recv()
                base = part * 16 + bits[part][0] * 8
                combine(i, (totals[i], base), base, 8, [(firsts[i].at[part], 0)])
                copies[i, 2].append(
                    push(
                        i,
                        3 + part,
                        totals[i].at[pl.ds(base + (1 - bits[part][1]) * 4, 4)],
                        seconds[i].at[part],
                        partners[part][1],
                    )
                )
        if step == 3:
            copies[i, 3] = []
            for part in (0, 1):
                copies[i, 2][part].wait_recv()
                base = part * 16 + bits[part][0] * 8 + bits[part][1] * 4
                combine(i, (totals[i], base), base, 4, [(seconds[i].at[part], 0)])
                for k in (1, 2, 3):
                    copies[i, 3].append(
                        push(
                            i,
                            5 + part * 3 + k - 1,
                            totals[i].at[base + (z + k) % 4],
                            lines[i].at[part, k - 1],
                            along[k - 1],
                        )
                    )
        if step == 4:
            copies[i, 4] = []
            for part in (0, 1):
                for k in (1, 2, 3):
                    copies[i, 3][part * 3 + k - 1].wait_recv()
                base = part * 16 + bits[part][0] * 8 + bits[part][1] * 4
                combine(
                    i, (fulls[i], c * 32 + base + z), base + z, 1, [(lines[i].at[part], k) for k in (0, 1, 2)]
                )
                for k in (1, 2, 3):
                    piece = fulls[i].at[c * 32 + base + z]
                    copies[i, 4].append(push(i, 11 + part * 3 + k - 1, piece, piece, along[k - 1]))
        if step == 5:
            copies[i, 5] = []
            for part in (0, 1):
                for k in (1, 2, 3):
                    copies[i, 4][part * 3 + k - 1].wait_recv()
                piece = fulls[i].at[pl.ds(c * 32 + part * 16 + bits[part][0] * 8 + bits[part][1] * 4, 4)]
                copies[i, 5].append(push(i, 17 + part, piece, piece, partners[part][1]))
        if step == 6:
            copies[i, 6] = []
            for part in (0, 1):
                copies[i, 5][part].wait_recv()
                piece = fulls[i].at[pl.ds(c * 32 + part * 16 + bits[part][0] * 8, 8)]
                copies[i, 6].append(push(i, 19 + part, piece, piece, partners[part][0]))
        if step == 7:
            for part in (0, 1):
                copies[i, 6][part].wait_recv()
            piece = fulls[i].at[pl.ds(c * 32, 32)]
            copies[i, 7] = [push(i, 21, piece, piece, sibling)]
        if step == 8:
            copies[i, 7][0].wait_recv()
            done = pltpu.make_async_copy(fulls[i], outs[i], local_sem.at[i])
            done.start()
            copies[i, 8] = [done]

    def small_stage(n, step):
        total, arrived = (small_sum, tiny_sum)[n], (small_in, tiny_in)[n]

        def small_push(slot, peer, source, target):
            copy = pltpu.make_async_remote_copy(
                src_ref=total.at[source],
                dst_ref=arrived.at[target],
                send_sem=small_send.at[n, slot],
                recv_sem=small_recv.at[n, slot],
                device_id=peer,
                device_id_type=MESH,
            )
            copy.start()
            copies.setdefault((n, "s", step), []).append(copy)

        if step == 0:
            small_push(0, sibling, 0, 0)
        if step in (1, 2, 3):
            copies[n, "s", step - 1][0].wait_recv()
            total[step] = total[step - 1] + arrived[step - 1]
        if step in (1, 2):
            small_push(step, (beside, across)[step - 1], step, step)
        if step == 3:
            for k in (1, 2, 3):
                small_push(2 + k, along[k - 1], 3, 3 + z)
            arrived[3 + z] = total[3]
        if step == 4:
            for copy in copies[n, "s", 3]:
                copy.wait_recv()
            (small_out, tiny_out)[n][...] = (arrived[3] + arrived[4]) + (arrived[5] + arrived[6])

    inner = upstream_in[...].astype(jnp.float32)
    slope_rows = jnp.concatenate([slopes[e // 4, e % 2, pl.ds((e // 2) % 2, 1), :] for e in range(16)], axis=0)
    soft_slope = slope_rows * live[...]
    soft_t = soft[...]
    dlogits = soft_t * (soft_slope - jnp.sum(soft_t * soft_slope, axis=0, keepdims=True))
    dlogits = dlogits.astype(jnp.bfloat16)
    small_sum[0] = jnp.zeros(small_sum.shape[1:], jnp.float32)
    small_sum[0, pl.ds(0, 16), :] = contract(dlogits, moe_in[...], 1, 0)
    small_sum[0, pl.ds(18, 1), :] = counts[...]
    dmoe_in = back[...] + contract(dlogits, router[...], 0, 0)
    mid = middle[...]
    output[...] = (mid + combined[...]).astype(jnp.bfloat16)
    inverse = lax.rsqrt(jnp.mean(mid * mid, axis=1, keepdims=True) + EPSILON)
    small_sum[0, pl.ds(17, 1), :] = jnp.sum(dmoe_in * mid * inverse, axis=0, keepdims=True)
    scaled = dmoe_in * moe_gain[...]
    dmiddle = inner + inverse * (
        scaled - mid * inverse * inverse * jnp.mean(scaled * mid, axis=1, keepdims=True)
    )
    input_grad[...] = dmiddle
    dattn = dmiddle.astype(jnp.bfloat16)

    def weight_grad(i, left, right):
        for r in range(4):
            rows = contract(left[:, pl.ds(r * 256, 256)], right, 0, 0).astype(jnp.bfloat16)
            grads[i][pl.ds(r * 16, 16)] = rows.reshape(16, 16, 512)

    small_stage(0, 0)
    weight_grad(0, mixed, dattn[:, :512])
    stage(0, 0)
    weight_grad(1, mixed, dattn[:, 512:])
    stage(1, 0)
    loads[1].wait()
    mixed_slope[...] = contract(dattn, w_out[...], 1, 1).astype(jnp.bfloat16)
    for g in range(8):
        keys[g] = key[:, pl.ds(g * 64, 64)]
        values[g] = value[:, pl.ds(g * 64, 64)]
    scale = HEAD_SIZE ** (-0.5)

    def group(g, carry):
        columns = pl.ds(pl.multiple_of(g * 128, 128), 128)
        key_g, value_g = keys[g], values[g]
        query_pair, slope_pair = query[:, columns], mixed_slope[:, columns]
        key_slope = jnp.zeros((256, 64), jnp.float32)
        value_slope = jnp.zeros((256, 64), jnp.float32)
        query_slopes = []
        for r in (0, 1):
            query_h, slope_h = query_pair[:, r * 64 : r * 64 + 64], slope_pair[:, r * 64 : r * 64 + 64]
            scores = contract(query_h, key_g, 1, 1) * scale + bias[...]
            weights = jnp.exp(scores - jnp.max(scores, axis=1, keepdims=True))
            probs = weights / jnp.sum(weights, axis=1, keepdims=True)
            prob_slope = contract(slope_h, value_g, 1, 1)
            value_slope = value_slope + contract(probs.astype(jnp.bfloat16), slope_h, 0, 0)
            delta = jnp.sum(probs * prob_slope, axis=1, keepdims=True)
            score_slope = (probs * (prob_slope - delta)).astype(jnp.bfloat16)
            query_slopes.append(contract(score_slope, key_g, 1, 0) * scale)
            key_slope = key_slope + contract(score_slope, query_h, 0, 0) * scale
        pair = turn(jnp.concatenate(query_slopes, axis=1), cosine[...], -sine[...])
        query_slope[:, columns] = pair.astype(jnp.bfloat16)
        key_slopes[g] = key_slope
        value_slopes[g] = value_slope
        return carry

    stage(0, 1)
    stage(1, 1)
    small_stage(0, 1)
    lax.fori_loop(0, 5, group, 0)
    small_stage(0, 2)
    stage(0, 2)
    stage(1, 2)
    lax.fori_loop(5, 8, group, 0)
    small_stage(0, 3)
    stage(0, 3)
    stage(1, 3)
    loads[2].wait()
    loads[3].wait()
    loads[4].wait()
    for n in (0, 1):
        weight_grad(2 + n, normed, query_slope[:, n * 512 : n * 512 + 512])
        stage(2 + n, 0)
    key_slope = jnp.concatenate(
        [
            turn(jnp.concatenate([key_slopes[2 * p], key_slopes[2 * p + 1]], axis=1), cosine[...], -sine[...])
            for p in range(4)
        ],
        axis=1,
    ).astype(jnp.bfloat16)
    weight_grad(4, normed, key_slope)
    stage(4, 0)
    value_slope = jnp.concatenate(
        [jnp.concatenate([value_slopes[2 * p], value_slopes[2 * p + 1]], axis=1) for p in range(4)], axis=1
    ).astype(jnp.bfloat16)
    weight_grad(5, normed, value_slope)
    stage(5, 0)
    todo = list(TAIL_ORDER)

    def proceed(steps):
        for _ in range(min(steps, len(todo))):
            stage(*todo.pop(0))

    proceed(6)
    dnormed = contract(query_slope[...], w_query[...], 1, 1)
    dnormed = dnormed + contract(key_slope, w_key[...], 1, 1)
    dnormed = dnormed + contract(value_slope, w_value[...], 1, 1)
    start = tokens[...].astype(jnp.float32)
    inverse = lax.rsqrt(jnp.mean(start * start, axis=1, keepdims=True) + EPSILON)
    gain_slope = jnp.sum(dnormed * start * inverse, axis=0, keepdims=True)
    for r in range(8):
        tiny_sum[0, pl.ds(r, 1), :] = gain_slope[:, r * 128 : r * 128 + 128]
    scaled = dnormed * attn_gain[...]
    input_grad[...] += inverse * (
        scaled - start * inverse * inverse * jnp.mean(scaled * start, axis=1, keepdims=True)
    )
    small_stage(1, 0)
    proceed(4)
    small_stage(1, 1)
    proceed(4)
    small_stage(1, 2)
    small_stage(0, 4)
    loads[5].wait()
    for copy in again_copies:
        copy.wait_recv()
    for a, target in enumerate((gate_grad, up_grad, down_grad)):
        for n in (0, 1):
            columns = pl.ds(n * 512, 512)
            summed = own[a, :, columns] + returned_again[n, a].astype(jnp.float32)
            if a < 2:
                target[columns, :] = summed.T
            else:
                target[:, columns] = summed
    proceed(4)
    small_stage(1, 3)
    proceed(4)
    small_stage(1, 4)
    proceed(len(todo))
    for key_of, made in copies.items():
        for copy in made:
            if key_of[1] == 8:
                copy.wait()
            else:
                copy.wait_send()
    for copy in again_copies:
        copy.wait_send()


def tail_part(operands, weights, again, own):
    tokens, model_dim = operands[0].shape
    narrow = weights[1].shape[1]
    vmem, anywhere = pl.BlockSpec(memory_space=pltpu.VMEM), pl.BlockSpec(memory_space=pl.ANY)
    f32, bf16, dma = jnp.float32, jnp.bfloat16, pltpu.SemaphoreType.DMA
    widths = (model_dim, model_dim, narrow, narrow)
    leads = ((64,), (32,), (32,), (64,), (2, 8), (2, 4), (2, 3))
    shape = jax.ShapeDtypeStruct
    width = own.shape[1]
    out = pl.pallas_call(
        tail_kernel,
        out_shape=[
            shape((tokens, model_dim), bf16),
            shape((tokens, model_dim), f32),
            *[shape((64, UNIT, w), bf16) for w in widths],
            shape((24, model_dim), f32),
            shape((8, 128), f32),
            shape((model_dim, width), f32),
            shape((model_dim, width), f32),
            shape((width, model_dim), f32),
        ],
        in_specs=[vmem] * len(operands) + [anywhere] * 6,
        out_specs=[vmem, vmem] + [anywhere] * 4 + [vmem] * 5,
        scratch_shapes=[
            *[pltpu.VMEM(w.shape, bf16) for w in weights],
            pltpu.VMEM((8, tokens, HEAD_SIZE), bf16),
            pltpu.VMEM((8, tokens, HEAD_SIZE), bf16),
            pltpu.VMEM((8, tokens, HEAD_SIZE), f32),
            pltpu.VMEM((8, tokens, HEAD_SIZE), f32),
            pltpu.VMEM((tokens, model_dim), bf16),
            pltpu.VMEM((tokens, model_dim), bf16),
            pltpu.VMEM(again.shape, bf16),
            pltpu.VMEM(again.shape, bf16),
            pltpu.VMEM(own.shape, f32),
            *[pltpu.VMEM((*lead, UNIT, 512), bf16) for lead in leads for _ in range(6)],
            pltpu.VMEM((4, 24, model_dim), f32),
            pltpu.VMEM((7, 24, model_dim), f32),
            pltpu.VMEM((4, 8, 128), f32),
            pltpu.VMEM((7, 8, 128), f32),
            dma((6, 22)),
            dma((6, 22)),
            dma((2, 6)),
            dma((2, 6)),
            dma((6,)),
            dma((6,)),
            dma((2,)),
            dma((2,)),
        ],
        compiler_params=pltpu.CompilerParams(
            collective_id=0, has_side_effects=True, vmem_limit_bytes=60 << 20
        ),
        name="tail_part",
    )(*operands, *weights, again, own)
    grads = [o.reshape(-1, o.shape[2]).astype(jnp.float32) for o in out[2:6]]
    return (out[0], out[1], grads, out[6], out[7], out[8:11])


def local(
    tokens,
    segment_ids,
    live_mask,
    routes,
    attn_gain,
    w_query,
    key_weight,
    value_weight,
    w_out,
    moe_gain,
    router,
    w_gate,
    w_up,
    w_down,
    cotangent,
):
    sequence_length = tokens.shape[0]
    model_dim = tokens.shape[1]
    experts_all = router.shape[1]
    query_per_key_head = QUERY_HEADS // KEY_VALUE_HEADS
    score_scale = HEAD_SIZE ** (-0.5)
    special = lax.axis_size("ep") == 16 and lax.axis_size("hs") == 2
    segment = segment_ids[0]
    live_row = live_mask[0]
    inputs = tokens.astype(jnp.float32)
    normed_rows, inverse_one = rms_forward(inputs, attn_gain)
    normed_rows_back = normed_rows.astype(jnp.bfloat16)
    query_pre = jnp.dot(normed_rows_back, w_query, preferred_element_type=jnp.float32).reshape(
        sequence_length, QUERY_HEADS, HEAD_SIZE
    )
    key_before_rotary = jnp.dot(
        normed_rows_back, key_weight, preferred_element_type=jnp.float32
    ).reshape(sequence_length, KEY_VALUE_HEADS, HEAD_SIZE)
    value_b = (
        jnp.dot(normed_rows_back, value_weight, preferred_element_type=jnp.float32)
        .astype(jnp.bfloat16)
        .reshape(sequence_length, KEY_VALUE_HEADS, HEAD_SIZE)
    )
    positions = positions_of(segment)
    cosine_table, sine_table = rotary_tables(positions, HEAD_SIZE)
    query_back_rows = rotary(query_pre, cosine_table, sine_table).astype(jnp.bfloat16)
    key_b = rotary(key_before_rotary, cosine_table, sine_table).astype(jnp.bfloat16)
    indices = jnp.arange(sequence_length)
    allowed = (
        (segment[:, None] == segment[None, :])
        & (indices[None, :] <= indices[:, None])
        & ((live_row[None, :] > 0) | (indices[None, :] == indices[:, None]))
    )
    grouped_rows = query_back_rows.reshape(
        sequence_length, KEY_VALUE_HEADS, query_per_key_head, HEAD_SIZE
    )
    scores = (
        jnp.einsum("qgrd,kgd->grqk", grouped_rows, key_b, preferred_element_type=jnp.float32)
        * score_scale
    )
    scores = jnp.where(allowed, scores, -1e30)
    highest = jnp.max(scores, axis=-1, keepdims=True)
    weights_exp = jnp.exp(scores - highest)
    denominator = jnp.sum(weights_exp, axis=-1, keepdims=True)
    log_total = highest + jnp.log(denominator)
    probabilities = weights_exp / denominator
    mixed = jnp.einsum(
        "grqk,kgd->qgrd",
        probabilities.astype(jnp.bfloat16),
        value_b,
        preferred_element_type=jnp.float32,
    )
    mixed_b = mixed.reshape(sequence_length, QUERY_HEADS * HEAD_SIZE).astype(jnp.bfloat16)
    middle = inputs + jnp.dot(mixed_b, w_out, preferred_element_type=jnp.float32)
    moe_normed, inverse_two = rms_forward(middle, moe_gain)
    moe_in = moe_normed.astype(jnp.bfloat16)
    logits = jnp.dot(moe_in, router, preferred_element_type=jnp.float32)
    route_hot = (routes[:, :, None] == jnp.arange(experts_all)[None, None, :]).astype(jnp.float32)
    chosen = jnp.sum(route_hot * logits[:, None, :], axis=-1)
    route_soft = jax.nn.softmax(chosen, axis=-1)
    live_column = live_row.astype(jnp.float32)[:, None]
    route_gates = route_soft * live_column
    counts_local = jnp.sum(route_hot * live_column[:, :, None], axis=(0, 1))
    dense_gates = jnp.sum(route_hot * route_gates[:, :, None], axis=1)
    if special:
        route_soft_dense = jnp.sum(route_hot * route_soft[:, :, None], axis=1)
        combined, back, slopes, own, again = expert_part(
            moe_in, cotangent, dense_gates, w_gate[0], w_up[0], w_down[0]
        )
        sign = jnp.concatenate([-sine_table[:, 0], sine_table[:, 0]], axis=1)
        operands = (
            tokens,
            normed_rows_back,
            query_back_rows.reshape(sequence_length, -1),
            key_b.reshape(sequence_length, -1),
            value_b.reshape(sequence_length, -1),
            mixed_b,
            middle,
            moe_in,
            cotangent,
            combined,
            back,
            slopes,
            route_soft_dense.T,
            live_row.astype(jnp.float32)[None],
            jnp.pad(counts_local, (0, model_dim - experts_all))[None],
            router.T,
            jnp.tile(cosine_table[:, 0], (1, 4)),
            jnp.tile(sign, (1, 2)),
            jnp.where(allowed, 0.0, -1e30),
            attn_gain[None],
            moe_gain[None],
        )
        output, input_grad, grads, small, tiny, expert_grads = tail_part(
            operands, (w_query, key_weight, value_weight, w_out), again, own
        )
        return (
            output,
            input_grad,
            tiny.reshape(model_dim),
            grads[1],
            grads[2],
            grads[3],
            grads[0],
            small[17],
            small[:experts_all].T,
            *[g[None] for g in expert_grads],
            small[18, :experts_all].astype(jnp.int32),
        )
    upstream_all = lax.all_gather(cotangent, "ep", axis=0, tiled=True)
    gate_all = lax.all_gather(w_gate, "hs", axis=0, tiled=True)
    up_all = lax.all_gather(w_up, "hs", axis=0, tiled=True)
    down_all = lax.all_gather(w_down, "hs", axis=0, tiled=True)
    rows_all = lax.all_gather(moe_in, "ep", axis=0, tiled=True)
    gates_all = lax.all_to_all(
        dense_gates.T.reshape(experts_all, 1, sequence_length), "ep", split_axis=0, concat_axis=1, tiled=True
    ).reshape(-1)
    weighted, back, gate_upstream_all, gate_w_grad, up_w_grad, down_w_grad = expert_pass(
        rows_all, upstream_all, gates_all, gate_all, up_all, down_all
    )
    combined = lax.psum_scatter(weighted, "ep", scatter_dimension=0, tiled=True).astype(jnp.float32)
    expert_input_grad = lax.psum_scatter(back, "ep", scatter_dimension=0, tiled=True).astype(jnp.float32)
    gate_upstream_dense = lax.all_to_all(
        gate_upstream_all.reshape(experts_all, 1, sequence_length), "ep", split_axis=0, concat_axis=1, tiled=True
    ).reshape(experts_all, sequence_length).T
    gate_w_grad = sum_halves(gate_w_grad, 1)[None]
    up_w_grad = sum_halves(up_w_grad, 1)[None]
    down_w_grad = sum_halves(down_w_grad, 0)[None]
    output = (middle + combined).astype(jnp.bfloat16)
    upstream = cotangent.astype(jnp.float32)
    gate_upstream = jnp.sum(route_hot * gate_upstream_dense[:, None, :], axis=-1)
    soft_upstream = gate_upstream * live_column
    chosen_grad = route_soft * (
        soft_upstream - jnp.sum(route_soft * soft_upstream, axis=-1, keepdims=True)
    )
    logit_grad = jnp.sum(route_hot * chosen_grad[:, :, None], axis=1).astype(jnp.bfloat16)
    router_w_grad = jnp.einsum("td,te->de", moe_in, logit_grad, preferred_element_type=jnp.float32)
    moe_in_grad = expert_input_grad + jnp.einsum(
        "te,de->td", logit_grad, router, preferred_element_type=jnp.float32
    )
    middle_norm_grad, moe_gain_grad = rms_backward(middle, inverse_two, moe_gain, moe_in_grad)
    middle_grad = upstream + middle_norm_grad
    attn_grad_b = middle_grad.astype(jnp.bfloat16)
    out_w_grad = jnp.einsum("tm,td->md", mixed_b, attn_grad_b, preferred_element_type=jnp.float32)
    attention_mixed_grad = jnp.einsum(
        "td,md->tm", attn_grad_b, w_out, preferred_element_type=jnp.float32
    ).astype(jnp.bfloat16)
    attention_mixed_grad = attention_mixed_grad.reshape(
        sequence_length, KEY_VALUE_HEADS, query_per_key_head, HEAD_SIZE
    )
    scores_again = (
        jnp.einsum("qgrd,kgd->grqk", grouped_rows, key_b, preferred_element_type=jnp.float32)
        * score_scale
    )
    scores_again = jnp.where(allowed, scores_again, -1e30)
    probs_again = jnp.exp(scores_again - log_total)
    prob_grad = jnp.einsum(
        "qgrd,kgd->grqk", attention_mixed_grad, value_b, preferred_element_type=jnp.float32
    )
    value_per_head_grad = jnp.einsum(
        "grqk,qgrd->kgd",
        probs_again.astype(jnp.bfloat16),
        attention_mixed_grad,
        preferred_element_type=jnp.float32,
    )
    value_per_head_grad = value_per_head_grad.astype(jnp.bfloat16).reshape(
        sequence_length, KEY_VALUE_HEADS * HEAD_SIZE
    )
    row_delta = jnp.sum(probs_again * prob_grad, axis=-1, keepdims=True)
    score_grad = (probs_again * (prob_grad - row_delta)).astype(jnp.bfloat16)
    query_rot_grad = (
        jnp.einsum("grqk,kgd->qgrd", score_grad, key_b, preferred_element_type=jnp.float32)
        * score_scale
    )
    rotated_key_grad = (
        jnp.einsum("grqk,qgrd->kgd", score_grad, grouped_rows, preferred_element_type=jnp.float32)
        * score_scale
    )
    query_head_grad = (
        rotary_backward(
            query_rot_grad.reshape(sequence_length, QUERY_HEADS, HEAD_SIZE),
            cosine_table,
            sine_table,
        )
        .astype(jnp.bfloat16)
        .reshape(sequence_length, QUERY_HEADS * HEAD_SIZE)
    )
    key_head_grad = (
        rotary_backward(rotated_key_grad, cosine_table, sine_table)
        .astype(jnp.bfloat16)
        .reshape(sequence_length, KEY_VALUE_HEADS * HEAD_SIZE)
    )
    query_w_grad = jnp.einsum(
        "td,te->de", normed_rows_back, query_head_grad, preferred_element_type=jnp.float32
    )
    key_w_grad = jnp.einsum(
        "td,te->de", normed_rows_back, key_head_grad, preferred_element_type=jnp.float32
    )
    value_w_grad = jnp.einsum(
        "td,te->de", normed_rows_back, value_per_head_grad, preferred_element_type=jnp.float32
    )
    normed_grad = jnp.einsum(
        "te,de->td", query_head_grad, w_query, preferred_element_type=jnp.float32
    )
    normed_grad = normed_grad + jnp.einsum(
        "te,de->td", key_head_grad, key_weight, preferred_element_type=jnp.float32
    )
    normed_grad = normed_grad + jnp.einsum(
        "te,de->td", value_per_head_grad, value_weight, preferred_element_type=jnp.float32
    )
    input_norm_grad, attn_gain_grad = rms_backward(inputs, inverse_one, attn_gain, normed_grad)
    input_grad = middle_grad + input_norm_grad
    (
        attn_gain_grad,
        query_w_grad,
        key_w_grad,
        value_w_grad,
        out_w_grad,
        moe_gain_grad,
        router_w_grad,
        counts,
    ) = lax.psum(
        (
            attn_gain_grad,
            query_w_grad,
            key_w_grad,
            value_w_grad,
            out_w_grad,
            moe_gain_grad,
            router_w_grad,
            counts_local,
        ),
        ("ep", "hs"),
    )
    return (
        output,
        input_grad,
        attn_gain_grad,
        query_w_grad,
        key_w_grad,
        value_w_grad,
        out_w_grad,
        moe_gain_grad,
        router_w_grad,
        gate_w_grad,
        up_w_grad,
        down_w_grad,
        counts.astype(jnp.int32),
    )


def solution(mesh):
    in_specs = (
        P(("ep", "hs"), None),
        P(("ep", "hs"), None),
        P(("ep", "hs"), None),
        P(("ep", "hs"), None),
        P(),
        P(),
        P(),
        P(),
        P(),
        P(),
        P(),
        P("ep", None, "hs"),
        P("ep", None, "hs"),
        P("ep", "hs", None),
        P(("ep", "hs"), None),
    )
    out_specs = (
        P(("ep", "hs"), None),
        P(("ep", "hs"), None),
        P(),
        P(),
        P(),
        P(),
        P(),
        P(),
        P(),
        P("ep", None, "hs"),
        P("ep", None, "hs"),
        P("ep", "hs", None),
        P(),
    )
    return jax.shard_map(local, mesh=mesh, in_specs=in_specs, out_specs=out_specs, check_vma=False)
```

```python
import jax
import jax.numpy as jnp
import numpy as np
from jax import lax
from jax.experimental import pallas as pl
from jax.experimental.pallas import tpu as pltpu
from jax.sharding import PartitionSpec as P

QUERY_HEADS = 16
KEY_VALUE_HEADS = 8
HEAD_SIZE = 64
TOP = 8


EPSILON = 1e-05


def rms_forward(value_rows, norm_gain):
    inverse = lax.rsqrt(jnp.mean(value_rows * value_rows, axis=-1, keepdims=True) + EPSILON)
    return (value_rows * inverse * norm_gain, inverse)


def rms_backward(value_rows, inverse, norm_gain, upstream):
    scaled = upstream * norm_gain
    gain_grad = jnp.sum(upstream * value_rows * inverse, axis=0)
    input_grad = inverse * (
        scaled
        - value_rows * inverse * inverse * jnp.mean(scaled * value_rows, axis=-1, keepdims=True)
    )
    return (input_grad, gain_grad)


def positions_of(segment):
    before = (segment[None, :] < segment[:, None]).astype(jnp.int32)
    return jnp.arange(segment.shape[-1], dtype=jnp.int32) - jnp.sum(before, axis=1)


def rotary_tables(positions, head_dim):
    half_dim = head_dim // 2
    frequency = 10000.0 ** (-(jnp.arange(half_dim, dtype=jnp.float32) * 2.0) / head_dim)
    angles = positions.astype(jnp.float32)[:, None] * frequency[None, :]
    return (jnp.cos(angles)[:, None, :], jnp.sin(angles)[:, None, :])


def rotary(heads, cosine_table, sine_table):
    half_dim = heads.shape[-1] // 2
    first_half = heads[..., :half_dim]
    second_half = heads[..., half_dim:]
    return jnp.concatenate(
        [
            first_half * cosine_table - second_half * sine_table,
            second_half * cosine_table + first_half * sine_table,
        ],
        axis=-1,
    )


def rotary_backward(grads, cosine_table, sine_table):
    half_dim = grads.shape[-1] // 2
    first_half = grads[..., :half_dim]
    second_half = grads[..., half_dim:]
    return jnp.concatenate(
        [
            first_half * cosine_table + second_half * sine_table,
            second_half * cosine_table - first_half * sine_table,
        ],
        axis=-1,
    )


def to_bf16(value):
    return lax.reduce_precision(value, 8, 7)


def expert_pass(rows, upstream, gates, gate_w, up_w, down_w):
    groups, model_dim, width = gate_w.shape
    gate_all = jnp.concatenate([gate_w[j] for j in range(groups)], axis=1)
    up_all = jnp.concatenate([up_w[j] for j in range(groups)], axis=1)
    down_all = down_w.reshape(groups * width, model_dim)
    gate_pre = jnp.dot(rows, gate_all, preferred_element_type=jnp.float32)
    up_pre = jnp.dot(rows, up_all, preferred_element_type=jnp.float32)
    sigmoid_part = jax.nn.sigmoid(gate_pre)
    activated = gate_pre * sigmoid_part
    hidden = (activated * up_pre).astype(jnp.bfloat16)
    total = jnp.zeros(rows.shape, jnp.float32)
    for j in range(groups):
        total = total + to_bf16(
            jnp.dot(hidden[:, j * width : (j + 1) * width], down_w[j], preferred_element_type=jnp.float32)
        )
    total = to_bf16(total)
    upstream_f = upstream.astype(jnp.float32)
    gate_upstream = jnp.sum(upstream_f * total, axis=-1)
    weighted = (gates[:, None] * total).astype(jnp.bfloat16)
    upstream_e = (gates[:, None] * upstream_f).astype(jnp.bfloat16)
    hidden_grad = jnp.einsum("td,fd->tf", upstream_e, down_all, preferred_element_type=jnp.float32)
    up_pre_grad = (hidden_grad * activated).astype(jnp.bfloat16)
    gate_pre_grad = (
        hidden_grad * up_pre * sigmoid_part * (1.0 + gate_pre * (1.0 - sigmoid_part))
    ).astype(jnp.bfloat16)
    down_grad = jnp.einsum("tf,td->fd", hidden, upstream_e, preferred_element_type=jnp.float32)
    gate_grad = jnp.einsum("td,tf->df", rows, gate_pre_grad, preferred_element_type=jnp.float32)
    up_grad = jnp.einsum("td,tf->df", rows, up_pre_grad, preferred_element_type=jnp.float32)
    back = jnp.zeros(rows.shape, jnp.float32)
    for j in range(groups):
        cut = slice(j * width, (j + 1) * width)
        back = back + to_bf16(
            jnp.einsum("tf,df->td", gate_pre_grad[:, cut], gate_w[j], preferred_element_type=jnp.float32)
            + jnp.einsum("tf,df->td", up_pre_grad[:, cut], up_w[j], preferred_element_type=jnp.float32)
        )
    return (weighted, back.astype(jnp.bfloat16), gate_upstream, gate_grad, up_grad, down_grad)


def sum_halves(grad, dim):
    return lax.psum_scatter(
        grad.astype(jnp.bfloat16), "hs", scatter_dimension=dim, tiled=True
    ).astype(jnp.float32)


MESH = pl.DeviceIdType.MESH
UNIT = 16


def place():
    ep, hs = lax.axis_index("ep"), lax.axis_index("hs")
    return (ep // 4, (ep // 2) % 2, ep % 2, hs)


def device(z, x, c, y):
    return (z * 4 + x * 2 + c, y)


def greet(peers):
    barrier = pltpu.get_barrier_semaphore()
    for peer in peers:
        pl.semaphore_signal(barrier, inc=1, device_id=peer, device_id_type=MESH)
    pl.semaphore_wait(barrier, len(peers))


EDGE_ORDER = (0, 1, 2, 6, 5, 4, 7, 3)
MIDDLE_ORDER = (0, 1, 2, 3, 7, 5, 6, 4)


def turn(value, cosine, sine):
    lane = lax.broadcasted_iota(jnp.int32, value.shape, 1) % HEAD_SIZE
    swapped = jnp.where(
        lane < HEAD_SIZE // 2, pltpu.roll(value, 128 - HEAD_SIZE // 2, 1), pltpu.roll(value, HEAD_SIZE // 2, 1)
    )
    return value * cosine + swapped * sine


def contract(left, right, left_dim, right_dim):
    return lax.dot_general(
        left, right, (((left_dim,), (right_dim,)), ((), ())), preferred_element_type=jnp.float32
    )


def expert_kernel(
    segment,
    live,
    routes,
    rotation,
    attn_gain,
    moe_gain,
    router,
    tokens_in,
    w_query_in,
    w_key_in,
    w_value_in,
    w_out_in,
    upstream_in,
    gate_w,
    up_w,
    down_w,
    rows_out,
    normed,
    query,
    key_value,
    mixed,
    middle_out,
    cosine,
    sine,
    bias,
    soft_out,
    counts,
    weighted_out,
    back_out,
    slope_out,
    own_out,
    again_out,
    keys,
    values,
    streams,
    gates_in,
    gates,
    slopes,
    slopes_in,
    w_gate,
    w_up,
    w_down,
    sums,
    partial,
    from_sibling,
    from_line,
    staged_x,
    staged_y,
    staged_again,
    returned_x,
    returned_y,
    load_sem,
    head_sem,
    gather_send,
    gather_recv,
    gate_send,
    gate_recv,
    slope_send,
    slope_recv,
    weight_send,
    weight_recv,
    pair_send,
    pair_recv,
    line_send,
    line_recv,
    grad_send,
    grad_recv,
):
    z, x, c, y = place()
    near, far, last = 1 + z % 2, (2 + 3 * z) % 5, 3 - 3 * (z // 2)
    middle = (z == 1) | (z == 2)
    edge = (z == 0) | (z == 3)
    sibling, beside, across = device(z, x, 1 - c, y), device(z, 1 - x, c, y), device(z, x, c, 1 - y)
    corner = device(z, 1 - x, c, 1 - y)
    line = [((z + k) % 4, (c + d) % 2) for k in range(4) for d in range(2) if k or d]

    def chip(k):
        half = z // 2
        inner = z + half * (3 - 2 * z)
        spot = k + inner * (1 - 3 * (k // 2) + 2 * (k // 3))
        return spot + half * (3 - 2 * spot)

    def remote(source, target, send, recv, peer):
        return pltpu.make_async_remote_copy(
            src_ref=source, dst_ref=target, send_sem=send, recv_sem=recv, device_id=peer, device_id_type=MESH
        )

    own = pltpu.make_async_copy(upstream_in, streams.at[1, z, c], load_sem.at[0])
    weights_own = [
        pltpu.make_async_copy(ref, held.at[x, y], load_sem.at[3 + a])
        for a, (ref, held) in enumerate(((gate_w, w_gate), (up_w, w_up), (down_w, w_down)))
    ]
    tokens = from_sibling.at[1, 0]
    head_loads = [pltpu.make_async_copy(tokens_in, tokens, head_sem.at[0])]
    for r in range(4):
        rows = pl.ds(r * 256, 256)
        for n, (source, target) in enumerate(
            (
                (w_query_in, partial.at[0, r // 2, r % 2]),
                (w_out_in, partial.at[1, r // 2, r % 2]),
                (w_key_in, from_sibling.at[0, r, :, pl.ds(0, 512)]),
                (w_value_in, from_sibling.at[0, r, :, pl.ds(512, 512)]),
            )
        ):
            head_loads.append(pltpu.make_async_copy(source.at[rows, :], target, head_sem.at[1 + r * 4 + n]))
    for copy in (own, *weights_own, *head_loads):
        copy.start()
    greet([device(a, x, b, y) for a, b in line] + [beside, across, corner])

    def gather(s, block, slot, peer):
        piece = streams.at[s, block, c]
        return remote(piece, piece, gather_send.at[s, slot], gather_recv.at[s, block, c], peer)

    def arrive(s, block, core):
        piece = streams.at[s, block, core]
        pltpu.make_async_copy(piece, piece, gather_recv.at[s, block, core]).wait()

    def gather_own(s):
        gather(s, z, 0, device(near, x, c, y)).start()
        gather(s, z, 2, sibling).start()

        @pl.when(middle)
        def _():
            gather(s, z, 1, device(far, x, c, y)).start()

    own.wait()
    gather_own(1)
    weight_copies = []
    for a, held in enumerate((w_gate, w_up, w_down)):
        weights_own[a].wait()
        for n, peer in enumerate((across, beside, corner)):
            piece = held.at[x, y]
            weight_copies.append(
                remote(piece, piece, weight_send.at[n, a], weight_recv.at[x, y, a], peer)
            )
    for n in range(3):
        for a in range(3):
            weight_copies[a * 3 + n].start()

    def weights_here(expert, group):
        for a, held in enumerate((w_gate, w_up, w_down)):
            piece = held.at[expert, group]
            pltpu.make_async_copy(piece, piece, weight_recv.at[expert, group, a]).wait()

    def zero(u, carry):
        for e in (0, 1):
            for a in range(3):
                sums[e, a, u // 16, pl.ds(pl.multiple_of((u % 16) * 16, 16), 16), :] = jnp.zeros(
                    (16, 1024), jnp.float32
                )
            partial[e, u // 8, (u // 4) % 2, pl.ds(pl.multiple_of((u % 4) * 64, 64), 64), :] = jnp.zeros(
                (64, 1024), jnp.bfloat16
            )
        return carry

    def handle(k, order=(1, 0)):
        block = chip(k)
        for s in order:
            arrive(s, block, c)
            gather(s, block, 4 + k, sibling).start()
            if k != 2:

                @pl.when(middle)
                def _():
                    gather(s, block, 2 + (k + 1) // 2, device(far, x, c, y)).start()

    row_id = lax.broadcasted_iota(jnp.int32, (256, 256), 0)
    lane_id = lax.broadcasted_iota(jnp.int32, (256, 256), 1)
    diagonal = row_id == lane_id
    segment_row = segment[...].astype(jnp.float32)
    segment_column = jnp.sum(jnp.where(diagonal, segment_row, 0.0), axis=1, keepdims=True)
    live_row = live[...].astype(jnp.float32)
    before = jnp.sum(jnp.where(segment_row < segment_column, 1.0, 0.0), axis=1, keepdims=True)
    position = lax.broadcasted_iota(jnp.int32, (256, 128), 0).astype(jnp.float32) - before
    angle = position * rotation[...]
    side = lax.broadcasted_iota(jnp.int32, (256, 128), 1) % HEAD_SIZE < HEAD_SIZE // 2
    cosine[...] = jnp.cos(angle)
    angle_sine = jnp.sin(angle)
    sine[...] = jnp.where(side, -angle_sine, angle_sine)
    allowed = (segment_row == segment_column) & (lane_id <= row_id) & ((live_row > 0.0) | diagonal)
    bias[...] = jnp.where(allowed, 0.0, -1e30)
    for copy in head_loads:
        copy.wait()
    start = tokens[...].astype(jnp.float32)
    inverse = lax.rsqrt(jnp.mean(start * start, axis=1, keepdims=True) + EPSILON)
    normed[...] = (start * inverse * attn_gain[...]).astype(jnp.bfloat16)

    def project(source, weight):
        total = jnp.zeros((256, 1024), jnp.float32)
        for r in range(4):
            total = total + contract(source[:, pl.ds(r * 256, 256)], weight(r), 1, 0)
        return total

    made = project(normed, lambda r: partial[0, r // 2, r % 2])
    for p in range(8):
        columns = pl.ds(p * 128, 128)
        query[:, columns] = turn(made[:, p * 128 : p * 128 + 128], cosine[...], sine[...]).astype(jnp.bfloat16)
    made = project(normed, lambda r: from_sibling[0, r])
    for p in range(4):
        columns = pl.ds(p * 128, 128)
        key_value[:, columns] = turn(made[:, p * 128 : p * 128 + 128], cosine[...], sine[...]).astype(jnp.bfloat16)
    key_value[:, pl.ds(512, 512)] = made[:, 512:].astype(jnp.bfloat16)
    for g in range(8):
        keys[g] = key_value[:, pl.ds(g * 64, 64)]
        values[g] = key_value[:, pl.ds(512 + g * 64, 64)]

    def attend(g, carry):
        columns = pl.ds(pl.multiple_of(g * 128, 128), 128)
        pair = query[:, columns]
        found = []
        for r in (0, 1):
            scores = contract(pair[:, r * 64 : r * 64 + 64], keys[g], 1, 1) * HEAD_SIZE ** (-0.5) + bias[...]
            weights = jnp.exp(scores - jnp.max(scores, axis=1, keepdims=True))
            probs = (weights / jnp.sum(weights, axis=1, keepdims=True)).astype(jnp.bfloat16)
            found.append(contract(probs, values[g], 1, 0))
        mixed[:, columns] = jnp.concatenate(found, axis=1).astype(jnp.bfloat16)
        return carry

    lax.fori_loop(0, 8, attend, 0)

    @pl.when(edge)
    def _():
        gather(1, z, 1, device(far, x, c, y)).start()

    handle(1, (1,))
    mid = start + project(mixed, lambda r: partial[1, r // 2, r % 2])
    middle_out[...] = mid
    inverse = lax.rsqrt(jnp.mean(mid * mid, axis=1, keepdims=True) + EPSILON)
    streams[0, z, c] = (mid * inverse * moe_gain[...]).astype(jnp.bfloat16)
    gather_own(0)
    rows_store = pltpu.make_async_copy(streams.at[0, z, c], rows_out, load_sem.at[1])
    rows_store.start()
    logits = contract(router[...], streams[0, z, c], 1, 1)
    expert_id = lax.broadcasted_iota(jnp.int32, (16, 256), 0)
    routed = routes[pl.ds(0, 1), :] == expert_id
    for n in range(1, TOP):
        routed = routed | (routes[pl.ds(n, 1), :] == expert_id)
    logits = jnp.where(routed, logits, -1e30)
    raised = jnp.where(routed, jnp.exp(logits - jnp.max(logits, axis=0, keepdims=True)), 0.0)
    soft = raised / jnp.sum(raised, axis=0, keepdims=True)
    soft_out[...] = soft
    held_gates = soft * live_row
    for e in range(16):
        gates_in[e // 4, e % 2, pl.ds((e // 2) % 2, 1), :] = held_gates[e : e + 1, :]
    count = jnp.sum(jnp.where(routed, live_row, 0.0), axis=1, keepdims=True)
    square = lax.broadcasted_iota(jnp.int32, (16, 128), 0) == lax.broadcasted_iota(jnp.int32, (16, 128), 1)
    counts[...] = jnp.sum(jnp.where(square, count, 0.0), axis=0, keepdims=True)
    gate_copies = [
        remote(
            gates_in.at[a, b], gates.at[z, c], gate_send.at[n], gate_recv.at[z, c], device(a, x, b, y)
        )
        for n, (a, b) in enumerate(line)
    ]
    for copy in gate_copies:
        copy.start()
    gates[z, c] = gates_in[z, c]
    lax.fori_loop(0, 32, zero, 0)

    @pl.when(edge)
    def _():
        gather(0, z, 0, device(near, x, c, y)).wait_send()
        gather(0, z, 1, device(far, x, c, y)).start()

    handle(1, (0,))
    for a, b in line:
        pltpu.make_async_copy(gates.at[a, b], gates.at[a, b], gate_recv.at[a, b]).wait()
    weights_here(x, 1 - y)

    def compute(expert, block, core):
        diagonal = lax.broadcasted_iota(jnp.int32, (256, 256), 0) == lax.broadcasted_iota(jnp.int32, (256, 256), 1)
        gate_row = gates[block, core, pl.ds(expert, 1), :]
        gate = jnp.sum(jnp.where(diagonal, gate_row, 0.0), axis=1, keepdims=True)
        rows = streams[0, block, core]
        total = jnp.zeros((256, 1024), jnp.float32)
        kept = []
        for j in (0, 1):
            gate_pre = contract(rows, w_gate[expert, j], 1, 0)
            up_pre = contract(rows, w_up[expert, j], 1, 0)
            sigmoid_part = jax.nn.sigmoid(gate_pre)
            activated = gate_pre * sigmoid_part
            hidden = (activated * up_pre).astype(jnp.bfloat16)
            part = contract(hidden, w_down[expert, j], 1, 0)
            total = total + part.astype(jnp.bfloat16).astype(jnp.float32)
            inner = up_pre * sigmoid_part * (1.0 + gate_pre * (1.0 - sigmoid_part))
            kept.append((activated, inner, hidden))
        total = total.astype(jnp.bfloat16).astype(jnp.float32)
        upstream = streams[1, block, core].astype(jnp.float32)
        slope = jnp.sum(upstream * total, axis=1, keepdims=True)
        slopes[block, core, pl.ds(expert, 1), :] = jnp.sum(
            jnp.where(diagonal, slope, 0.0), axis=0, keepdims=True
        )
        weighted = gate * total + partial[1, block, core].astype(jnp.float32)
        partial[1, block, core] = weighted.astype(jnp.bfloat16)
        upstream = (gate * upstream).astype(jnp.bfloat16)
        back = jnp.zeros((256, 1024), jnp.float32)
        for j in (0, 1):
            activated, inner, hidden = kept[j]
            hidden_grad = contract(upstream, w_down[expert, j], 1, 1)
            up_grad = (hidden_grad * activated).astype(jnp.bfloat16)
            gate_grad = (hidden_grad * inner).astype(jnp.bfloat16)
            sums[expert, 0, j] += contract(gate_grad, rows, 0, 0)
            sums[expert, 1, j] += contract(up_grad, rows, 0, 0)
            sums[expert, 2, j] += contract(hidden, upstream, 0, 0)
            step = contract(gate_grad, w_gate[expert, j], 1, 1) + contract(up_grad, w_up[expert, j], 1, 1)
            back = back + step.astype(jnp.bfloat16).astype(jnp.float32)
        back = back + partial[0, block, core].astype(jnp.float32)
        partial[0, block, core] = back.astype(jnp.bfloat16)

    def grad_copy(n, source, target, peer):
        return remote(source, target, grad_send.at[n], grad_recv.at[n], peer)

    def pair_copy(s, block):
        return remote(
            partial.at[s, block, 1 - c],
            from_sibling.at[s, block],
            pair_send.at[s, block],
            pair_recv.at[s, block],
            sibling,
        )

    def line_copy(s, block, slot, peer):
        return remote(
            partial.at[s, block, c],
            from_line.at[s, slot],
            line_send.at[s, block],
            line_recv.at[s, slot],
            device(peer, x, c, y),
        )

    def line_wait(s, slot):
        piece = from_line.at[s, slot]
        pltpu.make_async_copy(piece, piece, line_recv.at[s, slot]).wait()

    def add_to(s, block, ref):
        def body(u, carry):
            at = pl.ds(pl.multiple_of(u * 32, 32), 32)
            value = partial[s, block, c, at, :].astype(jnp.float32) + ref[at, :].astype(jnp.float32)
            partial[s, block, c, at, :] = value.astype(jnp.bfloat16)
            return carry

        lax.fori_loop(0, 8, body, 0)

    at_edge = (z * z - 3 * z + 2) // 2
    orders = [sum(code << (3 * t) for t, code in enumerate(codes)) for codes in (EDGE_ORDER, MIDDLE_ORDER)]
    order = at_edge * orders[0] + (1 - at_edge) * orders[1]

    def step(i, carry):
        t = i // 2
        code = lax.shift_right_logical(order, 3 * t) % 8
        again = at_edge * ((t // 3) % 2 + t // 7) + (1 - at_edge) * (t // 4)
        k = code % 4
        expert = x + (code // 4) * (1 - 2 * x)
        block, core = chip(k), (c + i + again) % 2

        @pl.when((i == 2) & middle | (i == 4) & edge)
        def _():
            handle(2)

        @pl.when((i == 4) & middle | (i == 12) & edge)
        def _():
            handle(3)

        @pl.when((i == 8) & middle | (i == 6) & edge)
        def _():
            weights_here(1 - x, y)
            weights_here(1 - x, 1 - y)

        @pl.when((i % 2 == 1) & (again == 0))
        def _():
            for s in (0, 1):
                arrive(s, block, 1 - c)

        compute(expert, block, core)

        @pl.when((i % 2 == 0) & (again == 1))
        def _():
            for s in (0, 1):
                pair_copy(s, block).start()

        @pl.when((i % 2 == 1) & (again == 1) & (k > 0))
        def _():
            for s in (0, 1):
                pair_copy(s, block).wait_recv()
                add_to(s, block, from_sibling.at[s, block])

                @pl.when(edge & (k == 2))
                def _():
                    line_copy(s, block, 3, near).start()

                @pl.when(edge & (k == 1))
                def _():
                    line_copy(s, block, 1, near).start()

                @pl.when(edge & (k == 3))
                def _():
                    line_copy(s, block, 2, last).start()

                @pl.when(middle & (k == 3))
                def _():
                    line_copy(s, block, 1, last).start()

                @pl.when(middle & (k == 2))
                def _():
                    line_copy(s, block, 0, far).start()

        return carry

    lax.fori_loop(0, 16, step, 0)
    low, high = pl.ds(0, 512), pl.ds(512, 512)

    def each(body):
        def rows_of(u, carry):
            at = pl.ds(pl.multiple_of(u * 32, 32), 32)
            for a in range(3):
                body(a, at)
            return carry

        lax.fori_loop(0, 8, rows_of, 0)

    def stage_low(a, at):
        for j in (0, 1):
            staged_x[j, a, at, :] = sums[1 - x, a, j, at, low].astype(jnp.bfloat16)

    def stage_high(a, at):
        staged_y[0, a, at, :] = sums[1 - x, a, 1 - y, at, high].astype(jnp.bfloat16)
        staged_y[1, a, at, :] = sums[x, a, 1 - y, at, high].astype(jnp.bfloat16)

    each(stage_low)
    grad_copy(0, staged_x, returned_x, beside).start()
    each(stage_high)
    grad_copy(1, staged_y, returned_y, across).start()
    slope_copies = [
        remote(
            slopes.at[a, b], slopes_in.at[z, c], slope_send.at[n], slope_recv.at[z, c], device(a, x, b, y)
        )
        for n, (a, b) in enumerate(line)
    ]
    for copy in slope_copies:
        copy.start()
    slopes_in[z, c] = slopes[z, c]

    @pl.when(middle)
    def _():
        for s in (0, 1):
            line_wait(s, 3)
            add_to(s, near, from_line.at[s, 3])
            line_copy(s, near, 0, near).start()

    grad_copy(0, staged_x, returned_x, beside).wait_recv()

    def second_low(a, at):
        value = sums[x, a, 1 - y, at, low] + returned_x[1 - y, a, at, :].astype(jnp.float32)
        staged_again[0, a, at, :] = value.astype(jnp.bfloat16)

    each(second_low)
    again_stores = [pltpu.make_async_copy(staged_again.at[0], again_out.at[0], load_sem.at[3])]
    again_stores[0].start()
    grad_copy(1, staged_y, returned_y, across).wait_recv()

    def second_high(a, at):
        value = sums[1 - x, a, y, at, high] + returned_y[0, a, at, :].astype(jnp.float32)
        staged_again[1, a, at, :] = value.astype(jnp.bfloat16)

    each(second_high)
    again_stores.append(pltpu.make_async_copy(staged_again.at[1], again_out.at[1], load_sem.at[4]))
    again_stores[1].start()

    def own_grad(a, at):
        sums[x, a, y, at, low] += returned_x[y, a, at, :].astype(jnp.float32)
        sums[x, a, y, at, high] += returned_y[1, a, at, :].astype(jnp.float32)

    each(own_grad)
    stores = [pltpu.make_async_copy(sums.at[x, a, y], own_out.at[a], load_sem.at[a]) for a in range(3)]
    for copy in stores:
        copy.start()

    def finish(slots):
        for s in (0, 1):
            for slot in slots:
                line_wait(s, slot)

            def body(u, carry):
                at = pl.ds(pl.multiple_of(u * 32, 32), 32)
                value = partial[s, z, c, at, :].astype(jnp.float32)
                value = value + from_sibling[s, z, at, :].astype(jnp.float32)
                for slot in slots:
                    value = value + from_line[s, slot, at, :].astype(jnp.float32)
                (back_out, weighted_out)[s][at, :] = value
                return carry

            lax.fori_loop(0, 8, body, 0)

    for s in (0, 1):
        pair_copy(s, z).wait_recv()

    @pl.when(middle)
    def _():
        finish((0, 1))

    @pl.when(edge)
    def _():
        finish((0, 1, 2))

    for a, b in line:
        pltpu.make_async_copy(slopes_in.at[a, b], slopes_in.at[a, b], slope_recv.at[a, b]).wait()
    slope_out[...] = slopes_in[...]
    gather(1, z, 0, device(near, x, c, y)).wait_send()

    @pl.when(middle)
    def _():
        gather(0, z, 0, device(near, x, c, y)).wait_send()

    for s in (0, 1):
        gather(s, z, 1, device(far, x, c, y)).wait_send()
        gather(s, z, 2, sibling).wait_send()
        for k in (1, 2, 3):
            gather(s, chip(k), 4 + k, sibling).wait_send()
            line_copy(s, chip(k), 0, near).wait_send()

        @pl.when(middle)
        def _():
            for k in (1, 3):
                gather(s, chip(k), 2 + (k + 1) // 2, device(far, x, c, y)).wait_send()

        for k in range(4):
            pair_copy(s, chip(k)).wait_send()
    for copy in (*gate_copies, *weight_copies, *slope_copies):
        copy.wait_send()
    grad_copy(0, staged_x, returned_x, beside).wait_send()
    grad_copy(1, staged_y, returned_y, across).wait_send()
    for copy in (rows_store, *stores, *again_stores):
        copy.wait()


def expert_part(
    segment_ids,
    live_mask,
    routes,
    attn_gain,
    moe_gain,
    router,
    tokens,
    attention_weights,
    upstream,
    gate_w,
    up_w,
    down_w,
):
    count, model_dim = tokens.shape
    width = gate_w.shape[1]
    vmem, anywhere = pl.BlockSpec(memory_space=pltpu.VMEM), pl.BlockSpec(memory_space=pl.ANY)
    f32, bf16, dma, shape = jnp.float32, jnp.bfloat16, pltpu.SemaphoreType.DMA, jax.ShapeDtypeStruct
    half = HEAD_SIZE // 2
    frequency = np.float32(10000.0) ** (-(np.arange(half, dtype=np.float32) * np.float32(2.0)) / np.float32(HEAD_SIZE))
    rotation = jnp.asarray(np.tile(frequency.astype(np.float32), 4)[None])
    block = (count, model_dim)
    return pl.pallas_call(
        expert_kernel,
        out_shape=[
            shape(block, bf16),
            shape(block, bf16),
            shape(block, bf16),
            shape(block, bf16),
            shape(block, bf16),
            shape(block, f32),
            shape((count, 128), f32),
            shape((count, 128), f32),
            shape((count, count), f32),
            shape((16, count), f32),
            shape((1, 128), f32),
            shape(block, f32),
            shape(block, f32),
            shape((4, 2, 8, count), f32),
            shape((3, width, model_dim), f32),
            shape((2, 3, width, model_dim // 2), bf16),
        ],
        in_specs=[vmem] * 7 + [anywhere] * 9,
        out_specs=[anywhere] + [vmem] * 13 + [anywhere] * 2,
        scratch_shapes=[
            pltpu.VMEM((8, count, HEAD_SIZE), bf16),
            pltpu.VMEM((8, count, HEAD_SIZE), bf16),
            pltpu.VMEM((2, 4, 2, *block), bf16),
            *[pltpu.VMEM((4, 2, 8, count), f32)] * 4,
            pltpu.VMEM((2, 2, model_dim, width), bf16),
            pltpu.VMEM((2, 2, model_dim, width), bf16),
            pltpu.VMEM((2, 2, width, model_dim), bf16),
            pltpu.VMEM((2, 3, 2, width, model_dim), f32),
            pltpu.VMEM((2, 4, 2, *block), bf16),
            pltpu.VMEM((2, 4, *block), bf16),
            pltpu.VMEM((2, 4, *block), bf16),
            *[pltpu.VMEM((2, 3, width, model_dim // 2), bf16)] * 5,
            dma((6,)),
            dma((17,)),
            dma((2, 8)),
            dma((2, 4, 2)),
            dma((7,)),
            dma((4, 2)),
            dma((7,)),
            dma((4, 2)),
            dma((3, 3)),
            dma((2, 2, 3)),
            dma((2, 4)),
            dma((2, 4)),
            dma((2, 4)),
            dma((2, 4)),
            dma((2,)),
            dma((2,)),
        ],
        compiler_params=pltpu.CompilerParams(
            collective_id=1, has_side_effects=True, vmem_limit_bytes=63 << 20
        ),
        name="expert_part",
    )(
        segment_ids,
        live_mask,
        routes.T,
        rotation,
        attn_gain[None],
        moe_gain[None],
        router.T,
        tokens,
        *attention_weights,
        upstream,
        gate_w,
        up_w,
        down_w,
    )


TAIL_ORDER = (
    (0, 4), (2, 1), (3, 1), (4, 1), (5, 1), (1, 4), (0, 5), (2, 2), (1, 5), (3, 2),
    (4, 2), (5, 2), (0, 6), (2, 3), (1, 6), (3, 3), (4, 3), (2, 4), (5, 3), (3, 4),
    (0, 7), (4, 4), (0, 8), (1, 7), (2, 5), (1, 8), (5, 4), (2, 6), (3, 5), (2, 7),
    (4, 5), (3, 6), (2, 8), (5, 5), (4, 6), (3, 7), (5, 6), (3, 8), (4, 7), (4, 8),
    (5, 7), (5, 8),
)


def tail_kernel(
    tokens,
    normed,
    query,
    key_value,
    mixed,
    middle,
    moe_in,
    upstream_in,
    combined,
    back,
    slopes,
    soft,
    live,
    counts,
    router,
    cosine,
    sine,
    bias,
    attn_gain,
    moe_gain,
    w_query_in,
    w_key_in,
    w_value_in,
    w_out_in,
    again_in,
    own_in,
    output,
    input_grad,
    out_sum,
    query_sum,
    key_sum,
    value_sum,
    small_out,
    tiny_out,
    gate_grad,
    up_grad,
    down_grad,
    w_query,
    w_key,
    w_value,
    w_out,
    keys,
    values,
    key_slopes,
    value_slopes,
    mixed_slope,
    query_slope,
    again,
    returned_again,
    own,
    *rest,
):
    count = 6
    grads, halves, totals, fulls, firsts, seconds, lines = [rest[n * count : (n + 1) * count] for n in range(7)]
    small_sum, small_in, tiny_sum, tiny_in, send, recv, small_send, small_recv, local_sem, load_sem, again_send, again_recv = rest[7 * count :]
    outs = [ref.at[:, :, pl.ds(n * 512, 512)] for ref in (out_sum, query_sum) for n in (0, 1)]
    outs += [key_sum, value_sum]
    z, x, c, y = place()
    sibling, beside, across = device(z, x, 1 - c, y), device(z, 1 - x, c, y), device(z, x, c, 1 - y)
    along = [device((z + k) % 4, x, c, y) for k in (1, 2, 3)]
    loads = [
        pltpu.make_async_copy(source, target, load_sem.at[n])
        for n, (source, target) in enumerate(
            (
                (again_in, again),
                (w_out_in, w_out),
                (w_query_in, w_query),
                (w_key_in, w_key),
                (w_value_in, w_value),
                (own_in, own),
            )
        )
    ]
    for copy in loads:
        copy.start()
    greet([sibling, beside, across] + along)
    loads[0].wait()
    again_copies = [
        pltpu.make_async_remote_copy(
            src_ref=again.at[n],
            dst_ref=returned_again.at[n],
            send_sem=again_send.at[n],
            recv_sem=again_recv.at[n],
            device_id=peer,
            device_id_type=MESH,
        )
        for n, peer in enumerate((across, beside))
    ]
    for copy in again_copies:
        copy.start()
    bits = ((x, y), (y, x))
    partners = ((beside, across), (across, beside))

    def push(i, slot, source, target, peer):
        copy = pltpu.make_async_remote_copy(
            src_ref=source,
            dst_ref=target,
            send_sem=send.at[i, slot],
            recv_sem=recv.at[i, slot],
            device_id=peer,
            device_id_type=MESH,
        )
        copy.start()
        return copy

    def combine(i, target, start, length, terms):
        def body(u, carry):
            value = totals[i][start + u].astype(jnp.float32)
            for ref, base in terms:
                value = value + ref[base + u].astype(jnp.float32)
            target[0][target[1] + u] = value.astype(jnp.bfloat16)
            return carry

        lax.fori_loop(0, length, body, 0)

    copies = {}

    def stage(i, step):
        if step == 0:
            copies[i, 0] = [
                push(i, 0, grads[i].at[pl.ds((1 - c) * 32, 32)], halves[i], sibling)
            ]
        if step == 1:
            copies[i, 0][0].wait_recv()

            def body(u, carry):
                value = grads[i][c * 32 + u].astype(jnp.float32) + halves[i][u].astype(jnp.float32)
                totals[i][u] = value.astype(jnp.bfloat16)
                return carry

            lax.fori_loop(0, 32, body, 0)
            copies[i, 1] = [
                push(
                    i,
                    1 + part,
                    totals[i].at[pl.ds(part * 16 + (1 - bits[part][0]) * 8, 8)],
                    firsts[i].at[part],
                    partners[part][0],
                )
                for part in (0, 1)
            ]
        if step == 2:
            copies[i, 2] = []
            for part in (0, 1):
                copies[i, 1][part].wait_recv()
                base = part * 16 + bits[part][0] * 8
                combine(i, (totals[i], base), base, 8, [(firsts[i].at[part], 0)])
                copies[i, 2].append(
                    push(
                        i,
                        3 + part,
                        totals[i].at[pl.ds(base + (1 - bits[part][1]) * 4, 4)],
                        seconds[i].at[part],
                        partners[part][1],
                    )
                )
        if step == 3:
            copies[i, 3] = []
            for part in (0, 1):
                copies[i, 2][part].wait_recv()
                base = part * 16 + bits[part][0] * 8 + bits[part][1] * 4
                combine(i, (totals[i], base), base, 4, [(seconds[i].at[part], 0)])
                for k in (1, 2, 3):
                    copies[i, 3].append(
                        push(
                            i,
                            5 + part * 3 + k - 1,
                            totals[i].at[base + (z + k) % 4],
                            lines[i].at[part, k - 1],
                            along[k - 1],
                        )
                    )
        if step == 4:
            copies[i, 4] = []
            for part in (0, 1):
                for k in (1, 2, 3):
                    copies[i, 3][part * 3 + k - 1].wait_recv()
                base = part * 16 + bits[part][0] * 8 + bits[part][1] * 4
                combine(
                    i, (fulls[i], c * 32 + base + z), base + z, 1, [(lines[i].at[part], k) for k in (0, 1, 2)]
                )
                for k in (1, 2, 3):
                    piece = fulls[i].at[c * 32 + base + z]
                    copies[i, 4].append(push(i, 11 + part * 3 + k - 1, piece, piece, along[k - 1]))
        if step == 5:
            copies[i, 5] = []
            for part in (0, 1):
                for k in (1, 2, 3):
                    copies[i, 4][part * 3 + k - 1].wait_recv()
                piece = fulls[i].at[pl.ds(c * 32 + part * 16 + bits[part][0] * 8 + bits[part][1] * 4, 4)]
                copies[i, 5].append(push(i, 17 + part, piece, piece, partners[part][1]))
        if step == 6:
            copies[i, 6] = []
            for part in (0, 1):
                copies[i, 5][part].wait_recv()
                piece = fulls[i].at[pl.ds(c * 32 + part * 16 + bits[part][0] * 8, 8)]
                copies[i, 6].append(push(i, 19 + part, piece, piece, partners[part][0]))
        if step == 7:
            for part in (0, 1):
                copies[i, 6][part].wait_recv()
            piece = fulls[i].at[pl.ds(c * 32, 32)]
            copies[i, 7] = [push(i, 21, piece, piece, sibling)]
        if step == 8:
            copies[i, 7][0].wait_recv()
            done = pltpu.make_async_copy(fulls[i], outs[i], local_sem.at[i])
            done.start()
            copies[i, 8] = [done]

    def small_stage(n, step):
        total, arrived = (small_sum, tiny_sum)[n], (small_in, tiny_in)[n]

        def small_push(slot, peer, source, target):
            copy = pltpu.make_async_remote_copy(
                src_ref=total.at[source],
                dst_ref=arrived.at[target],
                send_sem=small_send.at[n, slot],
                recv_sem=small_recv.at[n, slot],
                device_id=peer,
                device_id_type=MESH,
            )
            copy.start()
            copies.setdefault((n, "s", step), []).append(copy)

        if step == 0:
            small_push(0, sibling, 0, 0)
        if step in (1, 2, 3):
            copies[n, "s", step - 1][0].wait_recv()
            total[step] = total[step - 1] + arrived[step - 1]
        if step in (1, 2):
            small_push(step, (beside, across)[step - 1], step, step)
        if step == 3:
            for k in (1, 2, 3):
                small_push(2 + k, along[k - 1], 3, 3 + z)
            arrived[3 + z] = total[3]
        if step == 4:
            for copy in copies[n, "s", 3]:
                copy.wait_recv()
            (small_out, tiny_out)[n][...] = (arrived[3] + arrived[4]) + (arrived[5] + arrived[6])

    inner = upstream_in[...].astype(jnp.float32)
    slope_rows = jnp.concatenate([slopes[e // 4, e % 2, pl.ds((e // 2) % 2, 1), :] for e in range(16)], axis=0)
    soft_slope = slope_rows * live[...].astype(jnp.float32)
    soft_t = soft[...]
    dlogits = soft_t * (soft_slope - jnp.sum(soft_t * soft_slope, axis=0, keepdims=True))
    dlogits = dlogits.astype(jnp.bfloat16)
    small_sum[0] = jnp.zeros(small_sum.shape[1:], jnp.float32)
    small_sum[0, pl.ds(0, 16), :] = contract(dlogits, moe_in[...], 1, 0)
    small_sum[0, pl.ds(18, 1), pl.ds(0, 128)] = counts[...]
    dmoe_in = back[...] + contract(dlogits, router[...], 0, 0)
    mid = middle[...]
    output[...] = (mid + combined[...]).astype(jnp.bfloat16)
    inverse = lax.rsqrt(jnp.mean(mid * mid, axis=1, keepdims=True) + EPSILON)
    small_sum[0, pl.ds(17, 1), :] = jnp.sum(dmoe_in * mid * inverse, axis=0, keepdims=True)
    scaled = dmoe_in * moe_gain[...]
    dmiddle = inner + inverse * (
        scaled - mid * inverse * inverse * jnp.mean(scaled * mid, axis=1, keepdims=True)
    )
    input_grad[...] = dmiddle
    dattn = dmiddle.astype(jnp.bfloat16)

    def weight_grad(i, left, right):
        for r in range(4):
            rows = contract(left[:, pl.ds(r * 256, 256)], right, 0, 0).astype(jnp.bfloat16)
            grads[i][pl.ds(r * 16, 16)] = rows.reshape(16, 16, 512)

    small_stage(0, 0)
    weight_grad(0, mixed, dattn[:, :512])
    stage(0, 0)
    weight_grad(1, mixed, dattn[:, 512:])
    stage(1, 0)
    loads[1].wait()
    mixed_slope[...] = contract(dattn, w_out[...], 1, 1).astype(jnp.bfloat16)
    for g in range(8):
        keys[g] = key_value[:, pl.ds(g * 64, 64)]
        values[g] = key_value[:, pl.ds(512 + g * 64, 64)]
    scale = HEAD_SIZE ** (-0.5)

    def group(g, carry):
        columns = pl.ds(pl.multiple_of(g * 128, 128), 128)
        key_g, value_g = keys[g], values[g]
        query_pair, slope_pair = query[:, columns], mixed_slope[:, columns]
        key_slope = jnp.zeros((256, 64), jnp.float32)
        value_slope = jnp.zeros((256, 64), jnp.float32)
        query_slopes = []
        for r in (0, 1):
            query_h, slope_h = query_pair[:, r * 64 : r * 64 + 64], slope_pair[:, r * 64 : r * 64 + 64]
            scores = contract(query_h, key_g, 1, 1) * scale + bias[...]
            weights = jnp.exp(scores - jnp.max(scores, axis=1, keepdims=True))
            probs = weights / jnp.sum(weights, axis=1, keepdims=True)
            prob_slope = contract(slope_h, value_g, 1, 1)
            value_slope = value_slope + contract(probs.astype(jnp.bfloat16), slope_h, 0, 0)
            delta = jnp.sum(probs * prob_slope, axis=1, keepdims=True)
            score_slope = (probs * (prob_slope - delta)).astype(jnp.bfloat16)
            query_slopes.append(contract(score_slope, key_g, 1, 0) * scale)
            key_slope = key_slope + contract(score_slope, query_h, 0, 0) * scale
        pair = turn(jnp.concatenate(query_slopes, axis=1), cosine[...], -sine[...])
        query_slope[:, columns] = pair.astype(jnp.bfloat16)
        key_slopes[g] = key_slope
        value_slopes[g] = value_slope
        return carry

    stage(0, 1)
    stage(1, 1)
    small_stage(0, 1)
    lax.fori_loop(0, 5, group, 0)
    small_stage(0, 2)
    stage(0, 2)
    stage(1, 2)
    lax.fori_loop(5, 8, group, 0)
    small_stage(0, 3)
    stage(0, 3)
    stage(1, 3)
    loads[2].wait()
    loads[3].wait()
    loads[4].wait()
    for n in (0, 1):
        weight_grad(2 + n, normed, query_slope[:, n * 512 : n * 512 + 512])
        stage(2 + n, 0)
    key_slope = jnp.concatenate(
        [
            turn(jnp.concatenate([key_slopes[2 * p], key_slopes[2 * p + 1]], axis=1), cosine[...], -sine[...])
            for p in range(4)
        ],
        axis=1,
    ).astype(jnp.bfloat16)
    weight_grad(4, normed, key_slope)
    stage(4, 0)
    value_slope = jnp.concatenate(
        [jnp.concatenate([value_slopes[2 * p], value_slopes[2 * p + 1]], axis=1) for p in range(4)], axis=1
    ).astype(jnp.bfloat16)
    weight_grad(5, normed, value_slope)
    stage(5, 0)
    todo = list(TAIL_ORDER)

    def proceed(steps):
        for _ in range(min(steps, len(todo))):
            stage(*todo.pop(0))

    proceed(6)
    dnormed = contract(query_slope[...], w_query[...], 1, 1)
    dnormed = dnormed + contract(key_slope, w_key[...], 1, 1)
    dnormed = dnormed + contract(value_slope, w_value[...], 1, 1)
    start = tokens[...].astype(jnp.float32)
    inverse = lax.rsqrt(jnp.mean(start * start, axis=1, keepdims=True) + EPSILON)
    gain_slope = jnp.sum(dnormed * start * inverse, axis=0, keepdims=True)
    for r in range(8):
        tiny_sum[0, pl.ds(r, 1), :] = gain_slope[:, r * 128 : r * 128 + 128]
    scaled = dnormed * attn_gain[...]
    input_grad[...] += inverse * (
        scaled - start * inverse * inverse * jnp.mean(scaled * start, axis=1, keepdims=True)
    )
    small_stage(1, 0)
    proceed(4)
    small_stage(1, 1)
    proceed(4)
    small_stage(1, 2)
    small_stage(0, 4)
    loads[5].wait()
    for copy in again_copies:
        copy.wait_recv()
    for a, target in enumerate((gate_grad, up_grad, down_grad)):
        for n in (0, 1):
            columns = pl.ds(n * 512, 512)
            summed = own[a, :, columns] + returned_again[n, a].astype(jnp.float32)
            if a < 2:
                target[columns, :] = summed.T
            else:
                target[:, columns] = summed
    proceed(4)
    small_stage(1, 3)
    proceed(4)
    small_stage(1, 4)
    proceed(len(todo))
    for key_of, made in copies.items():
        for copy in made:
            if key_of[1] == 8:
                copy.wait()
            else:
                copy.wait_send()
    for copy in again_copies:
        copy.wait_send()


def tail_part(operands, weights, again, own):
    tokens, model_dim = operands[0].shape
    narrow = weights[1].shape[1]
    vmem, anywhere = pl.BlockSpec(memory_space=pltpu.VMEM), pl.BlockSpec(memory_space=pl.ANY)
    f32, bf16, dma = jnp.float32, jnp.bfloat16, pltpu.SemaphoreType.DMA
    widths = (model_dim, model_dim, narrow, narrow)
    leads = ((64,), (32,), (32,), (64,), (2, 8), (2, 4), (2, 3))
    shape = jax.ShapeDtypeStruct
    width = own.shape[1]
    out = pl.pallas_call(
        tail_kernel,
        out_shape=[
            shape((tokens, model_dim), bf16),
            shape((tokens, model_dim), f32),
            *[shape((64, UNIT, w), bf16) for w in widths],
            shape((24, model_dim), f32),
            shape((8, 128), f32),
            shape((model_dim, width), f32),
            shape((model_dim, width), f32),
            shape((width, model_dim), f32),
        ],
        in_specs=[vmem] * len(operands) + [anywhere] * 6,
        out_specs=[vmem, vmem] + [anywhere] * 4 + [vmem] * 5,
        scratch_shapes=[
            *[pltpu.VMEM(w.shape, bf16) for w in weights],
            pltpu.VMEM((8, tokens, HEAD_SIZE), bf16),
            pltpu.VMEM((8, tokens, HEAD_SIZE), bf16),
            pltpu.VMEM((8, tokens, HEAD_SIZE), f32),
            pltpu.VMEM((8, tokens, HEAD_SIZE), f32),
            pltpu.VMEM((tokens, model_dim), bf16),
            pltpu.VMEM((tokens, model_dim), bf16),
            pltpu.VMEM(again.shape, bf16),
            pltpu.VMEM(again.shape, bf16),
            pltpu.VMEM(own.shape, f32),
            *[pltpu.VMEM((*lead, UNIT, 512), bf16) for lead in leads for _ in range(6)],
            pltpu.VMEM((4, 24, model_dim), f32),
            pltpu.VMEM((7, 24, model_dim), f32),
            pltpu.VMEM((4, 8, 128), f32),
            pltpu.VMEM((7, 8, 128), f32),
            dma((6, 22)),
            dma((6, 22)),
            dma((2, 6)),
            dma((2, 6)),
            dma((6,)),
            dma((6,)),
            dma((2,)),
            dma((2,)),
        ],
        compiler_params=pltpu.CompilerParams(
            collective_id=0, has_side_effects=True, vmem_limit_bytes=60 << 20
        ),
        name="tail_part",
    )(*operands, *weights, again, own)
    grads = [o.reshape(-1, o.shape[2]).astype(jnp.float32) for o in out[2:6]]
    return (out[0], out[1], grads, out[6], out[7], out[8:11])


def local(
    tokens,
    segment_ids,
    live_mask,
    routes,
    attn_gain,
    w_query,
    key_weight,
    value_weight,
    w_out,
    moe_gain,
    router,
    w_gate,
    w_up,
    w_down,
    cotangent,
):
    sequence_length = tokens.shape[0]
    model_dim = tokens.shape[1]
    experts_all = router.shape[1]
    query_per_key_head = QUERY_HEADS // KEY_VALUE_HEADS
    score_scale = HEAD_SIZE ** (-0.5)
    if lax.axis_size("ep") == 16 and lax.axis_size("hs") == 2:
        attention_weights = (w_query, key_weight, value_weight, w_out)
        (
            rows,
            normed_rows,
            query_rows,
            key_value,
            mixed,
            middle,
            cosine,
            sine,
            bias,
            soft,
            counts,
            combined,
            back,
            slopes,
            own,
            again,
        ) = expert_part(
            segment_ids,
            live_mask,
            routes,
            attn_gain,
            moe_gain,
            router,
            tokens,
            attention_weights,
            cotangent,
            w_gate[0],
            w_up[0],
            w_down[0],
        )
        operands = (
            tokens,
            normed_rows,
            query_rows,
            key_value,
            mixed,
            middle,
            rows,
            cotangent,
            combined,
            back,
            slopes,
            soft,
            live_mask,
            counts,
            router.T,
            cosine,
            sine,
            bias,
            attn_gain[None],
            moe_gain[None],
        )
        output, input_grad, grads, small, tiny, expert_grads = tail_part(operands, attention_weights, again, own)
        return (
            output,
            input_grad,
            tiny.reshape(model_dim),
            grads[1],
            grads[2],
            grads[3],
            grads[0],
            small[17],
            small[:experts_all].T,
            *[g[None] for g in expert_grads],
            small[18, :experts_all].astype(jnp.int32),
        )
    segment = segment_ids[0]
    live_row = live_mask[0]
    inputs = tokens.astype(jnp.float32)
    normed_rows, inverse_one = rms_forward(inputs, attn_gain)
    normed_rows_back = normed_rows.astype(jnp.bfloat16)
    query_pre = jnp.dot(normed_rows_back, w_query, preferred_element_type=jnp.float32).reshape(
        sequence_length, QUERY_HEADS, HEAD_SIZE
    )
    key_before_rotary = jnp.dot(
        normed_rows_back, key_weight, preferred_element_type=jnp.float32
    ).reshape(sequence_length, KEY_VALUE_HEADS, HEAD_SIZE)
    value_b = (
        jnp.dot(normed_rows_back, value_weight, preferred_element_type=jnp.float32)
        .astype(jnp.bfloat16)
        .reshape(sequence_length, KEY_VALUE_HEADS, HEAD_SIZE)
    )
    positions = positions_of(segment)
    cosine_table, sine_table = rotary_tables(positions, HEAD_SIZE)
    query_back_rows = rotary(query_pre, cosine_table, sine_table).astype(jnp.bfloat16)
    key_b = rotary(key_before_rotary, cosine_table, sine_table).astype(jnp.bfloat16)
    indices = jnp.arange(sequence_length)
    allowed = (
        (segment[:, None] == segment[None, :])
        & (indices[None, :] <= indices[:, None])
        & ((live_row[None, :] > 0) | (indices[None, :] == indices[:, None]))
    )
    grouped_rows = query_back_rows.reshape(
        sequence_length, KEY_VALUE_HEADS, query_per_key_head, HEAD_SIZE
    )
    scores = (
        jnp.einsum("qgrd,kgd->grqk", grouped_rows, key_b, preferred_element_type=jnp.float32)
        * score_scale
    )
    scores = jnp.where(allowed, scores, -1e30)
    highest = jnp.max(scores, axis=-1, keepdims=True)
    weights_exp = jnp.exp(scores - highest)
    denominator = jnp.sum(weights_exp, axis=-1, keepdims=True)
    log_total = highest + jnp.log(denominator)
    probabilities = weights_exp / denominator
    mixed = jnp.einsum(
        "grqk,kgd->qgrd",
        probabilities.astype(jnp.bfloat16),
        value_b,
        preferred_element_type=jnp.float32,
    )
    mixed_b = mixed.reshape(sequence_length, QUERY_HEADS * HEAD_SIZE).astype(jnp.bfloat16)
    middle = inputs + jnp.dot(mixed_b, w_out, preferred_element_type=jnp.float32)
    moe_normed, inverse_two = rms_forward(middle, moe_gain)
    moe_in = moe_normed.astype(jnp.bfloat16)
    logits = jnp.dot(moe_in, router, preferred_element_type=jnp.float32)
    route_hot = (routes[:, :, None] == jnp.arange(experts_all)[None, None, :]).astype(jnp.float32)
    chosen = jnp.sum(route_hot * logits[:, None, :], axis=-1)
    route_soft = jax.nn.softmax(chosen, axis=-1)
    live_column = live_row.astype(jnp.float32)[:, None]
    route_gates = route_soft * live_column
    counts_local = jnp.sum(route_hot * live_column[:, :, None], axis=(0, 1))
    dense_gates = jnp.sum(route_hot * route_gates[:, :, None], axis=1)
    upstream_all = lax.all_gather(cotangent, "ep", axis=0, tiled=True)
    gate_all = lax.all_gather(w_gate, "hs", axis=0, tiled=True)
    up_all = lax.all_gather(w_up, "hs", axis=0, tiled=True)
    down_all = lax.all_gather(w_down, "hs", axis=0, tiled=True)
    rows_all = lax.all_gather(moe_in, "ep", axis=0, tiled=True)
    gates_all = lax.all_to_all(
        dense_gates.T.reshape(experts_all, 1, sequence_length), "ep", split_axis=0, concat_axis=1, tiled=True
    ).reshape(-1)
    weighted, back, gate_upstream_all, gate_w_grad, up_w_grad, down_w_grad = expert_pass(
        rows_all, upstream_all, gates_all, gate_all, up_all, down_all
    )
    combined = lax.psum_scatter(weighted, "ep", scatter_dimension=0, tiled=True).astype(jnp.float32)
    expert_input_grad = lax.psum_scatter(back, "ep", scatter_dimension=0, tiled=True).astype(jnp.float32)
    gate_upstream_dense = lax.all_to_all(
        gate_upstream_all.reshape(experts_all, 1, sequence_length), "ep", split_axis=0, concat_axis=1, tiled=True
    ).reshape(experts_all, sequence_length).T
    gate_w_grad = sum_halves(gate_w_grad, 1)[None]
    up_w_grad = sum_halves(up_w_grad, 1)[None]
    down_w_grad = sum_halves(down_w_grad, 0)[None]
    output = (middle + combined).astype(jnp.bfloat16)
    upstream = cotangent.astype(jnp.float32)
    gate_upstream = jnp.sum(route_hot * gate_upstream_dense[:, None, :], axis=-1)
    soft_upstream = gate_upstream * live_column
    chosen_grad = route_soft * (
        soft_upstream - jnp.sum(route_soft * soft_upstream, axis=-1, keepdims=True)
    )
    logit_grad = jnp.sum(route_hot * chosen_grad[:, :, None], axis=1).astype(jnp.bfloat16)
    router_w_grad = jnp.einsum("td,te->de", moe_in, logit_grad, preferred_element_type=jnp.float32)
    moe_in_grad = expert_input_grad + jnp.einsum(
        "te,de->td", logit_grad, router, preferred_element_type=jnp.float32
    )
    middle_norm_grad, moe_gain_grad = rms_backward(middle, inverse_two, moe_gain, moe_in_grad)
    middle_grad = upstream + middle_norm_grad
    attn_grad_b = middle_grad.astype(jnp.bfloat16)
    out_w_grad = jnp.einsum("tm,td->md", mixed_b, attn_grad_b, preferred_element_type=jnp.float32)
    attention_mixed_grad = jnp.einsum(
        "td,md->tm", attn_grad_b, w_out, preferred_element_type=jnp.float32
    ).astype(jnp.bfloat16)
    attention_mixed_grad = attention_mixed_grad.reshape(
        sequence_length, KEY_VALUE_HEADS, query_per_key_head, HEAD_SIZE
    )
    scores_again = (
        jnp.einsum("qgrd,kgd->grqk", grouped_rows, key_b, preferred_element_type=jnp.float32)
        * score_scale
    )
    scores_again = jnp.where(allowed, scores_again, -1e30)
    probs_again = jnp.exp(scores_again - log_total)
    prob_grad = jnp.einsum(
        "qgrd,kgd->grqk", attention_mixed_grad, value_b, preferred_element_type=jnp.float32
    )
    value_per_head_grad = jnp.einsum(
        "grqk,qgrd->kgd",
        probs_again.astype(jnp.bfloat16),
        attention_mixed_grad,
        preferred_element_type=jnp.float32,
    )
    value_per_head_grad = value_per_head_grad.astype(jnp.bfloat16).reshape(
        sequence_length, KEY_VALUE_HEADS * HEAD_SIZE
    )
    row_delta = jnp.sum(probs_again * prob_grad, axis=-1, keepdims=True)
    score_grad = (probs_again * (prob_grad - row_delta)).astype(jnp.bfloat16)
    query_rot_grad = (
        jnp.einsum("grqk,kgd->qgrd", score_grad, key_b, preferred_element_type=jnp.float32)
        * score_scale
    )
    rotated_key_grad = (
        jnp.einsum("grqk,qgrd->kgd", score_grad, grouped_rows, preferred_element_type=jnp.float32)
        * score_scale
    )
    query_head_grad = (
        rotary_backward(
            query_rot_grad.reshape(sequence_length, QUERY_HEADS, HEAD_SIZE),
            cosine_table,
            sine_table,
        )
        .astype(jnp.bfloat16)
        .reshape(sequence_length, QUERY_HEADS * HEAD_SIZE)
    )
    key_head_grad = (
        rotary_backward(rotated_key_grad, cosine_table, sine_table)
        .astype(jnp.bfloat16)
        .reshape(sequence_length, KEY_VALUE_HEADS * HEAD_SIZE)
    )
    query_w_grad = jnp.einsum(
        "td,te->de", normed_rows_back, query_head_grad, preferred_element_type=jnp.float32
    )
    key_w_grad = jnp.einsum(
        "td,te->de", normed_rows_back, key_head_grad, preferred_element_type=jnp.float32
    )
    value_w_grad = jnp.einsum(
        "td,te->de", normed_rows_back, value_per_head_grad, preferred_element_type=jnp.float32
    )
    normed_grad = jnp.einsum(
        "te,de->td", query_head_grad, w_query, preferred_element_type=jnp.float32
    )
    normed_grad = normed_grad + jnp.einsum(
        "te,de->td", key_head_grad, key_weight, preferred_element_type=jnp.float32
    )
    normed_grad = normed_grad + jnp.einsum(
        "te,de->td", value_per_head_grad, value_weight, preferred_element_type=jnp.float32
    )
    input_norm_grad, attn_gain_grad = rms_backward(inputs, inverse_one, attn_gain, normed_grad)
    input_grad = middle_grad + input_norm_grad
    (
        attn_gain_grad,
        query_w_grad,
        key_w_grad,
        value_w_grad,
        out_w_grad,
        moe_gain_grad,
        router_w_grad,
        counts,
    ) = lax.psum(
        (
            attn_gain_grad,
            query_w_grad,
            key_w_grad,
            value_w_grad,
            out_w_grad,
            moe_gain_grad,
            router_w_grad,
            counts_local,
        ),
        ("ep", "hs"),
    )
    return (
        output,
        input_grad,
        attn_gain_grad,
        query_w_grad,
        key_w_grad,
        value_w_grad,
        out_w_grad,
        moe_gain_grad,
        router_w_grad,
        gate_w_grad,
        up_w_grad,
        down_w_grad,
        counts.astype(jnp.int32),
    )


def solution(mesh):
    in_specs = (
        P(("ep", "hs"), None),
        P(("ep", "hs"), None),
        P(("ep", "hs"), None),
        P(("ep", "hs"), None),
        P(),
        P(),
        P(),
        P(),
        P(),
        P(),
        P(),
        P("ep", None, "hs"),
        P("ep", None, "hs"),
        P("ep", "hs", None),
        P(("ep", "hs"), None),
    )
    out_specs = (
        P(("ep", "hs"), None),
        P(("ep", "hs"), None),
        P(),
        P(),
        P(),
        P(),
        P(),
        P(),
        P(),
        P("ep", None, "hs"),
        P("ep", None, "hs"),
        P("ep", "hs", None),
        P(),
    )
    return jax.shard_map(local, mesh=mesh, in_specs=in_specs, out_specs=out_specs, check_vma=False)
```

```python
import jax
import jax.numpy as jnp
import numpy as np
from jax import lax
from jax.experimental import pallas as pl
from jax.experimental.pallas import tpu as pltpu
from jax.sharding import PartitionSpec as P

QUERY_HEADS = 16
KEY_VALUE_HEADS = 8
HEAD_SIZE = 64
TOP = 8


EPSILON = 1e-05


def rms_forward(value_rows, norm_gain):
    inverse = lax.rsqrt(jnp.mean(value_rows * value_rows, axis=-1, keepdims=True) + EPSILON)
    return (value_rows * inverse * norm_gain, inverse)


def rms_backward(value_rows, inverse, norm_gain, upstream):
    scaled = upstream * norm_gain
    gain_grad = jnp.sum(upstream * value_rows * inverse, axis=0)
    input_grad = inverse * (
        scaled
        - value_rows * inverse * inverse * jnp.mean(scaled * value_rows, axis=-1, keepdims=True)
    )
    return (input_grad, gain_grad)


def positions_of(segment):
    before = (segment[None, :] < segment[:, None]).astype(jnp.int32)
    return jnp.arange(segment.shape[-1], dtype=jnp.int32) - jnp.sum(before, axis=1)


def rotary_tables(positions, head_dim):
    half_dim = head_dim // 2
    frequency = 10000.0 ** (-(jnp.arange(half_dim, dtype=jnp.float32) * 2.0) / head_dim)
    angles = positions.astype(jnp.float32)[:, None] * frequency[None, :]
    return (jnp.cos(angles)[:, None, :], jnp.sin(angles)[:, None, :])


def rotary(heads, cosine_table, sine_table):
    half_dim = heads.shape[-1] // 2
    first_half = heads[..., :half_dim]
    second_half = heads[..., half_dim:]
    return jnp.concatenate(
        [
            first_half * cosine_table - second_half * sine_table,
            second_half * cosine_table + first_half * sine_table,
        ],
        axis=-1,
    )


def rotary_backward(grads, cosine_table, sine_table):
    half_dim = grads.shape[-1] // 2
    first_half = grads[..., :half_dim]
    second_half = grads[..., half_dim:]
    return jnp.concatenate(
        [
            first_half * cosine_table + second_half * sine_table,
            second_half * cosine_table - first_half * sine_table,
        ],
        axis=-1,
    )


def to_bf16(value):
    return lax.reduce_precision(value, 8, 7)


def expert_pass(rows, upstream, gates, gate_w, up_w, down_w):
    groups, model_dim, width = gate_w.shape
    gate_all = jnp.concatenate([gate_w[j] for j in range(groups)], axis=1)
    up_all = jnp.concatenate([up_w[j] for j in range(groups)], axis=1)
    down_all = down_w.reshape(groups * width, model_dim)
    gate_pre = jnp.dot(rows, gate_all, preferred_element_type=jnp.float32)
    up_pre = jnp.dot(rows, up_all, preferred_element_type=jnp.float32)
    sigmoid_part = jax.nn.sigmoid(gate_pre)
    activated = gate_pre * sigmoid_part
    hidden = (activated * up_pre).astype(jnp.bfloat16)
    total = jnp.zeros(rows.shape, jnp.float32)
    for j in range(groups):
        total = total + to_bf16(
            jnp.dot(hidden[:, j * width : (j + 1) * width], down_w[j], preferred_element_type=jnp.float32)
        )
    total = to_bf16(total)
    upstream_f = upstream.astype(jnp.float32)
    gate_upstream = jnp.sum(upstream_f * total, axis=-1)
    weighted = (gates[:, None] * total).astype(jnp.bfloat16)
    upstream_e = (gates[:, None] * upstream_f).astype(jnp.bfloat16)
    hidden_grad = jnp.einsum("td,fd->tf", upstream_e, down_all, preferred_element_type=jnp.float32)
    up_pre_grad = (hidden_grad * activated).astype(jnp.bfloat16)
    gate_pre_grad = (
        hidden_grad * up_pre * sigmoid_part * (1.0 + gate_pre * (1.0 - sigmoid_part))
    ).astype(jnp.bfloat16)
    down_grad = jnp.einsum("tf,td->fd", hidden, upstream_e, preferred_element_type=jnp.float32)
    gate_grad = jnp.einsum("td,tf->df", rows, gate_pre_grad, preferred_element_type=jnp.float32)
    up_grad = jnp.einsum("td,tf->df", rows, up_pre_grad, preferred_element_type=jnp.float32)
    back = jnp.zeros(rows.shape, jnp.float32)
    for j in range(groups):
        cut = slice(j * width, (j + 1) * width)
        back = back + to_bf16(
            jnp.einsum("tf,df->td", gate_pre_grad[:, cut], gate_w[j], preferred_element_type=jnp.float32)
            + jnp.einsum("tf,df->td", up_pre_grad[:, cut], up_w[j], preferred_element_type=jnp.float32)
        )
    return (weighted, back.astype(jnp.bfloat16), gate_upstream, gate_grad, up_grad, down_grad)


def sum_halves(grad, dim):
    return lax.psum_scatter(
        grad.astype(jnp.bfloat16), "hs", scatter_dimension=dim, tiled=True
    ).astype(jnp.float32)


MESH = pl.DeviceIdType.MESH
UNIT = 16


def place():
    ep, hs = lax.axis_index("ep"), lax.axis_index("hs")
    return (ep // 4, (ep // 2) % 2, ep % 2, hs)


def device(z, x, c, y):
    return (z * 4 + x * 2 + c, y)


def greet(peers):
    barrier = pltpu.get_barrier_semaphore()
    for peer in peers:
        pl.semaphore_signal(barrier, inc=1, device_id=peer, device_id_type=MESH)
    pl.semaphore_wait(barrier, len(peers))


EDGE_ORDER = (0, 1, 2, 6, 5, 4, 7, 3)
MIDDLE_ORDER = (0, 1, 2, 3, 7, 5, 6, 4)


def turn(value, cosine, sine):
    lane = lax.broadcasted_iota(jnp.int32, value.shape, 1) % HEAD_SIZE
    swapped = jnp.where(
        lane < HEAD_SIZE // 2, pltpu.roll(value, 128 - HEAD_SIZE // 2, 1), pltpu.roll(value, HEAD_SIZE // 2, 1)
    )
    return value * cosine + swapped * sine


def contract(left, right, left_dim, right_dim):
    return lax.dot_general(
        left, right, (((left_dim,), (right_dim,)), ((), ())), preferred_element_type=jnp.float32
    )


def expert_kernel(
    segment,
    live,
    routes,
    rotation,
    attn_gain,
    moe_gain,
    router,
    tokens_in,
    w_query_in,
    w_key_in,
    w_value_in,
    w_out_in,
    upstream_in,
    gate_w,
    up_w,
    down_w,
    middle_rows,
    input_grad,
    out_grad,
    query_grad,
    side_grad,
    small,
    tiny,
    own_out,
    again_out,
    weighted_out,
    normed,
    query,
    key_value,
    mixed,
    back,
    cosine,
    sine,
    bias,
    soft_rows,
    keys,
    values,
    streams,
    gates_in,
    gates,
    slopes,
    slopes_in,
    w_gate,
    w_up,
    w_down,
    sums,
    partial,
    from_sibling,
    from_line,
    staged_x,
    staged_y,
    staged_again,
    returned_x,
    returned_y,
    load_sem,
    head_sem,
    store_sem,
    weighted_sem,
    gather_send,
    gather_recv,
    gate_send,
    gate_recv,
    slope_send,
    slope_recv,
    weight_send,
    weight_recv,
    pair_send,
    pair_recv,
    line_send,
    line_recv,
    grad_send,
    grad_recv,
):
    z, x, c, y = place()
    near, far, last = 1 + z % 2, (2 + 3 * z) % 5, 3 - 3 * (z // 2)
    middle = (z == 1) | (z == 2)
    edge = (z == 0) | (z == 3)
    sibling, beside, across = device(z, x, 1 - c, y), device(z, 1 - x, c, y), device(z, x, c, 1 - y)
    corner = device(z, 1 - x, c, 1 - y)
    line = [((z + k) % 4, (c + d) % 2) for k in range(4) for d in range(2) if k or d]

    def chip(k):
        half = z // 2
        inner = z + half * (3 - 2 * z)
        spot = k + inner * (1 - 3 * (k // 2) + 2 * (k // 3))
        return spot + half * (3 - 2 * spot)

    def remote(source, target, send, recv, peer):
        return pltpu.make_async_remote_copy(
            src_ref=source, dst_ref=target, send_sem=send, recv_sem=recv, device_id=peer, device_id_type=MESH
        )

    own = pltpu.make_async_copy(upstream_in, streams.at[1, z, c], load_sem.at[0])
    weights_own = [
        pltpu.make_async_copy(ref, held.at[x, y], load_sem.at[3 + a])
        for a, (ref, held) in enumerate(((gate_w, w_gate), (up_w, w_up), (down_w, w_down)))
    ]
    tokens = from_sibling.at[1, 0]
    head_loads = [pltpu.make_async_copy(tokens_in, tokens, head_sem.at[0])]
    for r in range(4):
        rows = pl.ds(r * 256, 256)
        for n, (source, target) in enumerate(
            (
                (w_query_in, partial.at[0, r // 2, r % 2]),
                (w_out_in, partial.at[1, r // 2, r % 2]),
                (w_key_in, from_sibling.at[0, r, :, pl.ds(0, 512)]),
                (w_value_in, from_sibling.at[0, r, :, pl.ds(512, 512)]),
            )
        ):
            head_loads.append(pltpu.make_async_copy(source.at[rows, :], target, head_sem.at[1 + r * 4 + n]))
    for copy in (own, *weights_own, *head_loads):
        copy.start()
    greet([device(a, x, b, y) for a, b in line] + [beside, across, corner])

    def gather(s, block, slot, peer):
        piece = streams.at[s, block, c]
        return remote(piece, piece, gather_send.at[s, slot], gather_recv.at[s, block, c], peer)

    def arrive(s, block, core):
        piece = streams.at[s, block, core]
        pltpu.make_async_copy(piece, piece, gather_recv.at[s, block, core]).wait()

    def gather_own(s):
        gather(s, z, 0, device(near, x, c, y)).start()
        gather(s, z, 2, sibling).start()

        @pl.when(middle)
        def _():
            gather(s, z, 1, device(far, x, c, y)).start()

    own.wait()
    gather_own(1)
    weight_copies = []
    for a, held in enumerate((w_gate, w_up, w_down)):
        weights_own[a].wait()
        for n, peer in enumerate((across, beside, corner)):
            piece = held.at[x, y]
            weight_copies.append(
                remote(piece, piece, weight_send.at[n, a], weight_recv.at[x, y, a], peer)
            )
    for n in range(3):
        for a in range(3):
            weight_copies[a * 3 + n].start()

    def weights_here(expert, group):
        for a, held in enumerate((w_gate, w_up, w_down)):
            piece = held.at[expert, group]
            pltpu.make_async_copy(piece, piece, weight_recv.at[expert, group, a]).wait()

    def zero(u, carry):
        for e in (0, 1):
            for a in range(3):
                sums[e, a, u // 16, pl.ds(pl.multiple_of((u % 16) * 16, 16), 16), :] = jnp.zeros(
                    (16, 1024), jnp.float32
                )
            partial[e, u // 8, (u // 4) % 2, pl.ds(pl.multiple_of((u % 4) * 64, 64), 64), :] = jnp.zeros(
                (64, 1024), jnp.bfloat16
            )
        return carry

    def handle(k, order=(1, 0)):
        block = chip(k)
        for s in order:
            arrive(s, block, c)
            gather(s, block, 4 + k, sibling).start()
            if k != 2:

                @pl.when(middle)
                def _():
                    gather(s, block, 2 + (k + 1) // 2, device(far, x, c, y)).start()

    row_id = lax.broadcasted_iota(jnp.int32, (256, 256), 0)
    lane_id = lax.broadcasted_iota(jnp.int32, (256, 256), 1)
    diagonal = row_id == lane_id
    segment_row = segment[...].astype(jnp.float32)
    segment_column = jnp.sum(jnp.where(diagonal, segment_row, 0.0), axis=1, keepdims=True)
    live_row = live[...].astype(jnp.float32)
    before = jnp.sum(jnp.where(segment_row < segment_column, 1.0, 0.0), axis=1, keepdims=True)
    position = lax.broadcasted_iota(jnp.int32, (256, 128), 0).astype(jnp.float32) - before
    angle = position * rotation[...]
    side = lax.broadcasted_iota(jnp.int32, (256, 128), 1) % HEAD_SIZE < HEAD_SIZE // 2
    cosine[...] = jnp.cos(angle)
    angle_sine = jnp.sin(angle)
    sine[...] = jnp.where(side, -angle_sine, angle_sine)
    allowed = (segment_row == segment_column) & (lane_id <= row_id) & ((live_row > 0.0) | diagonal)
    bias[...] = jnp.where(allowed, 0.0, -1e30)
    for copy in head_loads:
        copy.wait()
    start = tokens[...].astype(jnp.float32)
    inverse = lax.rsqrt(jnp.mean(start * start, axis=1, keepdims=True) + EPSILON)
    normed[...] = (start * inverse * attn_gain[...]).astype(jnp.bfloat16)

    def project(source, weight):
        total = jnp.zeros((256, 1024), jnp.float32)
        for r in range(4):
            total = total + contract(source[:, pl.ds(r * 256, 256)], weight(r), 1, 0)
        return total

    made = project(normed, lambda r: partial[0, r // 2, r % 2])
    for p in range(8):
        columns = pl.ds(p * 128, 128)
        query[:, columns] = turn(made[:, p * 128 : p * 128 + 128], cosine[...], sine[...]).astype(jnp.bfloat16)
    made = project(normed, lambda r: from_sibling[0, r])
    for p in range(4):
        columns = pl.ds(p * 128, 128)
        key_value[:, columns] = turn(made[:, p * 128 : p * 128 + 128], cosine[...], sine[...]).astype(jnp.bfloat16)
    key_value[:, pl.ds(512, 512)] = made[:, 512:].astype(jnp.bfloat16)
    for g in range(8):
        keys[g] = key_value[:, pl.ds(g * 64, 64)]
        values[g] = key_value[:, pl.ds(512 + g * 64, 64)]

    def attend(g, carry):
        columns = pl.ds(pl.multiple_of(g * 128, 128), 128)
        pair = query[:, columns]
        found = []
        for r in (0, 1):
            scores = contract(pair[:, r * 64 : r * 64 + 64], keys[g], 1, 1) * HEAD_SIZE ** (-0.5) + bias[...]
            weights = jnp.exp(scores - jnp.max(scores, axis=1, keepdims=True))
            probs = (weights / jnp.sum(weights, axis=1, keepdims=True)).astype(jnp.bfloat16)
            found.append(contract(probs, values[g], 1, 0))
        mixed[:, columns] = jnp.concatenate(found, axis=1).astype(jnp.bfloat16)
        return carry

    lax.fori_loop(0, 8, attend, 0)

    @pl.when(edge)
    def _():
        gather(1, z, 1, device(far, x, c, y)).start()

    handle(1, (1,))
    mid = start + project(mixed, lambda r: partial[1, r // 2, r % 2])
    middle_rows[...] = mid
    inverse = lax.rsqrt(jnp.mean(mid * mid, axis=1, keepdims=True) + EPSILON)
    streams[0, z, c] = (mid * inverse * moe_gain[...]).astype(jnp.bfloat16)
    gather_own(0)
    logits = contract(router[...], streams[0, z, c], 1, 1)
    expert_id = lax.broadcasted_iota(jnp.int32, (16, 256), 0)
    routed = routes[pl.ds(0, 1), :] == expert_id
    for n in range(1, TOP):
        routed = routed | (routes[pl.ds(n, 1), :] == expert_id)
    logits = jnp.where(routed, logits, -1e30)
    raised = jnp.where(routed, jnp.exp(logits - jnp.max(logits, axis=0, keepdims=True)), 0.0)
    soft = raised / jnp.sum(raised, axis=0, keepdims=True)
    soft_rows[...] = soft
    held_gates = soft * live_row
    for e in range(16):
        gates_in[e // 4, e % 2, pl.ds((e // 2) % 2, 1), :] = held_gates[e : e + 1, :]
    count = jnp.sum(jnp.where(routed, live_row, 0.0), axis=1, keepdims=True)
    square = lax.broadcasted_iota(jnp.int32, (16, 128), 0) == lax.broadcasted_iota(jnp.int32, (16, 128), 1)
    small[...] = jnp.zeros((24, 1024), jnp.float32)
    small[pl.ds(18, 1), pl.ds(0, 128)] = jnp.sum(jnp.where(square, count, 0.0), axis=0, keepdims=True)
    gate_copies = [
        remote(
            gates_in.at[a, b], gates.at[z, c], gate_send.at[n], gate_recv.at[z, c], device(a, x, b, y)
        )
        for n, (a, b) in enumerate(line)
    ]
    for copy in gate_copies:
        copy.start()
    gates[z, c] = gates_in[z, c]
    lax.fori_loop(0, 32, zero, 0)

    @pl.when(edge)
    def _():
        gather(0, z, 0, device(near, x, c, y)).wait_send()
        gather(0, z, 1, device(far, x, c, y)).start()

    handle(1, (0,))
    for a, b in line:
        pltpu.make_async_copy(gates.at[a, b], gates.at[a, b], gate_recv.at[a, b]).wait()
    weights_here(x, 1 - y)

    def compute(expert, block, core):
        diagonal = lax.broadcasted_iota(jnp.int32, (256, 256), 0) == lax.broadcasted_iota(jnp.int32, (256, 256), 1)
        gate_row = gates[block, core, pl.ds(expert, 1), :]
        gate = jnp.sum(jnp.where(diagonal, gate_row, 0.0), axis=1, keepdims=True)
        rows = streams[0, block, core]
        total = jnp.zeros((256, 1024), jnp.float32)
        kept = []
        for j in (0, 1):
            gate_pre = contract(rows, w_gate[expert, j], 1, 0)
            up_pre = contract(rows, w_up[expert, j], 1, 0)
            sigmoid_part = jax.nn.sigmoid(gate_pre)
            activated = gate_pre * sigmoid_part
            hidden = (activated * up_pre).astype(jnp.bfloat16)
            part = contract(hidden, w_down[expert, j], 1, 0)
            total = total + part.astype(jnp.bfloat16).astype(jnp.float32)
            inner = up_pre * sigmoid_part * (1.0 + gate_pre * (1.0 - sigmoid_part))
            kept.append((activated, inner, hidden))
        total = total.astype(jnp.bfloat16).astype(jnp.float32)
        upstream = streams[1, block, core].astype(jnp.float32)
        slope = jnp.sum(upstream * total, axis=1, keepdims=True)
        slopes[block, core, pl.ds(expert, 1), :] = jnp.sum(
            jnp.where(diagonal, slope, 0.0), axis=0, keepdims=True
        )
        weighted = gate * total + partial[1, block, core].astype(jnp.float32)
        partial[1, block, core] = weighted.astype(jnp.bfloat16)
        upstream = (gate * upstream).astype(jnp.bfloat16)
        back = jnp.zeros((256, 1024), jnp.float32)
        for j in (0, 1):
            activated, inner, hidden = kept[j]
            hidden_grad = contract(upstream, w_down[expert, j], 1, 1)
            up_grad = (hidden_grad * activated).astype(jnp.bfloat16)
            gate_grad = (hidden_grad * inner).astype(jnp.bfloat16)
            sums[expert, 0, j] += contract(gate_grad, rows, 0, 0)
            sums[expert, 1, j] += contract(up_grad, rows, 0, 0)
            sums[expert, 2, j] += contract(hidden, upstream, 0, 0)
            step = contract(gate_grad, w_gate[expert, j], 1, 1) + contract(up_grad, w_up[expert, j], 1, 1)
            back = back + step.astype(jnp.bfloat16).astype(jnp.float32)
        back = back + partial[0, block, core].astype(jnp.float32)
        partial[0, block, core] = back.astype(jnp.bfloat16)

    def grad_copy(n, source, target, peer):
        return remote(source, target, grad_send.at[n], grad_recv.at[n], peer)

    def pair_copy(s, block):
        return remote(
            partial.at[s, block, 1 - c],
            from_sibling.at[s, block],
            pair_send.at[s, block],
            pair_recv.at[s, block],
            sibling,
        )

    def line_copy(s, block, slot, peer):
        return remote(
            partial.at[s, block, c],
            from_line.at[s, slot],
            line_send.at[s, block],
            line_recv.at[s, slot],
            device(peer, x, c, y),
        )

    def line_wait(s, slot):
        piece = from_line.at[s, slot]
        pltpu.make_async_copy(piece, piece, line_recv.at[s, slot]).wait()

    def add_to(s, block, ref):
        def body(u, carry):
            at = pl.ds(pl.multiple_of(u * 32, 32), 32)
            value = partial[s, block, c, at, :].astype(jnp.float32) + ref[at, :].astype(jnp.float32)
            partial[s, block, c, at, :] = value.astype(jnp.bfloat16)
            return carry

        lax.fori_loop(0, 8, body, 0)

    at_edge = (z * z - 3 * z + 2) // 2
    orders = [sum(code << (3 * t) for t, code in enumerate(codes)) for codes in (EDGE_ORDER, MIDDLE_ORDER)]
    order = at_edge * orders[0] + (1 - at_edge) * orders[1]

    def step(i, carry):
        t = i // 2
        code = lax.shift_right_logical(order, 3 * t) % 8
        again = at_edge * ((t // 3) % 2 + t // 7) + (1 - at_edge) * (t // 4)
        k = code % 4
        expert = x + (code // 4) * (1 - 2 * x)
        block, core = chip(k), (c + i + again) % 2

        @pl.when((i == 2) & middle | (i == 4) & edge)
        def _():
            handle(2)

        @pl.when((i == 4) & middle | (i == 12) & edge)
        def _():
            handle(3)

        @pl.when((i == 8) & middle | (i == 6) & edge)
        def _():
            weights_here(1 - x, y)
            weights_here(1 - x, 1 - y)

        @pl.when((i % 2 == 1) & (again == 0))
        def _():
            for s in (0, 1):
                arrive(s, block, 1 - c)

        compute(expert, block, core)

        @pl.when((i % 2 == 0) & (again == 1))
        def _():
            for s in (0, 1):
                pair_copy(s, block).start()

        @pl.when((i % 2 == 1) & (again == 1))
        def _():
            for s in (0, 1):
                pair_copy(s, block).wait_recv()
                add_to(s, block, from_sibling.at[s, block])

            @pl.when(edge & (k == 2))
            def _():
                line_copy(0, block, 2, near).start()

            @pl.when(edge & (k == 1))
            def _():
                line_copy(0, block, 1, near).start()

            @pl.when(edge & (k == 3))
            def _():
                line_copy(0, block, 2, last).start()

            @pl.when(middle & (k == 3))
            def _():
                line_copy(0, block, 1, last).start()

            @pl.when(middle & (k == 2))
            def _():
                line_copy(0, block, 0, far).start()

        return carry

    lax.fori_loop(0, 16, step, 0)
    low, high = pl.ds(0, 512), pl.ds(512, 512)

    def each(body):
        def rows_of(u, carry):
            at = pl.ds(pl.multiple_of(u * 32, 32), 32)
            for a in range(3):
                body(a, at)
            return carry

        lax.fori_loop(0, 8, rows_of, 0)

    def stage_low(a, at):
        for j in (0, 1):
            staged_x[j, a, at, :] = sums[1 - x, a, j, at, low].astype(jnp.bfloat16)

    def stage_high(a, at):
        staged_y[0, a, at, :] = sums[1 - x, a, 1 - y, at, high].astype(jnp.bfloat16)
        staged_y[1, a, at, :] = sums[x, a, 1 - y, at, high].astype(jnp.bfloat16)

    each(stage_low)
    grad_copy(0, staged_x, returned_x, beside).start()
    each(stage_high)
    grad_copy(1, staged_y, returned_y, across).start()
    slope_copies = [
        remote(
            slopes.at[a, b], slopes_in.at[z, c], slope_send.at[n], slope_recv.at[z, c], device(a, x, b, y)
        )
        for n, (a, b) in enumerate(line)
    ]
    for copy in slope_copies:
        copy.start()
    slopes_in[z, c] = slopes[z, c]


    weighted_stores = [
        pltpu.make_async_copy(partial.at[1, k, c], weighted_out.at[k], weighted_sem.at[k]) for k in range(4)
    ]
    for copy in weighted_stores:
        copy.start()

    @pl.when(middle)
    def _():
        line_wait(0, 2)
        add_to(0, near, from_line.at[0, 2])
        line_copy(0, near, 0, near).start()

    gather(1, z, 0, device(near, x, c, y)).wait_send()

    @pl.when(middle)
    def _():
        gather(0, z, 0, device(near, x, c, y)).wait_send()

    for s in (0, 1):
        gather(s, z, 1, device(far, x, c, y)).wait_send()
        gather(s, z, 2, sibling).wait_send()
        for k in (1, 2, 3):
            gather(s, chip(k), 4 + k, sibling).wait_send()

        @pl.when(middle)
        def _():
            for k in (1, 3):
                gather(s, chip(k), 2 + (k + 1) // 2, device(far, x, c, y)).wait_send()

    for copy in (*gate_copies, *weight_copies):
        copy.wait_send()

    def query_weight(r):
        return streams.at[0, chip(1 + r // 2), r % 2]

    reloads = []
    for r in range(4):
        rows = pl.ds(r * 256, 256)
        for n, (source, target) in enumerate(
            (
                (w_out_in, from_sibling.at[1, r]),
                (w_query_in, query_weight(r)),
                (w_key_in, from_sibling.at[0, r, :, pl.ds(0, 512)]),
                (w_value_in, from_sibling.at[0, r, :, pl.ds(512, 512)]),
            )
        ):
            reloads.append(pltpu.make_async_copy(source.at[rows, :], target, head_sem.at[1 + r * 4 + n]))
    for copy in reloads:
        copy.start()

    def combined(s, slots, body_of):
        for slot in slots:
            line_wait(s, slot)

        def body(u, carry):
            at = pl.ds(pl.multiple_of(u * 32, 32), 32)
            value = partial[s, z, c, at, :].astype(jnp.float32)
            for slot in slots:
                value = value + from_line[s, slot, at, :].astype(jnp.float32)
            body_of(at, value)
            return carry

        lax.fori_loop(0, 8, body, 0)

    def finish(s, body_of):
        @pl.when(middle)
        def _():
            combined(s, (0, 1), body_of)

        @pl.when(edge)
        def _():
            combined(s, (0, 1, 2), body_of)

    def store_back(at, value):
        back[at, :] = value

    finish(0, store_back)
    for a, b in line:
        pltpu.make_async_copy(slopes_in.at[a, b], slopes_in.at[a, b], slope_recv.at[a, b]).wait()
    upstream = streams[1, z, c].astype(jnp.float32)
    slope_rows = jnp.concatenate([slopes_in[e // 4, e % 2, pl.ds((e // 2) % 2, 1), :] for e in range(16)], axis=0)
    soft_slope = slope_rows * live[...].astype(jnp.float32)
    soft_t = soft_rows[...]
    dlogits = soft_t * (soft_slope - jnp.sum(soft_t * soft_slope, axis=0, keepdims=True))
    dlogits = dlogits.astype(jnp.bfloat16)
    small[pl.ds(0, 16), :] = contract(dlogits, streams[0, z, c], 1, 0)
    dmoe_in = back[...] + contract(dlogits, router[...], 0, 0)
    mid = middle_rows[...]
    inverse = lax.rsqrt(jnp.mean(mid * mid, axis=1, keepdims=True) + EPSILON)
    small[pl.ds(17, 1), :] = jnp.sum(dmoe_in * mid * inverse, axis=0, keepdims=True)
    scaled = dmoe_in * moe_gain[...]
    dmiddle = upstream + inverse * (
        scaled - mid * inverse * inverse * jnp.mean(scaled * mid, axis=1, keepdims=True)
    )
    input_grad[...] = dmiddle
    dattn = dmiddle.astype(jnp.bfloat16)
    outgoing = []

    def send_out(source, target):
        copy = pltpu.make_async_copy(source, target, store_sem.at[len(outgoing)])
        copy.start()
        outgoing.append(copy)

    def column_grad(left, right, held, target):
        for r in range(4):
            rows = contract(left[:, pl.ds(r * 256, 256)], right, 0, 0).astype(jnp.bfloat16)
            for n in range(4):
                held[n // 2, n % 2, pl.ds(r * 256, 256), :] = rows[:, n * 256 : n * 256 + 256]
        for n in range(4):
            send_out(held.at[n // 2, n % 2], target.at[:, pl.ds(n * 256, 256)])

    column_grad(mixed, dattn, w_gate, out_grad)
    for copy in reloads:
        copy.wait()
    mixed_slope, query_slope, side_slope = w_down.at[0, 0], w_down.at[0, 1], w_down.at[1, 0]
    for r in range(4):
        mixed_slope[:, pl.ds(r * 256, 256)] = contract(dattn, from_sibling[1, r], 1, 1).astype(jnp.bfloat16)
    scale = HEAD_SIZE ** (-0.5)

    def attend_back(p, carry):
        wide = pl.ds(pl.multiple_of(p * 256, 256), 256)
        queries, slopes_here = query[:, wide], mixed_slope[:, wide]
        key_slopes, value_slopes, query_slopes = [], [], []
        for n in (0, 1):
            key_g, value_g = keys[2 * p + n], values[2 * p + n]
            key_slope = jnp.zeros((256, 64), jnp.float32)
            value_slope = jnp.zeros((256, 64), jnp.float32)
            for r in (0, 1):
                cut = slice(n * 128 + r * 64, n * 128 + r * 64 + 64)
                query_h, slope_h = queries[:, cut], slopes_here[:, cut]
                scores = contract(query_h, key_g, 1, 1) * scale + bias[...]
                weights = jnp.exp(scores - jnp.max(scores, axis=1, keepdims=True))
                probs = weights / jnp.sum(weights, axis=1, keepdims=True)
                prob_slope = contract(slope_h, value_g, 1, 1)
                value_slope = value_slope + contract(probs.astype(jnp.bfloat16), slope_h, 0, 0)
                delta = jnp.sum(probs * prob_slope, axis=1, keepdims=True)
                score_slope = (probs * (prob_slope - delta)).astype(jnp.bfloat16)
                query_slopes.append(contract(score_slope, key_g, 1, 0) * scale)
                key_slope = key_slope + contract(score_slope, query_h, 0, 0) * scale
            key_slopes.append(key_slope)
            value_slopes.append(value_slope)
        for n in (0, 1):
            pair = turn(jnp.concatenate(query_slopes[2 * n : 2 * n + 2], axis=1), cosine[...], -sine[...])
            query_slope[:, pl.ds(pl.multiple_of(p * 256 + n * 128, 128), 128)] = pair.astype(jnp.bfloat16)
        pair = turn(jnp.concatenate(key_slopes, axis=1), cosine[...], -sine[...])
        side_slope[:, pl.ds(pl.multiple_of(p * 128, 128), 128)] = pair.astype(jnp.bfloat16)
        pair = jnp.concatenate(value_slopes, axis=1)
        side_slope[:, pl.ds(pl.multiple_of(512 + p * 128, 128), 128)] = pair.astype(jnp.bfloat16)
        return carry

    lax.fori_loop(0, 4, attend_back, 0)

    column_grad(normed, query_slope[...], w_up, query_grad)
    for r in range(4):
        rows = contract(normed[:, pl.ds(r * 256, 256)], side_slope[...], 0, 0).astype(jnp.bfloat16)
        streams[1, chip(1 + r // 2), r % 2] = rows
        send_out(streams.at[1, chip(1 + r // 2), r % 2], side_grad.at[pl.ds(r * 256, 256), :])
    dnormed = jnp.concatenate(
        [
            contract(query_slope[...], query_weight(r)[...], 1, 1)
            + contract(side_slope[...], from_sibling[0, r], 1, 1)
            for r in range(4)
        ],
        axis=1,
    )
    tokens_again = pltpu.make_async_copy(tokens_in, w_down.at[1, 1], head_sem.at[0])
    tokens_again.start()
    tokens_again.wait()
    start = w_down[1, 1].astype(jnp.float32)
    inverse = lax.rsqrt(jnp.mean(start * start, axis=1, keepdims=True) + EPSILON)
    gain_slope = jnp.sum(dnormed * start * inverse, axis=0, keepdims=True)
    for r in range(8):
        tiny[pl.ds(r, 1), :] = gain_slope[:, r * 128 : r * 128 + 128]
    scaled = dnormed * attn_gain[...]
    input_grad[...] += inverse * (
        scaled - start * inverse * inverse * jnp.mean(scaled * start, axis=1, keepdims=True)
    )

    grad_copy(0, staged_x, returned_x, beside).wait_recv()
    grad_copy(1, staged_y, returned_y, across).wait_recv()

    def stage_again(a, at):
        value = sums[x, a, 1 - y, at, low] + returned_x[1 - y, a, at, :].astype(jnp.float32)
        staged_again[0, a, at, :] = value.astype(jnp.bfloat16)
        value = sums[1 - x, a, y, at, high] + returned_y[0, a, at, :].astype(jnp.float32)
        staged_again[1, a, at, :] = value.astype(jnp.bfloat16)
        sums[x, a, y, at, low] += returned_x[y, a, at, :].astype(jnp.float32)
        sums[x, a, y, at, high] += returned_y[1, a, at, :].astype(jnp.float32)

    each(stage_again)
    send_out(staged_again, again_out)
    for a in range(3):
        send_out(sums.at[x, a, y], own_out.at[a])

    for k in (1, 2, 3):
        line_copy(0, chip(k), 0, near).wait_send()
    for s in (0, 1):
        for k in range(4):
            pair_copy(s, chip(k)).wait_send()
    for copy in slope_copies:
        copy.wait_send()
    grad_copy(0, staged_x, returned_x, beside).wait_send()
    grad_copy(1, staged_y, returned_y, across).wait_send()
    for copy in (*outgoing, *weighted_stores):
        copy.wait()


def expert_part(
    segment_ids,
    live_mask,
    routes,
    attn_gain,
    moe_gain,
    router,
    tokens,
    attention_weights,
    upstream,
    gate_w,
    up_w,
    down_w,
):
    count, model_dim = tokens.shape
    width = gate_w.shape[1]
    vmem, anywhere = pl.BlockSpec(memory_space=pltpu.VMEM), pl.BlockSpec(memory_space=pl.ANY)
    f32, bf16, dma, shape = jnp.float32, jnp.bfloat16, pltpu.SemaphoreType.DMA, jax.ShapeDtypeStruct
    half = HEAD_SIZE // 2
    frequency = np.float32(10000.0) ** (-(np.arange(half, dtype=np.float32) * np.float32(2.0)) / np.float32(HEAD_SIZE))
    rotation = jnp.asarray(np.tile(frequency.astype(np.float32), 4)[None])
    block = (count, model_dim)
    return pl.pallas_call(
        expert_kernel,
        out_shape=[
            shape(block, f32),
            shape(block, f32),
            shape((model_dim, model_dim), bf16),
            shape((model_dim, model_dim), bf16),
            shape((model_dim, model_dim), bf16),
            shape((24, model_dim), f32),
            shape((8, 128), f32),
            shape((3, width, model_dim), f32),
            shape((2, 3, width, model_dim // 2), bf16),
            shape((4, *block), bf16),
        ],
        in_specs=[vmem] * 7 + [anywhere] * 9,
        out_specs=[vmem] * 2 + [anywhere] * 3 + [vmem] * 2 + [anywhere] * 3,
        scratch_shapes=[
            *[pltpu.VMEM(block, bf16)] * 4,
            pltpu.VMEM(block, f32),
            *[pltpu.VMEM((count, 128), f32)] * 2,
            pltpu.VMEM((count, count), f32),
            pltpu.VMEM((16, count), f32),
            pltpu.VMEM((8, count, HEAD_SIZE), bf16),
            pltpu.VMEM((8, count, HEAD_SIZE), bf16),
            pltpu.VMEM((2, 4, 2, *block), bf16),
            *[pltpu.VMEM((4, 2, 8, count), f32)] * 4,
            pltpu.VMEM((2, 2, model_dim, width), bf16),
            pltpu.VMEM((2, 2, model_dim, width), bf16),
            pltpu.VMEM((2, 2, width, model_dim), bf16),
            pltpu.VMEM((2, 3, 2, width, model_dim), f32),
            pltpu.VMEM((2, 4, 2, *block), bf16),
            pltpu.VMEM((2, 4, *block), bf16),
            pltpu.VMEM((1, 3, *block), bf16),
            *[pltpu.VMEM((2, 3, width, model_dim // 2), bf16)] * 5,
            dma((6,)),
            dma((17,)),
            dma((16,)),
            dma((4,)),
            dma((2, 8)),
            dma((2, 4, 2)),
            dma((7,)),
            dma((4, 2)),
            dma((7,)),
            dma((4, 2)),
            dma((3, 3)),
            dma((2, 2, 3)),
            dma((2, 4)),
            dma((2, 4)),
            dma((2, 4)),
            dma((2, 4)),
            dma((2,)),
            dma((2,)),
        ],
        compiler_params=pltpu.CompilerParams(
            collective_id=1, has_side_effects=True, vmem_limit_bytes=63 << 20
        ),
        name="expert_part",
    )(
        segment_ids,
        live_mask,
        routes.T,
        rotation,
        attn_gain[None],
        moe_gain[None],
        router.T,
        tokens,
        *attention_weights,
        upstream,
        gate_w,
        up_w,
        down_w,
    )


AGAIN_AT = (0, 4, 8)
COMBINE_AT = 6
SMALL_AT = 9


def sum_kernel(
    small,
    tiny,
    out_in,
    query_in,
    side_in,
    again_in,
    own_in,
    weighted_in,
    middle_rows,
    output,
    out_sum,
    query_sum,
    side_sum,
    small_out,
    tiny_out,
    gate_grad,
    up_grad,
    down_grad,
    again,
    returned_again,
    own,
    weighted,
    from_line,
    *rest,
):
    count = 6
    grads, halves, totals, fulls, firsts, seconds, lines = [rest[n * count : (n + 1) * count] for n in range(7)]
    small_sum, small_in, tiny_sum, tiny_in, send, recv, small_send, small_recv, local_sem, load_sem, again_send, again_recv, line_send, line_recv = rest[7 * count :]
    windows = [(ref, pl.ds(n * 512, 512)) for ref in range(3) for n in (0, 1)]
    outs = [(out_sum, query_sum, side_sum)[ref].at[:, :, columns] for ref, columns in windows]
    z, x, c, y = place()
    sibling, beside, across = device(z, x, 1 - c, y), device(z, 1 - x, c, y), device(z, x, c, 1 - y)
    along = [device((z + k) % 4, x, c, y) for k in (1, 2, 3)]
    loads = [
        pltpu.make_async_copy((out_in, query_in, side_in)[ref].at[:, :, columns], grads[i], load_sem.at[i])
        for i, (ref, columns) in enumerate(windows)
    ]
    loads.append(pltpu.make_async_copy(again_in, again, load_sem.at[6]))
    loads.append(pltpu.make_async_copy(own_in, own, load_sem.at[7]))
    loads.append(pltpu.make_async_copy(weighted_in, weighted, load_sem.at[8]))
    for copy in loads:
        copy.start()
    small_sum[0] = small[...]
    tiny_sum[0] = tiny[...]
    greet([sibling, beside, across] + along)
    again_copies = [
        pltpu.make_async_remote_copy(
            src_ref=again.at[n, a],
            dst_ref=returned_again.at[n, a],
            send_sem=again_send.at[n, a],
            recv_sem=again_recv.at[n, a],
            device_id=peer,
            device_id_type=MESH,
        )
        for a in range(3)
        for n, peer in enumerate((across, beside))
    ]
    near, far, last = 1 + z % 2, (2 + 3 * z) % 5, 3 - 3 * (z // 2)
    middle, edge = (z == 1) | (z == 2), (z == 0) | (z == 3)

    def line_copy(block, piece, slot, peer):
        rows = pl.ds(piece * 64, 64)
        return pltpu.make_async_remote_copy(
            src_ref=weighted.at[block, rows, :],
            dst_ref=from_line.at[slot, rows, :],
            send_sem=line_send.at[block, piece],
            recv_sem=line_recv.at[slot, piece],
            device_id=device(peer, x, c, y),
            device_id_type=MESH,
        )

    def line_wait(slot, piece):
        part = from_line.at[slot, pl.ds(piece * 64, 64), :]
        pltpu.make_async_copy(part, part, line_recv.at[slot, piece]).wait()

    def line_stage(tick):
        @pl.when(edge)
        def _():
            for block, slot, peer, first in ((far, 2, near, 0), (near, 1, near, 4), (last, 2, last, 4)):
                if 0 <= tick - first < 4:
                    line_copy(block, tick - first, slot, peer).start()

        @pl.when(middle)
        def _():
            for block, slot, peer, first in ((last, 1, last, 0), (far, 0, far, 1)):
                if 0 <= tick - first < 4:
                    line_copy(block, tick - first, slot, peer).start()
            if 0 <= tick - COMBINE_AT < 4:
                piece = tick - COMBINE_AT
                line_wait(2, piece)
                for r in (0, 32):
                    at = pl.ds(piece * 64 + r, 32)
                    value = weighted[near, at, :].astype(jnp.float32) + from_line[2, at, :].astype(jnp.float32)
                    weighted[near, at, :] = value.astype(jnp.bfloat16)
                line_copy(near, piece, 0, near).start()

    bits = ((x, y), (y, x))
    partners = ((beside, across), (across, beside))

    def push(i, slot, source, target, peer):
        copy = pltpu.make_async_remote_copy(
            src_ref=source,
            dst_ref=target,
            send_sem=send.at[i, slot],
            recv_sem=recv.at[i, slot],
            device_id=peer,
            device_id_type=MESH,
        )
        copy.start()
        return copy

    def combine(i, target, start, length, terms):
        def body(u, carry):
            value = totals[i][start + u].astype(jnp.float32)
            for ref, base in terms:
                value = value + ref[base + u].astype(jnp.float32)
            target[0][target[1] + u] = value.astype(jnp.bfloat16)
            return carry

        lax.fori_loop(0, length, body, 0)

    copies = {}

    def stage(i, step):
        if step == 0:
            copies[i, 0] = [
                push(i, 0, grads[i].at[pl.ds((1 - c) * 32, 32)], halves[i], sibling)
            ]
        if step == 1:
            copies[i, 0][0].wait_recv()

            def body(u, carry):
                value = grads[i][c * 32 + u].astype(jnp.float32) + halves[i][u].astype(jnp.float32)
                totals[i][u] = value.astype(jnp.bfloat16)
                return carry

            lax.fori_loop(0, 32, body, 0)
            copies[i, 1] = [
                push(
                    i,
                    1 + part,
                    totals[i].at[pl.ds(part * 16 + (1 - bits[part][0]) * 8, 8)],
                    firsts[i].at[part],
                    partners[part][0],
                )
                for part in (0, 1)
            ]
        if step == 2:
            copies[i, 2] = []
            for part in (0, 1):
                copies[i, 1][part].wait_recv()
                base = part * 16 + bits[part][0] * 8
                combine(i, (totals[i], base), base, 8, [(firsts[i].at[part], 0)])
                copies[i, 2].append(
                    push(
                        i,
                        3 + part,
                        totals[i].at[pl.ds(base + (1 - bits[part][1]) * 4, 4)],
                        seconds[i].at[part],
                        partners[part][1],
                    )
                )
        if step == 3:
            copies[i, 3] = []
            for part in (0, 1):
                copies[i, 2][part].wait_recv()
                base = part * 16 + bits[part][0] * 8 + bits[part][1] * 4
                combine(i, (totals[i], base), base, 4, [(seconds[i].at[part], 0)])
                for k in (1, 2, 3):
                    copies[i, 3].append(
                        push(
                            i,
                            5 + part * 3 + k - 1,
                            totals[i].at[base + (z + k) % 4],
                            lines[i].at[part, k - 1],
                            along[k - 1],
                        )
                    )
        if step == 4:
            copies[i, 4] = []
            for part in (0, 1):
                for k in (1, 2, 3):
                    copies[i, 3][part * 3 + k - 1].wait_recv()
                base = part * 16 + bits[part][0] * 8 + bits[part][1] * 4
                combine(
                    i, (fulls[i], c * 32 + base + z), base + z, 1, [(lines[i].at[part], k) for k in (0, 1, 2)]
                )
                for k in (1, 2, 3):
                    piece = fulls[i].at[c * 32 + base + z]
                    copies[i, 4].append(push(i, 11 + part * 3 + k - 1, piece, piece, along[k - 1]))
        if step == 5:
            copies[i, 5] = []
            for part in (0, 1):
                for k in (1, 2, 3):
                    copies[i, 4][part * 3 + k - 1].wait_recv()
                piece = fulls[i].at[pl.ds(c * 32 + part * 16 + bits[part][0] * 8 + bits[part][1] * 4, 4)]
                copies[i, 5].append(push(i, 17 + part, piece, piece, partners[part][1]))
        if step == 6:
            copies[i, 6] = []
            for part in (0, 1):
                copies[i, 5][part].wait_recv()
                piece = fulls[i].at[pl.ds(c * 32 + part * 16 + bits[part][0] * 8, 8)]
                copies[i, 6].append(push(i, 19 + part, piece, piece, partners[part][0]))
        if step == 7:
            for part in (0, 1):
                copies[i, 6][part].wait_recv()
            piece = fulls[i].at[pl.ds(c * 32, 32)]
            copies[i, 7] = [push(i, 21, piece, piece, sibling)]
        if step == 8:
            copies[i, 7][0].wait_recv()
            done = pltpu.make_async_copy(fulls[i], outs[i], local_sem.at[i])
            done.start()
            copies[i, 8] = [done]

    def small_stage(n, step):
        total, arrived = (small_sum, tiny_sum)[n], (small_in, tiny_in)[n]

        def small_push(slot, peer, source, target):
            copy = pltpu.make_async_remote_copy(
                src_ref=total.at[source],
                dst_ref=arrived.at[target],
                send_sem=small_send.at[n, slot],
                recv_sem=small_recv.at[n, slot],
                device_id=peer,
                device_id_type=MESH,
            )
            copy.start()
            copies.setdefault((n, "s", step), []).append(copy)

        if step == 0:
            small_push(0, sibling, 0, 0)
        if step in (1, 2, 3):
            copies[n, "s", step - 1][0].wait_recv()
            total[step] = total[step - 1] + arrived[step - 1]
        if step in (1, 2):
            small_push(step, (beside, across)[step - 1], step, step)
        if step == 3:
            for k in (1, 2, 3):
                small_push(2 + k, along[k - 1], 3, 3 + z)
            arrived[3 + z] = total[3]
        if step == 4:
            for copy in copies[n, "s", 3]:
                copy.wait_recv()
            (small_out, tiny_out)[n][...] = (arrived[3] + arrived[4]) + (arrived[5] + arrived[6])

    for tick in range(count + 8):
        for i in range(count):
            if tick == i:
                loads[i].wait()
            if 0 <= tick - i <= 8:
                stage(i, tick - i)
        if tick == 0:
            loads[6].wait()
            loads[8].wait()
        if tick in AGAIN_AT:
            part = 2 * AGAIN_AT.index(tick)
            again_copies[part].start()
            again_copies[part + 1].start()
        line_stage(tick)
        if SMALL_AT <= tick <= SMALL_AT + 4:
            small_stage(0, tick - SMALL_AT)
            small_stage(1, tick - SMALL_AT)
    loads[7].wait()
    for copy in again_copies:
        copy.wait_recv()
    for a, target in enumerate((gate_grad, up_grad, down_grad)):
        for n in (0, 1):
            columns = pl.ds(n * 512, 512)
            summed = own[a, :, columns] + returned_again[n, a].astype(jnp.float32)
            if a < 2:
                target[columns, :] = summed.T
            else:
                target[:, columns] = summed

    def finish(slots):
        for slot in slots:
            for piece in range(4):
                line_wait(slot, piece)

        def body(u, carry):
            at = pl.ds(pl.multiple_of(u * 32, 32), 32)
            value = weighted[z, at, :].astype(jnp.float32)
            for slot in slots:
                value = value + from_line[slot, at, :].astype(jnp.float32)
            output[at, :] = (middle_rows[at, :] + value).astype(jnp.bfloat16)
            return carry

        lax.fori_loop(0, 8, body, 0)

    @pl.when(middle)
    def _():
        finish((0, 1))

    @pl.when(edge)
    def _():
        finish((0, 1, 2))

    for block in (near, far, last):
        for piece in range(4):
            line_copy(block, piece, 0, near).wait_send()
    for key_of, made in copies.items():
        for copy in made:
            if key_of[1] == 8:
                copy.wait()
            else:
                copy.wait_send()
    for copy in again_copies:
        copy.wait_send()


def sum_part(wide, small, tiny, again, own, weighted, middle):
    model_dim = small.shape[1]
    vmem, anywhere = pl.BlockSpec(memory_space=pltpu.VMEM), pl.BlockSpec(memory_space=pl.ANY)
    f32, bf16, dma = jnp.float32, jnp.bfloat16, pltpu.SemaphoreType.DMA
    leads = ((64,), (32,), (32,), (64,), (2, 8), (2, 4), (2, 3))
    shape = jax.ShapeDtypeStruct
    width = own.shape[1]
    units = [g.reshape(64, UNIT, model_dim) for g in wide]
    out = pl.pallas_call(
        sum_kernel,
        out_shape=[
            shape(middle.shape, bf16),
            *[shape(u.shape, bf16) for u in units],
            shape(small.shape, f32),
            shape(tiny.shape, f32),
            shape((model_dim, width), f32),
            shape((model_dim, width), f32),
            shape((width, model_dim), f32),
        ],
        in_specs=[vmem] * 2 + [anywhere] * 6 + [vmem],
        out_specs=[vmem] + [anywhere] * 3 + [vmem] * 5,
        scratch_shapes=[
            pltpu.VMEM(again.shape, bf16),
            pltpu.VMEM(again.shape, bf16),
            pltpu.VMEM(own.shape, f32),
            pltpu.VMEM(weighted.shape, bf16),
            pltpu.VMEM((3, *middle.shape), bf16),
            *[pltpu.VMEM((*lead, UNIT, 512), bf16) for lead in leads for _ in range(6)],
            pltpu.VMEM((4, *small.shape), f32),
            pltpu.VMEM((7, *small.shape), f32),
            pltpu.VMEM((4, *tiny.shape), f32),
            pltpu.VMEM((7, *tiny.shape), f32),
            dma((6, 22)),
            dma((6, 22)),
            dma((2, 6)),
            dma((2, 6)),
            dma((6,)),
            dma((9,)),
            dma((2, 3)),
            dma((2, 3)),
            dma((4, 4)),
            dma((3, 4)),
        ],
        compiler_params=pltpu.CompilerParams(
            collective_id=0, has_side_effects=True, vmem_limit_bytes=60 << 20
        ),
        name="sum_part",
    )(small, tiny, *units, again, own, weighted, middle)
    return out[0], [o.reshape(model_dim, model_dim) for o in out[1:4]], out[4], out[5], out[6:9]


def local(
    tokens,
    segment_ids,
    live_mask,
    routes,
    attn_gain,
    w_query,
    key_weight,
    value_weight,
    w_out,
    moe_gain,
    router,
    w_gate,
    w_up,
    w_down,
    cotangent,
):
    sequence_length = tokens.shape[0]
    model_dim = tokens.shape[1]
    experts_all = router.shape[1]
    query_per_key_head = QUERY_HEADS // KEY_VALUE_HEADS
    score_scale = HEAD_SIZE ** (-0.5)
    if lax.axis_size("ep") == 16 and lax.axis_size("hs") == 2:
        middle, input_grad, out_w_grad, query_w_grad, side_grad, small, tiny, own, again, weighted = expert_part(
            segment_ids,
            live_mask,
            routes,
            attn_gain,
            moe_gain,
            router,
            tokens,
            (w_query, key_weight, value_weight, w_out),
            cotangent,
            w_gate[0],
            w_up[0],
            w_down[0],
        )
        output, wide, small, tiny, expert_grads = sum_part(
            (out_w_grad, query_w_grad, side_grad), small, tiny, again, own, weighted, middle
        )
        narrow = key_weight.shape[1]
        return (
            output,
            input_grad,
            tiny.reshape(model_dim),
            wide[1].astype(jnp.float32),
            wide[2][:, :narrow].astype(jnp.float32),
            wide[2][:, narrow:].astype(jnp.float32),
            wide[0].astype(jnp.float32),
            small[17],
            small[:experts_all].T,
            *[g[None] for g in expert_grads],
            small[18, :experts_all].astype(jnp.int32),
        )
    segment = segment_ids[0]
    live_row = live_mask[0]
    inputs = tokens.astype(jnp.float32)
    normed_rows, inverse_one = rms_forward(inputs, attn_gain)
    normed_rows_back = normed_rows.astype(jnp.bfloat16)
    query_pre = jnp.dot(normed_rows_back, w_query, preferred_element_type=jnp.float32).reshape(
        sequence_length, QUERY_HEADS, HEAD_SIZE
    )
    key_before_rotary = jnp.dot(
        normed_rows_back, key_weight, preferred_element_type=jnp.float32
    ).reshape(sequence_length, KEY_VALUE_HEADS, HEAD_SIZE)
    value_b = (
        jnp.dot(normed_rows_back, value_weight, preferred_element_type=jnp.float32)
        .astype(jnp.bfloat16)
        .reshape(sequence_length, KEY_VALUE_HEADS, HEAD_SIZE)
    )
    positions = positions_of(segment)
    cosine_table, sine_table = rotary_tables(positions, HEAD_SIZE)
    query_back_rows = rotary(query_pre, cosine_table, sine_table).astype(jnp.bfloat16)
    key_b = rotary(key_before_rotary, cosine_table, sine_table).astype(jnp.bfloat16)
    indices = jnp.arange(sequence_length)
    allowed = (
        (segment[:, None] == segment[None, :])
        & (indices[None, :] <= indices[:, None])
        & ((live_row[None, :] > 0) | (indices[None, :] == indices[:, None]))
    )
    grouped_rows = query_back_rows.reshape(
        sequence_length, KEY_VALUE_HEADS, query_per_key_head, HEAD_SIZE
    )
    scores = (
        jnp.einsum("qgrd,kgd->grqk", grouped_rows, key_b, preferred_element_type=jnp.float32)
        * score_scale
    )
    scores = jnp.where(allowed, scores, -1e30)
    highest = jnp.max(scores, axis=-1, keepdims=True)
    weights_exp = jnp.exp(scores - highest)
    denominator = jnp.sum(weights_exp, axis=-1, keepdims=True)
    log_total = highest + jnp.log(denominator)
    probabilities = weights_exp / denominator
    mixed = jnp.einsum(
        "grqk,kgd->qgrd",
        probabilities.astype(jnp.bfloat16),
        value_b,
        preferred_element_type=jnp.float32,
    )
    mixed_b = mixed.reshape(sequence_length, QUERY_HEADS * HEAD_SIZE).astype(jnp.bfloat16)
    middle = inputs + jnp.dot(mixed_b, w_out, preferred_element_type=jnp.float32)
    moe_normed, inverse_two = rms_forward(middle, moe_gain)
    moe_in = moe_normed.astype(jnp.bfloat16)
    logits = jnp.dot(moe_in, router, preferred_element_type=jnp.float32)
    route_hot = (routes[:, :, None] == jnp.arange(experts_all)[None, None, :]).astype(jnp.float32)
    chosen = jnp.sum(route_hot * logits[:, None, :], axis=-1)
    route_soft = jax.nn.softmax(chosen, axis=-1)
    live_column = live_row.astype(jnp.float32)[:, None]
    route_gates = route_soft * live_column
    counts_local = jnp.sum(route_hot * live_column[:, :, None], axis=(0, 1))
    dense_gates = jnp.sum(route_hot * route_gates[:, :, None], axis=1)
    upstream_all = lax.all_gather(cotangent, "ep", axis=0, tiled=True)
    gate_all = lax.all_gather(w_gate, "hs", axis=0, tiled=True)
    up_all = lax.all_gather(w_up, "hs", axis=0, tiled=True)
    down_all = lax.all_gather(w_down, "hs", axis=0, tiled=True)
    rows_all = lax.all_gather(moe_in, "ep", axis=0, tiled=True)
    gates_all = lax.all_to_all(
        dense_gates.T.reshape(experts_all, 1, sequence_length), "ep", split_axis=0, concat_axis=1, tiled=True
    ).reshape(-1)
    weighted, back, gate_upstream_all, gate_w_grad, up_w_grad, down_w_grad = expert_pass(
        rows_all, upstream_all, gates_all, gate_all, up_all, down_all
    )
    combined = lax.psum_scatter(weighted, "ep", scatter_dimension=0, tiled=True).astype(jnp.float32)
    expert_input_grad = lax.psum_scatter(back, "ep", scatter_dimension=0, tiled=True).astype(jnp.float32)
    gate_upstream_dense = lax.all_to_all(
        gate_upstream_all.reshape(experts_all, 1, sequence_length), "ep", split_axis=0, concat_axis=1, tiled=True
    ).reshape(experts_all, sequence_length).T
    gate_w_grad = sum_halves(gate_w_grad, 1)[None]
    up_w_grad = sum_halves(up_w_grad, 1)[None]
    down_w_grad = sum_halves(down_w_grad, 0)[None]
    output = (middle + combined).astype(jnp.bfloat16)
    upstream = cotangent.astype(jnp.float32)
    gate_upstream = jnp.sum(route_hot * gate_upstream_dense[:, None, :], axis=-1)
    soft_upstream = gate_upstream * live_column
    chosen_grad = route_soft * (
        soft_upstream - jnp.sum(route_soft * soft_upstream, axis=-1, keepdims=True)
    )
    logit_grad = jnp.sum(route_hot * chosen_grad[:, :, None], axis=1).astype(jnp.bfloat16)
    router_w_grad = jnp.einsum("td,te->de", moe_in, logit_grad, preferred_element_type=jnp.float32)
    moe_in_grad = expert_input_grad + jnp.einsum(
        "te,de->td", logit_grad, router, preferred_element_type=jnp.float32
    )
    middle_norm_grad, moe_gain_grad = rms_backward(middle, inverse_two, moe_gain, moe_in_grad)
    middle_grad = upstream + middle_norm_grad
    attn_grad_b = middle_grad.astype(jnp.bfloat16)
    out_w_grad = jnp.einsum("tm,td->md", mixed_b, attn_grad_b, preferred_element_type=jnp.float32)
    attention_mixed_grad = jnp.einsum(
        "td,md->tm", attn_grad_b, w_out, preferred_element_type=jnp.float32
    ).astype(jnp.bfloat16)
    attention_mixed_grad = attention_mixed_grad.reshape(
        sequence_length, KEY_VALUE_HEADS, query_per_key_head, HEAD_SIZE
    )
    scores_again = (
        jnp.einsum("qgrd,kgd->grqk", grouped_rows, key_b, preferred_element_type=jnp.float32)
        * score_scale
    )
    scores_again = jnp.where(allowed, scores_again, -1e30)
    probs_again = jnp.exp(scores_again - log_total)
    prob_grad = jnp.einsum(
        "qgrd,kgd->grqk", attention_mixed_grad, value_b, preferred_element_type=jnp.float32
    )
    value_per_head_grad = jnp.einsum(
        "grqk,qgrd->kgd",
        probs_again.astype(jnp.bfloat16),
        attention_mixed_grad,
        preferred_element_type=jnp.float32,
    )
    value_per_head_grad = value_per_head_grad.astype(jnp.bfloat16).reshape(
        sequence_length, KEY_VALUE_HEADS * HEAD_SIZE
    )
    row_delta = jnp.sum(probs_again * prob_grad, axis=-1, keepdims=True)
    score_grad = (probs_again * (prob_grad - row_delta)).astype(jnp.bfloat16)
    query_rot_grad = (
        jnp.einsum("grqk,kgd->qgrd", score_grad, key_b, preferred_element_type=jnp.float32)
        * score_scale
    )
    rotated_key_grad = (
        jnp.einsum("grqk,qgrd->kgd", score_grad, grouped_rows, preferred_element_type=jnp.float32)
        * score_scale
    )
    query_head_grad = (
        rotary_backward(
            query_rot_grad.reshape(sequence_length, QUERY_HEADS, HEAD_SIZE),
            cosine_table,
            sine_table,
        )
        .astype(jnp.bfloat16)
        .reshape(sequence_length, QUERY_HEADS * HEAD_SIZE)
    )
    key_head_grad = (
        rotary_backward(rotated_key_grad, cosine_table, sine_table)
        .astype(jnp.bfloat16)
        .reshape(sequence_length, KEY_VALUE_HEADS * HEAD_SIZE)
    )
    query_w_grad = jnp.einsum(
        "td,te->de", normed_rows_back, query_head_grad, preferred_element_type=jnp.float32
    )
    key_w_grad = jnp.einsum(
        "td,te->de", normed_rows_back, key_head_grad, preferred_element_type=jnp.float32
    )
    value_w_grad = jnp.einsum(
        "td,te->de", normed_rows_back, value_per_head_grad, preferred_element_type=jnp.float32
    )
    normed_grad = jnp.einsum(
        "te,de->td", query_head_grad, w_query, preferred_element_type=jnp.float32
    )
    normed_grad = normed_grad + jnp.einsum(
        "te,de->td", key_head_grad, key_weight, preferred_element_type=jnp.float32
    )
    normed_grad = normed_grad + jnp.einsum(
        "te,de->td", value_per_head_grad, value_weight, preferred_element_type=jnp.float32
    )
    input_norm_grad, attn_gain_grad = rms_backward(inputs, inverse_one, attn_gain, normed_grad)
    input_grad = middle_grad + input_norm_grad
    (
        attn_gain_grad,
        query_w_grad,
        key_w_grad,
        value_w_grad,
        out_w_grad,
        moe_gain_grad,
        router_w_grad,
        counts,
    ) = lax.psum(
        (
            attn_gain_grad,
            query_w_grad,
            key_w_grad,
            value_w_grad,
            out_w_grad,
            moe_gain_grad,
            router_w_grad,
            counts_local,
        ),
        ("ep", "hs"),
    )
    return (
        output,
        input_grad,
        attn_gain_grad,
        query_w_grad,
        key_w_grad,
        value_w_grad,
        out_w_grad,
        moe_gain_grad,
        router_w_grad,
        gate_w_grad,
        up_w_grad,
        down_w_grad,
        counts.astype(jnp.int32),
    )


def solution(mesh):
    in_specs = (
        P(("ep", "hs"), None),
        P(("ep", "hs"), None),
        P(("ep", "hs"), None),
        P(("ep", "hs"), None),
        P(),
        P(),
        P(),
        P(),
        P(),
        P(),
        P(),
        P("ep", None, "hs"),
        P("ep", None, "hs"),
        P("ep", "hs", None),
        P(("ep", "hs"), None),
    )
    out_specs = (
        P(("ep", "hs"), None),
        P(("ep", "hs"), None),
        P(),
        P(),
        P(),
        P(),
        P(),
        P(),
        P(),
        P("ep", None, "hs"),
        P("ep", None, "hs"),
        P("ep", "hs", None),
        P(),
    )
    return jax.shard_map(local, mesh=mesh, in_specs=in_specs, out_specs=out_specs, check_vma=False)
```

```python
import jax
import jax.numpy as jnp
import numpy as np
from jax import lax
from jax.experimental import pallas as pl
from jax.experimental.pallas import tpu as pltpu
from jax.sharding import PartitionSpec as P

QUERY_HEADS = 16
KEY_VALUE_HEADS = 8
HEAD_SIZE = 64
TOP = 8


EPSILON = 1e-05


def rms_forward(value_rows, norm_gain):
    inverse = lax.rsqrt(jnp.mean(value_rows * value_rows, axis=-1, keepdims=True) + EPSILON)
    return (value_rows * inverse * norm_gain, inverse)


def rms_backward(value_rows, inverse, norm_gain, upstream):
    scaled = upstream * norm_gain
    gain_grad = jnp.sum(upstream * value_rows * inverse, axis=0)
    input_grad = inverse * (
        scaled
        - value_rows * inverse * inverse * jnp.mean(scaled * value_rows, axis=-1, keepdims=True)
    )
    return (input_grad, gain_grad)


def positions_of(segment):
    before = (segment[None, :] < segment[:, None]).astype(jnp.int32)
    return jnp.arange(segment.shape[-1], dtype=jnp.int32) - jnp.sum(before, axis=1)


def rotary_tables(positions, head_dim):
    half_dim = head_dim // 2
    frequency = 10000.0 ** (-(jnp.arange(half_dim, dtype=jnp.float32) * 2.0) / head_dim)
    angles = positions.astype(jnp.float32)[:, None] * frequency[None, :]
    return (jnp.cos(angles)[:, None, :], jnp.sin(angles)[:, None, :])


def rotary(heads, cosine_table, sine_table):
    half_dim = heads.shape[-1] // 2
    first_half = heads[..., :half_dim]
    second_half = heads[..., half_dim:]
    return jnp.concatenate(
        [
            first_half * cosine_table - second_half * sine_table,
            second_half * cosine_table + first_half * sine_table,
        ],
        axis=-1,
    )


def rotary_backward(grads, cosine_table, sine_table):
    half_dim = grads.shape[-1] // 2
    first_half = grads[..., :half_dim]
    second_half = grads[..., half_dim:]
    return jnp.concatenate(
        [
            first_half * cosine_table + second_half * sine_table,
            second_half * cosine_table - first_half * sine_table,
        ],
        axis=-1,
    )


def to_bf16(value):
    return lax.reduce_precision(value, 8, 7)


def expert_pass(rows, upstream, gates, gate_w, up_w, down_w):
    groups, model_dim, width = gate_w.shape
    gate_all = jnp.concatenate([gate_w[j] for j in range(groups)], axis=1)
    up_all = jnp.concatenate([up_w[j] for j in range(groups)], axis=1)
    down_all = down_w.reshape(groups * width, model_dim)
    gate_pre = jnp.dot(rows, gate_all, preferred_element_type=jnp.float32)
    up_pre = jnp.dot(rows, up_all, preferred_element_type=jnp.float32)
    sigmoid_part = jax.nn.sigmoid(gate_pre)
    activated = gate_pre * sigmoid_part
    hidden = (activated * up_pre).astype(jnp.bfloat16)
    total = jnp.zeros(rows.shape, jnp.float32)
    for j in range(groups):
        total = total + to_bf16(
            jnp.dot(hidden[:, j * width : (j + 1) * width], down_w[j], preferred_element_type=jnp.float32)
        )
    total = to_bf16(total)
    upstream_f = upstream.astype(jnp.float32)
    gate_upstream = jnp.sum(upstream_f * total, axis=-1)
    weighted = (gates[:, None] * total).astype(jnp.bfloat16)
    upstream_e = (gates[:, None] * upstream_f).astype(jnp.bfloat16)
    hidden_grad = jnp.einsum("td,fd->tf", upstream_e, down_all, preferred_element_type=jnp.float32)
    up_pre_grad = (hidden_grad * activated).astype(jnp.bfloat16)
    gate_pre_grad = (
        hidden_grad * up_pre * sigmoid_part * (1.0 + gate_pre * (1.0 - sigmoid_part))
    ).astype(jnp.bfloat16)
    down_grad = jnp.einsum("tf,td->fd", hidden, upstream_e, preferred_element_type=jnp.float32)
    gate_grad = jnp.einsum("td,tf->df", rows, gate_pre_grad, preferred_element_type=jnp.float32)
    up_grad = jnp.einsum("td,tf->df", rows, up_pre_grad, preferred_element_type=jnp.float32)
    back = jnp.zeros(rows.shape, jnp.float32)
    for j in range(groups):
        cut = slice(j * width, (j + 1) * width)
        back = back + to_bf16(
            jnp.einsum("tf,df->td", gate_pre_grad[:, cut], gate_w[j], preferred_element_type=jnp.float32)
            + jnp.einsum("tf,df->td", up_pre_grad[:, cut], up_w[j], preferred_element_type=jnp.float32)
        )
    return (weighted, back.astype(jnp.bfloat16), gate_upstream, gate_grad, up_grad, down_grad)


def sum_halves(grad, dim):
    return lax.psum_scatter(
        grad.astype(jnp.bfloat16), "hs", scatter_dimension=dim, tiled=True
    ).astype(jnp.float32)


MESH = pl.DeviceIdType.MESH
UNIT = 16


def place():
    ep, hs = lax.axis_index("ep"), lax.axis_index("hs")
    return (ep // 4, (ep // 2) % 2, ep % 2, hs)


def device(z, x, c, y):
    return (z * 4 + x * 2 + c, y)


def greet(peers):
    barrier = pltpu.get_barrier_semaphore()
    for peer in peers:
        pl.semaphore_signal(barrier, inc=1, device_id=peer, device_id_type=MESH)
    pl.semaphore_wait(barrier, len(peers))


EDGE_ORDER = (0, 1, 2, 6, 5, 4, 7, 3)
MIDDLE_ORDER = (0, 1, 2, 3, 7, 5, 6, 4)


def turn(value, cosine, sine):
    lane = lax.broadcasted_iota(jnp.int32, value.shape, 1) % HEAD_SIZE
    swapped = jnp.where(
        lane < HEAD_SIZE // 2, pltpu.roll(value, 128 - HEAD_SIZE // 2, 1), pltpu.roll(value, HEAD_SIZE // 2, 1)
    )
    return value * cosine + swapped * sine


def contract(left, right, left_dim, right_dim):
    return lax.dot_general(
        left, right, (((left_dim,), (right_dim,)), ((), ())), preferred_element_type=jnp.float32
    )


def expert_kernel(
    segment,
    live,
    routes,
    rotation,
    attn_gain,
    moe_gain,
    router,
    tokens_in,
    w_query_in,
    w_key_in,
    w_value_in,
    w_out_in,
    upstream_in,
    gate_w,
    up_w,
    down_w,
    middle_rows,
    input_grad,
    out_grad,
    query_grad,
    side_grad,
    small,
    tiny,
    own_out,
    again_out,
    weighted_out,
    normed,
    query,
    key_value,
    mixed,
    back,
    cosine,
    sine,
    bias,
    soft_rows,
    keys,
    values,
    streams,
    gates_in,
    gates,
    slopes,
    slopes_in,
    w_gate,
    w_up,
    w_down,
    sums,
    partial,
    from_sibling,
    from_line,
    staged_x,
    staged_y,
    staged_again,
    returned_x,
    returned_y,
    load_sem,
    head_sem,
    store_sem,
    weighted_sem,
    gather_send,
    gather_recv,
    gate_send,
    gate_recv,
    slope_send,
    slope_recv,
    weight_send,
    weight_recv,
    pair_send,
    pair_recv,
    line_send,
    line_recv,
    grad_send,
    grad_recv,
):
    z, x, c, y = place()
    near, far, last = 1 + z % 2, (2 + 3 * z) % 5, 3 - 3 * (z // 2)
    middle = (z == 1) | (z == 2)
    edge = (z == 0) | (z == 3)
    sibling, beside, across = device(z, x, 1 - c, y), device(z, 1 - x, c, y), device(z, x, c, 1 - y)
    line = [((z + k) % 4, (c + d) % 2) for k in range(4) for d in range(2) if k or d]

    def chip(k):
        half = z // 2
        inner = z + half * (3 - 2 * z)
        spot = k + inner * (1 - 3 * (k // 2) + 2 * (k // 3))
        return spot + half * (3 - 2 * spot)

    def remote(source, target, send, recv, peer):
        return pltpu.make_async_remote_copy(
            src_ref=source, dst_ref=target, send_sem=send, recv_sem=recv, device_id=peer, device_id_type=MESH
        )

    own = pltpu.make_async_copy(upstream_in, streams.at[1, z, c], load_sem.at[0])
    weights_own = [
        pltpu.make_async_copy(ref, held.at[x, y], load_sem.at[3 + a])
        for a, (ref, held) in enumerate(((gate_w, w_gate), (up_w, w_up), (down_w, w_down)))
    ]
    tokens = from_sibling.at[1, 0]
    head_loads = [pltpu.make_async_copy(tokens_in, tokens, head_sem.at[0])]
    for r in range(4):
        rows = pl.ds(r * 256, 256)
        for n, (source, target) in enumerate(
            (
                (w_query_in, partial.at[0, r // 2, r % 2]),
                (w_out_in, partial.at[1, r // 2, r % 2]),
                (w_key_in, from_sibling.at[0, r, :, pl.ds(0, 512)]),
                (w_value_in, from_sibling.at[0, r, :, pl.ds(512, 512)]),
            )
        ):
            head_loads.append(pltpu.make_async_copy(source.at[rows, :], target, head_sem.at[1 + r * 4 + n]))
    for copy in (own, *weights_own, *head_loads):
        copy.start()
    greet([device(a, x, b, y) for a, b in line] + [beside, across])

    def gather(s, block, slot, peer):
        piece = streams.at[s, block, c]
        return remote(piece, piece, gather_send.at[s, slot], gather_recv.at[s, block, c], peer)

    def arrive(s, block, core):
        piece = streams.at[s, block, core]
        pltpu.make_async_copy(piece, piece, gather_recv.at[s, block, core]).wait()

    def gather_own(s):
        gather(s, z, 0, device(near, x, c, y)).start()
        gather(s, z, 2, sibling).start()

        @pl.when(middle)
        def _():
            gather(s, z, 1, device(far, x, c, y)).start()

    own.wait()
    gather_own(1)
    weight_copies = []
    for a, held in enumerate((w_gate, w_up, w_down)):
        weights_own[a].wait()
        for n, peer in enumerate((across, beside)):
            piece = held.at[x, y]
            weight_copies.append(
                remote(piece, piece, weight_send.at[n, a], weight_recv.at[x, y, a], peer)
            )
    for copy in weight_copies:
        copy.start()
    upper, lower = pl.ds(0, 128), pl.ds(128, 128)

    def relay(n, expert, group, peer):
        if n < 2:
            piece = (w_gate, w_up)[n].at[expert, group]
        else:
            piece = w_down.at[expert, group, (upper, lower)[n - 2], :]
        return remote(piece, piece, weight_send.at[2, n], weight_recv.at[expert, group, n], peer)

    def corner_here():
        for n in range(4):
            relay(n, 1 - x, 1 - y, beside).wait_recv()

    def weights_here(expert, group):
        for a, held in enumerate((w_gate, w_up, w_down)):
            piece = held.at[expert, group]
            pltpu.make_async_copy(piece, piece, weight_recv.at[expert, group, a]).wait()

    def zero(u, carry):
        for e in (0, 1):
            for a in range(3):
                sums[e, a, u // 16, pl.ds(pl.multiple_of((u % 16) * 16, 16), 16), :] = jnp.zeros(
                    (16, 1024), jnp.float32
                )
            partial[e, u // 8, (u // 4) % 2, pl.ds(pl.multiple_of((u % 4) * 64, 64), 64), :] = jnp.zeros(
                (64, 1024), jnp.bfloat16
            )
        return carry

    def handle(k, order=(1, 0)):
        block = chip(k)
        for s in order:
            arrive(s, block, c)
            gather(s, block, 4 + k, sibling).start()
            if k != 2:

                @pl.when(middle)
                def _():
                    gather(s, block, 2 + (k + 1) // 2, device(far, x, c, y)).start()

    row_id = lax.broadcasted_iota(jnp.int32, (256, 256), 0)
    lane_id = lax.broadcasted_iota(jnp.int32, (256, 256), 1)
    diagonal = row_id == lane_id
    segment_row = segment[...].astype(jnp.float32)
    segment_column = jnp.sum(jnp.where(diagonal, segment_row, 0.0), axis=1, keepdims=True)
    live_row = live[...].astype(jnp.float32)
    before = jnp.sum(jnp.where(segment_row < segment_column, 1.0, 0.0), axis=1, keepdims=True)
    position = lax.broadcasted_iota(jnp.int32, (256, 128), 0).astype(jnp.float32) - before
    angle = position * rotation[...]
    side = lax.broadcasted_iota(jnp.int32, (256, 128), 1) % HEAD_SIZE < HEAD_SIZE // 2
    cosine[...] = jnp.cos(angle)
    angle_sine = jnp.sin(angle)
    sine[...] = jnp.where(side, -angle_sine, angle_sine)
    allowed = (segment_row == segment_column) & (lane_id <= row_id) & ((live_row > 0.0) | diagonal)
    bias[...] = jnp.where(allowed, 0.0, -1e30)
    for copy in head_loads:
        copy.wait()
    start = tokens[...].astype(jnp.float32)
    inverse = lax.rsqrt(jnp.mean(start * start, axis=1, keepdims=True) + EPSILON)
    normed[...] = (start * inverse * attn_gain[...]).astype(jnp.bfloat16)

    def project(source, weight):
        total = jnp.zeros((256, 1024), jnp.float32)
        for r in range(4):
            total = total + contract(source[:, pl.ds(r * 256, 256)], weight(r), 1, 0)
        return total

    made = project(normed, lambda r: partial[0, r // 2, r % 2])
    for p in range(8):
        columns = pl.ds(p * 128, 128)
        query[:, columns] = turn(made[:, p * 128 : p * 128 + 128], cosine[...], sine[...]).astype(jnp.bfloat16)
    made = project(normed, lambda r: from_sibling[0, r])
    for p in range(4):
        columns = pl.ds(p * 128, 128)
        key_value[:, columns] = turn(made[:, p * 128 : p * 128 + 128], cosine[...], sine[...]).astype(jnp.bfloat16)
    key_value[:, pl.ds(512, 512)] = made[:, 512:].astype(jnp.bfloat16)
    for g in range(8):
        keys[g] = key_value[:, pl.ds(g * 64, 64)]
        values[g] = key_value[:, pl.ds(512 + g * 64, 64)]

    def attend(g, carry):
        columns = pl.ds(pl.multiple_of(g * 128, 128), 128)
        pair = query[:, columns]
        found = []
        for r in (0, 1):
            scores = contract(pair[:, r * 64 : r * 64 + 64], keys[g], 1, 1) * HEAD_SIZE ** (-0.5) + bias[...]
            weights = jnp.exp(scores - jnp.max(scores, axis=1, keepdims=True))
            probs = (weights / jnp.sum(weights, axis=1, keepdims=True)).astype(jnp.bfloat16)
            found.append(contract(probs, values[g], 1, 0))
        mixed[:, columns] = jnp.concatenate(found, axis=1).astype(jnp.bfloat16)
        return carry

    lax.fori_loop(0, 8, attend, 0)

    @pl.when(edge)
    def _():
        gather(1, z, 1, device(far, x, c, y)).start()

    handle(1, (1,))
    mid = start + project(mixed, lambda r: partial[1, r // 2, r % 2])
    middle_rows[...] = mid
    inverse = lax.rsqrt(jnp.mean(mid * mid, axis=1, keepdims=True) + EPSILON)
    streams[0, z, c] = (mid * inverse * moe_gain[...]).astype(jnp.bfloat16)
    gather_own(0)
    logits = contract(router[...], streams[0, z, c], 1, 1)
    expert_id = lax.broadcasted_iota(jnp.int32, (16, 256), 0)
    routed = routes[pl.ds(0, 1), :] == expert_id
    for n in range(1, TOP):
        routed = routed | (routes[pl.ds(n, 1), :] == expert_id)
    logits = jnp.where(routed, logits, -1e30)
    raised = jnp.where(routed, jnp.exp(logits - jnp.max(logits, axis=0, keepdims=True)), 0.0)
    soft = raised / jnp.sum(raised, axis=0, keepdims=True)
    soft_rows[...] = soft
    held_gates = soft * live_row
    for e in range(16):
        gates_in[e // 4, e % 2, pl.ds((e // 2) % 2, 1), :] = held_gates[e : e + 1, :]
    count = jnp.sum(jnp.where(routed, live_row, 0.0), axis=1, keepdims=True)
    square = lax.broadcasted_iota(jnp.int32, (16, 128), 0) == lax.broadcasted_iota(jnp.int32, (16, 128), 1)
    small[...] = jnp.zeros((24, 1024), jnp.float32)
    small[pl.ds(18, 1), pl.ds(0, 128)] = jnp.sum(jnp.where(square, count, 0.0), axis=0, keepdims=True)
    gate_copies = [
        remote(
            gates_in.at[a, b], gates.at[z, c], gate_send.at[n], gate_recv.at[z, c], device(a, x, b, y)
        )
        for n, (a, b) in enumerate(line)
    ]
    for copy in gate_copies:
        copy.start()
    gates[z, c] = gates_in[z, c]
    lax.fori_loop(0, 32, zero, 0)

    @pl.when(edge)
    def _():
        gather(0, z, 0, device(near, x, c, y)).wait_send()
        gather(0, z, 1, device(far, x, c, y)).start()

    @pl.when(middle)
    def _():
        handle(2, (1,))
        handle(3, (1,))

    handle(1, (0,))
    for a, b in line:
        pltpu.make_async_copy(gates.at[a, b], gates.at[a, b], gate_recv.at[a, b]).wait()
    weights_here(x, 1 - y)
    weights_here(1 - x, y)
    relays = [relay(n, x, 1 - y, beside) for n in (0, 2)] + [relay(n, 1 - x, y, across) for n in (1, 3)]
    for copy in relays:
        copy.start()

    def compute(expert, block, core):
        diagonal = lax.broadcasted_iota(jnp.int32, (256, 256), 0) == lax.broadcasted_iota(jnp.int32, (256, 256), 1)
        gate_row = gates[block, core, pl.ds(expert, 1), :]
        gate = jnp.sum(jnp.where(diagonal, gate_row, 0.0), axis=1, keepdims=True)
        rows = streams[0, block, core]
        total = jnp.zeros((256, 1024), jnp.float32)
        kept = []
        for j in (0, 1):
            gate_pre = contract(rows, w_gate[expert, j], 1, 0)
            up_pre = contract(rows, w_up[expert, j], 1, 0)
            sigmoid_part = jax.nn.sigmoid(gate_pre)
            activated = gate_pre * sigmoid_part
            hidden = (activated * up_pre).astype(jnp.bfloat16)
            part = contract(hidden, w_down[expert, j], 1, 0)
            total = total + part.astype(jnp.bfloat16).astype(jnp.float32)
            inner = up_pre * sigmoid_part * (1.0 + gate_pre * (1.0 - sigmoid_part))
            kept.append((activated, inner, hidden))
        total = total.astype(jnp.bfloat16).astype(jnp.float32)
        upstream = streams[1, block, core].astype(jnp.float32)
        slope = jnp.sum(upstream * total, axis=1, keepdims=True)
        slopes[block, core, pl.ds(expert, 1), :] = jnp.sum(
            jnp.where(diagonal, slope, 0.0), axis=0, keepdims=True
        )
        weighted = gate * total + partial[1, block, core].astype(jnp.float32)
        partial[1, block, core] = weighted.astype(jnp.bfloat16)
        upstream = (gate * upstream).astype(jnp.bfloat16)
        back = jnp.zeros((256, 1024), jnp.float32)
        for j in (0, 1):
            activated, inner, hidden = kept[j]
            hidden_grad = contract(upstream, w_down[expert, j], 1, 1)
            up_grad = (hidden_grad * activated).astype(jnp.bfloat16)
            gate_grad = (hidden_grad * inner).astype(jnp.bfloat16)
            sums[expert, 0, j] += contract(gate_grad, rows, 0, 0)
            sums[expert, 1, j] += contract(up_grad, rows, 0, 0)
            sums[expert, 2, j] += contract(hidden, upstream, 0, 0)
            step = contract(gate_grad, w_gate[expert, j], 1, 1) + contract(up_grad, w_up[expert, j], 1, 1)
            back = back + step.astype(jnp.bfloat16).astype(jnp.float32)
        back = back + partial[0, block, core].astype(jnp.float32)
        partial[0, block, core] = back.astype(jnp.bfloat16)

    def grad_copy(n, source, target, peer):
        return remote(source, target, grad_send.at[n], grad_recv.at[n], peer)

    def pair_copy(s, block):
        return remote(
            partial.at[s, block, 1 - c],
            from_sibling.at[s, block],
            pair_send.at[s, block],
            pair_recv.at[s, block],
            sibling,
        )

    def line_copy(s, block, slot, peer):
        return remote(
            partial.at[s, block, c],
            from_line.at[s, slot],
            line_send.at[s, block],
            line_recv.at[s, slot],
            device(peer, x, c, y),
        )

    def line_wait(s, slot):
        piece = from_line.at[s, slot]
        pltpu.make_async_copy(piece, piece, line_recv.at[s, slot]).wait()

    def add_to(s, block, ref):
        def body(u, carry):
            at = pl.ds(pl.multiple_of(u * 32, 32), 32)
            value = partial[s, block, c, at, :].astype(jnp.float32) + ref[at, :].astype(jnp.float32)
            partial[s, block, c, at, :] = value.astype(jnp.bfloat16)
            return carry

        lax.fori_loop(0, 8, body, 0)

    at_edge = (z * z - 3 * z + 2) // 2
    orders = [sum(code << (3 * t) for t, code in enumerate(codes)) for codes in (EDGE_ORDER, MIDDLE_ORDER)]
    order = at_edge * orders[0] + (1 - at_edge) * orders[1]

    def step(i, carry):
        t = i // 2
        code = lax.shift_right_logical(order, 3 * t) % 8
        again = at_edge * ((t // 3) % 2 + t // 7) + (1 - at_edge) * (t // 4)
        k = code % 4
        expert = x + (code // 4) * (1 - 2 * x)
        block, core = chip(k), (c + i + again) % 2

        @pl.when((i == 2) & middle)
        def _():
            handle(2, (0,))

        @pl.when((i == 4) & middle)
        def _():
            handle(3, (0,))

        @pl.when((i == 4) & edge)
        def _():
            handle(2)

        @pl.when((i == 12) & edge)
        def _():
            handle(3)

        @pl.when((i == 8) & middle | (i == 6) & edge)
        def _():
            corner_here()

        @pl.when((i % 2 == 1) & (again == 0))
        def _():
            for s in (0, 1):
                arrive(s, block, 1 - c)

        compute(expert, block, core)

        @pl.when((i % 2 == 0) & (again == 1))
        def _():
            for s in (0, 1):
                pair_copy(s, block).start()

        @pl.when((i % 2 == 1) & (again == 1))
        def _():
            for s in (0, 1):
                pair_copy(s, block).wait_recv()
                add_to(s, block, from_sibling.at[s, block])

            @pl.when(edge & (k == 2))
            def _():
                line_copy(0, block, 2, near).start()

            @pl.when(edge & (k == 1))
            def _():
                line_copy(0, block, 1, near).start()

            @pl.when(edge & (k == 3))
            def _():
                line_copy(0, block, 2, last).start()

            @pl.when(middle & (k == 3))
            def _():
                line_copy(0, block, 1, last).start()

            @pl.when(middle & (k == 2))
            def _():
                line_copy(0, block, 0, far).start()

        return carry

    lax.fori_loop(0, 16, step, 0)
    low, high = pl.ds(0, 512), pl.ds(512, 512)

    def each(body):
        def rows_of(u, carry):
            at = pl.ds(pl.multiple_of(u * 32, 32), 32)
            for a in range(3):
                body(a, at)
            return carry

        lax.fori_loop(0, 8, rows_of, 0)

    def stage_low(a, at):
        for j in (0, 1):
            staged_x[j, a, at, :] = sums[1 - x, a, j, at, low].astype(jnp.bfloat16)

    def stage_high(a, at):
        staged_y[0, a, at, :] = sums[1 - x, a, 1 - y, at, high].astype(jnp.bfloat16)
        staged_y[1, a, at, :] = sums[x, a, 1 - y, at, high].astype(jnp.bfloat16)

    each(stage_low)
    grad_copy(0, staged_x, returned_x, beside).start()
    each(stage_high)
    grad_copy(1, staged_y, returned_y, across).start()
    slope_copies = [
        remote(
            slopes.at[a, b], slopes_in.at[z, c], slope_send.at[n], slope_recv.at[z, c], device(a, x, b, y)
        )
        for n, (a, b) in enumerate(line)
    ]
    for copy in slope_copies:
        copy.start()
    slopes_in[z, c] = slopes[z, c]


    weighted_stores = [
        pltpu.make_async_copy(partial.at[1, k, c], weighted_out.at[k], weighted_sem.at[k]) for k in range(4)
    ]
    for copy in weighted_stores:
        copy.start()

    @pl.when(middle)
    def _():
        line_wait(0, 2)
        add_to(0, near, from_line.at[0, 2])
        line_copy(0, near, 0, near).start()

    gather(1, z, 0, device(near, x, c, y)).wait_send()

    @pl.when(middle)
    def _():
        gather(0, z, 0, device(near, x, c, y)).wait_send()

    for s in (0, 1):
        gather(s, z, 1, device(far, x, c, y)).wait_send()
        gather(s, z, 2, sibling).wait_send()
        for k in (1, 2, 3):
            gather(s, chip(k), 4 + k, sibling).wait_send()

        @pl.when(middle)
        def _():
            for k in (1, 3):
                gather(s, chip(k), 2 + (k + 1) // 2, device(far, x, c, y)).wait_send()

    for copy in (*gate_copies, *weight_copies, *relays):
        copy.wait_send()

    def query_weight(r):
        return streams.at[0, chip(1 + r // 2), r % 2]

    reloads = []
    for r in range(4):
        rows = pl.ds(r * 256, 256)
        for n, (source, target) in enumerate(
            (
                (w_out_in, from_sibling.at[1, r]),
                (w_query_in, query_weight(r)),
                (w_key_in, from_sibling.at[0, r, :, pl.ds(0, 512)]),
                (w_value_in, from_sibling.at[0, r, :, pl.ds(512, 512)]),
            )
        ):
            reloads.append(pltpu.make_async_copy(source.at[rows, :], target, head_sem.at[1 + r * 4 + n]))
    for copy in reloads:
        copy.start()

    def combined(s, slots, body_of):
        for slot in slots:
            line_wait(s, slot)

        def body(u, carry):
            at = pl.ds(pl.multiple_of(u * 32, 32), 32)
            value = partial[s, z, c, at, :].astype(jnp.float32)
            for slot in slots:
                value = value + from_line[s, slot, at, :].astype(jnp.float32)
            body_of(at, value)
            return carry

        lax.fori_loop(0, 8, body, 0)

    def finish(s, body_of):
        @pl.when(middle)
        def _():
            combined(s, (0, 1), body_of)

        @pl.when(edge)
        def _():
            combined(s, (0, 1, 2), body_of)

    def store_back(at, value):
        back[at, :] = value

    finish(0, store_back)
    for a, b in line:
        pltpu.make_async_copy(slopes_in.at[a, b], slopes_in.at[a, b], slope_recv.at[a, b]).wait()
    upstream = streams[1, z, c].astype(jnp.float32)
    slope_rows = jnp.concatenate([slopes_in[e // 4, e % 2, pl.ds((e // 2) % 2, 1), :] for e in range(16)], axis=0)
    soft_slope = slope_rows * live[...].astype(jnp.float32)
    soft_t = soft_rows[...]
    dlogits = soft_t * (soft_slope - jnp.sum(soft_t * soft_slope, axis=0, keepdims=True))
    dlogits = dlogits.astype(jnp.bfloat16)
    small[pl.ds(0, 16), :] = contract(dlogits, streams[0, z, c], 1, 0)
    dmoe_in = back[...] + contract(dlogits, router[...], 0, 0)
    mid = middle_rows[...]
    inverse = lax.rsqrt(jnp.mean(mid * mid, axis=1, keepdims=True) + EPSILON)
    small[pl.ds(17, 1), :] = jnp.sum(dmoe_in * mid * inverse, axis=0, keepdims=True)
    scaled = dmoe_in * moe_gain[...]
    dmiddle = upstream + inverse * (
        scaled - mid * inverse * inverse * jnp.mean(scaled * mid, axis=1, keepdims=True)
    )
    input_grad[...] = dmiddle
    dattn = dmiddle.astype(jnp.bfloat16)
    outgoing = []

    def send_out(source, target):
        copy = pltpu.make_async_copy(source, target, store_sem.at[len(outgoing)])
        copy.start()
        outgoing.append(copy)

    def column_grad(left, right, held, target):
        for r in range(4):
            rows = contract(left[:, pl.ds(r * 256, 256)], right, 0, 0).astype(jnp.bfloat16)
            for n in range(4):
                held[n // 2, n % 2, pl.ds(r * 256, 256), :] = rows[:, n * 256 : n * 256 + 256]
        for n in range(4):
            send_out(held.at[n // 2, n % 2], target.at[:, pl.ds(n * 256, 256)])

    column_grad(mixed, dattn, w_gate, out_grad)
    for copy in reloads:
        copy.wait()
    mixed_slope, query_slope, side_slope = w_down.at[0, 0], w_down.at[0, 1], w_down.at[1, 0]
    for r in range(4):
        mixed_slope[:, pl.ds(r * 256, 256)] = contract(dattn, from_sibling[1, r], 1, 1).astype(jnp.bfloat16)
    scale = HEAD_SIZE ** (-0.5)

    def attend_back(p, carry):
        wide = pl.ds(pl.multiple_of(p * 256, 256), 256)
        queries, slopes_here = query[:, wide], mixed_slope[:, wide]
        key_slopes, value_slopes, query_slopes = [], [], []
        for n in (0, 1):
            key_g, value_g = keys[2 * p + n], values[2 * p + n]
            key_slope = jnp.zeros((256, 64), jnp.float32)
            value_slope = jnp.zeros((256, 64), jnp.float32)
            for r in (0, 1):
                cut = slice(n * 128 + r * 64, n * 128 + r * 64 + 64)
                query_h, slope_h = queries[:, cut], slopes_here[:, cut]
                scores = contract(query_h, key_g, 1, 1) * scale + bias[...]
                weights = jnp.exp(scores - jnp.max(scores, axis=1, keepdims=True))
                probs = weights / jnp.sum(weights, axis=1, keepdims=True)
                prob_slope = contract(slope_h, value_g, 1, 1)
                value_slope = value_slope + contract(probs.astype(jnp.bfloat16), slope_h, 0, 0)
                delta = jnp.sum(probs * prob_slope, axis=1, keepdims=True)
                score_slope = (probs * (prob_slope - delta)).astype(jnp.bfloat16)
                query_slopes.append(contract(score_slope, key_g, 1, 0) * scale)
                key_slope = key_slope + contract(score_slope, query_h, 0, 0) * scale
            key_slopes.append(key_slope)
            value_slopes.append(value_slope)
        for n in (0, 1):
            pair = turn(jnp.concatenate(query_slopes[2 * n : 2 * n + 2], axis=1), cosine[...], -sine[...])
            query_slope[:, pl.ds(pl.multiple_of(p * 256 + n * 128, 128), 128)] = pair.astype(jnp.bfloat16)
        pair = turn(jnp.concatenate(key_slopes, axis=1), cosine[...], -sine[...])
        side_slope[:, pl.ds(pl.multiple_of(p * 128, 128), 128)] = pair.astype(jnp.bfloat16)
        pair = jnp.concatenate(value_slopes, axis=1)
        side_slope[:, pl.ds(pl.multiple_of(512 + p * 128, 128), 128)] = pair.astype(jnp.bfloat16)
        return carry

    lax.fori_loop(0, 4, attend_back, 0)

    column_grad(normed, query_slope[...], w_up, query_grad)
    for r in range(4):
        rows = contract(normed[:, pl.ds(r * 256, 256)], side_slope[...], 0, 0).astype(jnp.bfloat16)
        streams[1, chip(1 + r // 2), r % 2] = rows
        send_out(streams.at[1, chip(1 + r // 2), r % 2], side_grad.at[pl.ds(r * 256, 256), :])
    dnormed = jnp.concatenate(
        [
            contract(query_slope[...], query_weight(r)[...], 1, 1)
            + contract(side_slope[...], from_sibling[0, r], 1, 1)
            for r in range(4)
        ],
        axis=1,
    )
    tokens_again = pltpu.make_async_copy(tokens_in, w_down.at[1, 1], head_sem.at[0])
    tokens_again.start()
    tokens_again.wait()
    start = w_down[1, 1].astype(jnp.float32)
    inverse = lax.rsqrt(jnp.mean(start * start, axis=1, keepdims=True) + EPSILON)
    gain_slope = jnp.sum(dnormed * start * inverse, axis=0, keepdims=True)
    for r in range(8):
        tiny[pl.ds(r, 1), :] = gain_slope[:, r * 128 : r * 128 + 128]
    scaled = dnormed * attn_gain[...]
    input_grad[...] += inverse * (
        scaled - start * inverse * inverse * jnp.mean(scaled * start, axis=1, keepdims=True)
    )

    grad_copy(0, staged_x, returned_x, beside).wait_recv()
    grad_copy(1, staged_y, returned_y, across).wait_recv()

    def stage_again(a, at):
        value = sums[x, a, 1 - y, at, low] + returned_x[1 - y, a, at, :].astype(jnp.float32)
        staged_again[0, a, at, :] = value.astype(jnp.bfloat16)
        value = sums[1 - x, a, y, at, high] + returned_y[0, a, at, :].astype(jnp.float32)
        staged_again[1, a, at, :] = value.astype(jnp.bfloat16)
        sums[x, a, y, at, low] += returned_x[y, a, at, :].astype(jnp.float32)
        sums[x, a, y, at, high] += returned_y[1, a, at, :].astype(jnp.float32)

    each(stage_again)
    send_out(staged_again, again_out)
    for a in range(3):
        send_out(sums.at[x, a, y], own_out.at[a])

    for k in (1, 2, 3):
        line_copy(0, chip(k), 0, near).wait_send()
    for s in (0, 1):
        for k in range(4):
            pair_copy(s, chip(k)).wait_send()
    for copy in slope_copies:
        copy.wait_send()
    grad_copy(0, staged_x, returned_x, beside).wait_send()
    grad_copy(1, staged_y, returned_y, across).wait_send()
    for copy in (*outgoing, *weighted_stores):
        copy.wait()


def expert_part(
    segment_ids,
    live_mask,
    routes,
    attn_gain,
    moe_gain,
    router,
    tokens,
    attention_weights,
    upstream,
    gate_w,
    up_w,
    down_w,
):
    count, model_dim = tokens.shape
    width = gate_w.shape[1]
    vmem, anywhere = pl.BlockSpec(memory_space=pltpu.VMEM), pl.BlockSpec(memory_space=pl.ANY)
    f32, bf16, dma, shape = jnp.float32, jnp.bfloat16, pltpu.SemaphoreType.DMA, jax.ShapeDtypeStruct
    half = HEAD_SIZE // 2
    frequency = np.float32(10000.0) ** (-(np.arange(half, dtype=np.float32) * np.float32(2.0)) / np.float32(HEAD_SIZE))
    rotation = jnp.asarray(np.tile(frequency.astype(np.float32), 4)[None])
    block = (count, model_dim)
    return pl.pallas_call(
        expert_kernel,
        out_shape=[
            shape(block, f32),
            shape(block, f32),
            shape((model_dim, model_dim), bf16),
            shape((model_dim, model_dim), bf16),
            shape((model_dim, model_dim), bf16),
            shape((24, model_dim), f32),
            shape((8, 128), f32),
            shape((3, width, model_dim), f32),
            shape((2, 3, width, model_dim // 2), bf16),
            shape((4, *block), bf16),
        ],
        in_specs=[vmem] * 7 + [anywhere] * 9,
        out_specs=[vmem] * 2 + [anywhere] * 3 + [vmem] * 2 + [anywhere] * 3,
        scratch_shapes=[
            *[pltpu.VMEM(block, bf16)] * 4,
            pltpu.VMEM(block, f32),
            *[pltpu.VMEM((count, 128), f32)] * 2,
            pltpu.VMEM((count, count), f32),
            pltpu.VMEM((16, count), f32),
            pltpu.VMEM((8, count, HEAD_SIZE), bf16),
            pltpu.VMEM((8, count, HEAD_SIZE), bf16),
            pltpu.VMEM((2, 4, 2, *block), bf16),
            *[pltpu.VMEM((4, 2, 8, count), f32)] * 4,
            pltpu.VMEM((2, 2, model_dim, width), bf16),
            pltpu.VMEM((2, 2, model_dim, width), bf16),
            pltpu.VMEM((2, 2, width, model_dim), bf16),
            pltpu.VMEM((2, 3, 2, width, model_dim), f32),
            pltpu.VMEM((2, 4, 2, *block), bf16),
            pltpu.VMEM((2, 4, *block), bf16),
            pltpu.VMEM((1, 3, *block), bf16),
            *[pltpu.VMEM((2, 3, width, model_dim // 2), bf16)] * 5,
            dma((6,)),
            dma((17,)),
            dma((16,)),
            dma((4,)),
            dma((2, 8)),
            dma((2, 4, 2)),
            dma((7,)),
            dma((4, 2)),
            dma((7,)),
            dma((4, 2)),
            dma((3, 4)),
            dma((2, 2, 4)),
            dma((2, 4)),
            dma((2, 4)),
            dma((2, 4)),
            dma((2, 4)),
            dma((2,)),
            dma((2,)),
        ],
        compiler_params=pltpu.CompilerParams(
            collective_id=1, has_side_effects=True, vmem_limit_bytes=63 << 20
        ),
        name="expert_part",
    )(
        segment_ids,
        live_mask,
        routes.T,
        rotation,
        attn_gain[None],
        moe_gain[None],
        router.T,
        tokens,
        *attention_weights,
        upstream,
        gate_w,
        up_w,
        down_w,
    )


ROWS_AT_ONCE = 256
AGAIN_AT = (0, 4, 8)
COMBINE_AT = 6
SMALL_AT = 9


def sum_kernel(
    small,
    tiny,
    out_in,
    query_in,
    side_in,
    again_in,
    own_in,
    weighted_in,
    middle_rows,
    output,
    out_sum,
    query_sum,
    side_sum,
    small_out,
    tiny_out,
    gate_grad,
    up_grad,
    down_grad,
    again,
    returned_again,
    own,
    weighted,
    from_line,
    *rest,
):
    count = 6
    grads, halves, totals, fulls, firsts, seconds, lines = [rest[n * count : (n + 1) * count] for n in range(7)]
    small_sum, small_in, tiny_sum, tiny_in, send, recv, small_send, small_recv, local_sem, load_sem, again_send, again_recv, line_send, line_recv = rest[7 * count :]
    windows = [(ref, pl.ds(n * 512, 512)) for ref in range(3) for n in (0, 1)]
    outs = [(out_sum, query_sum, side_sum)[ref].at[:, :, columns] for ref, columns in windows]
    z, x, c, y = place()
    sibling, beside, across = device(z, x, 1 - c, y), device(z, 1 - x, c, y), device(z, x, c, 1 - y)
    along = [device((z + k) % 4, x, c, y) for k in (1, 2, 3)]
    loads = [
        pltpu.make_async_copy((out_in, query_in, side_in)[ref].at[:, :, columns], grads[i], load_sem.at[i])
        for i, (ref, columns) in enumerate(windows)
    ]
    loads.append(pltpu.make_async_copy(again_in, again, load_sem.at[6]))
    loads.append(pltpu.make_async_copy(own_in, own, load_sem.at[7]))
    loads.append(pltpu.make_async_copy(weighted_in, weighted, load_sem.at[8]))
    for copy in loads:
        copy.start()
    small_sum[0] = small[...]
    tiny_sum[0] = tiny[...]
    greet([sibling, beside, across] + along)
    again_copies = [
        pltpu.make_async_remote_copy(
            src_ref=again.at[n, a],
            dst_ref=returned_again.at[n, a],
            send_sem=again_send.at[n, a],
            recv_sem=again_recv.at[n, a],
            device_id=peer,
            device_id_type=MESH,
        )
        for a in range(3)
        for n, peer in enumerate((across, beside))
    ]
    near, far, last = 1 + z % 2, (2 + 3 * z) % 5, 3 - 3 * (z // 2)
    middle, edge = (z == 1) | (z == 2), (z == 0) | (z == 3)

    def line_copy(block, piece, slot, peer):
        rows = pl.ds(piece * 64, 64)
        return pltpu.make_async_remote_copy(
            src_ref=weighted.at[block, rows, :],
            dst_ref=from_line.at[slot, rows, :],
            send_sem=line_send.at[block, piece],
            recv_sem=line_recv.at[slot, piece],
            device_id=device(peer, x, c, y),
            device_id_type=MESH,
        )

    def line_wait(slot, piece):
        part = from_line.at[slot, pl.ds(piece * 64, 64), :]
        pltpu.make_async_copy(part, part, line_recv.at[slot, piece]).wait()

    def line_stage(tick):
        @pl.when(edge)
        def _():
            for block, slot, peer, first in ((far, 2, near, 0), (near, 1, near, 4), (last, 2, last, 4)):
                if 0 <= tick - first < 4:
                    line_copy(block, tick - first, slot, peer).start()

        @pl.when(middle)
        def _():
            for block, slot, peer, first in ((last, 1, last, 0), (far, 0, far, 1)):
                if 0 <= tick - first < 4:
                    line_copy(block, tick - first, slot, peer).start()
            if 0 <= tick - COMBINE_AT < 4:
                piece = tick - COMBINE_AT
                line_wait(2, piece)
                for r in (0, 32):
                    at = pl.ds(piece * 64 + r, 32)
                    value = weighted[near, at, :].astype(jnp.float32) + from_line[2, at, :].astype(jnp.float32)
                    weighted[near, at, :] = value.astype(jnp.bfloat16)
                line_copy(near, piece, 0, near).start()

    bits = ((x, y), (y, x))
    partners = ((beside, across), (across, beside))

    def push(i, slot, source, target, peer):
        copy = pltpu.make_async_remote_copy(
            src_ref=source,
            dst_ref=target,
            send_sem=send.at[i, slot],
            recv_sem=recv.at[i, slot],
            device_id=peer,
            device_id_type=MESH,
        )
        copy.start()
        return copy

    def combine(i, target, start, length, terms):
        def body(u, carry):
            value = totals[i][start + u].astype(jnp.float32)
            for ref, base in terms:
                value = value + ref[base + u].astype(jnp.float32)
            target[0][target[1] + u] = value.astype(jnp.bfloat16)
            return carry

        lax.fori_loop(0, length, body, 0)

    copies = {}

    def stage(i, step):
        if step == 0:
            copies[i, 0] = [
                push(i, 0, grads[i].at[pl.ds((1 - c) * 32, 32)], halves[i], sibling)
            ]
        if step == 1:
            copies[i, 0][0].wait_recv()

            def body(u, carry):
                value = grads[i][c * 32 + u].astype(jnp.float32) + halves[i][u].astype(jnp.float32)
                totals[i][u] = value.astype(jnp.bfloat16)
                return carry

            lax.fori_loop(0, 32, body, 0)
            copies[i, 1] = [
                push(
                    i,
                    1 + part,
                    totals[i].at[pl.ds(part * 16 + (1 - bits[part][0]) * 8, 8)],
                    firsts[i].at[part],
                    partners[part][0],
                )
                for part in (0, 1)
            ]
        if step == 2:
            copies[i, 2] = []
            for part in (0, 1):
                copies[i, 1][part].wait_recv()
                base = part * 16 + bits[part][0] * 8
                combine(i, (totals[i], base), base, 8, [(firsts[i].at[part], 0)])
                copies[i, 2].append(
                    push(
                        i,
                        3 + part,
                        totals[i].at[pl.ds(base + (1 - bits[part][1]) * 4, 4)],
                        seconds[i].at[part],
                        partners[part][1],
                    )
                )
        if step == 3:
            copies[i, 3] = []
            for part in (0, 1):
                copies[i, 2][part].wait_recv()
                base = part * 16 + bits[part][0] * 8 + bits[part][1] * 4
                combine(i, (totals[i], base), base, 4, [(seconds[i].at[part], 0)])
                for k in (1, 2, 3):
                    copies[i, 3].append(
                        push(
                            i,
                            5 + part * 3 + k - 1,
                            totals[i].at[base + (z + k) % 4],
                            lines[i].at[part, k - 1],
                            along[k - 1],
                        )
                    )
        if step == 4:
            copies[i, 4] = []
            for part in (0, 1):
                for k in (1, 2, 3):
                    copies[i, 3][part * 3 + k - 1].wait_recv()
                base = part * 16 + bits[part][0] * 8 + bits[part][1] * 4
                combine(
                    i, (fulls[i], c * 32 + base + z), base + z, 1, [(lines[i].at[part], k) for k in (0, 1, 2)]
                )
                for k in (1, 2, 3):
                    piece = fulls[i].at[c * 32 + base + z]
                    copies[i, 4].append(push(i, 11 + part * 3 + k - 1, piece, piece, along[k - 1]))
        if step == 5:
            copies[i, 5] = []
            for part in (0, 1):
                for k in (1, 2, 3):
                    copies[i, 4][part * 3 + k - 1].wait_recv()
                piece = fulls[i].at[pl.ds(c * 32 + part * 16 + bits[part][0] * 8 + bits[part][1] * 4, 4)]
                copies[i, 5].append(push(i, 17 + part, piece, piece, partners[part][1]))
        if step == 6:
            copies[i, 6] = []
            for part in (0, 1):
                copies[i, 5][part].wait_recv()
                piece = fulls[i].at[pl.ds(c * 32 + part * 16 + bits[part][0] * 8, 8)]
                copies[i, 6].append(push(i, 19 + part, piece, piece, partners[part][0]))
        if step == 7:
            for part in (0, 1):
                copies[i, 6][part].wait_recv()
            piece = fulls[i].at[pl.ds(c * 32, 32)]
            copies[i, 7] = [push(i, 21, piece, piece, sibling)]
        if step == 8:
            copies[i, 7][0].wait_recv()
            done = pltpu.make_async_copy(fulls[i], outs[i], local_sem.at[i])
            done.start()
            copies[i, 8] = [done]

    def small_stage(n, step):
        total, arrived = (small_sum, tiny_sum)[n], (small_in, tiny_in)[n]

        def small_push(slot, peer, source, target):
            copy = pltpu.make_async_remote_copy(
                src_ref=total.at[source],
                dst_ref=arrived.at[target],
                send_sem=small_send.at[n, slot],
                recv_sem=small_recv.at[n, slot],
                device_id=peer,
                device_id_type=MESH,
            )
            copy.start()
            copies.setdefault((n, "s", step), []).append(copy)

        if step == 0:
            small_push(0, sibling, 0, 0)
        if step in (1, 2, 3):
            copies[n, "s", step - 1][0].wait_recv()
            total[step] = total[step - 1] + arrived[step - 1]
        if step in (1, 2):
            small_push(step, (beside, across)[step - 1], step, step)
        if step == 3:
            for k in (1, 2, 3):
                small_push(2 + k, along[k - 1], 3, 3 + z)
            arrived[3 + z] = total[3]
        if step == 4:
            for copy in copies[n, "s", 3]:
                copy.wait_recv()
            (small_out, tiny_out)[n][...] = (arrived[3] + arrived[4]) + (arrived[5] + arrived[6])

    for tick in range(count + 8):
        for i in range(count):
            if tick == i:
                loads[i].wait()
            if 0 <= tick - i <= 8:
                stage(i, tick - i)
        if tick == 0:
            loads[6].wait()
            loads[8].wait()
        if tick in AGAIN_AT:
            part = 2 * AGAIN_AT.index(tick)
            again_copies[part].start()
            again_copies[part + 1].start()
        line_stage(tick)
        if SMALL_AT <= tick <= SMALL_AT + 4:
            small_stage(0, tick - SMALL_AT)
            small_stage(1, tick - SMALL_AT)
    loads[7].wait()
    for copy in again_copies:
        copy.wait_recv()
    for a, target in enumerate((gate_grad, up_grad, down_grad)):
        for n in (0, 1):
            columns = pl.ds(n * 512, 512)
            summed = own[a, :, columns] + returned_again[n, a].astype(jnp.float32)
            if a < 2:
                target[columns, :] = summed.T
            else:
                target[:, columns] = summed

    def finish(slots):
        for slot in slots:
            for piece in range(4):
                line_wait(slot, piece)

        def body(u, carry):
            at = pl.ds(pl.multiple_of(u * 32, 32), 32)
            value = weighted[z, at, :].astype(jnp.float32)
            for slot in slots:
                value = value + from_line[slot, at, :].astype(jnp.float32)
            output[at, :] = (middle_rows[at, :] + value).astype(jnp.bfloat16)
            return carry

        lax.fori_loop(0, 8, body, 0)

    @pl.when(middle)
    def _():
        finish((0, 1))

    @pl.when(edge)
    def _():
        finish((0, 1, 2))

    for block in (near, far, last):
        for piece in range(4):
            line_copy(block, piece, 0, near).wait_send()
    for key_of, made in copies.items():
        for copy in made:
            if key_of[1] == 8:
                copy.wait()
            else:
                copy.wait_send()
    for copy in again_copies:
        copy.wait_send()


def sum_part(wide, small, tiny, again, own, weighted, middle):
    model_dim = small.shape[1]
    vmem, anywhere = pl.BlockSpec(memory_space=pltpu.VMEM), pl.BlockSpec(memory_space=pl.ANY)
    f32, bf16, dma = jnp.float32, jnp.bfloat16, pltpu.SemaphoreType.DMA
    leads = ((64,), (32,), (32,), (64,), (2, 8), (2, 4), (2, 3))
    shape = jax.ShapeDtypeStruct
    width = own.shape[1]
    units = [g.reshape(64, UNIT, model_dim) for g in wide]
    out = pl.pallas_call(
        sum_kernel,
        out_shape=[
            shape(middle.shape, bf16),
            *[shape(u.shape, bf16) for u in units],
            shape(small.shape, f32),
            shape(tiny.shape, f32),
            shape((model_dim, width), f32),
            shape((model_dim, width), f32),
            shape((width, model_dim), f32),
        ],
        in_specs=[vmem] * 2 + [anywhere] * 6 + [vmem],
        out_specs=[vmem] + [anywhere] * 3 + [vmem] * 5,
        scratch_shapes=[
            pltpu.VMEM(again.shape, bf16),
            pltpu.VMEM(again.shape, bf16),
            pltpu.VMEM(own.shape, f32),
            pltpu.VMEM(weighted.shape, bf16),
            pltpu.VMEM((3, *middle.shape), bf16),
            *[pltpu.VMEM((*lead, UNIT, 512), bf16) for lead in leads for _ in range(6)],
            pltpu.VMEM((4, *small.shape), f32),
            pltpu.VMEM((7, *small.shape), f32),
            pltpu.VMEM((4, *tiny.shape), f32),
            pltpu.VMEM((7, *tiny.shape), f32),
            dma((6, 22)),
            dma((6, 22)),
            dma((2, 6)),
            dma((2, 6)),
            dma((6,)),
            dma((9,)),
            dma((2, 3)),
            dma((2, 3)),
            dma((4, 4)),
            dma((3, 4)),
        ],
        compiler_params=pltpu.CompilerParams(
            collective_id=0, has_side_effects=True, vmem_limit_bytes=60 << 20
        ),
        name="sum_part",
    )(small, tiny, *units, again, own, weighted, middle)
    return out[0], [o.reshape(model_dim, model_dim) for o in out[1:4]], out[4], out[5], out[6:9]


def finish_kernel(
    out_in,
    query_in,
    side_in,
    small,
    output_in,
    input_grad_in,
    gate_in,
    up_in,
    down_in,
    tiny_in,
    out_grad,
    query_grad,
    key_grad,
    value_grad,
    router_grad,
    gain_grad,
    counts,
    output,
    input_grad,
    gate_grad,
    up_grad,
    down_grad,
    tiny,
):
    for source, target in (
        (input_grad_in, input_grad),
        (gate_in, gate_grad),
        (up_in, up_grad),
        (down_in, down_grad),
        (output_in, output),
    ):
        target[...] = source[...]

    @pl.when(pl.program_id(0) == 0)
    def _():
        tiny[...] = tiny_in[...]
        router_grad[...] = small[pl.ds(0, 16), :]
        for r in range(8):
            gain_grad[pl.ds(r, 1), :] = small[pl.ds(17, 1), pl.ds(r * 128, 128)]
        counts[...] = small[pl.ds(18, 1), pl.ds(0, 16)].astype(jnp.int32)

    out_grad[...] = out_in[...].astype(jnp.float32)
    query_grad[...] = query_in[...].astype(jnp.float32)
    key_grad[...] = side_in[:, :512].astype(jnp.float32)
    value_grad[...] = side_in[:, 512:].astype(jnp.float32)


def finish_part(wide, small, output, input_grad, expert_grads, tiny):
    model_dim = small.shape[1]
    narrow = model_dim // 2
    f32, shape = jnp.float32, jax.ShapeDtypeStruct
    steps = model_dim // ROWS_AT_ONCE
    full = pl.BlockSpec((ROWS_AT_ONCE, model_dim), lambda i: (i, 0))
    part = pl.BlockSpec((ROWS_AT_ONCE, narrow), lambda i: (i, 0))

    def fixed(*dims):
        return pl.BlockSpec(dims, lambda i: (0, 0))

    def rows_of(array):
        return pl.BlockSpec((array.shape[0] // steps, array.shape[1]), lambda i: (i, 0))

    raw = (output, input_grad, *expert_grads, tiny)
    raw_specs = [rows_of(r) for r in raw[:5]] + [fixed(8, 128)]
    return pl.pallas_call(
        finish_kernel,
        grid=(steps,),
        out_shape=[
            shape((model_dim, model_dim), f32),
            shape((model_dim, model_dim), f32),
            shape((model_dim, narrow), f32),
            shape((model_dim, narrow), f32),
            shape((16, model_dim), f32),
            shape((8, 128), f32),
            shape((1, 16), jnp.int32),
            *[shape(r.shape, r.dtype) for r in raw],
        ],
        in_specs=[full] * 3 + [fixed(*small.shape)] + raw_specs,
        out_specs=[full, full, part, part, fixed(16, model_dim), fixed(8, 128), fixed(1, 16)] + raw_specs,
        compiler_params=pltpu.CompilerParams(vmem_limit_bytes=62 << 20),
        name="finish_part",
    )(*wide, small, *raw)


def local(
    tokens,
    segment_ids,
    live_mask,
    routes,
    attn_gain,
    w_query,
    key_weight,
    value_weight,
    w_out,
    moe_gain,
    router,
    w_gate,
    w_up,
    w_down,
    cotangent,
):
    sequence_length = tokens.shape[0]
    model_dim = tokens.shape[1]
    experts_all = router.shape[1]
    query_per_key_head = QUERY_HEADS // KEY_VALUE_HEADS
    score_scale = HEAD_SIZE ** (-0.5)
    if lax.axis_size("ep") == 16 and lax.axis_size("hs") == 2:
        middle, input_grad, out_w_grad, query_w_grad, side_grad, small, tiny, own, again, weighted = expert_part(
            segment_ids,
            live_mask,
            routes,
            attn_gain,
            moe_gain,
            router,
            tokens,
            (w_query, key_weight, value_weight, w_out),
            cotangent,
            w_gate[0],
            w_up[0],
            w_down[0],
        )
        output, wide, small, tiny, expert_grads = sum_part(
            (out_w_grad, query_w_grad, side_grad), small, tiny, again, own, weighted, middle
        )
        (
            out_w_grad,
            query_w_grad,
            key_w_grad,
            value_w_grad,
            router_w_grad,
            moe_gain_grad,
            counts,
            output,
            input_grad,
            *expert_grads,
            tiny,
        ) = finish_part(wide, small, output, input_grad, expert_grads, tiny)
        return (
            output,
            input_grad,
            tiny.reshape(model_dim),
            query_w_grad,
            key_w_grad,
            value_w_grad,
            out_w_grad,
            moe_gain_grad.reshape(model_dim),
            router_w_grad.T,
            *[g[None] for g in expert_grads],
            counts.reshape(experts_all),
        )
    segment = segment_ids[0]
    live_row = live_mask[0]
    inputs = tokens.astype(jnp.float32)
    normed_rows, inverse_one = rms_forward(inputs, attn_gain)
    normed_rows_back = normed_rows.astype(jnp.bfloat16)
    query_pre = jnp.dot(normed_rows_back, w_query, preferred_element_type=jnp.float32).reshape(
        sequence_length, QUERY_HEADS, HEAD_SIZE
    )
    key_before_rotary = jnp.dot(
        normed_rows_back, key_weight, preferred_element_type=jnp.float32
    ).reshape(sequence_length, KEY_VALUE_HEADS, HEAD_SIZE)
    value_b = (
        jnp.dot(normed_rows_back, value_weight, preferred_element_type=jnp.float32)
        .astype(jnp.bfloat16)
        .reshape(sequence_length, KEY_VALUE_HEADS, HEAD_SIZE)
    )
    positions = positions_of(segment)
    cosine_table, sine_table = rotary_tables(positions, HEAD_SIZE)
    query_back_rows = rotary(query_pre, cosine_table, sine_table).astype(jnp.bfloat16)
    key_b = rotary(key_before_rotary, cosine_table, sine_table).astype(jnp.bfloat16)
    indices = jnp.arange(sequence_length)
    allowed = (
        (segment[:, None] == segment[None, :])
        & (indices[None, :] <= indices[:, None])
        & ((live_row[None, :] > 0) | (indices[None, :] == indices[:, None]))
    )
    grouped_rows = query_back_rows.reshape(
        sequence_length, KEY_VALUE_HEADS, query_per_key_head, HEAD_SIZE
    )
    scores = (
        jnp.einsum("qgrd,kgd->grqk", grouped_rows, key_b, preferred_element_type=jnp.float32)
        * score_scale
    )
    scores = jnp.where(allowed, scores, -1e30)
    highest = jnp.max(scores, axis=-1, keepdims=True)
    weights_exp = jnp.exp(scores - highest)
    denominator = jnp.sum(weights_exp, axis=-1, keepdims=True)
    log_total = highest + jnp.log(denominator)
    probabilities = weights_exp / denominator
    mixed = jnp.einsum(
        "grqk,kgd->qgrd",
        probabilities.astype(jnp.bfloat16),
        value_b,
        preferred_element_type=jnp.float32,
    )
    mixed_b = mixed.reshape(sequence_length, QUERY_HEADS * HEAD_SIZE).astype(jnp.bfloat16)
    middle = inputs + jnp.dot(mixed_b, w_out, preferred_element_type=jnp.float32)
    moe_normed, inverse_two = rms_forward(middle, moe_gain)
    moe_in = moe_normed.astype(jnp.bfloat16)
    logits = jnp.dot(moe_in, router, preferred_element_type=jnp.float32)
    route_hot = (routes[:, :, None] == jnp.arange(experts_all)[None, None, :]).astype(jnp.float32)
    chosen = jnp.sum(route_hot * logits[:, None, :], axis=-1)
    route_soft = jax.nn.softmax(chosen, axis=-1)
    live_column = live_row.astype(jnp.float32)[:, None]
    route_gates = route_soft * live_column
    counts_local = jnp.sum(route_hot * live_column[:, :, None], axis=(0, 1))
    dense_gates = jnp.sum(route_hot * route_gates[:, :, None], axis=1)
    upstream_all = lax.all_gather(cotangent, "ep", axis=0, tiled=True)
    gate_all = lax.all_gather(w_gate, "hs", axis=0, tiled=True)
    up_all = lax.all_gather(w_up, "hs", axis=0, tiled=True)
    down_all = lax.all_gather(w_down, "hs", axis=0, tiled=True)
    rows_all = lax.all_gather(moe_in, "ep", axis=0, tiled=True)
    gates_all = lax.all_to_all(
        dense_gates.T.reshape(experts_all, 1, sequence_length), "ep", split_axis=0, concat_axis=1, tiled=True
    ).reshape(-1)
    weighted, back, gate_upstream_all, gate_w_grad, up_w_grad, down_w_grad = expert_pass(
        rows_all, upstream_all, gates_all, gate_all, up_all, down_all
    )
    combined = lax.psum_scatter(weighted, "ep", scatter_dimension=0, tiled=True).astype(jnp.float32)
    expert_input_grad = lax.psum_scatter(back, "ep", scatter_dimension=0, tiled=True).astype(jnp.float32)
    gate_upstream_dense = lax.all_to_all(
        gate_upstream_all.reshape(experts_all, 1, sequence_length), "ep", split_axis=0, concat_axis=1, tiled=True
    ).reshape(experts_all, sequence_length).T
    gate_w_grad = sum_halves(gate_w_grad, 1)[None]
    up_w_grad = sum_halves(up_w_grad, 1)[None]
    down_w_grad = sum_halves(down_w_grad, 0)[None]
    output = (middle + combined).astype(jnp.bfloat16)
    upstream = cotangent.astype(jnp.float32)
    gate_upstream = jnp.sum(route_hot * gate_upstream_dense[:, None, :], axis=-1)
    soft_upstream = gate_upstream * live_column
    chosen_grad = route_soft * (
        soft_upstream - jnp.sum(route_soft * soft_upstream, axis=-1, keepdims=True)
    )
    logit_grad = jnp.sum(route_hot * chosen_grad[:, :, None], axis=1).astype(jnp.bfloat16)
    router_w_grad = jnp.einsum("td,te->de", moe_in, logit_grad, preferred_element_type=jnp.float32)
    moe_in_grad = expert_input_grad + jnp.einsum(
        "te,de->td", logit_grad, router, preferred_element_type=jnp.float32
    )
    middle_norm_grad, moe_gain_grad = rms_backward(middle, inverse_two, moe_gain, moe_in_grad)
    middle_grad = upstream + middle_norm_grad
    attn_grad_b = middle_grad.astype(jnp.bfloat16)
    out_w_grad = jnp.einsum("tm,td->md", mixed_b, attn_grad_b, preferred_element_type=jnp.float32)
    attention_mixed_grad = jnp.einsum(
        "td,md->tm", attn_grad_b, w_out, preferred_element_type=jnp.float32
    ).astype(jnp.bfloat16)
    attention_mixed_grad = attention_mixed_grad.reshape(
        sequence_length, KEY_VALUE_HEADS, query_per_key_head, HEAD_SIZE
    )
    scores_again = (
        jnp.einsum("qgrd,kgd->grqk", grouped_rows, key_b, preferred_element_type=jnp.float32)
        * score_scale
    )
    scores_again = jnp.where(allowed, scores_again, -1e30)
    probs_again = jnp.exp(scores_again - log_total)
    prob_grad = jnp.einsum(
        "qgrd,kgd->grqk", attention_mixed_grad, value_b, preferred_element_type=jnp.float32
    )
    value_per_head_grad = jnp.einsum(
        "grqk,qgrd->kgd",
        probs_again.astype(jnp.bfloat16),
        attention_mixed_grad,
        preferred_element_type=jnp.float32,
    )
    value_per_head_grad = value_per_head_grad.astype(jnp.bfloat16).reshape(
        sequence_length, KEY_VALUE_HEADS * HEAD_SIZE
    )
    row_delta = jnp.sum(probs_again * prob_grad, axis=-1, keepdims=True)
    score_grad = (probs_again * (prob_grad - row_delta)).astype(jnp.bfloat16)
    query_rot_grad = (
        jnp.einsum("grqk,kgd->qgrd", score_grad, key_b, preferred_element_type=jnp.float32)
        * score_scale
    )
    rotated_key_grad = (
        jnp.einsum("grqk,qgrd->kgd", score_grad, grouped_rows, preferred_element_type=jnp.float32)
        * score_scale
    )
    query_head_grad = (
        rotary_backward(
            query_rot_grad.reshape(sequence_length, QUERY_HEADS, HEAD_SIZE),
            cosine_table,
            sine_table,
        )
        .astype(jnp.bfloat16)
        .reshape(sequence_length, QUERY_HEADS * HEAD_SIZE)
    )
    key_head_grad = (
        rotary_backward(rotated_key_grad, cosine_table, sine_table)
        .astype(jnp.bfloat16)
        .reshape(sequence_length, KEY_VALUE_HEADS * HEAD_SIZE)
    )
    query_w_grad = jnp.einsum(
        "td,te->de", normed_rows_back, query_head_grad, preferred_element_type=jnp.float32
    )
    key_w_grad = jnp.einsum(
        "td,te->de", normed_rows_back, key_head_grad, preferred_element_type=jnp.float32
    )
    value_w_grad = jnp.einsum(
        "td,te->de", normed_rows_back, value_per_head_grad, preferred_element_type=jnp.float32
    )
    normed_grad = jnp.einsum(
        "te,de->td", query_head_grad, w_query, preferred_element_type=jnp.float32
    )
    normed_grad = normed_grad + jnp.einsum(
        "te,de->td", key_head_grad, key_weight, preferred_element_type=jnp.float32
    )
    normed_grad = normed_grad + jnp.einsum(
        "te,de->td", value_per_head_grad, value_weight, preferred_element_type=jnp.float32
    )
    input_norm_grad, attn_gain_grad = rms_backward(inputs, inverse_one, attn_gain, normed_grad)
    input_grad = middle_grad + input_norm_grad
    (
        attn_gain_grad,
        query_w_grad,
        key_w_grad,
        value_w_grad,
        out_w_grad,
        moe_gain_grad,
        router_w_grad,
        counts,
    ) = lax.psum(
        (
            attn_gain_grad,
            query_w_grad,
            key_w_grad,
            value_w_grad,
            out_w_grad,
            moe_gain_grad,
            router_w_grad,
            counts_local,
        ),
        ("ep", "hs"),
    )
    return (
        output,
        input_grad,
        attn_gain_grad,
        query_w_grad,
        key_w_grad,
        value_w_grad,
        out_w_grad,
        moe_gain_grad,
        router_w_grad,
        gate_w_grad,
        up_w_grad,
        down_w_grad,
        counts.astype(jnp.int32),
    )


def solution(mesh):
    in_specs = (
        P(("ep", "hs"), None),
        P(("ep", "hs"), None),
        P(("ep", "hs"), None),
        P(("ep", "hs"), None),
        P(),
        P(),
        P(),
        P(),
        P(),
        P(),
        P(),
        P("ep", None, "hs"),
        P("ep", None, "hs"),
        P("ep", "hs", None),
        P(("ep", "hs"), None),
    )
    out_specs = (
        P(("ep", "hs"), None),
        P(("ep", "hs"), None),
        P(),
        P(),
        P(),
        P(),
        P(),
        P(),
        P(),
        P("ep", None, "hs"),
        P("ep", None, "hs"),
        P("ep", "hs", None),
        P(),
    )
    return jax.shard_map(local, mesh=mesh, in_specs=in_specs, out_specs=out_specs, check_vma=False)
```

```python
import jax
import jax.numpy as jnp
import numpy as np
from jax import lax
from jax.experimental import pallas as pl
from jax.experimental.pallas import tpu as pltpu
from jax.sharding import PartitionSpec as P

QUERY_HEADS = 16
KEY_VALUE_HEADS = 8
HEAD_SIZE = 64
TOP = 8


EPSILON = 1e-05


def rms_forward(value_rows, norm_gain):
    inverse = lax.rsqrt(jnp.mean(value_rows * value_rows, axis=-1, keepdims=True) + EPSILON)
    return (value_rows * inverse * norm_gain, inverse)


def rms_backward(value_rows, inverse, norm_gain, upstream):
    scaled = upstream * norm_gain
    gain_grad = jnp.sum(upstream * value_rows * inverse, axis=0)
    input_grad = inverse * (
        scaled
        - value_rows * inverse * inverse * jnp.mean(scaled * value_rows, axis=-1, keepdims=True)
    )
    return (input_grad, gain_grad)


def positions_of(segment):
    before = (segment[None, :] < segment[:, None]).astype(jnp.int32)
    return jnp.arange(segment.shape[-1], dtype=jnp.int32) - jnp.sum(before, axis=1)


def rotary_tables(positions, head_dim):
    half_dim = head_dim // 2
    frequency = 10000.0 ** (-(jnp.arange(half_dim, dtype=jnp.float32) * 2.0) / head_dim)
    angles = positions.astype(jnp.float32)[:, None] * frequency[None, :]
    return (jnp.cos(angles)[:, None, :], jnp.sin(angles)[:, None, :])


def rotary(heads, cosine_table, sine_table):
    half_dim = heads.shape[-1] // 2
    first_half = heads[..., :half_dim]
    second_half = heads[..., half_dim:]
    return jnp.concatenate(
        [
            first_half * cosine_table - second_half * sine_table,
            second_half * cosine_table + first_half * sine_table,
        ],
        axis=-1,
    )


def rotary_backward(grads, cosine_table, sine_table):
    half_dim = grads.shape[-1] // 2
    first_half = grads[..., :half_dim]
    second_half = grads[..., half_dim:]
    return jnp.concatenate(
        [
            first_half * cosine_table + second_half * sine_table,
            second_half * cosine_table - first_half * sine_table,
        ],
        axis=-1,
    )


def to_bf16(value):
    return lax.reduce_precision(value, 8, 7)


def expert_pass(rows, upstream, gates, gate_w, up_w, down_w):
    groups, model_dim, width = gate_w.shape
    gate_all = jnp.concatenate([gate_w[j] for j in range(groups)], axis=1)
    up_all = jnp.concatenate([up_w[j] for j in range(groups)], axis=1)
    down_all = down_w.reshape(groups * width, model_dim)
    gate_pre = jnp.dot(rows, gate_all, preferred_element_type=jnp.float32)
    up_pre = jnp.dot(rows, up_all, preferred_element_type=jnp.float32)
    sigmoid_part = jax.nn.sigmoid(gate_pre)
    activated = gate_pre * sigmoid_part
    hidden = (activated * up_pre).astype(jnp.bfloat16)
    total = jnp.zeros(rows.shape, jnp.float32)
    for j in range(groups):
        total = total + to_bf16(
            jnp.dot(hidden[:, j * width : (j + 1) * width], down_w[j], preferred_element_type=jnp.float32)
        )
    total = to_bf16(total)
    upstream_f = upstream.astype(jnp.float32)
    gate_upstream = jnp.sum(upstream_f * total, axis=-1)
    weighted = (gates[:, None] * total).astype(jnp.bfloat16)
    upstream_e = (gates[:, None] * upstream_f).astype(jnp.bfloat16)
    hidden_grad = jnp.einsum("td,fd->tf", upstream_e, down_all, preferred_element_type=jnp.float32)
    up_pre_grad = (hidden_grad * activated).astype(jnp.bfloat16)
    gate_pre_grad = (
        hidden_grad * up_pre * sigmoid_part * (1.0 + gate_pre * (1.0 - sigmoid_part))
    ).astype(jnp.bfloat16)
    down_grad = jnp.einsum("tf,td->fd", hidden, upstream_e, preferred_element_type=jnp.float32)
    gate_grad = jnp.einsum("td,tf->df", rows, gate_pre_grad, preferred_element_type=jnp.float32)
    up_grad = jnp.einsum("td,tf->df", rows, up_pre_grad, preferred_element_type=jnp.float32)
    back = jnp.zeros(rows.shape, jnp.float32)
    for j in range(groups):
        cut = slice(j * width, (j + 1) * width)
        back = back + to_bf16(
            jnp.einsum("tf,df->td", gate_pre_grad[:, cut], gate_w[j], preferred_element_type=jnp.float32)
            + jnp.einsum("tf,df->td", up_pre_grad[:, cut], up_w[j], preferred_element_type=jnp.float32)
        )
    return (weighted, back.astype(jnp.bfloat16), gate_upstream, gate_grad, up_grad, down_grad)


def sum_halves(grad, dim):
    return lax.psum_scatter(
        grad.astype(jnp.bfloat16), "hs", scatter_dimension=dim, tiled=True
    ).astype(jnp.float32)


MESH = pl.DeviceIdType.MESH
UNIT = 16


def place():
    ep, hs = lax.axis_index("ep"), lax.axis_index("hs")
    return (ep // 4, (ep // 2) % 2, ep % 2, hs)


def device(z, x, c, y):
    return (z * 4 + x * 2 + c, y)


def greet(peers):
    barrier = pltpu.get_barrier_semaphore()
    for peer in peers:
        pl.semaphore_signal(barrier, inc=1, device_id=peer, device_id_type=MESH)
    pl.semaphore_wait(barrier, len(peers))


EDGE_ORDER = (0, 1, 2, 6, 5, 4, 7, 3)
MIDDLE_ORDER = (0, 1, 2, 3, 7, 5, 6, 4)


def turn(value, cosine, sine):
    lane = lax.broadcasted_iota(jnp.int32, value.shape, 1) % HEAD_SIZE
    swapped = jnp.where(
        lane < HEAD_SIZE // 2, pltpu.roll(value, 128 - HEAD_SIZE // 2, 1), pltpu.roll(value, HEAD_SIZE // 2, 1)
    )
    return value * cosine + swapped * sine


def contract(left, right, left_dim, right_dim):
    return lax.dot_general(
        left, right, (((left_dim,), (right_dim,)), ((), ())), preferred_element_type=jnp.float32
    )


def expert_kernel(
    segment,
    live,
    routes,
    rotation,
    attn_gain,
    moe_gain,
    router,
    tokens_in,
    w_query_in,
    w_key_in,
    w_value_in,
    w_out_in,
    upstream_in,
    gate_w,
    up_w,
    down_w,
    middle_rows,
    input_grad,
    out_grad,
    query_grad,
    side_grad,
    small,
    tiny,
    own_out,
    again_out,
    weighted_out,
    normed,
    query,
    key_value,
    mixed,
    back,
    cosine,
    sine,
    bias,
    soft_rows,
    keys,
    values,
    streams,
    gates_in,
    gates,
    slopes,
    slopes_in,
    w_gate,
    w_up,
    w_down,
    sums,
    partial,
    from_sibling,
    from_line,
    staged_x,
    staged_y,
    staged_again,
    returned_x,
    returned_y,
    load_sem,
    head_sem,
    store_sem,
    weighted_sem,
    gather_send,
    gather_recv,
    gate_send,
    gate_recv,
    slope_send,
    slope_recv,
    weight_send,
    weight_recv,
    pair_send,
    pair_recv,
    line_send,
    line_recv,
    grad_send,
    grad_recv,
):
    z, x, c, y = place()
    near, far, last = 1 + z % 2, (2 + 3 * z) % 5, 3 - 3 * (z // 2)
    middle = (z == 1) | (z == 2)
    edge = (z == 0) | (z == 3)
    sibling, beside, across = device(z, x, 1 - c, y), device(z, 1 - x, c, y), device(z, x, c, 1 - y)
    line = [((z + k) % 4, (c + d) % 2) for k in range(4) for d in range(2) if k or d]

    def chip(k):
        half = z // 2
        inner = z + half * (3 - 2 * z)
        spot = k + inner * (1 - 3 * (k // 2) + 2 * (k // 3))
        return spot + half * (3 - 2 * spot)

    def remote(source, target, send, recv, peer):
        return pltpu.make_async_remote_copy(
            src_ref=source, dst_ref=target, send_sem=send, recv_sem=recv, device_id=peer, device_id_type=MESH
        )

    own = pltpu.make_async_copy(upstream_in, streams.at[1, z, c], load_sem.at[0])
    weights_own = [
        pltpu.make_async_copy(ref, held.at[x, y], load_sem.at[3 + a])
        for a, (ref, held) in enumerate(((gate_w, w_gate), (up_w, w_up), (down_w, w_down)))
    ]
    tokens = from_sibling.at[1, 0]
    head_loads = [pltpu.make_async_copy(tokens_in, tokens, head_sem.at[0])]
    for r in range(4):
        rows = pl.ds(r * 256, 256)
        for n, (source, target) in enumerate(
            (
                (w_query_in, partial.at[0, r // 2, r % 2]),
                (w_out_in, partial.at[1, r // 2, r % 2]),
                (w_key_in, from_sibling.at[0, r, :, pl.ds(0, 512)]),
                (w_value_in, from_sibling.at[0, r, :, pl.ds(512, 512)]),
            )
        ):
            head_loads.append(pltpu.make_async_copy(source.at[rows, :], target, head_sem.at[1 + r * 4 + n]))
    for copy in (own, *weights_own, *head_loads):
        copy.start()
    greet([device(a, x, b, y) for a, b in line] + [beside, across])

    def gather(s, block, slot, peer):
        piece = streams.at[s, block, c]
        return remote(piece, piece, gather_send.at[s, slot], gather_recv.at[s, block, c], peer)

    def arrive(s, block, core):
        piece = streams.at[s, block, core]
        pltpu.make_async_copy(piece, piece, gather_recv.at[s, block, core]).wait()

    def gather_own(s):
        gather(s, z, 0, device(near, x, c, y)).start()
        gather(s, z, 2, sibling).start()

        @pl.when(middle)
        def _():
            gather(s, z, 1, device(far, x, c, y)).start()

    own.wait()
    gather_own(1)
    weight_copies = []
    for a, held in enumerate((w_gate, w_up, w_down)):
        weights_own[a].wait()
        for n, peer in enumerate((across, beside)):
            piece = held.at[x, y]
            weight_copies.append(
                remote(piece, piece, weight_send.at[n, a], weight_recv.at[x, y, a], peer)
            )
    for copy in weight_copies:
        copy.start()
    upper, lower = pl.ds(0, 128), pl.ds(128, 128)

    def relay(n, expert, group, peer):
        if n < 2:
            piece = (w_gate, w_up)[n].at[expert, group]
        else:
            piece = w_down.at[expert, group, (upper, lower)[n - 2], :]
        return remote(piece, piece, weight_send.at[2, n], weight_recv.at[expert, group, n], peer)

    def corner_here():
        for n in range(4):
            relay(n, 1 - x, 1 - y, beside).wait_recv()

    def weights_here(expert, group):
        for a, held in enumerate((w_gate, w_up, w_down)):
            piece = held.at[expert, group]
            pltpu.make_async_copy(piece, piece, weight_recv.at[expert, group, a]).wait()

    def zero(u, carry):
        for e in (0, 1):
            for a in range(3):
                sums[e, a, u // 16, pl.ds(pl.multiple_of((u % 16) * 16, 16), 16), :] = jnp.zeros(
                    (16, 1024), jnp.float32
                )
            partial[e, u // 8, (u // 4) % 2, pl.ds(pl.multiple_of((u % 4) * 64, 64), 64), :] = jnp.zeros(
                (64, 1024), jnp.bfloat16
            )
        return carry

    def handle(k, order=(1, 0)):
        block = chip(k)
        for s in order:
            arrive(s, block, c)
            gather(s, block, 4 + k, sibling).start()
            if k != 2:

                @pl.when(middle)
                def _():
                    gather(s, block, 2 + (k + 1) // 2, device(far, x, c, y)).start()

    row_id = lax.broadcasted_iota(jnp.int32, (256, 256), 0)
    lane_id = lax.broadcasted_iota(jnp.int32, (256, 256), 1)
    diagonal = row_id == lane_id
    segment_row = segment[...].astype(jnp.float32)
    segment_column = jnp.sum(jnp.where(diagonal, segment_row, 0.0), axis=1, keepdims=True)
    live_row = live[...].astype(jnp.float32)
    before = jnp.sum(jnp.where(segment_row < segment_column, 1.0, 0.0), axis=1, keepdims=True)
    position = lax.broadcasted_iota(jnp.int32, (256, 128), 0).astype(jnp.float32) - before
    angle = position * rotation[...]
    side = lax.broadcasted_iota(jnp.int32, (256, 128), 1) % HEAD_SIZE < HEAD_SIZE // 2
    cosine[...] = jnp.cos(angle)
    angle_sine = jnp.sin(angle)
    sine[...] = jnp.where(side, -angle_sine, angle_sine)
    allowed = (segment_row == segment_column) & (lane_id <= row_id) & ((live_row > 0.0) | diagonal)
    bias[...] = jnp.where(allowed, 0.0, -1e30)
    for copy in head_loads:
        copy.wait()
    start = tokens[...].astype(jnp.float32)
    inverse = lax.rsqrt(jnp.mean(start * start, axis=1, keepdims=True) + EPSILON)
    normed[...] = (start * inverse * attn_gain[...]).astype(jnp.bfloat16)

    def project(source, weight):
        total = jnp.zeros((256, 1024), jnp.float32)
        for r in range(4):
            total = total + contract(source[:, pl.ds(r * 256, 256)], weight(r), 1, 0)
        return total

    made = project(normed, lambda r: partial[0, r // 2, r % 2])
    for p in range(8):
        columns = pl.ds(p * 128, 128)
        query[:, columns] = turn(made[:, p * 128 : p * 128 + 128], cosine[...], sine[...]).astype(jnp.bfloat16)
    made = project(normed, lambda r: from_sibling[0, r])
    for p in range(4):
        columns = pl.ds(p * 128, 128)
        key_value[:, columns] = turn(made[:, p * 128 : p * 128 + 128], cosine[...], sine[...]).astype(jnp.bfloat16)
    key_value[:, pl.ds(512, 512)] = made[:, 512:].astype(jnp.bfloat16)
    for g in range(8):
        keys[g] = key_value[:, pl.ds(g * 64, 64)]
        values[g] = key_value[:, pl.ds(512 + g * 64, 64)]

    def attend(g, carry):
        columns = pl.ds(pl.multiple_of(g * 128, 128), 128)
        pair = query[:, columns]
        found = []
        for r in (0, 1):
            scores = contract(pair[:, r * 64 : r * 64 + 64], keys[g], 1, 1) * HEAD_SIZE ** (-0.5) + bias[...]
            weights = jnp.exp(scores - jnp.max(scores, axis=1, keepdims=True))
            probs = (weights / jnp.sum(weights, axis=1, keepdims=True)).astype(jnp.bfloat16)
            found.append(contract(probs, values[g], 1, 0))
        mixed[:, columns] = jnp.concatenate(found, axis=1).astype(jnp.bfloat16)
        return carry

    lax.fori_loop(0, 8, attend, 0)

    @pl.when(edge)
    def _():
        gather(1, z, 1, device(far, x, c, y)).start()

    handle(1, (1,))
    mid = start + project(mixed, lambda r: partial[1, r // 2, r % 2])
    middle_rows[...] = mid
    inverse = lax.rsqrt(jnp.mean(mid * mid, axis=1, keepdims=True) + EPSILON)
    streams[0, z, c] = (mid * inverse * moe_gain[...]).astype(jnp.bfloat16)
    gather_own(0)
    logits = contract(router[...], streams[0, z, c], 1, 1)
    expert_id = lax.broadcasted_iota(jnp.int32, (16, 256), 0)
    routed = routes[pl.ds(0, 1), :] == expert_id
    for n in range(1, TOP):
        routed = routed | (routes[pl.ds(n, 1), :] == expert_id)
    logits = jnp.where(routed, logits, -1e30)
    raised = jnp.where(routed, jnp.exp(logits - jnp.max(logits, axis=0, keepdims=True)), 0.0)
    soft = raised / jnp.sum(raised, axis=0, keepdims=True)
    soft_rows[...] = soft
    held_gates = soft * live_row
    for e in range(16):
        gates_in[e // 4, e % 2, pl.ds((e // 2) % 2, 1), :] = held_gates[e : e + 1, :]
    count = jnp.sum(jnp.where(routed, live_row, 0.0), axis=1, keepdims=True)
    square = lax.broadcasted_iota(jnp.int32, (16, 128), 0) == lax.broadcasted_iota(jnp.int32, (16, 128), 1)
    small[...] = jnp.zeros((24, 1024), jnp.float32)
    tiny[pl.ds(8, 8), :] = jnp.zeros((8, 128), jnp.float32)
    tiny[pl.ds(8, 1), :] = jnp.sum(jnp.where(square, count, 0.0), axis=0, keepdims=True)
    gate_copies = [
        remote(
            gates_in.at[a, b], gates.at[z, c], gate_send.at[n], gate_recv.at[z, c], device(a, x, b, y)
        )
        for n, (a, b) in enumerate(line)
    ]
    for copy in gate_copies:
        copy.start()
    gates[z, c] = gates_in[z, c]
    lax.fori_loop(0, 32, zero, 0)

    @pl.when(edge)
    def _():
        gather(0, z, 0, device(near, x, c, y)).wait_send()
        gather(0, z, 1, device(far, x, c, y)).start()

    @pl.when(middle)
    def _():
        handle(2, (1,))
        handle(3, (1,))

    handle(1, (0,))
    for a, b in line:
        pltpu.make_async_copy(gates.at[a, b], gates.at[a, b], gate_recv.at[a, b]).wait()
    weights_here(x, 1 - y)
    weights_here(1 - x, y)
    relays = [relay(n, x, 1 - y, beside) for n in (0, 2)] + [relay(n, 1 - x, y, across) for n in (1, 3)]
    for copy in relays:
        copy.start()

    def compute(expert, block, core):
        diagonal = lax.broadcasted_iota(jnp.int32, (256, 256), 0) == lax.broadcasted_iota(jnp.int32, (256, 256), 1)
        gate_row = gates[block, core, pl.ds(expert, 1), :]
        gate = jnp.sum(jnp.where(diagonal, gate_row, 0.0), axis=1, keepdims=True)
        rows = streams[0, block, core]
        total = jnp.zeros((256, 1024), jnp.float32)
        kept = []
        for j in (0, 1):
            gate_pre = contract(rows, w_gate[expert, j], 1, 0)
            up_pre = contract(rows, w_up[expert, j], 1, 0)
            sigmoid_part = jax.nn.sigmoid(gate_pre)
            activated = gate_pre * sigmoid_part
            hidden = (activated * up_pre).astype(jnp.bfloat16)
            part = contract(hidden, w_down[expert, j], 1, 0)
            total = total + part.astype(jnp.bfloat16).astype(jnp.float32)
            inner = up_pre * sigmoid_part * (1.0 + gate_pre * (1.0 - sigmoid_part))
            kept.append((activated, inner, hidden))
        total = total.astype(jnp.bfloat16).astype(jnp.float32)
        upstream = streams[1, block, core].astype(jnp.float32)
        slope = jnp.sum(upstream * total, axis=1, keepdims=True)
        slopes[block, core, pl.ds(expert, 1), :] = jnp.sum(
            jnp.where(diagonal, slope, 0.0), axis=0, keepdims=True
        )
        weighted = gate * total + partial[1, block, core].astype(jnp.float32)
        partial[1, block, core] = weighted.astype(jnp.bfloat16)
        upstream = (gate * upstream).astype(jnp.bfloat16)
        back = jnp.zeros((256, 1024), jnp.float32)
        for j in (0, 1):
            activated, inner, hidden = kept[j]
            hidden_grad = contract(upstream, w_down[expert, j], 1, 1)
            up_grad = (hidden_grad * activated).astype(jnp.bfloat16)
            gate_grad = (hidden_grad * inner).astype(jnp.bfloat16)
            sums[expert, 0, j] += contract(gate_grad, rows, 0, 0)
            sums[expert, 1, j] += contract(up_grad, rows, 0, 0)
            sums[expert, 2, j] += contract(hidden, upstream, 0, 0)
            step = contract(gate_grad, w_gate[expert, j], 1, 1) + contract(up_grad, w_up[expert, j], 1, 1)
            back = back + step.astype(jnp.bfloat16).astype(jnp.float32)
        back = back + partial[0, block, core].astype(jnp.float32)
        partial[0, block, core] = back.astype(jnp.bfloat16)

    def grad_copy(n, source, target, peer):
        return remote(source, target, grad_send.at[n], grad_recv.at[n], peer)

    def pair_copy(s, block):
        return remote(
            partial.at[s, block, 1 - c],
            from_sibling.at[s, block],
            pair_send.at[s, block],
            pair_recv.at[s, block],
            sibling,
        )

    def line_copy(s, block, slot, peer):
        return remote(
            partial.at[s, block, c],
            from_line.at[s, slot],
            line_send.at[s, block],
            line_recv.at[s, slot],
            device(peer, x, c, y),
        )

    def line_wait(s, slot):
        piece = from_line.at[s, slot]
        pltpu.make_async_copy(piece, piece, line_recv.at[s, slot]).wait()

    def add_to(s, block, ref):
        def body(u, carry):
            at = pl.ds(pl.multiple_of(u * 32, 32), 32)
            value = partial[s, block, c, at, :].astype(jnp.float32) + ref[at, :].astype(jnp.float32)
            partial[s, block, c, at, :] = value.astype(jnp.bfloat16)
            return carry

        lax.fori_loop(0, 8, body, 0)

    at_edge = (z * z - 3 * z + 2) // 2
    orders = [sum(code << (3 * t) for t, code in enumerate(codes)) for codes in (EDGE_ORDER, MIDDLE_ORDER)]
    order = at_edge * orders[0] + (1 - at_edge) * orders[1]

    def step(i, carry):
        t = i // 2
        code = lax.shift_right_logical(order, 3 * t) % 8
        again = at_edge * ((t // 3) % 2 + t // 7) + (1 - at_edge) * (t // 4)
        k = code % 4
        expert = x + (code // 4) * (1 - 2 * x)
        block, core = chip(k), (c + i + again) % 2

        @pl.when((i == 2) & middle)
        def _():
            handle(2, (0,))

        @pl.when((i == 4) & middle)
        def _():
            handle(3, (0,))

        @pl.when((i == 4) & edge)
        def _():
            handle(2)

        @pl.when((i == 12) & edge)
        def _():
            handle(3)

        @pl.when((i == 8) & middle | (i == 6) & edge)
        def _():
            corner_here()

        @pl.when((i % 2 == 1) & (again == 0))
        def _():
            for s in (0, 1):
                arrive(s, block, 1 - c)

        compute(expert, block, core)

        @pl.when((i % 2 == 0) & (again == 1))
        def _():
            for s in (0, 1):
                pair_copy(s, block).start()

        @pl.when((i % 2 == 1) & (again == 1))
        def _():
            for s in (0, 1):
                pair_copy(s, block).wait_recv()
                add_to(s, block, from_sibling.at[s, block])

            @pl.when(edge & (k == 2))
            def _():
                line_copy(0, block, 2, near).start()

            @pl.when(edge & (k == 1))
            def _():
                line_copy(0, block, 1, near).start()

            @pl.when(edge & (k == 3))
            def _():
                line_copy(0, block, 2, last).start()

            @pl.when(middle & (k == 3))
            def _():
                line_copy(0, block, 1, last).start()

            @pl.when(middle & (k == 2))
            def _():
                line_copy(0, block, 0, far).start()

        return carry

    lax.fori_loop(0, 16, step, 0)
    low, high = pl.ds(0, 512), pl.ds(512, 512)

    def each(body):
        def rows_of(u, carry):
            at = pl.ds(pl.multiple_of(u * 32, 32), 32)
            for a in range(3):
                body(a, at)
            return carry

        lax.fori_loop(0, 8, rows_of, 0)

    def stage_low(a, at):
        for j in (0, 1):
            staged_x[j, a, at, :] = sums[1 - x, a, j, at, low].astype(jnp.bfloat16)

    def stage_high(a, at):
        staged_y[0, a, at, :] = sums[1 - x, a, 1 - y, at, high].astype(jnp.bfloat16)
        staged_y[1, a, at, :] = sums[x, a, 1 - y, at, high].astype(jnp.bfloat16)

    each(stage_low)
    grad_copy(0, staged_x, returned_x, beside).start()
    each(stage_high)
    grad_copy(1, staged_y, returned_y, across).start()
    slope_copies = [
        remote(
            slopes.at[a, b], slopes_in.at[z, c], slope_send.at[n], slope_recv.at[z, c], device(a, x, b, y)
        )
        for n, (a, b) in enumerate(line)
    ]
    for copy in slope_copies:
        copy.start()
    slopes_in[z, c] = slopes[z, c]


    weighted_stores = [
        pltpu.make_async_copy(partial.at[1, k, c], weighted_out.at[k], weighted_sem.at[k]) for k in range(4)
    ]
    for copy in weighted_stores:
        copy.start()

    @pl.when(middle)
    def _():
        line_wait(0, 2)
        add_to(0, near, from_line.at[0, 2])
        line_copy(0, near, 0, near).start()

    gather(1, z, 0, device(near, x, c, y)).wait_send()

    @pl.when(middle)
    def _():
        gather(0, z, 0, device(near, x, c, y)).wait_send()

    for s in (0, 1):
        gather(s, z, 1, device(far, x, c, y)).wait_send()
        gather(s, z, 2, sibling).wait_send()
        for k in (1, 2, 3):
            gather(s, chip(k), 4 + k, sibling).wait_send()

        @pl.when(middle)
        def _():
            for k in (1, 3):
                gather(s, chip(k), 2 + (k + 1) // 2, device(far, x, c, y)).wait_send()

    for copy in (*gate_copies, *weight_copies, *relays):
        copy.wait_send()

    def query_weight(r):
        return streams.at[0, chip(1 + r // 2), r % 2]

    reloads = []
    for r in range(4):
        rows = pl.ds(r * 256, 256)
        for n, (source, target) in enumerate(
            (
                (w_out_in, from_sibling.at[1, r]),
                (w_query_in, query_weight(r)),
                (w_key_in, from_sibling.at[0, r, :, pl.ds(0, 512)]),
                (w_value_in, from_sibling.at[0, r, :, pl.ds(512, 512)]),
            )
        ):
            reloads.append(pltpu.make_async_copy(source.at[rows, :], target, head_sem.at[1 + r * 4 + n]))
    for copy in reloads:
        copy.start()

    def combined(s, slots, body_of):
        for slot in slots:
            line_wait(s, slot)

        def body(u, carry):
            at = pl.ds(pl.multiple_of(u * 32, 32), 32)
            value = partial[s, z, c, at, :].astype(jnp.float32)
            for slot in slots:
                value = value + from_line[s, slot, at, :].astype(jnp.float32)
            body_of(at, value)
            return carry

        lax.fori_loop(0, 8, body, 0)

    def finish(s, body_of):
        @pl.when(middle)
        def _():
            combined(s, (0, 1), body_of)

        @pl.when(edge)
        def _():
            combined(s, (0, 1, 2), body_of)

    def store_back(at, value):
        back[at, :] = value

    finish(0, store_back)
    for a, b in line:
        pltpu.make_async_copy(slopes_in.at[a, b], slopes_in.at[a, b], slope_recv.at[a, b]).wait()
    upstream = streams[1, z, c].astype(jnp.float32)
    slope_rows = jnp.concatenate([slopes_in[e // 4, e % 2, pl.ds((e // 2) % 2, 1), :] for e in range(16)], axis=0)
    soft_slope = slope_rows * live[...].astype(jnp.float32)
    soft_t = soft_rows[...]
    dlogits = soft_t * (soft_slope - jnp.sum(soft_t * soft_slope, axis=0, keepdims=True))
    dlogits = dlogits.astype(jnp.bfloat16)
    small[pl.ds(0, 16), :] = contract(dlogits, streams[0, z, c], 1, 0)
    dmoe_in = back[...] + contract(dlogits, router[...], 0, 0)
    mid = middle_rows[...]
    inverse = lax.rsqrt(jnp.mean(mid * mid, axis=1, keepdims=True) + EPSILON)
    small[pl.ds(17, 1), :] = jnp.sum(dmoe_in * mid * inverse, axis=0, keepdims=True)
    scaled = dmoe_in * moe_gain[...]
    dmiddle = upstream + inverse * (
        scaled - mid * inverse * inverse * jnp.mean(scaled * mid, axis=1, keepdims=True)
    )
    input_grad[...] = dmiddle
    dattn = dmiddle.astype(jnp.bfloat16)
    outgoing = []

    def send_out(source, target):
        copy = pltpu.make_async_copy(source, target, store_sem.at[len(outgoing)])
        copy.start()
        outgoing.append(copy)

    def column_grad(left, right, held, target):
        for r in range(4):
            rows = contract(left[:, pl.ds(r * 256, 256)], right, 0, 0).astype(jnp.bfloat16)
            for n in range(4):
                held[n // 2, n % 2, pl.ds(r * 256, 256), :] = rows[:, n * 256 : n * 256 + 256]
        for n in range(4):
            send_out(held.at[n // 2, n % 2], target.at[:, pl.ds(n * 256, 256)])

    column_grad(mixed, dattn, w_gate, out_grad)
    for copy in reloads:
        copy.wait()
    mixed_slope, query_slope, side_slope = w_down.at[0, 0], w_down.at[0, 1], w_down.at[1, 0]
    for r in range(4):
        mixed_slope[:, pl.ds(r * 256, 256)] = contract(dattn, from_sibling[1, r], 1, 1).astype(jnp.bfloat16)
    scale = HEAD_SIZE ** (-0.5)

    def attend_back(p, carry):
        wide = pl.ds(pl.multiple_of(p * 256, 256), 256)
        queries, slopes_here = query[:, wide], mixed_slope[:, wide]
        key_slopes, value_slopes, query_slopes = [], [], []
        for n in (0, 1):
            key_g, value_g = keys[2 * p + n], values[2 * p + n]
            key_slope = jnp.zeros((256, 64), jnp.float32)
            value_slope = jnp.zeros((256, 64), jnp.float32)
            for r in (0, 1):
                cut = slice(n * 128 + r * 64, n * 128 + r * 64 + 64)
                query_h, slope_h = queries[:, cut], slopes_here[:, cut]
                scores = contract(query_h, key_g, 1, 1) * scale + bias[...]
                weights = jnp.exp(scores - jnp.max(scores, axis=1, keepdims=True))
                probs = weights / jnp.sum(weights, axis=1, keepdims=True)
                prob_slope = contract(slope_h, value_g, 1, 1)
                value_slope = value_slope + contract(probs.astype(jnp.bfloat16), slope_h, 0, 0)
                delta = jnp.sum(probs * prob_slope, axis=1, keepdims=True)
                score_slope = (probs * (prob_slope - delta)).astype(jnp.bfloat16)
                query_slopes.append(contract(score_slope, key_g, 1, 0) * scale)
                key_slope = key_slope + contract(score_slope, query_h, 0, 0) * scale
            key_slopes.append(key_slope)
            value_slopes.append(value_slope)
        for n in (0, 1):
            pair = turn(jnp.concatenate(query_slopes[2 * n : 2 * n + 2], axis=1), cosine[...], -sine[...])
            query_slope[:, pl.ds(pl.multiple_of(p * 256 + n * 128, 128), 128)] = pair.astype(jnp.bfloat16)
        pair = turn(jnp.concatenate(key_slopes, axis=1), cosine[...], -sine[...])
        side_slope[:, pl.ds(pl.multiple_of(p * 128, 128), 128)] = pair.astype(jnp.bfloat16)
        pair = jnp.concatenate(value_slopes, axis=1)
        side_slope[:, pl.ds(pl.multiple_of(512 + p * 128, 128), 128)] = pair.astype(jnp.bfloat16)
        return carry

    lax.fori_loop(0, 4, attend_back, 0)

    column_grad(normed, query_slope[...], w_up, query_grad)
    for r in range(4):
        rows = contract(normed[:, pl.ds(r * 256, 256)], side_slope[...], 0, 0).astype(jnp.bfloat16)
        streams[1, chip(1 + r // 2), r % 2] = rows
        send_out(streams.at[1, chip(1 + r // 2), r % 2], side_grad.at[pl.ds(r * 256, 256), :])
    dnormed = jnp.concatenate(
        [
            contract(query_slope[...], query_weight(r)[...], 1, 1)
            + contract(side_slope[...], from_sibling[0, r], 1, 1)
            for r in range(4)
        ],
        axis=1,
    )
    tokens_again = pltpu.make_async_copy(tokens_in, w_down.at[1, 1], head_sem.at[0])
    tokens_again.start()
    tokens_again.wait()
    start = w_down[1, 1].astype(jnp.float32)
    inverse = lax.rsqrt(jnp.mean(start * start, axis=1, keepdims=True) + EPSILON)
    gain_slope = jnp.sum(dnormed * start * inverse, axis=0, keepdims=True)
    for r in range(8):
        tiny[pl.ds(r, 1), :] = gain_slope[:, r * 128 : r * 128 + 128]
    scaled = dnormed * attn_gain[...]
    input_grad[...] += inverse * (
        scaled - start * inverse * inverse * jnp.mean(scaled * start, axis=1, keepdims=True)
    )

    grad_copy(0, staged_x, returned_x, beside).wait_recv()
    grad_copy(1, staged_y, returned_y, across).wait_recv()

    def stage_again(a, at):
        value = sums[x, a, 1 - y, at, low] + returned_x[1 - y, a, at, :].astype(jnp.float32)
        staged_again[0, a, at, :] = value.astype(jnp.bfloat16)
        value = sums[1 - x, a, y, at, high] + returned_y[0, a, at, :].astype(jnp.float32)
        staged_again[1, a, at, :] = value.astype(jnp.bfloat16)
        sums[x, a, y, at, low] += returned_x[y, a, at, :].astype(jnp.float32)
        sums[x, a, y, at, high] += returned_y[1, a, at, :].astype(jnp.float32)

    each(stage_again)
    send_out(staged_again, again_out)
    for a in range(3):
        send_out(sums.at[x, a, y], own_out.at[a])

    for k in (1, 2, 3):
        line_copy(0, chip(k), 0, near).wait_send()
    for s in (0, 1):
        for k in range(4):
            pair_copy(s, chip(k)).wait_send()
    for copy in slope_copies:
        copy.wait_send()
    grad_copy(0, staged_x, returned_x, beside).wait_send()
    grad_copy(1, staged_y, returned_y, across).wait_send()
    for copy in (*outgoing, *weighted_stores):
        copy.wait()


def expert_part(
    segment_ids,
    live_mask,
    routes,
    attn_gain,
    moe_gain,
    router,
    tokens,
    attention_weights,
    upstream,
    gate_w,
    up_w,
    down_w,
):
    count, model_dim = tokens.shape
    width = gate_w.shape[1]
    vmem, anywhere = pl.BlockSpec(memory_space=pltpu.VMEM), pl.BlockSpec(memory_space=pl.ANY)
    f32, bf16, dma, shape = jnp.float32, jnp.bfloat16, pltpu.SemaphoreType.DMA, jax.ShapeDtypeStruct
    half = HEAD_SIZE // 2
    frequency = np.float32(10000.0) ** (-(np.arange(half, dtype=np.float32) * np.float32(2.0)) / np.float32(HEAD_SIZE))
    rotation = jnp.asarray(np.tile(frequency.astype(np.float32), 4)[None])
    block = (count, model_dim)
    return pl.pallas_call(
        expert_kernel,
        out_shape=[
            shape(block, f32),
            shape(block, f32),
            shape((model_dim, model_dim), bf16),
            shape((model_dim, model_dim), bf16),
            shape((model_dim, model_dim), bf16),
            shape((24, model_dim), f32),
            shape((16, 128), f32),
            shape((3, width, model_dim), f32),
            shape((2, 3, width, model_dim // 2), bf16),
            shape((4, *block), bf16),
        ],
        in_specs=[vmem] * 7 + [anywhere] * 9,
        out_specs=[vmem] * 2 + [anywhere] * 3 + [vmem] * 2 + [anywhere] * 3,
        scratch_shapes=[
            *[pltpu.VMEM(block, bf16)] * 4,
            pltpu.VMEM(block, f32),
            *[pltpu.VMEM((count, 128), f32)] * 2,
            pltpu.VMEM((count, count), f32),
            pltpu.VMEM((16, count), f32),
            pltpu.VMEM((8, count, HEAD_SIZE), bf16),
            pltpu.VMEM((8, count, HEAD_SIZE), bf16),
            pltpu.VMEM((2, 4, 2, *block), bf16),
            *[pltpu.VMEM((4, 2, 8, count), f32)] * 4,
            pltpu.VMEM((2, 2, model_dim, width), bf16),
            pltpu.VMEM((2, 2, model_dim, width), bf16),
            pltpu.VMEM((2, 2, width, model_dim), bf16),
            pltpu.VMEM((2, 3, 2, width, model_dim), f32),
            pltpu.VMEM((2, 4, 2, *block), bf16),
            pltpu.VMEM((2, 4, *block), bf16),
            pltpu.VMEM((1, 3, *block), bf16),
            *[pltpu.VMEM((2, 3, width, model_dim // 2), bf16)] * 5,
            dma((6,)),
            dma((17,)),
            dma((16,)),
            dma((4,)),
            dma((2, 8)),
            dma((2, 4, 2)),
            dma((7,)),
            dma((4, 2)),
            dma((7,)),
            dma((4, 2)),
            dma((3, 4)),
            dma((2, 2, 4)),
            dma((2, 4)),
            dma((2, 4)),
            dma((2, 4)),
            dma((2, 4)),
            dma((2,)),
            dma((2,)),
        ],
        compiler_params=pltpu.CompilerParams(
            collective_id=1, has_side_effects=True, vmem_limit_bytes=63 << 20
        ),
        name="expert_part",
    )(
        segment_ids,
        live_mask,
        routes.T,
        rotation,
        attn_gain[None],
        moe_gain[None],
        router.T,
        tokens,
        *attention_weights,
        upstream,
        gate_w,
        up_w,
        down_w,
    )


ROWS_AT_ONCE = 256
AGAIN_AT = (0, 4, 8)
COMBINE_AT = 6
SMALL_AT = 9


def sum_kernel(
    small,
    tiny,
    out_in,
    query_in,
    side_in,
    again_in,
    own_in,
    weighted_in,
    middle_rows,
    output,
    out_sum,
    query_sum,
    side_sum,
    small_out,
    tiny_out,
    gate_grad,
    up_grad,
    down_grad,
    again,
    returned_again,
    own,
    weighted,
    from_line,
    *rest,
):
    count = 6
    grads, halves, totals, fulls, firsts, seconds, lines = [rest[n * count : (n + 1) * count] for n in range(7)]
    small_sum, small_in, tiny_sum, tiny_in, send, recv, small_send, small_recv, local_sem, load_sem, again_send, again_recv, line_send, line_recv = rest[7 * count :]
    windows = [(ref, pl.ds(n * 512, 512)) for ref in range(3) for n in (0, 1)]
    outs = [(out_sum, query_sum, side_sum)[ref].at[:, :, columns] for ref, columns in windows]
    z, x, c, y = place()
    sibling, beside, across = device(z, x, 1 - c, y), device(z, 1 - x, c, y), device(z, x, c, 1 - y)
    along = [device((z + k) % 4, x, c, y) for k in (1, 2, 3)]
    loads = [
        pltpu.make_async_copy((out_in, query_in, side_in)[ref].at[:, :, columns], grads[i], load_sem.at[i])
        for i, (ref, columns) in enumerate(windows)
    ]
    loads.append(pltpu.make_async_copy(again_in, again, load_sem.at[6]))
    loads.append(pltpu.make_async_copy(own_in, own, load_sem.at[7]))
    loads.append(pltpu.make_async_copy(weighted_in, weighted, load_sem.at[8]))
    for copy in loads:
        copy.start()
    small_sum[0] = small[...].astype(jnp.bfloat16)
    tiny_sum[0] = tiny[...]
    greet([sibling, beside, across] + along)
    again_copies = [
        pltpu.make_async_remote_copy(
            src_ref=again.at[n, a],
            dst_ref=returned_again.at[n, a],
            send_sem=again_send.at[n, a],
            recv_sem=again_recv.at[n, a],
            device_id=peer,
            device_id_type=MESH,
        )
        for a in range(3)
        for n, peer in enumerate((across, beside))
    ]
    near, far, last = 1 + z % 2, (2 + 3 * z) % 5, 3 - 3 * (z // 2)
    middle, edge = (z == 1) | (z == 2), (z == 0) | (z == 3)

    def line_copy(block, piece, slot, peer):
        rows = pl.ds(piece * 64, 64)
        return pltpu.make_async_remote_copy(
            src_ref=weighted.at[block, rows, :],
            dst_ref=from_line.at[slot, rows, :],
            send_sem=line_send.at[block, piece],
            recv_sem=line_recv.at[slot, piece],
            device_id=device(peer, x, c, y),
            device_id_type=MESH,
        )

    def line_wait(slot, piece):
        part = from_line.at[slot, pl.ds(piece * 64, 64), :]
        pltpu.make_async_copy(part, part, line_recv.at[slot, piece]).wait()

    def line_stage(tick):
        @pl.when(edge)
        def _():
            for block, slot, peer, first in ((far, 2, near, 0), (near, 1, near, 4), (last, 2, last, 4)):
                if 0 <= tick - first < 4:
                    line_copy(block, tick - first, slot, peer).start()

        @pl.when(middle)
        def _():
            for block, slot, peer, first in ((last, 1, last, 0), (far, 0, far, 1)):
                if 0 <= tick - first < 4:
                    line_copy(block, tick - first, slot, peer).start()
            if 0 <= tick - COMBINE_AT < 4:
                piece = tick - COMBINE_AT
                line_wait(2, piece)
                for r in (0, 32):
                    at = pl.ds(piece * 64 + r, 32)
                    value = weighted[near, at, :].astype(jnp.float32) + from_line[2, at, :].astype(jnp.float32)
                    weighted[near, at, :] = value.astype(jnp.bfloat16)
                line_copy(near, piece, 0, near).start()

    bits = ((x, y), (y, x))
    partners = ((beside, across), (across, beside))

    def push(i, slot, source, target, peer):
        copy = pltpu.make_async_remote_copy(
            src_ref=source,
            dst_ref=target,
            send_sem=send.at[i, slot],
            recv_sem=recv.at[i, slot],
            device_id=peer,
            device_id_type=MESH,
        )
        copy.start()
        return copy

    def combine(i, target, start, length, terms):
        def body(u, carry):
            value = totals[i][start + u].astype(jnp.float32)
            for ref, base in terms:
                value = value + ref[base + u].astype(jnp.float32)
            target[0][target[1] + u] = value.astype(jnp.bfloat16)
            return carry

        lax.fori_loop(0, length, body, 0)

    copies = {}

    def stage(i, step):
        if step == 0:
            copies[i, 0] = [
                push(i, 0, grads[i].at[pl.ds((1 - c) * 32, 32)], halves[i], sibling)
            ]
        if step == 1:
            copies[i, 0][0].wait_recv()

            def body(u, carry):
                value = grads[i][c * 32 + u].astype(jnp.float32) + halves[i][u].astype(jnp.float32)
                totals[i][u] = value.astype(jnp.bfloat16)
                return carry

            lax.fori_loop(0, 32, body, 0)
            copies[i, 1] = [
                push(
                    i,
                    1 + part,
                    totals[i].at[pl.ds(part * 16 + (1 - bits[part][0]) * 8, 8)],
                    firsts[i].at[part],
                    partners[part][0],
                )
                for part in (0, 1)
            ]
        if step == 2:
            copies[i, 2] = []
            for part in (0, 1):
                copies[i, 1][part].wait_recv()
                base = part * 16 + bits[part][0] * 8
                combine(i, (totals[i], base), base, 8, [(firsts[i].at[part], 0)])
                copies[i, 2].append(
                    push(
                        i,
                        3 + part,
                        totals[i].at[pl.ds(base + (1 - bits[part][1]) * 4, 4)],
                        seconds[i].at[part],
                        partners[part][1],
                    )
                )
        if step == 3:
            copies[i, 3] = []
            for part in (0, 1):
                copies[i, 2][part].wait_recv()
                base = part * 16 + bits[part][0] * 8 + bits[part][1] * 4
                combine(i, (totals[i], base), base, 4, [(seconds[i].at[part], 0)])
                for k in (1, 2, 3):
                    copies[i, 3].append(
                        push(
                            i,
                            5 + part * 3 + k - 1,
                            totals[i].at[base + (z + k) % 4],
                            lines[i].at[part, k - 1],
                            along[k - 1],
                        )
                    )
        if step == 4:
            copies[i, 4] = []
            for part in (0, 1):
                for k in (1, 2, 3):
                    copies[i, 3][part * 3 + k - 1].wait_recv()
                base = part * 16 + bits[part][0] * 8 + bits[part][1] * 4
                combine(
                    i, (fulls[i], c * 32 + base + z), base + z, 1, [(lines[i].at[part], k) for k in (0, 1, 2)]
                )
                for k in (1, 2, 3):
                    piece = fulls[i].at[c * 32 + base + z]
                    copies[i, 4].append(push(i, 11 + part * 3 + k - 1, piece, piece, along[k - 1]))
        if step == 5:
            copies[i, 5] = []
            for part in (0, 1):
                for k in (1, 2, 3):
                    copies[i, 4][part * 3 + k - 1].wait_recv()
                piece = fulls[i].at[pl.ds(c * 32 + part * 16 + bits[part][0] * 8 + bits[part][1] * 4, 4)]
                copies[i, 5].append(push(i, 17 + part, piece, piece, partners[part][1]))
        if step == 6:
            copies[i, 6] = []
            for part in (0, 1):
                copies[i, 5][part].wait_recv()
                piece = fulls[i].at[pl.ds(c * 32 + part * 16 + bits[part][0] * 8, 8)]
                copies[i, 6].append(push(i, 19 + part, piece, piece, partners[part][0]))
        if step == 7:
            for part in (0, 1):
                copies[i, 6][part].wait_recv()
            piece = fulls[i].at[pl.ds(c * 32, 32)]
            copies[i, 7] = [push(i, 21, piece, piece, sibling)]
        if step == 8:
            copies[i, 7][0].wait_recv()
            done = pltpu.make_async_copy(fulls[i], outs[i], local_sem.at[i])
            done.start()
            copies[i, 8] = [done]

    def small_stage(n, step):
        total, arrived = (small_sum, tiny_sum)[n], (small_in, tiny_in)[n]

        def small_push(slot, peer, source, target):
            copy = pltpu.make_async_remote_copy(
                src_ref=total.at[source],
                dst_ref=arrived.at[target],
                send_sem=small_send.at[n, slot],
                recv_sem=small_recv.at[n, slot],
                device_id=peer,
                device_id_type=MESH,
            )
            copy.start()
            copies.setdefault((n, "s", step), []).append(copy)

        if step == 0:
            small_push(0, sibling, 0, 0)
        if step in (1, 2, 3):
            copies[n, "s", step - 1][0].wait_recv()
            value = total[step - 1].astype(jnp.float32) + arrived[step - 1].astype(jnp.float32)
            total[step] = value.astype(total.dtype)
        if step in (1, 2):
            small_push(step, (beside, across)[step - 1], step, step)
        if step == 3:
            for k in (1, 2, 3):
                small_push(2 + k, along[k - 1], 3, 3 + z)
            arrived[3 + z] = total[3]
        if step == 4:
            for copy in copies[n, "s", 3]:
                copy.wait_recv()
            parts = [arrived[3 + k].astype(jnp.float32) for k in range(4)]
            (small_out, tiny_out)[n][...] = (parts[0] + parts[1]) + (parts[2] + parts[3])

    for tick in range(count + 8):
        for i in range(count):
            if tick == i:
                loads[i].wait()
            if 0 <= tick - i <= 8:
                stage(i, tick - i)
        if tick == 0:
            loads[6].wait()
            loads[8].wait()
        if tick in AGAIN_AT:
            part = 2 * AGAIN_AT.index(tick)
            again_copies[part].start()
            again_copies[part + 1].start()
        line_stage(tick)
        if SMALL_AT <= tick <= SMALL_AT + 4:
            small_stage(0, tick - SMALL_AT)
            small_stage(1, tick - SMALL_AT)
    loads[7].wait()
    for copy in again_copies:
        copy.wait_recv()
    for a, target in enumerate((gate_grad, up_grad, down_grad)):
        for n in (0, 1):
            columns = pl.ds(n * 512, 512)
            summed = own[a, :, columns] + returned_again[n, a].astype(jnp.float32)
            if a < 2:
                target[columns, :] = summed.T
            else:
                target[:, columns] = summed

    def finish(slots):
        for slot in slots:
            for piece in range(4):
                line_wait(slot, piece)

        def body(u, carry):
            at = pl.ds(pl.multiple_of(u * 32, 32), 32)
            value = weighted[z, at, :].astype(jnp.float32)
            for slot in slots:
                value = value + from_line[slot, at, :].astype(jnp.float32)
            output[at, :] = (middle_rows[at, :] + value).astype(jnp.bfloat16)
            return carry

        lax.fori_loop(0, 8, body, 0)

    @pl.when(middle)
    def _():
        finish((0, 1))

    @pl.when(edge)
    def _():
        finish((0, 1, 2))

    for block in (near, far, last):
        for piece in range(4):
            line_copy(block, piece, 0, near).wait_send()
    for key_of, made in copies.items():
        for copy in made:
            if key_of[1] == 8:
                copy.wait()
            else:
                copy.wait_send()
    for copy in again_copies:
        copy.wait_send()


def sum_part(wide, small, tiny, again, own, weighted, middle):
    model_dim = small.shape[1]
    vmem, anywhere = pl.BlockSpec(memory_space=pltpu.VMEM), pl.BlockSpec(memory_space=pl.ANY)
    f32, bf16, dma = jnp.float32, jnp.bfloat16, pltpu.SemaphoreType.DMA
    leads = ((64,), (32,), (32,), (64,), (2, 8), (2, 4), (2, 3))
    shape = jax.ShapeDtypeStruct
    width = own.shape[1]
    units = [g.reshape(64, UNIT, model_dim) for g in wide]
    out = pl.pallas_call(
        sum_kernel,
        out_shape=[
            shape(middle.shape, bf16),
            *[shape(u.shape, bf16) for u in units],
            shape(small.shape, f32),
            shape(tiny.shape, f32),
            shape((model_dim, width), f32),
            shape((model_dim, width), f32),
            shape((width, model_dim), f32),
        ],
        in_specs=[vmem] * 2 + [anywhere] * 6 + [vmem],
        out_specs=[vmem] + [anywhere] * 3 + [vmem] * 5,
        scratch_shapes=[
            pltpu.VMEM(again.shape, bf16),
            pltpu.VMEM(again.shape, bf16),
            pltpu.VMEM(own.shape, f32),
            pltpu.VMEM(weighted.shape, bf16),
            pltpu.VMEM((3, *middle.shape), bf16),
            *[pltpu.VMEM((*lead, UNIT, 512), bf16) for lead in leads for _ in range(6)],
            pltpu.VMEM((4, *small.shape), bf16),
            pltpu.VMEM((7, *small.shape), bf16),
            pltpu.VMEM((4, *tiny.shape), f32),
            pltpu.VMEM((7, *tiny.shape), f32),
            dma((6, 22)),
            dma((6, 22)),
            dma((2, 6)),
            dma((2, 6)),
            dma((6,)),
            dma((9,)),
            dma((2, 3)),
            dma((2, 3)),
            dma((4, 4)),
            dma((3, 4)),
        ],
        compiler_params=pltpu.CompilerParams(
            collective_id=0, has_side_effects=True, vmem_limit_bytes=60 << 20
        ),
        name="sum_part",
    )(small, tiny, *units, again, own, weighted, middle)
    return out[0], [o.reshape(model_dim, model_dim) for o in out[1:4]], out[4], out[5], out[6:9]


def finish_kernel(
    out_in,
    query_in,
    side_in,
    small,
    output_in,
    input_grad_in,
    gate_in,
    up_in,
    down_in,
    tiny_in,
    out_grad,
    query_grad,
    key_grad,
    value_grad,
    router_grad,
    gain_grad,
    counts,
    output,
    input_grad,
    gate_grad,
    up_grad,
    down_grad,
    tiny,
):
    for source, target in (
        (input_grad_in, input_grad),
        (gate_in, gate_grad),
        (up_in, up_grad),
        (down_in, down_grad),
        (output_in, output),
    ):
        target[...] = source[...]

    @pl.when(pl.program_id(0) == 0)
    def _():
        tiny[...] = tiny_in[pl.ds(0, 8), :]
        router_grad[...] = small[pl.ds(0, 16), :]
        for r in range(8):
            gain_grad[pl.ds(r, 1), :] = small[pl.ds(17, 1), pl.ds(r * 128, 128)]
        counts[...] = tiny_in[pl.ds(8, 1), pl.ds(0, 16)].astype(jnp.int32)

    out_grad[...] = out_in[...].astype(jnp.float32)
    query_grad[...] = query_in[...].astype(jnp.float32)
    key_grad[...] = side_in[:, :512].astype(jnp.float32)
    value_grad[...] = side_in[:, 512:].astype(jnp.float32)


def finish_part(wide, small, output, input_grad, expert_grads, tiny):
    model_dim = small.shape[1]
    narrow = model_dim // 2
    f32, shape = jnp.float32, jax.ShapeDtypeStruct
    steps = model_dim // ROWS_AT_ONCE
    full = pl.BlockSpec((ROWS_AT_ONCE, model_dim), lambda i: (i, 0))
    part = pl.BlockSpec((ROWS_AT_ONCE, narrow), lambda i: (i, 0))

    def fixed(*dims):
        return pl.BlockSpec(dims, lambda i: (0, 0))

    def rows_of(array):
        return pl.BlockSpec((array.shape[0] // steps, array.shape[1]), lambda i: (i, 0))

    raw = (output, input_grad, *expert_grads, tiny)
    raw_specs = [rows_of(r) for r in raw[:5]]
    return pl.pallas_call(
        finish_kernel,
        grid=(steps,),
        out_shape=[
            shape((model_dim, model_dim), f32),
            shape((model_dim, model_dim), f32),
            shape((model_dim, narrow), f32),
            shape((model_dim, narrow), f32),
            shape((16, model_dim), f32),
            shape((8, 128), f32),
            shape((1, 16), jnp.int32),
            *[shape(r.shape, r.dtype) for r in raw[:5]],
            shape((8, 128), f32),
        ],
        in_specs=[full] * 3 + [fixed(*small.shape)] + raw_specs + [fixed(16, 128)],
        out_specs=[full, full, part, part, fixed(16, model_dim), fixed(8, 128), fixed(1, 16)] + raw_specs + [fixed(8, 128)],
        compiler_params=pltpu.CompilerParams(vmem_limit_bytes=62 << 20),
        name="finish_part",
    )(*wide, small, *raw)


def local(
    tokens,
    segment_ids,
    live_mask,
    routes,
    attn_gain,
    w_query,
    key_weight,
    value_weight,
    w_out,
    moe_gain,
    router,
    w_gate,
    w_up,
    w_down,
    cotangent,
):
    sequence_length = tokens.shape[0]
    model_dim = tokens.shape[1]
    experts_all = router.shape[1]
    query_per_key_head = QUERY_HEADS // KEY_VALUE_HEADS
    score_scale = HEAD_SIZE ** (-0.5)
    if lax.axis_size("ep") == 16 and lax.axis_size("hs") == 2:
        middle, input_grad, out_w_grad, query_w_grad, side_grad, small, tiny, own, again, weighted = expert_part(
            segment_ids,
            live_mask,
            routes,
            attn_gain,
            moe_gain,
            router,
            tokens,
            (w_query, key_weight, value_weight, w_out),
            cotangent,
            w_gate[0],
            w_up[0],
            w_down[0],
        )
        output, wide, small, tiny, expert_grads = sum_part(
            (out_w_grad, query_w_grad, side_grad), small, tiny, again, own, weighted, middle
        )
        (
            out_w_grad,
            query_w_grad,
            key_w_grad,
            value_w_grad,
            router_w_grad,
            moe_gain_grad,
            counts,
            output,
            input_grad,
            *expert_grads,
            tiny,
        ) = finish_part(wide, small, output, input_grad, expert_grads, tiny)
        return (
            output,
            input_grad,
            tiny.reshape(model_dim),
            query_w_grad,
            key_w_grad,
            value_w_grad,
            out_w_grad,
            moe_gain_grad.reshape(model_dim),
            router_w_grad.T,
            *[g[None] for g in expert_grads],
            counts.reshape(experts_all),
        )
    segment = segment_ids[0]
    live_row = live_mask[0]
    inputs = tokens.astype(jnp.float32)
    normed_rows, inverse_one = rms_forward(inputs, attn_gain)
    normed_rows_back = normed_rows.astype(jnp.bfloat16)
    query_pre = jnp.dot(normed_rows_back, w_query, preferred_element_type=jnp.float32).reshape(
        sequence_length, QUERY_HEADS, HEAD_SIZE
    )
    key_before_rotary = jnp.dot(
        normed_rows_back, key_weight, preferred_element_type=jnp.float32
    ).reshape(sequence_length, KEY_VALUE_HEADS, HEAD_SIZE)
    value_b = (
        jnp.dot(normed_rows_back, value_weight, preferred_element_type=jnp.float32)
        .astype(jnp.bfloat16)
        .reshape(sequence_length, KEY_VALUE_HEADS, HEAD_SIZE)
    )
    positions = positions_of(segment)
    cosine_table, sine_table = rotary_tables(positions, HEAD_SIZE)
    query_back_rows = rotary(query_pre, cosine_table, sine_table).astype(jnp.bfloat16)
    key_b = rotary(key_before_rotary, cosine_table, sine_table).astype(jnp.bfloat16)
    indices = jnp.arange(sequence_length)
    allowed = (
        (segment[:, None] == segment[None, :])
        & (indices[None, :] <= indices[:, None])
        & ((live_row[None, :] > 0) | (indices[None, :] == indices[:, None]))
    )
    grouped_rows = query_back_rows.reshape(
        sequence_length, KEY_VALUE_HEADS, query_per_key_head, HEAD_SIZE
    )
    scores = (
        jnp.einsum("qgrd,kgd->grqk", grouped_rows, key_b, preferred_element_type=jnp.float32)
        * score_scale
    )
    scores = jnp.where(allowed, scores, -1e30)
    highest = jnp.max(scores, axis=-1, keepdims=True)
    weights_exp = jnp.exp(scores - highest)
    denominator = jnp.sum(weights_exp, axis=-1, keepdims=True)
    log_total = highest + jnp.log(denominator)
    probabilities = weights_exp / denominator
    mixed = jnp.einsum(
        "grqk,kgd->qgrd",
        probabilities.astype(jnp.bfloat16),
        value_b,
        preferred_element_type=jnp.float32,
    )
    mixed_b = mixed.reshape(sequence_length, QUERY_HEADS * HEAD_SIZE).astype(jnp.bfloat16)
    middle = inputs + jnp.dot(mixed_b, w_out, preferred_element_type=jnp.float32)
    moe_normed, inverse_two = rms_forward(middle, moe_gain)
    moe_in = moe_normed.astype(jnp.bfloat16)
    logits = jnp.dot(moe_in, router, preferred_element_type=jnp.float32)
    route_hot = (routes[:, :, None] == jnp.arange(experts_all)[None, None, :]).astype(jnp.float32)
    chosen = jnp.sum(route_hot * logits[:, None, :], axis=-1)
    route_soft = jax.nn.softmax(chosen, axis=-1)
    live_column = live_row.astype(jnp.float32)[:, None]
    route_gates = route_soft * live_column
    counts_local = jnp.sum(route_hot * live_column[:, :, None], axis=(0, 1))
    dense_gates = jnp.sum(route_hot * route_gates[:, :, None], axis=1)
    upstream_all = lax.all_gather(cotangent, "ep", axis=0, tiled=True)
    gate_all = lax.all_gather(w_gate, "hs", axis=0, tiled=True)
    up_all = lax.all_gather(w_up, "hs", axis=0, tiled=True)
    down_all = lax.all_gather(w_down, "hs", axis=0, tiled=True)
    rows_all = lax.all_gather(moe_in, "ep", axis=0, tiled=True)
    gates_all = lax.all_to_all(
        dense_gates.T.reshape(experts_all, 1, sequence_length), "ep", split_axis=0, concat_axis=1, tiled=True
    ).reshape(-1)
    weighted, back, gate_upstream_all, gate_w_grad, up_w_grad, down_w_grad = expert_pass(
        rows_all, upstream_all, gates_all, gate_all, up_all, down_all
    )
    combined = lax.psum_scatter(weighted, "ep", scatter_dimension=0, tiled=True).astype(jnp.float32)
    expert_input_grad = lax.psum_scatter(back, "ep", scatter_dimension=0, tiled=True).astype(jnp.float32)
    gate_upstream_dense = lax.all_to_all(
        gate_upstream_all.reshape(experts_all, 1, sequence_length), "ep", split_axis=0, concat_axis=1, tiled=True
    ).reshape(experts_all, sequence_length).T
    gate_w_grad = sum_halves(gate_w_grad, 1)[None]
    up_w_grad = sum_halves(up_w_grad, 1)[None]
    down_w_grad = sum_halves(down_w_grad, 0)[None]
    output = (middle + combined).astype(jnp.bfloat16)
    upstream = cotangent.astype(jnp.float32)
    gate_upstream = jnp.sum(route_hot * gate_upstream_dense[:, None, :], axis=-1)
    soft_upstream = gate_upstream * live_column
    chosen_grad = route_soft * (
        soft_upstream - jnp.sum(route_soft * soft_upstream, axis=-1, keepdims=True)
    )
    logit_grad = jnp.sum(route_hot * chosen_grad[:, :, None], axis=1).astype(jnp.bfloat16)
    router_w_grad = jnp.einsum("td,te->de", moe_in, logit_grad, preferred_element_type=jnp.float32)
    moe_in_grad = expert_input_grad + jnp.einsum(
        "te,de->td", logit_grad, router, preferred_element_type=jnp.float32
    )
    middle_norm_grad, moe_gain_grad = rms_backward(middle, inverse_two, moe_gain, moe_in_grad)
    middle_grad = upstream + middle_norm_grad
    attn_grad_b = middle_grad.astype(jnp.bfloat16)
    out_w_grad = jnp.einsum("tm,td->md", mixed_b, attn_grad_b, preferred_element_type=jnp.float32)
    attention_mixed_grad = jnp.einsum(
        "td,md->tm", attn_grad_b, w_out, preferred_element_type=jnp.float32
    ).astype(jnp.bfloat16)
    attention_mixed_grad = attention_mixed_grad.reshape(
        sequence_length, KEY_VALUE_HEADS, query_per_key_head, HEAD_SIZE
    )
    scores_again = (
        jnp.einsum("qgrd,kgd->grqk", grouped_rows, key_b, preferred_element_type=jnp.float32)
        * score_scale
    )
    scores_again = jnp.where(allowed, scores_again, -1e30)
    probs_again = jnp.exp(scores_again - log_total)
    prob_grad = jnp.einsum(
        "qgrd,kgd->grqk", attention_mixed_grad, value_b, preferred_element_type=jnp.float32
    )
    value_per_head_grad = jnp.einsum(
        "grqk,qgrd->kgd",
        probs_again.astype(jnp.bfloat16),
        attention_mixed_grad,
        preferred_element_type=jnp.float32,
    )
    value_per_head_grad = value_per_head_grad.astype(jnp.bfloat16).reshape(
        sequence_length, KEY_VALUE_HEADS * HEAD_SIZE
    )
    row_delta = jnp.sum(probs_again * prob_grad, axis=-1, keepdims=True)
    score_grad = (probs_again * (prob_grad - row_delta)).astype(jnp.bfloat16)
    query_rot_grad = (
        jnp.einsum("grqk,kgd->qgrd", score_grad, key_b, preferred_element_type=jnp.float32)
        * score_scale
    )
    rotated_key_grad = (
        jnp.einsum("grqk,qgrd->kgd", score_grad, grouped_rows, preferred_element_type=jnp.float32)
        * score_scale
    )
    query_head_grad = (
        rotary_backward(
            query_rot_grad.reshape(sequence_length, QUERY_HEADS, HEAD_SIZE),
            cosine_table,
            sine_table,
        )
        .astype(jnp.bfloat16)
        .reshape(sequence_length, QUERY_HEADS * HEAD_SIZE)
    )
    key_head_grad = (
        rotary_backward(rotated_key_grad, cosine_table, sine_table)
        .astype(jnp.bfloat16)
        .reshape(sequence_length, KEY_VALUE_HEADS * HEAD_SIZE)
    )
    query_w_grad = jnp.einsum(
        "td,te->de", normed_rows_back, query_head_grad, preferred_element_type=jnp.float32
    )
    key_w_grad = jnp.einsum(
        "td,te->de", normed_rows_back, key_head_grad, preferred_element_type=jnp.float32
    )
    value_w_grad = jnp.einsum(
        "td,te->de", normed_rows_back, value_per_head_grad, preferred_element_type=jnp.float32
    )
    normed_grad = jnp.einsum(
        "te,de->td", query_head_grad, w_query, preferred_element_type=jnp.float32
    )
    normed_grad = normed_grad + jnp.einsum(
        "te,de->td", key_head_grad, key_weight, preferred_element_type=jnp.float32
    )
    normed_grad = normed_grad + jnp.einsum(
        "te,de->td", value_per_head_grad, value_weight, preferred_element_type=jnp.float32
    )
    input_norm_grad, attn_gain_grad = rms_backward(inputs, inverse_one, attn_gain, normed_grad)
    input_grad = middle_grad + input_norm_grad
    (
        attn_gain_grad,
        query_w_grad,
        key_w_grad,
        value_w_grad,
        out_w_grad,
        moe_gain_grad,
        router_w_grad,
        counts,
    ) = lax.psum(
        (
            attn_gain_grad,
            query_w_grad,
            key_w_grad,
            value_w_grad,
            out_w_grad,
            moe_gain_grad,
            router_w_grad,
            counts_local,
        ),
        ("ep", "hs"),
    )
    return (
        output,
        input_grad,
        attn_gain_grad,
        query_w_grad,
        key_w_grad,
        value_w_grad,
        out_w_grad,
        moe_gain_grad,
        router_w_grad,
        gate_w_grad,
        up_w_grad,
        down_w_grad,
        counts.astype(jnp.int32),
    )


def solution(mesh):
    in_specs = (
        P(("ep", "hs"), None),
        P(("ep", "hs"), None),
        P(("ep", "hs"), None),
        P(("ep", "hs"), None),
        P(),
        P(),
        P(),
        P(),
        P(),
        P(),
        P(),
        P("ep", None, "hs"),
        P("ep", None, "hs"),
        P("ep", "hs", None),
        P(("ep", "hs"), None),
    )
    out_specs = (
        P(("ep", "hs"), None),
        P(("ep", "hs"), None),
        P(),
        P(),
        P(),
        P(),
        P(),
        P(),
        P(),
        P("ep", None, "hs"),
        P("ep", None, "hs"),
        P("ep", "hs", None),
        P(),
    )
    return jax.shard_map(local, mesh=mesh, in_specs=in_specs, out_specs=out_specs, check_vma=False)
```

```python
import jax
import jax.numpy as jnp
import numpy as np
from jax import lax
from jax.experimental import pallas as pl
from jax.experimental.pallas import tpu as pltpu
from jax.sharding import PartitionSpec as P

QUERY_HEADS = 16
KEY_VALUE_HEADS = 8
HEAD_SIZE = 64
TOP = 8


EPSILON = 1e-05


def rms_forward(value_rows, norm_gain):
    inverse = lax.rsqrt(jnp.mean(value_rows * value_rows, axis=-1, keepdims=True) + EPSILON)
    return (value_rows * inverse * norm_gain, inverse)


def rms_backward(value_rows, inverse, norm_gain, upstream):
    scaled = upstream * norm_gain
    gain_grad = jnp.sum(upstream * value_rows * inverse, axis=0)
    input_grad = inverse * (
        scaled
        - value_rows * inverse * inverse * jnp.mean(scaled * value_rows, axis=-1, keepdims=True)
    )
    return (input_grad, gain_grad)


def positions_of(segment):
    before = (segment[None, :] < segment[:, None]).astype(jnp.int32)
    return jnp.arange(segment.shape[-1], dtype=jnp.int32) - jnp.sum(before, axis=1)


def rotary_tables(positions, head_dim):
    half_dim = head_dim // 2
    frequency = 10000.0 ** (-(jnp.arange(half_dim, dtype=jnp.float32) * 2.0) / head_dim)
    angles = positions.astype(jnp.float32)[:, None] * frequency[None, :]
    return (jnp.cos(angles)[:, None, :], jnp.sin(angles)[:, None, :])


def rotary(heads, cosine_table, sine_table):
    half_dim = heads.shape[-1] // 2
    first_half = heads[..., :half_dim]
    second_half = heads[..., half_dim:]
    return jnp.concatenate(
        [
            first_half * cosine_table - second_half * sine_table,
            second_half * cosine_table + first_half * sine_table,
        ],
        axis=-1,
    )


def rotary_backward(grads, cosine_table, sine_table):
    half_dim = grads.shape[-1] // 2
    first_half = grads[..., :half_dim]
    second_half = grads[..., half_dim:]
    return jnp.concatenate(
        [
            first_half * cosine_table + second_half * sine_table,
            second_half * cosine_table - first_half * sine_table,
        ],
        axis=-1,
    )


def to_bf16(value):
    return lax.reduce_precision(value, 8, 7)


def expert_pass(rows, upstream, gates, gate_w, up_w, down_w):
    groups, model_dim, width = gate_w.shape
    gate_all = jnp.concatenate([gate_w[j] for j in range(groups)], axis=1)
    up_all = jnp.concatenate([up_w[j] for j in range(groups)], axis=1)
    down_all = down_w.reshape(groups * width, model_dim)
    gate_pre = jnp.dot(rows, gate_all, preferred_element_type=jnp.float32)
    up_pre = jnp.dot(rows, up_all, preferred_element_type=jnp.float32)
    sigmoid_part = jax.nn.sigmoid(gate_pre)
    activated = gate_pre * sigmoid_part
    hidden = (activated * up_pre).astype(jnp.bfloat16)
    total = jnp.zeros(rows.shape, jnp.float32)
    for j in range(groups):
        total = total + to_bf16(
            jnp.dot(hidden[:, j * width : (j + 1) * width], down_w[j], preferred_element_type=jnp.float32)
        )
    total = to_bf16(total)
    upstream_f = upstream.astype(jnp.float32)
    gate_upstream = jnp.sum(upstream_f * total, axis=-1)
    weighted = (gates[:, None] * total).astype(jnp.bfloat16)
    upstream_e = (gates[:, None] * upstream_f).astype(jnp.bfloat16)
    hidden_grad = jnp.einsum("td,fd->tf", upstream_e, down_all, preferred_element_type=jnp.float32)
    up_pre_grad = (hidden_grad * activated).astype(jnp.bfloat16)
    gate_pre_grad = (
        hidden_grad * up_pre * sigmoid_part * (1.0 + gate_pre * (1.0 - sigmoid_part))
    ).astype(jnp.bfloat16)
    down_grad = jnp.einsum("tf,td->fd", hidden, upstream_e, preferred_element_type=jnp.float32)
    gate_grad = jnp.einsum("td,tf->df", rows, gate_pre_grad, preferred_element_type=jnp.float32)
    up_grad = jnp.einsum("td,tf->df", rows, up_pre_grad, preferred_element_type=jnp.float32)
    back = jnp.zeros(rows.shape, jnp.float32)
    for j in range(groups):
        cut = slice(j * width, (j + 1) * width)
        back = back + to_bf16(
            jnp.einsum("tf,df->td", gate_pre_grad[:, cut], gate_w[j], preferred_element_type=jnp.float32)
            + jnp.einsum("tf,df->td", up_pre_grad[:, cut], up_w[j], preferred_element_type=jnp.float32)
        )
    return (weighted, back.astype(jnp.bfloat16), gate_upstream, gate_grad, up_grad, down_grad)


def sum_halves(grad, dim):
    return lax.psum_scatter(
        grad.astype(jnp.bfloat16), "hs", scatter_dimension=dim, tiled=True
    ).astype(jnp.float32)


MESH = pl.DeviceIdType.MESH
UNIT = 16


def place():
    ep, hs = lax.axis_index("ep"), lax.axis_index("hs")
    return (ep // 4, (ep // 2) % 2, ep % 2, hs)


def device(z, x, c, y):
    return (z * 4 + x * 2 + c, y)


def greet(peers):
    barrier = pltpu.get_barrier_semaphore()
    for peer in peers:
        pl.semaphore_signal(barrier, inc=1, device_id=peer, device_id_type=MESH)
    pl.semaphore_wait(barrier, len(peers))


EDGE_ORDER = (0, 1, 2, 6, 5, 4, 7, 3)
MIDDLE_ORDER = (0, 1, 2, 3, 7, 5, 6, 4)


def turn(value, cosine, sine):
    lane = lax.broadcasted_iota(jnp.int32, value.shape, 1) % HEAD_SIZE
    swapped = jnp.where(
        lane < HEAD_SIZE // 2, pltpu.roll(value, 128 - HEAD_SIZE // 2, 1), pltpu.roll(value, HEAD_SIZE // 2, 1)
    )
    return value * cosine + swapped * sine


def contract(left, right, left_dim, right_dim):
    return lax.dot_general(
        left, right, (((left_dim,), (right_dim,)), ((), ())), preferred_element_type=jnp.float32
    )


def expert_kernel(
    segment,
    live,
    routes,
    rotation,
    attn_gain,
    moe_gain,
    router,
    tokens_in,
    w_query_in,
    w_key_in,
    w_value_in,
    w_out_in,
    upstream_in,
    gate_w,
    up_w,
    down_w,
    middle_rows,
    input_grad,
    out_grad,
    query_grad,
    side_grad,
    small,
    tiny,
    own_out,
    again_out,
    weighted_out,
    normed,
    query,
    key_value,
    mixed,
    back,
    cosine,
    sine,
    bias,
    soft_rows,
    keys,
    values,
    streams,
    gates_in,
    gates,
    slopes,
    slopes_in,
    w_gate,
    w_up,
    w_down,
    sums,
    partial,
    from_sibling,
    from_line,
    staged_x,
    staged_y,
    staged_again,
    returned_x,
    returned_y,
    load_sem,
    head_sem,
    store_sem,
    weighted_sem,
    gather_send,
    gather_recv,
    gate_send,
    gate_recv,
    slope_send,
    slope_recv,
    weight_send,
    weight_recv,
    pair_send,
    pair_recv,
    line_send,
    line_recv,
    grad_send,
    grad_recv,
):
    z, x, c, y = place()
    near, far, last = 1 + z % 2, (2 + 3 * z) % 5, 3 - 3 * (z // 2)
    middle = (z == 1) | (z == 2)
    edge = (z == 0) | (z == 3)
    sibling, beside, across = device(z, x, 1 - c, y), device(z, 1 - x, c, y), device(z, x, c, 1 - y)
    line = [((z + k) % 4, (c + d) % 2) for k in range(4) for d in range(2) if k or d]

    def chip(k):
        half = z // 2
        inner = z + half * (3 - 2 * z)
        spot = k + inner * (1 - 3 * (k // 2) + 2 * (k // 3))
        return spot + half * (3 - 2 * spot)

    def remote(source, target, send, recv, peer):
        return pltpu.make_async_remote_copy(
            src_ref=source, dst_ref=target, send_sem=send, recv_sem=recv, device_id=peer, device_id_type=MESH
        )

    own = pltpu.make_async_copy(upstream_in, streams.at[1, z, c], load_sem.at[0])
    weights_own = [
        pltpu.make_async_copy(ref, held.at[x, y], load_sem.at[3 + a])
        for a, (ref, held) in enumerate(((gate_w, w_gate), (up_w, w_up), (down_w, w_down)))
    ]
    tokens = from_sibling.at[1, 0]
    head_loads = [pltpu.make_async_copy(tokens_in, tokens, head_sem.at[0])]
    for r in range(4):
        rows = pl.ds(r * 256, 256)
        for n, (source, target) in enumerate(
            (
                (w_query_in, partial.at[0, r // 2, r % 2]),
                (w_out_in, partial.at[1, r // 2, r % 2]),
                (w_key_in, from_sibling.at[0, r, :, pl.ds(0, 512)]),
                (w_value_in, from_sibling.at[0, r, :, pl.ds(512, 512)]),
            )
        ):
            head_loads.append(pltpu.make_async_copy(source.at[rows, :], target, head_sem.at[1 + r * 4 + n]))
    for copy in (own, *weights_own, *head_loads):
        copy.start()
    greet([device(a, x, b, y) for a, b in line] + [beside, across])

    def gather(s, block, slot, peer):
        piece = streams.at[s, block, c]
        return remote(piece, piece, gather_send.at[s, slot], gather_recv.at[s, block, c], peer)

    def arrive(s, block, core):
        piece = streams.at[s, block, core]
        pltpu.make_async_copy(piece, piece, gather_recv.at[s, block, core]).wait()

    def gather_own(s):
        gather(s, z, 0, device(near, x, c, y)).start()
        gather(s, z, 2, sibling).start()

        @pl.when(middle)
        def _():
            gather(s, z, 1, device(far, x, c, y)).start()

    own.wait()
    gather_own(1)
    weight_copies = []
    for a, held in enumerate((w_gate, w_up, w_down)):
        weights_own[a].wait()
        for n, peer in enumerate((across, beside)):
            piece = held.at[x, y]
            weight_copies.append(
                remote(piece, piece, weight_send.at[n, a], weight_recv.at[x, y, a], peer)
            )
    for copy in weight_copies:
        copy.start()
    upper, lower = pl.ds(0, 128), pl.ds(128, 128)

    def relay(n, expert, group, peer):
        if n < 2:
            piece = (w_gate, w_up)[n].at[expert, group]
        else:
            piece = w_down.at[expert, group, (upper, lower)[n - 2], :]
        return remote(piece, piece, weight_send.at[2, n], weight_recv.at[expert, group, n], peer)

    def corner_here():
        for n in range(4):
            relay(n, 1 - x, 1 - y, beside).wait_recv()

    def weights_here(expert, group):
        for a, held in enumerate((w_gate, w_up, w_down)):
            piece = held.at[expert, group]
            pltpu.make_async_copy(piece, piece, weight_recv.at[expert, group, a]).wait()

    def zero(u, carry):
        for e in (0, 1):
            for a in range(3):
                sums[e, a, u // 16, pl.ds(pl.multiple_of((u % 16) * 16, 16), 16), :] = jnp.zeros(
                    (16, 1024), jnp.float32
                )
            partial[e, u // 8, (u // 4) % 2, pl.ds(pl.multiple_of((u % 4) * 64, 64), 64), :] = jnp.zeros(
                (64, 1024), jnp.bfloat16
            )
        return carry

    def handle(k, order=(1, 0)):
        block = chip(k)
        for s in order:
            arrive(s, block, c)
            gather(s, block, 4 + k, sibling).start()
            if k != 2:

                @pl.when(middle)
                def _():
                    gather(s, block, 2 + (k + 1) // 2, device(far, x, c, y)).start()

    row_id = lax.broadcasted_iota(jnp.int32, (256, 256), 0)
    lane_id = lax.broadcasted_iota(jnp.int32, (256, 256), 1)
    diagonal = row_id == lane_id
    segment_row = segment[...].astype(jnp.float32)
    segment_column = jnp.sum(jnp.where(diagonal, segment_row, 0.0), axis=1, keepdims=True)
    live_row = live[...].astype(jnp.float32)
    before = jnp.sum(jnp.where(segment_row < segment_column, 1.0, 0.0), axis=1, keepdims=True)
    position = lax.broadcasted_iota(jnp.int32, (256, 128), 0).astype(jnp.float32) - before
    angle = position * rotation[...]
    side = lax.broadcasted_iota(jnp.int32, (256, 128), 1) % HEAD_SIZE < HEAD_SIZE // 2
    cosine[...] = jnp.cos(angle)
    angle_sine = jnp.sin(angle)
    sine[...] = jnp.where(side, -angle_sine, angle_sine)
    allowed = (segment_row == segment_column) & (lane_id <= row_id) & ((live_row > 0.0) | diagonal)
    bias[...] = jnp.where(allowed, 0.0, -1e30)
    for copy in head_loads:
        copy.wait()
    start = tokens[...].astype(jnp.float32)
    inverse = lax.rsqrt(jnp.mean(start * start, axis=1, keepdims=True) + EPSILON)
    normed[...] = (start * inverse * attn_gain[...]).astype(jnp.bfloat16)

    def project(source, weight):
        total = jnp.zeros((256, 1024), jnp.float32)
        for r in range(4):
            total = total + contract(source[:, pl.ds(r * 256, 256)], weight(r), 1, 0)
        return total

    made = project(normed, lambda r: partial[0, r // 2, r % 2])
    for p in range(8):
        columns = pl.ds(p * 128, 128)
        query[:, columns] = turn(made[:, p * 128 : p * 128 + 128], cosine[...], sine[...]).astype(jnp.bfloat16)
    made = project(normed, lambda r: from_sibling[0, r])
    for p in range(4):
        columns = pl.ds(p * 128, 128)
        key_value[:, columns] = turn(made[:, p * 128 : p * 128 + 128], cosine[...], sine[...]).astype(jnp.bfloat16)
    key_value[:, pl.ds(512, 512)] = made[:, 512:].astype(jnp.bfloat16)
    for g in range(8):
        keys[g] = key_value[:, pl.ds(g * 64, 64)]
        values[g] = key_value[:, pl.ds(512 + g * 64, 64)]

    def attend(g, carry):
        columns = pl.ds(pl.multiple_of(g * 128, 128), 128)
        pair = query[:, columns]
        found = []
        for r in (0, 1):
            scores = contract(pair[:, r * 64 : r * 64 + 64], keys[g], 1, 1) * HEAD_SIZE ** (-0.5) + bias[...]
            weights = jnp.exp(scores - jnp.max(scores, axis=1, keepdims=True))
            probs = (weights / jnp.sum(weights, axis=1, keepdims=True)).astype(jnp.bfloat16)
            found.append(contract(probs, values[g], 1, 0))
        mixed[:, columns] = jnp.concatenate(found, axis=1).astype(jnp.bfloat16)
        return carry

    lax.fori_loop(0, 8, attend, 0)

    @pl.when(edge)
    def _():
        gather(1, z, 1, device(far, x, c, y)).start()

    handle(1, (1,))
    mid = start + project(mixed, lambda r: partial[1, r // 2, r % 2])
    middle_rows[...] = mid
    inverse = lax.rsqrt(jnp.mean(mid * mid, axis=1, keepdims=True) + EPSILON)
    streams[0, z, c] = (mid * inverse * moe_gain[...]).astype(jnp.bfloat16)
    gather_own(0)
    logits = contract(router[...], streams[0, z, c], 1, 1)
    expert_id = lax.broadcasted_iota(jnp.int32, (16, 256), 0)
    routed = routes[pl.ds(0, 1), :] == expert_id
    for n in range(1, TOP):
        routed = routed | (routes[pl.ds(n, 1), :] == expert_id)
    logits = jnp.where(routed, logits, -1e30)
    raised = jnp.where(routed, jnp.exp(logits - jnp.max(logits, axis=0, keepdims=True)), 0.0)
    soft = raised / jnp.sum(raised, axis=0, keepdims=True)
    soft_rows[...] = soft
    held_gates = soft * live_row
    for e in range(16):
        gates_in[e // 4, e % 2, pl.ds((e // 2) % 2, 1), :] = held_gates[e : e + 1, :]
    count = jnp.sum(jnp.where(routed, live_row, 0.0), axis=1, keepdims=True)
    square = lax.broadcasted_iota(jnp.int32, (16, 128), 0) == lax.broadcasted_iota(jnp.int32, (16, 128), 1)
    small[...] = jnp.zeros((24, 1024), jnp.float32)
    tiny[pl.ds(8, 8), :] = jnp.zeros((8, 128), jnp.float32)
    tiny[pl.ds(8, 1), :] = jnp.sum(jnp.where(square, count, 0.0), axis=0, keepdims=True)
    gate_copies = [
        remote(
            gates_in.at[a, b], gates.at[z, c], gate_send.at[n], gate_recv.at[z, c], device(a, x, b, y)
        )
        for n, (a, b) in enumerate(line)
    ]
    for copy in gate_copies:
        copy.start()
    gates[z, c] = gates_in[z, c]
    lax.fori_loop(0, 32, zero, 0)

    @pl.when(edge)
    def _():
        gather(0, z, 0, device(near, x, c, y)).wait_send()
        gather(0, z, 1, device(far, x, c, y)).start()

    @pl.when(middle)
    def _():
        handle(2, (1,))
        handle(3, (1,))

    handle(1, (0,))
    for a, b in line:
        pltpu.make_async_copy(gates.at[a, b], gates.at[a, b], gate_recv.at[a, b]).wait()
    weights_here(x, 1 - y)
    weights_here(1 - x, y)
    relays = [relay(n, x, 1 - y, beside) for n in (0, 2)] + [relay(n, 1 - x, y, across) for n in (1, 3)]
    for copy in relays:
        copy.start()

    def compute(expert, block, core):
        diagonal = lax.broadcasted_iota(jnp.int32, (256, 256), 0) == lax.broadcasted_iota(jnp.int32, (256, 256), 1)
        gate_row = gates[block, core, pl.ds(expert, 1), :]
        gate = jnp.sum(jnp.where(diagonal, gate_row, 0.0), axis=1, keepdims=True)
        rows = streams[0, block, core]
        total = jnp.zeros((256, 1024), jnp.float32)
        kept = []
        for j in (0, 1):
            gate_pre = contract(rows, w_gate[expert, j], 1, 0)
            up_pre = contract(rows, w_up[expert, j], 1, 0)
            sigmoid_part = jax.nn.sigmoid(gate_pre)
            activated = gate_pre * sigmoid_part
            hidden = (activated * up_pre).astype(jnp.bfloat16)
            part = contract(hidden, w_down[expert, j], 1, 0)
            total = total + part.astype(jnp.bfloat16).astype(jnp.float32)
            inner = up_pre * sigmoid_part * (1.0 + gate_pre * (1.0 - sigmoid_part))
            kept.append((activated, inner, hidden))
        total = total.astype(jnp.bfloat16).astype(jnp.float32)
        upstream = streams[1, block, core].astype(jnp.float32)
        slope = jnp.sum(upstream * total, axis=1, keepdims=True)
        slopes[block, core, pl.ds(expert, 1), :] = jnp.sum(
            jnp.where(diagonal, slope, 0.0), axis=0, keepdims=True
        )
        weighted = gate * total + partial[1, block, core].astype(jnp.float32)
        partial[1, block, core] = weighted.astype(jnp.bfloat16)
        upstream = (gate * upstream).astype(jnp.bfloat16)
        back = jnp.zeros((256, 1024), jnp.float32)
        for j in (0, 1):
            activated, inner, hidden = kept[j]
            hidden_grad = contract(upstream, w_down[expert, j], 1, 1)
            up_grad = (hidden_grad * activated).astype(jnp.bfloat16)
            gate_grad = (hidden_grad * inner).astype(jnp.bfloat16)
            sums[expert, 0, j] += contract(gate_grad, rows, 0, 0)
            sums[expert, 1, j] += contract(up_grad, rows, 0, 0)
            sums[expert, 2, j] += contract(hidden, upstream, 0, 0)
            step = contract(gate_grad, w_gate[expert, j], 1, 1) + contract(up_grad, w_up[expert, j], 1, 1)
            back = back + step.astype(jnp.bfloat16).astype(jnp.float32)
        back = back + partial[0, block, core].astype(jnp.float32)
        partial[0, block, core] = back.astype(jnp.bfloat16)

    def grad_copy(n, source, target, peer):
        return remote(source, target, grad_send.at[n], grad_recv.at[n], peer)

    def pair_copy(s, block):
        return remote(
            partial.at[s, block, 1 - c],
            from_sibling.at[s, block],
            pair_send.at[s, block],
            pair_recv.at[s, block],
            sibling,
        )

    def line_copy(s, block, slot, peer):
        return remote(
            partial.at[s, block, c],
            from_line.at[s, slot],
            line_send.at[s, block],
            line_recv.at[s, slot],
            device(peer, x, c, y),
        )

    def line_wait(s, slot):
        piece = from_line.at[s, slot]
        pltpu.make_async_copy(piece, piece, line_recv.at[s, slot]).wait()

    def add_to(s, block, ref):
        def body(u, carry):
            at = pl.ds(pl.multiple_of(u * 32, 32), 32)
            value = partial[s, block, c, at, :].astype(jnp.float32) + ref[at, :].astype(jnp.float32)
            partial[s, block, c, at, :] = value.astype(jnp.bfloat16)
            return carry

        lax.fori_loop(0, 8, body, 0)

    at_edge = (z * z - 3 * z + 2) // 2
    orders = [sum(code << (3 * t) for t, code in enumerate(codes)) for codes in (EDGE_ORDER, MIDDLE_ORDER)]
    order = at_edge * orders[0] + (1 - at_edge) * orders[1]

    def step(i, carry):
        t = i // 2
        code = lax.shift_right_logical(order, 3 * t) % 8
        again = at_edge * ((t // 3) % 2 + t // 7) + (1 - at_edge) * (t // 4)
        k = code % 4
        expert = x + (code // 4) * (1 - 2 * x)
        block, core = chip(k), (c + i + again) % 2

        @pl.when((i == 2) & middle)
        def _():
            handle(2, (0,))

        @pl.when((i == 4) & middle)
        def _():
            handle(3, (0,))

        @pl.when((i == 4) & edge)
        def _():
            handle(2)

        @pl.when((i == 12) & edge)
        def _():
            handle(3)

        @pl.when((i == 8) & middle | (i == 6) & edge)
        def _():
            corner_here()

        @pl.when((i % 2 == 1) & (again == 0))
        def _():
            for s in (0, 1):
                arrive(s, block, 1 - c)

        compute(expert, block, core)

        @pl.when((i % 2 == 0) & (again == 1))
        def _():
            for s in (0, 1):
                pair_copy(s, block).start()

        @pl.when((i % 2 == 1) & (again == 1))
        def _():
            for s in (0, 1):
                pair_copy(s, block).wait_recv()
                add_to(s, block, from_sibling.at[s, block])

            @pl.when(edge & (k == 2))
            def _():
                line_copy(0, block, 2, near).start()

            @pl.when(edge & (k == 1))
            def _():
                line_copy(0, block, 1, near).start()

            @pl.when(edge & (k == 3))
            def _():
                line_copy(0, block, 2, last).start()

            @pl.when(middle & (k == 3))
            def _():
                line_copy(0, block, 1, last).start()

            @pl.when(middle & (k == 2))
            def _():
                line_copy(0, block, 0, far).start()

        return carry

    lax.fori_loop(0, 16, step, 0)
    low, high = pl.ds(0, 512), pl.ds(512, 512)

    def each(body):
        def rows_of(u, carry):
            at = pl.ds(pl.multiple_of(u * 32, 32), 32)
            for a in range(3):
                body(a, at)
            return carry

        lax.fori_loop(0, 8, rows_of, 0)

    def stage_low(a, at):
        for j in (0, 1):
            staged_x[j, a, at, :] = sums[1 - x, a, j, at, low].astype(jnp.bfloat16)

    def stage_high(a, at):
        staged_y[0, a, at, :] = sums[1 - x, a, 1 - y, at, high].astype(jnp.bfloat16)
        staged_y[1, a, at, :] = sums[x, a, 1 - y, at, high].astype(jnp.bfloat16)

    each(stage_low)
    grad_copy(0, staged_x, returned_x, beside).start()
    each(stage_high)
    grad_copy(1, staged_y, returned_y, across).start()
    slope_copies = [
        remote(
            slopes.at[a, b], slopes_in.at[z, c], slope_send.at[n], slope_recv.at[z, c], device(a, x, b, y)
        )
        for n, (a, b) in enumerate(line)
    ]
    for copy in slope_copies:
        copy.start()
    slopes_in[z, c] = slopes[z, c]


    weighted_stores = [
        pltpu.make_async_copy(partial.at[1, k, c], weighted_out.at[k], weighted_sem.at[k]) for k in range(4)
    ]
    for copy in weighted_stores:
        copy.start()

    @pl.when(middle)
    def _():
        line_wait(0, 2)
        add_to(0, near, from_line.at[0, 2])
        line_copy(0, near, 0, near).start()

    gather(1, z, 0, device(near, x, c, y)).wait_send()

    @pl.when(middle)
    def _():
        gather(0, z, 0, device(near, x, c, y)).wait_send()

    for s in (0, 1):
        gather(s, z, 1, device(far, x, c, y)).wait_send()
        gather(s, z, 2, sibling).wait_send()
        for k in (1, 2, 3):
            gather(s, chip(k), 4 + k, sibling).wait_send()

        @pl.when(middle)
        def _():
            for k in (1, 3):
                gather(s, chip(k), 2 + (k + 1) // 2, device(far, x, c, y)).wait_send()

    for copy in (*gate_copies, *weight_copies, *relays):
        copy.wait_send()

    def query_weight(r):
        return streams.at[0, chip(1 + r // 2), r % 2]

    reloads = []
    for r in range(4):
        rows = pl.ds(r * 256, 256)
        for n, (source, target) in enumerate(
            (
                (w_out_in, from_sibling.at[1, r]),
                (w_query_in, query_weight(r)),
                (w_key_in, from_sibling.at[0, r, :, pl.ds(0, 512)]),
                (w_value_in, from_sibling.at[0, r, :, pl.ds(512, 512)]),
            )
        ):
            reloads.append(pltpu.make_async_copy(source.at[rows, :], target, head_sem.at[1 + r * 4 + n]))
    for copy in reloads:
        copy.start()

    def combined(s, slots, body_of):
        for slot in slots:
            line_wait(s, slot)

        def body(u, carry):
            at = pl.ds(pl.multiple_of(u * 32, 32), 32)
            value = partial[s, z, c, at, :].astype(jnp.float32)
            for slot in slots:
                value = value + from_line[s, slot, at, :].astype(jnp.float32)
            body_of(at, value)
            return carry

        lax.fori_loop(0, 8, body, 0)

    def finish(s, body_of):
        @pl.when(middle)
        def _():
            combined(s, (0, 1), body_of)

        @pl.when(edge)
        def _():
            combined(s, (0, 1, 2), body_of)

    def store_back(at, value):
        back[at, :] = value

    finish(0, store_back)
    for a, b in line:
        pltpu.make_async_copy(slopes_in.at[a, b], slopes_in.at[a, b], slope_recv.at[a, b]).wait()
    upstream = streams[1, z, c].astype(jnp.float32)
    slope_rows = jnp.concatenate([slopes_in[e // 4, e % 2, pl.ds((e // 2) % 2, 1), :] for e in range(16)], axis=0)
    soft_slope = slope_rows * live[...].astype(jnp.float32)
    soft_t = soft_rows[...]
    dlogits = soft_t * (soft_slope - jnp.sum(soft_t * soft_slope, axis=0, keepdims=True))
    dlogits = dlogits.astype(jnp.bfloat16)
    small[pl.ds(0, 16), :] = contract(dlogits, streams[0, z, c], 1, 0)
    dmoe_in = back[...] + contract(dlogits, router[...], 0, 0)
    mid = middle_rows[...]
    inverse = lax.rsqrt(jnp.mean(mid * mid, axis=1, keepdims=True) + EPSILON)
    small[pl.ds(17, 1), :] = jnp.sum(dmoe_in * mid * inverse, axis=0, keepdims=True)
    scaled = dmoe_in * moe_gain[...]
    dmiddle = upstream + inverse * (
        scaled - mid * inverse * inverse * jnp.mean(scaled * mid, axis=1, keepdims=True)
    )
    input_grad[...] = dmiddle
    dattn = dmiddle.astype(jnp.bfloat16)
    outgoing = []

    def send_out(source, target):
        copy = pltpu.make_async_copy(source, target, store_sem.at[len(outgoing)])
        copy.start()
        outgoing.append(copy)

    def column_grad(left, right, held, target):
        for r in range(4):
            rows = contract(left[:, pl.ds(r * 256, 256)], right, 0, 0).astype(jnp.bfloat16)
            for n in range(4):
                held[n // 2, n % 2, pl.ds(r * 256, 256), :] = rows[:, n * 256 : n * 256 + 256]
        for n in range(4):
            send_out(held.at[n // 2, n % 2], target.at[:, pl.ds(n * 256, 256)])

    column_grad(mixed, dattn, w_gate, out_grad)
    for copy in reloads:
        copy.wait()
    mixed_slope, query_slope, side_slope = w_down.at[0, 0], w_down.at[0, 1], w_down.at[1, 0]
    for r in range(4):
        mixed_slope[:, pl.ds(r * 256, 256)] = contract(dattn, from_sibling[1, r], 1, 1).astype(jnp.bfloat16)
    scale = HEAD_SIZE ** (-0.5)

    def attend_back(p, carry):
        wide = pl.ds(pl.multiple_of(p * 256, 256), 256)
        queries, slopes_here = query[:, wide], mixed_slope[:, wide]
        key_slopes, value_slopes, query_slopes = [], [], []
        for n in (0, 1):
            key_g, value_g = keys[2 * p + n], values[2 * p + n]
            key_slope = jnp.zeros((256, 64), jnp.float32)
            value_slope = jnp.zeros((256, 64), jnp.float32)
            for r in (0, 1):
                cut = slice(n * 128 + r * 64, n * 128 + r * 64 + 64)
                query_h, slope_h = queries[:, cut], slopes_here[:, cut]
                scores = contract(query_h, key_g, 1, 1) * scale + bias[...]
                weights = jnp.exp(scores - jnp.max(scores, axis=1, keepdims=True))
                probs = weights / jnp.sum(weights, axis=1, keepdims=True)
                prob_slope = contract(slope_h, value_g, 1, 1)
                value_slope = value_slope + contract(probs.astype(jnp.bfloat16), slope_h, 0, 0)
                delta = jnp.sum(probs * prob_slope, axis=1, keepdims=True)
                score_slope = (probs * (prob_slope - delta)).astype(jnp.bfloat16)
                query_slopes.append(contract(score_slope, key_g, 1, 0) * scale)
                key_slope = key_slope + contract(score_slope, query_h, 0, 0) * scale
            key_slopes.append(key_slope)
            value_slopes.append(value_slope)
        for n in (0, 1):
            pair = turn(jnp.concatenate(query_slopes[2 * n : 2 * n + 2], axis=1), cosine[...], -sine[...])
            query_slope[:, pl.ds(pl.multiple_of(p * 256 + n * 128, 128), 128)] = pair.astype(jnp.bfloat16)
        pair = turn(jnp.concatenate(key_slopes, axis=1), cosine[...], -sine[...])
        side_slope[:, pl.ds(pl.multiple_of(p * 128, 128), 128)] = pair.astype(jnp.bfloat16)
        pair = jnp.concatenate(value_slopes, axis=1)
        side_slope[:, pl.ds(pl.multiple_of(512 + p * 128, 128), 128)] = pair.astype(jnp.bfloat16)
        return carry

    lax.fori_loop(0, 4, attend_back, 0)

    column_grad(normed, query_slope[...], w_up, query_grad)
    for r in range(4):
        rows = contract(normed[:, pl.ds(r * 256, 256)], side_slope[...], 0, 0).astype(jnp.bfloat16)
        streams[1, chip(1 + r // 2), r % 2] = rows
        send_out(streams.at[1, chip(1 + r // 2), r % 2], side_grad.at[pl.ds(r * 256, 256), :])
    dnormed = jnp.concatenate(
        [
            contract(query_slope[...], query_weight(r)[...], 1, 1)
            + contract(side_slope[...], from_sibling[0, r], 1, 1)
            for r in range(4)
        ],
        axis=1,
    )
    tokens_again = pltpu.make_async_copy(tokens_in, w_down.at[1, 1], head_sem.at[0])
    tokens_again.start()
    tokens_again.wait()
    start = w_down[1, 1].astype(jnp.float32)
    inverse = lax.rsqrt(jnp.mean(start * start, axis=1, keepdims=True) + EPSILON)
    gain_slope = jnp.sum(dnormed * start * inverse, axis=0, keepdims=True)
    for r in range(8):
        tiny[pl.ds(r, 1), :] = gain_slope[:, r * 128 : r * 128 + 128]
    scaled = dnormed * attn_gain[...]
    input_grad[...] += inverse * (
        scaled - start * inverse * inverse * jnp.mean(scaled * start, axis=1, keepdims=True)
    )

    grad_copy(0, staged_x, returned_x, beside).wait_recv()
    grad_copy(1, staged_y, returned_y, across).wait_recv()

    def stage_again(a, at):
        value = sums[x, a, 1 - y, at, low] + returned_x[1 - y, a, at, :].astype(jnp.float32)
        staged_again[0, a, at, :] = value.astype(jnp.bfloat16)
        value = sums[1 - x, a, y, at, high] + returned_y[0, a, at, :].astype(jnp.float32)
        staged_again[1, a, at, :] = value.astype(jnp.bfloat16)
        sums[x, a, y, at, low] += returned_x[y, a, at, :].astype(jnp.float32)
        sums[x, a, y, at, high] += returned_y[1, a, at, :].astype(jnp.float32)

    each(stage_again)
    send_out(staged_again, again_out)
    for a in range(3):
        send_out(sums.at[x, a, y], own_out.at[a])

    for k in (1, 2, 3):
        line_copy(0, chip(k), 0, near).wait_send()
    for s in (0, 1):
        for k in range(4):
            pair_copy(s, chip(k)).wait_send()
    for copy in slope_copies:
        copy.wait_send()
    grad_copy(0, staged_x, returned_x, beside).wait_send()
    grad_copy(1, staged_y, returned_y, across).wait_send()
    for copy in (*outgoing, *weighted_stores):
        copy.wait()


def expert_part(
    segment_ids,
    live_mask,
    routes,
    attn_gain,
    moe_gain,
    router,
    tokens,
    attention_weights,
    upstream,
    gate_w,
    up_w,
    down_w,
):
    count, model_dim = tokens.shape
    width = gate_w.shape[1]
    vmem, anywhere = pl.BlockSpec(memory_space=pltpu.VMEM), pl.BlockSpec(memory_space=pl.ANY)
    f32, bf16, dma, shape = jnp.float32, jnp.bfloat16, pltpu.SemaphoreType.DMA, jax.ShapeDtypeStruct
    half = HEAD_SIZE // 2
    frequency = np.float32(10000.0) ** (-(np.arange(half, dtype=np.float32) * np.float32(2.0)) / np.float32(HEAD_SIZE))
    rotation = jnp.asarray(np.tile(frequency.astype(np.float32), 4)[None])
    block = (count, model_dim)
    return pl.pallas_call(
        expert_kernel,
        out_shape=[
            shape(block, f32),
            shape(block, f32),
            shape((model_dim, model_dim), bf16),
            shape((model_dim, model_dim), bf16),
            shape((model_dim, model_dim), bf16),
            shape((24, model_dim), f32),
            shape((16, 128), f32),
            shape((3, width, model_dim), f32),
            shape((2, 3, width, model_dim // 2), bf16),
            shape((4, *block), bf16),
        ],
        in_specs=[vmem] * 7 + [anywhere] * 9,
        out_specs=[vmem] * 2 + [anywhere] * 3 + [vmem] * 2 + [anywhere] * 3,
        scratch_shapes=[
            *[pltpu.VMEM(block, bf16)] * 4,
            pltpu.VMEM(block, f32),
            *[pltpu.VMEM((count, 128), f32)] * 2,
            pltpu.VMEM((count, count), f32),
            pltpu.VMEM((16, count), f32),
            pltpu.VMEM((8, count, HEAD_SIZE), bf16),
            pltpu.VMEM((8, count, HEAD_SIZE), bf16),
            pltpu.VMEM((2, 4, 2, *block), bf16),
            *[pltpu.VMEM((4, 2, 8, count), f32)] * 4,
            pltpu.VMEM((2, 2, model_dim, width), bf16),
            pltpu.VMEM((2, 2, model_dim, width), bf16),
            pltpu.VMEM((2, 2, width, model_dim), bf16),
            pltpu.VMEM((2, 3, 2, width, model_dim), f32),
            pltpu.VMEM((2, 4, 2, *block), bf16),
            pltpu.VMEM((2, 4, *block), bf16),
            pltpu.VMEM((1, 3, *block), bf16),
            *[pltpu.VMEM((2, 3, width, model_dim // 2), bf16)] * 5,
            dma((6,)),
            dma((17,)),
            dma((16,)),
            dma((4,)),
            dma((2, 8)),
            dma((2, 4, 2)),
            dma((7,)),
            dma((4, 2)),
            dma((7,)),
            dma((4, 2)),
            dma((3, 4)),
            dma((2, 2, 4)),
            dma((2, 4)),
            dma((2, 4)),
            dma((2, 4)),
            dma((2, 4)),
            dma((2,)),
            dma((2,)),
        ],
        compiler_params=pltpu.CompilerParams(
            collective_id=1, has_side_effects=True, vmem_limit_bytes=63 << 20
        ),
        name="expert_part",
    )(
        segment_ids,
        live_mask,
        routes.T,
        rotation,
        attn_gain[None],
        moe_gain[None],
        router.T,
        tokens,
        *attention_weights,
        upstream,
        gate_w,
        up_w,
        down_w,
    )


ROWS_AT_ONCE = 256
AGAIN_AT = (0, 4, 8)
COMBINE_AT = 9
SMALL_AT = 6


def sum_kernel(
    small,
    tiny,
    out_in,
    query_in,
    side_in,
    again_in,
    own_in,
    weighted_in,
    middle_rows,
    output,
    out_sum,
    query_sum,
    side_sum,
    small_out,
    tiny_out,
    gate_grad,
    up_grad,
    down_grad,
    again,
    returned_again,
    own,
    weighted,
    from_line,
    *rest,
):
    count = 6
    grads, halves, totals, fulls, firsts, seconds, lines = [rest[n * count : (n + 1) * count] for n in range(7)]
    small_sum, small_in, tiny_sum, tiny_in, send, recv, small_send, small_recv, local_sem, load_sem, again_send, again_recv, line_send, line_recv = rest[7 * count :]
    windows = [(ref, pl.ds(n * 512, 512)) for ref in range(3) for n in (0, 1)]
    outs = [(out_sum, query_sum, side_sum)[ref].at[:, :, columns] for ref, columns in windows]
    z, x, c, y = place()
    sibling, beside, across = device(z, x, 1 - c, y), device(z, 1 - x, c, y), device(z, x, c, 1 - y)
    along = [device((z + k) % 4, x, c, y) for k in (1, 2, 3)]
    loads = [
        pltpu.make_async_copy((out_in, query_in, side_in)[ref].at[:, :, columns], grads[i], load_sem.at[i])
        for i, (ref, columns) in enumerate(windows)
    ]
    loads.append(pltpu.make_async_copy(again_in, again, load_sem.at[6]))
    loads.append(pltpu.make_async_copy(own_in, own, load_sem.at[7]))
    loads.append(pltpu.make_async_copy(weighted_in, weighted, load_sem.at[8]))
    for copy in loads:
        copy.start()
    small_sum[0] = small[...].astype(jnp.bfloat16)
    tiny_sum[0] = tiny[...]
    greet([sibling, beside, across] + along)
    again_copies = [
        pltpu.make_async_remote_copy(
            src_ref=again.at[n, a],
            dst_ref=returned_again.at[n, a],
            send_sem=again_send.at[n, a],
            recv_sem=again_recv.at[n, a],
            device_id=peer,
            device_id_type=MESH,
        )
        for a in range(3)
        for n, peer in enumerate((across, beside))
    ]
    near, far, last = 1 + z % 2, (2 + 3 * z) % 5, 3 - 3 * (z // 2)
    middle, edge = (z == 1) | (z == 2), (z == 0) | (z == 3)

    def line_copy(block, piece, slot, peer):
        rows = pl.ds(piece * 64, 64)
        return pltpu.make_async_remote_copy(
            src_ref=weighted.at[block, rows, :],
            dst_ref=from_line.at[slot, rows, :],
            send_sem=line_send.at[block, piece],
            recv_sem=line_recv.at[slot, piece],
            device_id=device(peer, x, c, y),
            device_id_type=MESH,
        )

    def line_wait(slot, piece):
        part = from_line.at[slot, pl.ds(piece * 64, 64), :]
        pltpu.make_async_copy(part, part, line_recv.at[slot, piece]).wait()

    def line_stage(tick):
        @pl.when(edge)
        def _():
            for block, slot, peer, first in ((far, 2, near, 0), (near, 1, near, 4), (last, 2, last, 4)):
                if 0 <= tick - first < 4:
                    line_copy(block, tick - first, slot, peer).start()

        @pl.when(middle)
        def _():
            for block, slot, peer, first in ((last, 1, last, 0), (far, 0, far, 1)):
                if 0 <= tick - first < 4:
                    line_copy(block, tick - first, slot, peer).start()
            if 0 <= tick - COMBINE_AT < 4:
                piece = tick - COMBINE_AT
                line_wait(2, piece)
                for r in (0, 32):
                    at = pl.ds(piece * 64 + r, 32)
                    value = weighted[near, at, :].astype(jnp.float32) + from_line[2, at, :].astype(jnp.float32)
                    weighted[near, at, :] = value.astype(jnp.bfloat16)
                line_copy(near, piece, 0, near).start()

    bits = ((x, y), (y, x))
    partners = ((beside, across), (across, beside))

    def push(i, slot, source, target, peer):
        copy = pltpu.make_async_remote_copy(
            src_ref=source,
            dst_ref=target,
            send_sem=send.at[i, slot],
            recv_sem=recv.at[i, slot],
            device_id=peer,
            device_id_type=MESH,
        )
        copy.start()
        return copy

    def combine(i, target, start, length, terms):
        def body(u, carry):
            value = totals[i][start + u].astype(jnp.float32)
            for ref, base in terms:
                value = value + ref[base + u].astype(jnp.float32)
            target[0][target[1] + u] = value.astype(jnp.bfloat16)
            return carry

        lax.fori_loop(0, length, body, 0)

    copies = {}

    def stage(i, step):
        if step == 0:
            copies[i, 0] = [
                push(i, 0, grads[i].at[pl.ds((1 - c) * 32, 32)], halves[i], sibling)
            ]
        if step == 1:
            copies[i, 0][0].wait_recv()

            def body(u, carry):
                value = grads[i][c * 32 + u].astype(jnp.float32) + halves[i][u].astype(jnp.float32)
                totals[i][u] = value.astype(jnp.bfloat16)
                return carry

            lax.fori_loop(0, 32, body, 0)
            copies[i, 1] = [
                push(
                    i,
                    1 + part,
                    totals[i].at[pl.ds(part * 16 + (1 - bits[part][0]) * 8, 8)],
                    firsts[i].at[part],
                    partners[part][0],
                )
                for part in (0, 1)
            ]
        if step == 2:
            copies[i, 2] = []
            for part in (0, 1):
                copies[i, 1][part].wait_recv()
                base = part * 16 + bits[part][0] * 8
                combine(i, (totals[i], base), base, 8, [(firsts[i].at[part], 0)])
                copies[i, 2].append(
                    push(
                        i,
                        3 + part,
                        totals[i].at[pl.ds(base + (1 - bits[part][1]) * 4, 4)],
                        seconds[i].at[part],
                        partners[part][1],
                    )
                )
        if step == 3:
            copies[i, 3] = []
            for part in (0, 1):
                copies[i, 2][part].wait_recv()
                base = part * 16 + bits[part][0] * 8 + bits[part][1] * 4
                combine(i, (totals[i], base), base, 4, [(seconds[i].at[part], 0)])
                for k in (1, 2, 3):
                    copies[i, 3].append(
                        push(
                            i,
                            5 + part * 3 + k - 1,
                            totals[i].at[base + (z + k) % 4],
                            lines[i].at[part, k - 1],
                            along[k - 1],
                        )
                    )
        if step == 4:
            copies[i, 4] = []
            for part in (0, 1):
                for k in (1, 2, 3):
                    copies[i, 3][part * 3 + k - 1].wait_recv()
                base = part * 16 + bits[part][0] * 8 + bits[part][1] * 4
                combine(
                    i, (fulls[i], c * 32 + base + z), base + z, 1, [(lines[i].at[part], k) for k in (0, 1, 2)]
                )
                for k in (1, 2, 3):
                    piece = fulls[i].at[c * 32 + base + z]
                    copies[i, 4].append(push(i, 11 + part * 3 + k - 1, piece, piece, along[k - 1]))
        if step == 5:
            copies[i, 5] = []
            for part in (0, 1):
                for k in (1, 2, 3):
                    copies[i, 4][part * 3 + k - 1].wait_recv()
                piece = fulls[i].at[pl.ds(c * 32 + part * 16 + bits[part][0] * 8 + bits[part][1] * 4, 4)]
                copies[i, 5].append(push(i, 17 + part, piece, piece, partners[part][1]))
        if step == 6:
            copies[i, 6] = []
            for part in (0, 1):
                copies[i, 5][part].wait_recv()
                piece = fulls[i].at[pl.ds(c * 32 + part * 16 + bits[part][0] * 8, 8)]
                copies[i, 6].append(push(i, 19 + part, piece, piece, partners[part][0]))
        if step == 7:
            for part in (0, 1):
                copies[i, 6][part].wait_recv()
            piece = fulls[i].at[pl.ds(c * 32, 32)]
            copies[i, 7] = [push(i, 21, piece, piece, sibling)]
        if step == 8:
            copies[i, 7][0].wait_recv()
            done = pltpu.make_async_copy(fulls[i], outs[i], local_sem.at[i])
            done.start()
            copies[i, 8] = [done]

    def small_stage(n, step):
        total, arrived = (small_sum, tiny_sum)[n], (small_in, tiny_in)[n]

        def small_push(slot, peer, source, target):
            copy = pltpu.make_async_remote_copy(
                src_ref=total.at[source],
                dst_ref=arrived.at[target],
                send_sem=small_send.at[n, slot],
                recv_sem=small_recv.at[n, slot],
                device_id=peer,
                device_id_type=MESH,
            )
            copy.start()
            copies.setdefault((n, "s", step), []).append(copy)

        if step == 0:
            small_push(0, sibling, 0, 0)
        if step in (1, 2, 3):
            copies[n, "s", step - 1][0].wait_recv()
            value = total[step - 1].astype(jnp.float32) + arrived[step - 1].astype(jnp.float32)
            total[step] = value.astype(total.dtype)
        if step in (1, 2):
            small_push(step, (beside, across)[step - 1], step, step)
        if step == 3:
            for k in (1, 2, 3):
                small_push(2 + k, along[k - 1], 3, 3 + z)
            arrived[3 + z] = total[3]
        if step == 4:
            for copy in copies[n, "s", 3]:
                copy.wait_recv()
            parts = [arrived[3 + k].astype(jnp.float32) for k in range(4)]
            (small_out, tiny_out)[n][...] = (parts[0] + parts[1]) + (parts[2] + parts[3])

    for tick in range(count + 8):
        for i in range(count):
            if tick == i:
                loads[i].wait()
            if 0 <= tick - i <= 8:
                stage(i, tick - i)
        if tick == 0:
            loads[6].wait()
            loads[8].wait()
        if tick in AGAIN_AT:
            part = 2 * AGAIN_AT.index(tick)
            again_copies[part].start()
            again_copies[part + 1].start()
        line_stage(tick)
        if SMALL_AT <= tick <= SMALL_AT + 4:
            small_stage(0, tick - SMALL_AT)
            small_stage(1, tick - SMALL_AT)
    loads[7].wait()
    for copy in again_copies:
        copy.wait_recv()
    for a, target in enumerate((gate_grad, up_grad, down_grad)):
        for n in (0, 1):
            columns = pl.ds(n * 512, 512)
            summed = own[a, :, columns] + returned_again[n, a].astype(jnp.float32)
            if a < 2:
                target[columns, :] = summed.T
            else:
                target[:, columns] = summed

    def finish(slots):
        for slot in slots:
            for piece in range(4):
                line_wait(slot, piece)

        def body(u, carry):
            at = pl.ds(pl.multiple_of(u * 32, 32), 32)
            value = weighted[z, at, :].astype(jnp.float32)
            for slot in slots:
                value = value + from_line[slot, at, :].astype(jnp.float32)
            output[at, :] = (middle_rows[at, :] + value).astype(jnp.bfloat16)
            return carry

        lax.fori_loop(0, 8, body, 0)

    @pl.when(middle)
    def _():
        finish((0, 1))

    @pl.when(edge)
    def _():
        finish((0, 1, 2))

    for block in (near, far, last):
        for piece in range(4):
            line_copy(block, piece, 0, near).wait_send()
    for key_of, made in copies.items():
        for copy in made:
            if key_of[1] == 8:
                copy.wait()
            else:
                copy.wait_send()
    for copy in again_copies:
        copy.wait_send()


def sum_part(wide, small, tiny, again, own, weighted, middle):
    model_dim = small.shape[1]
    vmem, anywhere = pl.BlockSpec(memory_space=pltpu.VMEM), pl.BlockSpec(memory_space=pl.ANY)
    f32, bf16, dma = jnp.float32, jnp.bfloat16, pltpu.SemaphoreType.DMA
    leads = ((64,), (32,), (32,), (64,), (2, 8), (2, 4), (2, 3))
    shape = jax.ShapeDtypeStruct
    width = own.shape[1]
    units = [g.reshape(64, UNIT, model_dim) for g in wide]
    out = pl.pallas_call(
        sum_kernel,
        out_shape=[
            shape(middle.shape, bf16),
            *[shape(u.shape, bf16) for u in units],
            shape(small.shape, f32),
            shape(tiny.shape, f32),
            shape((model_dim, width), f32),
            shape((model_dim, width), f32),
            shape((width, model_dim), f32),
        ],
        in_specs=[vmem] * 2 + [anywhere] * 6 + [vmem],
        out_specs=[vmem] + [anywhere] * 3 + [vmem] * 5,
        scratch_shapes=[
            pltpu.VMEM(again.shape, bf16),
            pltpu.VMEM(again.shape, bf16),
            pltpu.VMEM(own.shape, f32),
            pltpu.VMEM(weighted.shape, bf16),
            pltpu.VMEM((3, *middle.shape), bf16),
            *[pltpu.VMEM((*lead, UNIT, 512), bf16) for lead in leads for _ in range(6)],
            pltpu.VMEM((4, *small.shape), bf16),
            pltpu.VMEM((7, *small.shape), bf16),
            pltpu.VMEM((4, *tiny.shape), f32),
            pltpu.VMEM((7, *tiny.shape), f32),
            dma((6, 22)),
            dma((6, 22)),
            dma((2, 6)),
            dma((2, 6)),
            dma((6,)),
            dma((9,)),
            dma((2, 3)),
            dma((2, 3)),
            dma((4, 4)),
            dma((3, 4)),
        ],
        compiler_params=pltpu.CompilerParams(
            collective_id=0, has_side_effects=True, vmem_limit_bytes=60 << 20
        ),
        name="sum_part",
    )(small, tiny, *units, again, own, weighted, middle)
    return out[0], [o.reshape(model_dim, model_dim) for o in out[1:4]], out[4], out[5], out[6:9]


def finish_kernel(
    out_in,
    query_in,
    side_in,
    small,
    output_in,
    input_grad_in,
    gate_in,
    up_in,
    down_in,
    tiny_in,
    out_grad,
    query_grad,
    key_grad,
    value_grad,
    router_grad,
    gain_grad,
    counts,
    output,
    input_grad,
    gate_grad,
    up_grad,
    down_grad,
    tiny,
):
    for source, target in (
        (input_grad_in, input_grad),
        (gate_in, gate_grad),
        (up_in, up_grad),
        (down_in, down_grad),
        (output_in, output),
    ):
        target[...] = source[...]

    @pl.when(pl.program_id(0) == 0)
    def _():
        tiny[...] = tiny_in[pl.ds(0, 8), :]
        router_grad[...] = small[pl.ds(0, 16), :]
        for r in range(8):
            gain_grad[pl.ds(r, 1), :] = small[pl.ds(17, 1), pl.ds(r * 128, 128)]
        counts[...] = tiny_in[pl.ds(8, 1), pl.ds(0, 16)].astype(jnp.int32)

    out_grad[...] = out_in[...].astype(jnp.float32)
    query_grad[...] = query_in[...].astype(jnp.float32)
    key_grad[...] = side_in[:, :512].astype(jnp.float32)
    value_grad[...] = side_in[:, 512:].astype(jnp.float32)


def finish_part(wide, small, output, input_grad, expert_grads, tiny):
    model_dim = small.shape[1]
    narrow = model_dim // 2
    f32, shape = jnp.float32, jax.ShapeDtypeStruct
    steps = model_dim // ROWS_AT_ONCE
    full = pl.BlockSpec((ROWS_AT_ONCE, model_dim), lambda i: (i, 0))
    part = pl.BlockSpec((ROWS_AT_ONCE, narrow), lambda i: (i, 0))

    def fixed(*dims):
        return pl.BlockSpec(dims, lambda i: (0, 0))

    def rows_of(array):
        return pl.BlockSpec((array.shape[0] // steps, array.shape[1]), lambda i: (i, 0))

    raw = (output, input_grad, *expert_grads, tiny)
    raw_specs = [rows_of(r) for r in raw[:5]]
    return pl.pallas_call(
        finish_kernel,
        grid=(steps,),
        out_shape=[
            shape((model_dim, model_dim), f32),
            shape((model_dim, model_dim), f32),
            shape((model_dim, narrow), f32),
            shape((model_dim, narrow), f32),
            shape((16, model_dim), f32),
            shape((8, 128), f32),
            shape((1, 16), jnp.int32),
            *[shape(r.shape, r.dtype) for r in raw[:5]],
            shape((8, 128), f32),
        ],
        in_specs=[full] * 3 + [fixed(*small.shape)] + raw_specs + [fixed(16, 128)],
        out_specs=[full, full, part, part, fixed(16, model_dim), fixed(8, 128), fixed(1, 16)] + raw_specs + [fixed(8, 128)],
        compiler_params=pltpu.CompilerParams(vmem_limit_bytes=62 << 20),
        name="finish_part",
    )(*wide, small, *raw)


def local(
    tokens,
    segment_ids,
    live_mask,
    routes,
    attn_gain,
    w_query,
    key_weight,
    value_weight,
    w_out,
    moe_gain,
    router,
    w_gate,
    w_up,
    w_down,
    cotangent,
):
    sequence_length = tokens.shape[0]
    model_dim = tokens.shape[1]
    experts_all = router.shape[1]
    query_per_key_head = QUERY_HEADS // KEY_VALUE_HEADS
    score_scale = HEAD_SIZE ** (-0.5)
    if lax.axis_size("ep") == 16 and lax.axis_size("hs") == 2:
        middle, input_grad, out_w_grad, query_w_grad, side_grad, small, tiny, own, again, weighted = expert_part(
            segment_ids,
            live_mask,
            routes,
            attn_gain,
            moe_gain,
            router,
            tokens,
            (w_query, key_weight, value_weight, w_out),
            cotangent,
            w_gate[0],
            w_up[0],
            w_down[0],
        )
        output, wide, small, tiny, expert_grads = sum_part(
            (out_w_grad, query_w_grad, side_grad), small, tiny, again, own, weighted, middle
        )
        (
            out_w_grad,
            query_w_grad,
            key_w_grad,
            value_w_grad,
            router_w_grad,
            moe_gain_grad,
            counts,
            output,
            input_grad,
            *expert_grads,
            tiny,
        ) = finish_part(wide, small, output, input_grad, expert_grads, tiny)
        return (
            output,
            input_grad,
            tiny.reshape(model_dim),
            query_w_grad,
            key_w_grad,
            value_w_grad,
            out_w_grad,
            moe_gain_grad.reshape(model_dim),
            router_w_grad.T,
            *[g[None] for g in expert_grads],
            counts.reshape(experts_all),
        )
    segment = segment_ids[0]
    live_row = live_mask[0]
    inputs = tokens.astype(jnp.float32)
    normed_rows, inverse_one = rms_forward(inputs, attn_gain)
    normed_rows_back = normed_rows.astype(jnp.bfloat16)
    query_pre = jnp.dot(normed_rows_back, w_query, preferred_element_type=jnp.float32).reshape(
        sequence_length, QUERY_HEADS, HEAD_SIZE
    )
    key_before_rotary = jnp.dot(
        normed_rows_back, key_weight, preferred_element_type=jnp.float32
    ).reshape(sequence_length, KEY_VALUE_HEADS, HEAD_SIZE)
    value_b = (
        jnp.dot(normed_rows_back, value_weight, preferred_element_type=jnp.float32)
        .astype(jnp.bfloat16)
        .reshape(sequence_length, KEY_VALUE_HEADS, HEAD_SIZE)
    )
    positions = positions_of(segment)
    cosine_table, sine_table = rotary_tables(positions, HEAD_SIZE)
    query_back_rows = rotary(query_pre, cosine_table, sine_table).astype(jnp.bfloat16)
    key_b = rotary(key_before_rotary, cosine_table, sine_table).astype(jnp.bfloat16)
    indices = jnp.arange(sequence_length)
    allowed = (
        (segment[:, None] == segment[None, :])
        & (indices[None, :] <= indices[:, None])
        & ((live_row[None, :] > 0) | (indices[None, :] == indices[:, None]))
    )
    grouped_rows = query_back_rows.reshape(
        sequence_length, KEY_VALUE_HEADS, query_per_key_head, HEAD_SIZE
    )
    scores = (
        jnp.einsum("qgrd,kgd->grqk", grouped_rows, key_b, preferred_element_type=jnp.float32)
        * score_scale
    )
    scores = jnp.where(allowed, scores, -1e30)
    highest = jnp.max(scores, axis=-1, keepdims=True)
    weights_exp = jnp.exp(scores - highest)
    denominator = jnp.sum(weights_exp, axis=-1, keepdims=True)
    log_total = highest + jnp.log(denominator)
    probabilities = weights_exp / denominator
    mixed = jnp.einsum(
        "grqk,kgd->qgrd",
        probabilities.astype(jnp.bfloat16),
        value_b,
        preferred_element_type=jnp.float32,
    )
    mixed_b = mixed.reshape(sequence_length, QUERY_HEADS * HEAD_SIZE).astype(jnp.bfloat16)
    middle = inputs + jnp.dot(mixed_b, w_out, preferred_element_type=jnp.float32)
    moe_normed, inverse_two = rms_forward(middle, moe_gain)
    moe_in = moe_normed.astype(jnp.bfloat16)
    logits = jnp.dot(moe_in, router, preferred_element_type=jnp.float32)
    route_hot = (routes[:, :, None] == jnp.arange(experts_all)[None, None, :]).astype(jnp.float32)
    chosen = jnp.sum(route_hot * logits[:, None, :], axis=-1)
    route_soft = jax.nn.softmax(chosen, axis=-1)
    live_column = live_row.astype(jnp.float32)[:, None]
    route_gates = route_soft * live_column
    counts_local = jnp.sum(route_hot * live_column[:, :, None], axis=(0, 1))
    dense_gates = jnp.sum(route_hot * route_gates[:, :, None], axis=1)
    upstream_all = lax.all_gather(cotangent, "ep", axis=0, tiled=True)
    gate_all = lax.all_gather(w_gate, "hs", axis=0, tiled=True)
    up_all = lax.all_gather(w_up, "hs", axis=0, tiled=True)
    down_all = lax.all_gather(w_down, "hs", axis=0, tiled=True)
    rows_all = lax.all_gather(moe_in, "ep", axis=0, tiled=True)
    gates_all = lax.all_to_all(
        dense_gates.T.reshape(experts_all, 1, sequence_length), "ep", split_axis=0, concat_axis=1, tiled=True
    ).reshape(-1)
    weighted, back, gate_upstream_all, gate_w_grad, up_w_grad, down_w_grad = expert_pass(
        rows_all, upstream_all, gates_all, gate_all, up_all, down_all
    )
    combined = lax.psum_scatter(weighted, "ep", scatter_dimension=0, tiled=True).astype(jnp.float32)
    expert_input_grad = lax.psum_scatter(back, "ep", scatter_dimension=0, tiled=True).astype(jnp.float32)
    gate_upstream_dense = lax.all_to_all(
        gate_upstream_all.reshape(experts_all, 1, sequence_length), "ep", split_axis=0, concat_axis=1, tiled=True
    ).reshape(experts_all, sequence_length).T
    gate_w_grad = sum_halves(gate_w_grad, 1)[None]
    up_w_grad = sum_halves(up_w_grad, 1)[None]
    down_w_grad = sum_halves(down_w_grad, 0)[None]
    output = (middle + combined).astype(jnp.bfloat16)
    upstream = cotangent.astype(jnp.float32)
    gate_upstream = jnp.sum(route_hot * gate_upstream_dense[:, None, :], axis=-1)
    soft_upstream = gate_upstream * live_column
    chosen_grad = route_soft * (
        soft_upstream - jnp.sum(route_soft * soft_upstream, axis=-1, keepdims=True)
    )
    logit_grad = jnp.sum(route_hot * chosen_grad[:, :, None], axis=1).astype(jnp.bfloat16)
    router_w_grad = jnp.einsum("td,te->de", moe_in, logit_grad, preferred_element_type=jnp.float32)
    moe_in_grad = expert_input_grad + jnp.einsum(
        "te,de->td", logit_grad, router, preferred_element_type=jnp.float32
    )
    middle_norm_grad, moe_gain_grad = rms_backward(middle, inverse_two, moe_gain, moe_in_grad)
    middle_grad = upstream + middle_norm_grad
    attn_grad_b = middle_grad.astype(jnp.bfloat16)
    out_w_grad = jnp.einsum("tm,td->md", mixed_b, attn_grad_b, preferred_element_type=jnp.float32)
    attention_mixed_grad = jnp.einsum(
        "td,md->tm", attn_grad_b, w_out, preferred_element_type=jnp.float32
    ).astype(jnp.bfloat16)
    attention_mixed_grad = attention_mixed_grad.reshape(
        sequence_length, KEY_VALUE_HEADS, query_per_key_head, HEAD_SIZE
    )
    scores_again = (
        jnp.einsum("qgrd,kgd->grqk", grouped_rows, key_b, preferred_element_type=jnp.float32)
        * score_scale
    )
    scores_again = jnp.where(allowed, scores_again, -1e30)
    probs_again = jnp.exp(scores_again - log_total)
    prob_grad = jnp.einsum(
        "qgrd,kgd->grqk", attention_mixed_grad, value_b, preferred_element_type=jnp.float32
    )
    value_per_head_grad = jnp.einsum(
        "grqk,qgrd->kgd",
        probs_again.astype(jnp.bfloat16),
        attention_mixed_grad,
        preferred_element_type=jnp.float32,
    )
    value_per_head_grad = value_per_head_grad.astype(jnp.bfloat16).reshape(
        sequence_length, KEY_VALUE_HEADS * HEAD_SIZE
    )
    row_delta = jnp.sum(probs_again * prob_grad, axis=-1, keepdims=True)
    score_grad = (probs_again * (prob_grad - row_delta)).astype(jnp.bfloat16)
    query_rot_grad = (
        jnp.einsum("grqk,kgd->qgrd", score_grad, key_b, preferred_element_type=jnp.float32)
        * score_scale
    )
    rotated_key_grad = (
        jnp.einsum("grqk,qgrd->kgd", score_grad, grouped_rows, preferred_element_type=jnp.float32)
        * score_scale
    )
    query_head_grad = (
        rotary_backward(
            query_rot_grad.reshape(sequence_length, QUERY_HEADS, HEAD_SIZE),
            cosine_table,
            sine_table,
        )
        .astype(jnp.bfloat16)
        .reshape(sequence_length, QUERY_HEADS * HEAD_SIZE)
    )
    key_head_grad = (
        rotary_backward(rotated_key_grad, cosine_table, sine_table)
        .astype(jnp.bfloat16)
        .reshape(sequence_length, KEY_VALUE_HEADS * HEAD_SIZE)
    )
    query_w_grad = jnp.einsum(
        "td,te->de", normed_rows_back, query_head_grad, preferred_element_type=jnp.float32
    )
    key_w_grad = jnp.einsum(
        "td,te->de", normed_rows_back, key_head_grad, preferred_element_type=jnp.float32
    )
    value_w_grad = jnp.einsum(
        "td,te->de", normed_rows_back, value_per_head_grad, preferred_element_type=jnp.float32
    )
    normed_grad = jnp.einsum(
        "te,de->td", query_head_grad, w_query, preferred_element_type=jnp.float32
    )
    normed_grad = normed_grad + jnp.einsum(
        "te,de->td", key_head_grad, key_weight, preferred_element_type=jnp.float32
    )
    normed_grad = normed_grad + jnp.einsum(
        "te,de->td", value_per_head_grad, value_weight, preferred_element_type=jnp.float32
    )
    input_norm_grad, attn_gain_grad = rms_backward(inputs, inverse_one, attn_gain, normed_grad)
    input_grad = middle_grad + input_norm_grad
    (
        attn_gain_grad,
        query_w_grad,
        key_w_grad,
        value_w_grad,
        out_w_grad,
        moe_gain_grad,
        router_w_grad,
        counts,
    ) = lax.psum(
        (
            attn_gain_grad,
            query_w_grad,
            key_w_grad,
            value_w_grad,
            out_w_grad,
            moe_gain_grad,
            router_w_grad,
            counts_local,
        ),
        ("ep", "hs"),
    )
    return (
        output,
        input_grad,
        attn_gain_grad,
        query_w_grad,
        key_w_grad,
        value_w_grad,
        out_w_grad,
        moe_gain_grad,
        router_w_grad,
        gate_w_grad,
        up_w_grad,
        down_w_grad,
        counts.astype(jnp.int32),
    )


def solution(mesh):
    in_specs = (
        P(("ep", "hs"), None),
        P(("ep", "hs"), None),
        P(("ep", "hs"), None),
        P(("ep", "hs"), None),
        P(),
        P(),
        P(),
        P(),
        P(),
        P(),
        P(),
        P("ep", None, "hs"),
        P("ep", None, "hs"),
        P("ep", "hs", None),
        P(("ep", "hs"), None),
    )
    out_specs = (
        P(("ep", "hs"), None),
        P(("ep", "hs"), None),
        P(),
        P(),
        P(),
        P(),
        P(),
        P(),
        P(),
        P("ep", None, "hs"),
        P("ep", None, "hs"),
        P("ep", "hs", None),
        P(),
    )
    return jax.shard_map(local, mesh=mesh, in_specs=in_specs, out_specs=out_specs, check_vma=False)
```
